32 devices in a mesh: dp: 8 (over z, y), fsdp: 4 (over x, core).
Axes of the slice: x: 2, y: 2, z: 4, core: 2. Of those that a mesh axis runs over, the one named last changes fastest.
Arguments:
- tokens: bfloat16 [8192, 1024], P(('dp', 'fsdp')), may hold values from -6 to 6
- lengths: int32 [8, 6], P('dp'), may hold values from 0 to 1024, as said below
- visibility_mask: int32 [8192], P(('dp', 'fsdp')), may hold values from 0 to 1, as said below
- visible_counts: int32 [8, 4], P('dp', 'fsdp'), may hold values from 0 to 256, as said below
- ln1_gain: float32 [1024], P(('dp', 'fsdp')), may hold values from 0.5 to 1.5
- ln1_bias: float32 [1024], P(('dp', 'fsdp')), may hold values from -1.25 to 1.25
- qkv_weight: float32 [1024, 3072], P(('dp', 'fsdp')), may hold values from -0.1875 to 0.1875
- qkv_bias: float32 [3072], P(('dp', 'fsdp')), may hold values from -1.25 to 1.25
- out_weight: float32 [1024, 1024], P(('dp', 'fsdp')), may hold values from -1.5 to 1.5
- out_bias: float32 [1024], P(('dp', 'fsdp')), may hold values from -1.25 to 1.25
- ln2_gain: float32 [1024], P(('dp', 'fsdp')), may hold values from 0.5 to 1.5
- ln2_bias: float32 [1024], P(('dp', 'fsdp')), may hold values from -1.25 to 1.25
- fc1_weight: float32 [1024, 4096], P(('dp', 'fsdp')), may hold values from -0.1875 to 0.1875
- fc1_bias: float32 [4096], P(('dp', 'fsdp')), may hold values from -1.25 to 1.25
- fc2_weight: float32 [4096, 1024], P(('dp', 'fsdp')), may hold values from -0.09375 to 0.09375
- fc2_bias: float32 [1024], P(('dp', 'fsdp')), may hold values from -1.25 to 1.25
- context_cot: bfloat16 [8192, 1024], P(('dp', 'fsdp')), may hold values from -12 to 12
Outputs:
- target_out: bfloat16 [8192, 1024], P(('dp', 'fsdp'))
- context_out: bfloat16 [8192, 1024], P(('dp', 'fsdp'))
- tokens_grad: bfloat16 [8192, 1024], P(('dp', 'fsdp'))
- ln1_gain_grad: float32 [1024], P(('dp', 'fsdp'))
- ln1_bias_grad: float32 [1024], P(('dp', 'fsdp'))
- qkv_weight_grad: float32 [1024, 3072], P(('dp', 'fsdp'))
- qkv_bias_grad: float32 [3072], P(('dp', 'fsdp'))
- out_weight_grad: float32 [1024, 1024], P(('dp', 'fsdp'))
- out_bias_grad: float32 [1024], P(('dp', 'fsdp'))
- ln2_gain_grad: float32 [1024], P(('dp', 'fsdp'))
- ln2_bias_grad: float32 [1024], P(('dp', 'fsdp'))
- fc1_weight_grad: float32 [1024, 4096], P(('dp', 'fsdp'))
- fc1_bias_grad: float32 [4096], P(('dp', 'fsdp'))
- fc2_weight_grad: float32 [4096, 1024], P(('dp', 'fsdp'))
- fc2_bias_grad: float32 [1024], P(('dp', 'fsdp'))
The draws below stay inside these ranges and needn't reach their ends.
Inputs may be any that keep to these rules, and one draw needn't show every extreme that they name: Each pack's lengths sum to 1024: either images of 196 tokens, or one video of 1024 tokens followed by images of 196 tokens; in both, the last image is shorter if the rest is no multiple of 196. At least one pack holds a video. `visibility_mask`: each pack holds exactly 256 ones. `visible_counts`: each entry is the number of ones of visibility_mask among the 256 tokens of that device.
All inputs are finite; a program needn't handle non-finite values.
Results may differ from the reference program's by a relative error of at most 0.014.
Values may be sent and summed in bfloat16 or wider, within the bound.
A program may use at most 256 MiB of HBM per device.

```python
import math
import jax
import jax.numpy as jnp
from jax import lax

D = 1024
HEADS = 16
HDIM = 64
FF = 4096
TOK_DEV = 256
GRID = 14
FRAMES = 8
IMG = 196
PACK = 1024
PACKS = 8
TOKENS = 8192
VIS_PACK = 256
SLOTS = 6
N_FSDP = 4


def visible_parts(key):
    base_key = jax.random.fold_in(key, 7)
    heavy_key, noise_key, forced_key = jax.random.split(base_key, 3)
    heavy = jax.random.randint(heavy_key, (PACKS, N_FSDP, 1), 1, 9)
    noise = jax.random.randint(noise_key, (PACKS, N_FSDP, TOK_DEV), 0, 4096)
    forced = jax.random.randint(forced_key, (), 0, PACKS)
    boost = ((jnp.arange(PACKS) == forced)[:, None, None] & (jnp.arange(N_FSDP) == 0)[None, :, None]).astype(jnp.int32) * 40000
    scores = (noise * heavy + boost).reshape(PACKS, PACK) * PACK + (PACK - 1 - jnp.arange(PACK, dtype=jnp.int32))[None, :]
    chosen = lax.top_k(scores, VIS_PACK)[1]
    picked = jnp.zeros((PACKS, PACK), jnp.int32).at[jnp.arange(PACKS)[:, None], chosen].set(1)
    return picked


def draw_visibility_mask(key, part):
    return visible_parts(key).reshape(TOKENS).astype(jnp.int32)


def draw_visible_counts(key, part):
    return jnp.sum(visible_parts(key).reshape(PACKS, N_FSDP, TOK_DEV), axis=2).astype(jnp.int32)


def draw_lengths(key, part):
    base_key = jax.random.fold_in(key, 11)
    kind_key, forced_key = jax.random.split(base_key, 2)
    video = jax.random.randint(kind_key, (PACKS,), 0, 4) == 0
    forced = jax.random.randint(forced_key, (), 0, PACKS)
    video = video | (jnp.arange(PACKS) == forced)
    slot_index = jnp.arange(SLOTS, dtype=jnp.int32)
    image_row = jnp.clip(PACK - slot_index * IMG, 0, IMG)
    video_len = min(FRAMES * IMG, PACK)
    remain = PACK - video_len
    video_row = jnp.where(slot_index == 0, video_len, jnp.clip(remain - (slot_index - 1) * IMG, 0, IMG))
    return jnp.where(video[:, None], video_row[None, :], image_row[None, :]).astype(jnp.int32)


def strengthened(entries, rng, source, target, blocks, factor):
    def block_of(axis_at):
        return (jnp.arange(entries.shape[axis_at]) // (entries.shape[axis_at] // blocks)).reshape((-1,) + (1,) * (entries.ndim - 1 - axis_at))

    near = jax.random.permutation(rng, blocks)[block_of(target)]
    second = (block_of(target) + blocks // 2) % blocks
    return jnp.where((block_of(source) == near) | (block_of(source) == second), factor * entries, entries)


def levels(rng, dims, shards, smallest, top_value):
    loudness, own = 1.0, jax.random.fold_in(rng, 6)
    for dim, shards_of in shards:
        draws = jnp.exp(jax.random.uniform(jax.random.fold_in(own, dim), (shards_of,), jnp.float32, smallest / len(shards), top_value / len(shards)))
        loudness = loudness * jnp.repeat(draws, dims[dim] // shards_of).reshape([-1 if axis == dim else 1 for axis in range(len(dims))])
    return loudness


def bell_draw(key, shape, width, reach, cuts=(), kind=jnp.bfloat16):
    factor_of = levels(key, shape, cuts, -0.22, 0.18) if cuts else 1.0
    drawn = jax.random.normal(key, shape, jnp.float32) * width * factor_of
    return jnp.minimum(jnp.maximum(drawn, -reach), reach).astype(kind)


def gaussian_with(own_key, dims, width, most, pieces, heavy, held_as=jnp.bfloat16):
    values = width * jax.random.normal(own_key, dims, jnp.float32)
    if pieces:
        values = values * levels(own_key, dims, pieces, -0.22, 0.18)
    return jnp.clip(strengthened(values, jax.random.fold_in(own_key, 3), *heavy), -most, most).astype(held_as)


def setup_inputs(seed: int = 0) -> dict:
    streams_of = jax.random.split(jax.random.key(seed), 18)
    tokens = bell_draw(streams_of[0], (TOKENS, D), 1.0, 6.0, ((0, 32),))
    lengths = draw_lengths(jax.random.fold_in(streams_of[17], 71), 0)
    visibility_mask = draw_visibility_mask(jax.random.fold_in(streams_of[17], 71), 0)
    visible_counts = draw_visible_counts(jax.random.fold_in(streams_of[17], 71), 0)
    ln1_gain = jnp.clip(1.0 + 0.1 * jax.random.normal(streams_of[4], (D,), jnp.float32), 0.5, 1.5)
    ln1_bias = bell_draw(streams_of[5], (D,), 0.2, 1.25, ((0, 32),), jnp.float32)
    qkv_weight = bell_draw(streams_of[6], (D, 3 * D), D ** -0.5, 0.1875, ((0, 32),), jnp.float32)
    qkv_bias = bell_draw(streams_of[7], (3 * D,), 0.2, 1.25, ((0, 32),), jnp.float32)
    out_weight = bell_draw(streams_of[8], (D, D), (D // 64) ** -0.5, 1.5, ((0, 32),), jnp.float32)
    out_bias = bell_draw(streams_of[9], (D,), 0.2, 1.25, ((0, 32),), jnp.float32)
    ln2_gain = jnp.clip(1.0 + 0.1 * jax.random.normal(streams_of[10], (D,), jnp.float32), 0.5, 1.5)
    ln2_bias = bell_draw(streams_of[11], (D,), 0.2, 1.25, ((0, 32),), jnp.float32)
    fc1_weight = bell_draw(streams_of[12], (D, FF), D ** -0.5, 0.1875, ((0, 32),), jnp.float32)
    fc1_bias = bell_draw(streams_of[13], (FF,), 0.2, 1.25, ((0, 32),), jnp.float32)
    fc2_weight = bell_draw(streams_of[14], (FF, D), FF ** -0.5, 0.09375, ((0, 32),), jnp.float32)
    fc2_bias = bell_draw(streams_of[15], (D,), 0.2, 1.25, ((0, 32),), jnp.float32)
    context_cot = gaussian_with(streams_of[16], (TOKENS, D), 1.0, 12.0, ((0, 32),), (0, 1, 32, 2.75))
    return {"tokens": tokens, "lengths": lengths, "visibility_mask": visibility_mask, "visible_counts": visible_counts, "ln1_gain": ln1_gain, "ln1_bias": ln1_bias, "qkv_weight": qkv_weight, "qkv_bias": qkv_bias, "out_weight": out_weight, "out_bias": out_bias, "ln2_gain": ln2_gain, "ln2_bias": ln2_bias, "fc1_weight": fc1_weight, "fc1_bias": fc1_bias, "fc2_weight": fc2_weight, "fc2_bias": fc2_bias, "context_cot": context_cot}


@jax.custom_vjp
def low(v):
    return lax.optimization_barrier(v.astype(jnp.bfloat16)).astype(jnp.float32)

@jax.custom_vjp
def low_back(v):
    return v

def low_keep(v):
    return (low(v), None)

def low_pass(kept, grad):
    return (grad,)

def back_keep(v):
    return (v, None)

def back_low(kept, grad):
    return (low(grad),)
low.defvjp(low_keep, low_pass)
low_back.defvjp(back_keep, back_low)
exact_prec = lax.Precision.HIGHEST
norm_eps = 1e-06
masked_fill = -1e+30

def layer_norm(inputs, scale_vec, shift_vec):
    center = inputs - lax.optimization_barrier(jnp.mean(inputs, axis=-1, keepdims=True))
    spread = lax.optimization_barrier(jnp.mean(center * center, axis=-1, keepdims=True))
    return center * lax.rsqrt(spread + norm_eps) * scale_vec + shift_vec

def pack_layout(seq_lens):
    seq_lens = seq_lens.astype(jnp.int32)
    seq_ends = jnp.cumsum(seq_lens).astype(jnp.int32)
    places = jnp.arange(PACK, dtype=jnp.int32)
    passed = places[:, None] >= seq_ends[None, :]
    segment = lax.optimization_barrier(jnp.sum(passed.astype(jnp.int32), axis=1))
    before = lax.optimization_barrier(jnp.sum(jnp.where(passed, seq_lens[None, :], 0), axis=1)).astype(jnp.int32)
    return (segment, places - before)

def rope_tables(places):
    frame_index = (places // (GRID * GRID)).astype(jnp.float32)
    grid_row = (places // GRID % GRID).astype(jnp.float32)
    grid_col = (places % GRID).astype(jnp.float32)
    pair_index = jnp.arange(HDIM // 2, dtype=jnp.int32)
    axis_pick = jnp.minimum(pair_index // 11, 2)
    pair_order = (pair_index - 11 * axis_pick).astype(jnp.float32)
    frequency = jnp.exp(pair_order * (-math.log(10000.0) / 11.0))
    angles = (frame_index[:, None] * (axis_pick == 0).astype(jnp.float32)[None, :] + grid_row[:, None] * (axis_pick == 1).astype(jnp.float32)[None, :] + grid_col[:, None] * (axis_pick == 2).astype(jnp.float32)[None, :]) * frequency[None, :]
    return (jnp.cos(angles), jnp.sin(angles))

def rotate(heads, cosine_table, sine_table):
    half_size = heads.shape[-1] // 2
    first_half = heads[..., :half_size]
    second_half = heads[..., half_size:]
    cosine_cols = cosine_table[:, None, :]
    sine_cols = sine_table[:, None, :]
    return jnp.concatenate([first_half * cosine_cols - second_half * sine_cols, second_half * cosine_cols + first_half * sine_cols], axis=-1)

def pack_layer(params, inputs, visible, seq_lens):
    gain_one, shift_one, w_qkv, b_qkv, w_out, b_out, gain_two, shift_two, w_fc1, b_fc1, w_fc2, b_fc2 = [low(weight) for weight in params]
    segment, places = pack_layout(seq_lens)
    cosine_table, sine_table = rope_tables(places)
    row_count = inputs.shape[0]
    normed = low(layer_norm(inputs, gain_one, shift_one))
    joined = low_back(jnp.dot(normed, w_qkv, precision=exact_prec) + b_qkv)
    query_heads = low(rotate(joined[:, :D].reshape(row_count, HEADS, HDIM), cosine_table, sine_table))
    key_heads = low(rotate(joined[:, D:2 * D].reshape(row_count, HEADS, HDIM), cosine_table, sine_table))
    value_heads = low(joined[:, 2 * D:].reshape(row_count, HEADS, HDIM))
    scores = low_back(jnp.einsum('qhd,khd->hqk', query_heads, key_heads, precision=exact_prec) * HDIM ** (-0.5))
    allowed = (segment[:, None] == segment[None, :]) & ((visible[None, :] > 0.5) | (visible[:, None] < 0.5))
    masked = jnp.where(allowed[None], scores, masked_fill)
    row_max = lax.optimization_barrier(jnp.max(masked, axis=-1, keepdims=True))
    raised = jnp.exp(masked - row_max)
    totals = lax.optimization_barrier(jnp.sum(raised, axis=-1, keepdims=True))
    attn_probs = low(raised / totals)
    attended = jnp.einsum('hqk,khd->qhd', attn_probs, value_heads, precision=exact_prec).reshape(row_count, D)
    attended = low(low_back(attended))
    middle = inputs + low_back(jnp.dot(attended, w_out, precision=exact_prec) + b_out)
    second = low(layer_norm(middle, gain_two, shift_two))
    hidden = low_back(jnp.dot(second, w_fc1, precision=exact_prec) + b_fc1)
    activated = low(jax.nn.gelu(hidden, approximate=False))
    result = middle + low_back(jnp.dot(activated, w_fc2, precision=exact_prec) + b_fc2)
    return result * visible[:, None]

def reference(tokens, lengths, visibility_mask, visible_counts, ln1_gain, ln1_bias, qkv_weight, qkv_bias, out_weight, out_bias, ln2_gain, ln2_bias, fc1_weight, fc1_bias, fc2_weight, fc2_bias, context_cot):
    params = tuple((weight.astype(jnp.float32) for weight in (ln1_gain, ln1_bias, qkv_weight, qkv_bias, out_weight, out_bias, ln2_gain, ln2_bias, fc1_weight, fc1_bias, fc2_weight, fc2_bias)))
    inputs = tokens.astype(jnp.float32).reshape(PACKS, PACK, D)
    grouped = visibility_mask.astype(jnp.int32).reshape(PACKS, N_FSDP, TOK_DEV)
    running = jnp.cumsum(grouped, axis=2).astype(jnp.int32)
    visible = (grouped * (running <= visible_counts.astype(jnp.int32)[:, :, None]).astype(jnp.int32)).reshape(PACKS, PACK).astype(jnp.float32)
    pack_block = jax.checkpoint(pack_layer)
    everyone = jnp.ones((PACK,), jnp.float32)

    def target_step(state_in, sliced):
        return (state_in, pack_block(params, sliced[0], everyone, sliced[1]))
    target = lax.scan(target_step, None, (inputs, lengths))[1]

    def context_all(weights, source):

        def scan_step(state_in, sliced):
            return (state_in, pack_block(weights, sliced[0], sliced[1], sliced[2]))
        return lax.scan(scan_step, None, (source, visible, lengths))[1]
    context, pullback = jax.vjp(context_all, params, inputs)
    weight_grads, input_grad = pullback(context_cot.astype(jnp.float32).reshape(PACKS, PACK, D))
    return (target.reshape(TOKENS, D).astype(jnp.bfloat16), context.reshape(TOKENS, D).astype(jnp.bfloat16), input_grad.reshape(TOKENS, D).astype(jnp.bfloat16), weight_grads[0], weight_grads[1], weight_grads[2], weight_grads[3], weight_grads[4], weight_grads[5], weight_grads[6], weight_grads[7], weight_grads[8], weight_grads[9], weight_grads[10], weight_grads[11])
```

```python
import functools
import math
import types

import jax
import jax.numpy as jnp
import numpy as np
from jax import lax
from jax.experimental import pallas as pl
from jax.experimental.pallas import tpu as pltpu
from jax.sharding import PartitionSpec as P

HEADS = 16
HDIM = 64
GRID = 14
VIS_DEV = 64
norm_eps = 1e-06
masked_fill = -1e30
FRAMES = 8
EPS = 1e-06
FILL = -1e30
BF = jnp.bfloat16
F32 = jnp.float32
MESH = pl.DeviceIdType.MESH
NT = (((1,), (1,)), ((), ()))
NN = (((1,), (0,)), ((), ()))
TN = (((0,), (0,)), ((), ()))


def dot(a, b, dims=NN):
    return lax.dot_general(a, b, dims, preferred_element_type=F32)


def trig_table():
    width = FRAMES + 2 * GRID
    lane = np.arange(2 * HDIM)
    pair = lane % (HDIM // 2)
    axis = np.minimum(pair // 11, 2)
    freq = np.exp(((pair - 11 * axis).astype(np.float32)) * np.float32(-math.log(10000.0) / 11.0))
    sign = np.where(lane % HDIM < HDIM // 2, -1.0, 1.0)
    table = np.zeros((128, 4 * HDIM), np.float32)
    row = np.arange(width)
    kind = np.where(row < FRAMES, 0, np.where(row < FRAMES + GRID, 1, 2))
    coord = np.where(kind == 0, row, np.where(kind == 1, row - FRAMES, row - FRAMES - GRID))
    angle = (coord[:, None].astype(np.float32) * freq[None, :].astype(np.float32)).astype(np.float64)
    here = kind[:, None] == axis[None, :]
    table[:width, : 2 * HDIM] = np.where(here, np.cos(angle), 0.0)
    table[:width, 2 * HDIM :] = np.where(here, np.sin(angle) * sign[None, :], 0.0)
    parts = []
    rest = table
    for _ in range(3):
        part = rest.astype(jnp.bfloat16)
        parts.append(part)
        rest = rest - part.astype(np.float32)
    return np.stack(parts)


def norm_stats(v):
    center = v - jnp.mean(v, axis=-1, keepdims=True)
    inv = lax.rsqrt(jnp.mean(center * center, axis=-1, keepdims=True) + EPS)
    return center * inv, inv


def norm_back(v, gain, grad):
    xhat, inv = norm_stats(v)
    gg = grad * gain
    dv = inv * (
        gg - jnp.mean(gg, axis=-1, keepdims=True) - xhat * jnp.mean(gg * xhat, axis=-1, keepdims=True)
    )
    return (
        dv,
        jnp.sum(grad * xhat, axis=0, keepdims=True),
        jnp.sum(grad, axis=0, keepdims=True),
    )


def swap_halves(u):
    lane = lax.broadcasted_iota(jnp.int32, u.shape, 1)
    return jnp.where(
        lax.rem(lane, HDIM) < HDIM // 2,
        pltpu.roll(u, u.shape[1] - HDIM // 2, 1),
        pltpu.roll(u, HDIM // 2, 1),
    )


def column_segment(start, rows, ends):
    row = start + lax.broadcasted_iota(jnp.int32, (rows, 1), 0)
    seg = jnp.zeros((rows, 1), jnp.int32)
    for end in ends:
        seg += (row >= end).astype(jnp.int32)
    return row, seg


ALIASES = dict(N2="N1", PT="N1", D2="w2_v", D1="w1_v", DOo="wo_v", DQo="wqkv_v")


class Sems:
    def __init__(self, send, recv):
        self.send, self.recv, self.used = send, recv, 0

    def take(self):
        at = self.used
        self.used += 1
        return self.send.at[at], self.recv.at[at]


def layer_kernel(dims, names, *refs):
    n, D, FF, T, V = dims
    NF = 4
    R = D // (n * NF)
    RP = R * NF
    HC = FF // (NF * n)
    HF = FF // NF
    C = D // NF
    VP = V * NF
    S_ = T * NF
    last = n // 2 - 1
    given = dict(zip(names, refs))
    g = types.SimpleNamespace(**given, **{a: given[b] for a, b in ALIASES.items()})
    sems = Sems(g.send_sems, g.recv_sems)
    lsem = g.local_sems

    p = lax.axis_index("dp")
    f = lax.axis_index("fsdp")
    f1 = f + 1 - 2 * lax.rem(f, 2)
    f2 = lax.rem(f + 2, NF)
    f3 = NF - 1 - f
    par = lax.rem(p, 2)
    half_p = lax.div(p, 2)
    pos = (1 - par) * half_p + par * (n - 1 - half_p)

    def idx(q):
        q = lax.rem(q + 2 * n, n)
        up = lax.div(q, n // 2)
        return (1 - up) * (2 * q) + up * (2 * (n - 1 - q) + 1)

    right, left = idx(pos + 1), idx(pos - 1)

    pending = []

    def remote(src, dst, to):
        ss, rs = sems.take()
        c = pltpu.make_async_remote_copy(
            src_ref=src, dst_ref=dst, send_sem=ss, recv_sem=rs, device_id=to, device_id_type=MESH
        )
        c.start()
        pending.append(c)
        return c, ss, rs

    def drain(*copies):
        for c in copies:
            pending[:] = [d for d in pending if d is not c]
            c.wait_send()

    def arrival(dst, ss, rs, to):
        return pltpu.make_async_remote_copy(
            src_ref=dst, dst_ref=dst, send_sem=ss, recv_sem=rs, device_id=to, device_id_type=MESH
        )

    to1, to2, to3 = {"fsdp": f1}, {"fsdp": f2}, {"fsdp": f3}
    peers = ((f1, to1), (f2, to2), (f3, to3))

    loads = {}
    for i, (src, dst) in enumerate(
        (
            (g.wqkv, g.wqkv_v),
            (g.w1, g.w1_v),
            (g.wo, g.wo_v),
            (g.small, g.small_v),
            (g.tok, g.TA.at[f]),
            (g.w2, g.w2_v),
            (g.cot, g.CA.at[f]),
            (g.trig, g.trig_v),
        )
    ):
        c = pltpu.make_async_copy(src, dst, lsem.at[i])
        c.start()
        loads[i] = c

    barrier = pltpu.get_barrier_semaphore()
    for to in (to1, to2, to3, {"dp": right}, {"dp": left}):
        pl.semaphore_signal(barrier, inc=1, device_id=to, device_id_type=MESH)

    AS, AQ, WO, A1, A2 = g.AS, g.AQ, g.WO, g.A1, g.A2
    TA, CA = g.TA, g.CA

    loads[0].wait()
    for j in range(NF):
        for t in range(3):
            g.sq[j, :, C * t : C * t + C] = g.wqkv_v[:, D * t + C * j : D * t + C * j + C].astype(BF)
    loads[2].wait()
    WO[p, f] = g.wo_v[...].astype(BF)
    loads[3].wait()
    AS[p, f] = g.small_v[...]
    AQ[p, pl.ds(pl.multiple_of(R * f, R), R), :] = g.sq[f]
    pl.semaphore_wait(barrier, 5)

    def scatter(src, dst):
        got = []
        for fj, to in peers:
            _, ss, rs = remote(src(fj), dst(f), to)
            got.append(arrival(dst(fj), ss, rs, to))
        return got

    got_q = scatter(lambda j: g.sq.at[j], lambda j: AQ.at[p, pl.ds(pl.multiple_of(R * j, R), R), :])
    got_s = scatter(lambda j: AS.at[p, f], lambda j: AS.at[p, j])

    class AllGather4:
        def __init__(self, slot):
            self.slot = slot
            _, self.sx, self.rx = remote(slot(f), slot(f), to2)
            _, self.sc, self.rc = remote(slot(f), slot(f), to1)

        def forward(self):
            arrival(self.slot(f2), self.sx, self.rx, to2).wait_recv()
            _, self.sd, self.rd = remote(self.slot(f2), self.slot(f2), to1)

        def finish(self):
            arrival(self.slot(f1), self.sc, self.rc, to1).wait_recv()
            arrival(self.slot(f3), self.sd, self.rd, to1).wait_recv()

    class ReduceScatter4:
        def __init__(self, part, r1, xs, r2):
            self.part, self.r1, self.xs, self.r2 = part, r1, xs, r2
            self.ca, self.sa, self.ra = remote(part.at[f3], r1.at[1], to1)
            self.cb, self.sb, self.rb = remote(part.at[f1], r1.at[0], to1)

        def forward(self):
            arrival(self.r1.at[1], self.sa, self.ra, to1).wait_recv()
            self.xs[...] = (self.part[f2].astype(F32) + self.r1[1].astype(F32)).astype(BF)
            _, self.sc, self.rc = remote(self.xs, self.r2, to2)

        def finish(self):
            arrival(self.r1.at[0], self.sb, self.rb, to1).wait_recv()
            arrival(self.r2, self.sc, self.rc, to2).wait_recv()

        def total(self):
            return self.part[f].astype(F32) + self.r1[0].astype(F32) + self.r2[...].astype(F32)

    class RingGather:
        def __init__(self, view, rows):
            self.view, self.rows = view, rows
            self.arrivals = []

        def step(self, r):
            for a in self.arrivals:
                a.wait_recv()
            self.arrivals = []
            h = self.rows // 2
            spans = ((0, self.rows), (0, self.rows)) if r < last else ((0, h), (h, h))
            for way, (s, c) in zip((1, -1), spans):
                to, frm = ({"dp": right}, {"dp": left}) if way == 1 else ({"dp": left}, {"dp": right})
                mine = self.view(idx(pos - way * r), s, c)
                _, ss, rs = remote(mine, mine, to)
                self.arrivals.append(arrival(self.view(idx(pos - way * (r + 1)), s, c), ss, rs, frm))

        def finish(self):
            for a in self.arrivals:
                a.wait_recv()
            self.arrivals = []

    def rows_view(ref, offset):
        return lambda slot, s, c: ref.at[slot, pl.ds(offset + s, c), :]

    h = RP // 2
    q_ring = [RingGather(rows_view(AQ, 0), h), RingGather(rows_view(AQ, h), h)]
    w1_ring = [RingGather(rows_view(A1, 0), h), RingGather(rows_view(A1, h), h)]
    w2_ring = [RingGather(rows_view(A2, 0), HC // 2), RingGather(rows_view(A2, HC // 2), HC // 2)]
    o_ring = RingGather(lambda slot, s, c: WO.at[slot, f, pl.ds(s, c), :], R)
    s_ring = RingGather(lambda slot, s, c: AS.at[slot, pl.ds(s, c)], NF)

    class RingReduce:
        def __init__(self, grads, start, rows, st, rr, rl, wire=BF):
            self.G, self.o, self.rows, self.st, self.rr, self.rl = grads, start, rows, st, rr, rl
            self.wire = wire
            self.arrivals = []

        def piece(self, ref, slot, s, c):
            return ref.at[slot, pl.ds(self.o + s, c), :]

        def step(self, r):
            for a in self.arrivals:
                a.wait_recv()
            self.arrivals = []
            o, rows = self.o, self.rows
            hh = rows // 2
            if r == 0:
                far = idx(pos + n // 2)
                self.st[pl.ds(o, rows), :] = self.G[far, pl.ds(o, rows), :].astype(self.wire)
                for buf, s, to, frm in (
                    (self.rr, 0, {"dp": right}, {"dp": left}),
                    (self.rl, hh, {"dp": left}, {"dp": right}),
                ):
                    dst = self.piece(buf, 0, s, hh)
                    _, ss, rs = remote(self.st.at[pl.ds(o + s, hh), :], dst, to)
                    self.arrivals.append(arrival(dst, ss, rs, frm))
                return
            for way, buf, s, to, frm in (
                (1, self.rr, 0, {"dp": right}, {"dp": left}),
                (-1, self.rl, hh, {"dp": left}, {"dp": right}),
            ):
                c = idx(pos + way * (n // 2 - r))
                if r == 1:
                    other = hh - s
                    buf[0, pl.ds(o + s, hh), :] = (
                        buf[0, pl.ds(o + s, hh), :].astype(F32) + self.G[c, pl.ds(o + s, hh), :]
                    ).astype(self.wire)
                    buf[0, pl.ds(o + other, hh), :] = self.G[c, pl.ds(o + other, hh), :].astype(self.wire)
                else:
                    buf[r - 1, pl.ds(o, rows), :] = (
                        buf[r - 1, pl.ds(o, rows), :].astype(F32) + self.G[c, pl.ds(o, rows), :]
                    ).astype(self.wire)
                src, dst = self.piece(buf, r - 1, 0, rows), self.piece(buf, r, 0, rows)
                _, ss, rs = remote(src, dst, to)
                self.arrivals.append(arrival(dst, ss, rs, frm))

        def finish(self):
            for a in self.arrivals:
                a.wait_recv()
            self.arrivals = []

        def total(self):
            o, rows = self.o, self.rows
            return (
                self.G[p, pl.ds(o, rows), :]
                + self.rr[last, pl.ds(o, rows), :].astype(F32)
                + self.rl[last, pl.ds(o, rows), :].astype(F32)
            )

    queue = []

    def svc(count=1):
        for _ in range(count):
            if queue:
                queue.pop(0)()

    o_ring.step(0)
    loads[1].wait()
    for j in range(NF):
        for t in range(n):
            at = HC * (NF * t + j)
            g.s1[j, :, HC * t : HC * t + HC] = g.w1_v[:, at : at + HC].astype(BF)
    A1[p, pl.ds(pl.multiple_of(R * f, R), R), :] = g.s1[f]
    for a in got_q:
        a.wait_recv()
    q_ring[0].step(0)
    q_ring[1].step(0)
    loads[4].wait()
    tok_ag = AllGather4(lambda j: TA.at[j])
    got_1 = scatter(lambda j: g.s1.at[j], lambda j: A1.at[p, pl.ds(pl.multiple_of(R * j, R), R), :])
    for a in got_s:
        a.wait_recv()
    s_ring.step(0)
    loads[5].wait()
    A2[p] = g.w2_v[...].astype(BF)
    o_ring.step(1)
    q_ring[0].step(1)
    q_ring[1].step(1)
    loads[6].wait()
    cot_ag = AllGather4(lambda j: CA.at[j])
    s_ring.step(1)

    ends = []
    total_len = jnp.int32(0)
    for k in range(g.lengths.shape[1]):
        total_len = total_len + g.lengths[0, k]
        ends.append(total_len)
    row, seg = column_segment(0, S_, ends)
    before = jnp.zeros((S_, 1), jnp.int32)
    for k, end in enumerate(ends):
        before += jnp.where(row >= end, g.lengths[0, k], 0)
    place = row - before
    img = GRID * GRID
    frame = jnp.zeros((S_, 1), jnp.int32)
    for t in range(1, FRAMES):
        frame += (place >= img * t).astype(jnp.int32)
    rest = place - img * frame
    grow = jnp.zeros((S_, 1), jnp.int32)
    for t in range(1, GRID):
        grow += (rest >= GRID * t).astype(jnp.int32)
    gcol = rest - GRID * grow
    lane = lax.broadcasted_iota(jnp.int32, (S_, 128), 1)
    hot = (lane == frame) | (lane == grow + FRAMES) | (lane == gcol + (FRAMES + GRID))
    g.OH[...] = jnp.where(hot, 1.0, 0.0).astype(BF)
    o_ring.step(2)
    q_ring[0].step(2)
    q_ring[1].step(2)
    s_ring.step(2)
    loads[7].wait()
    g.CS[...] = sum(dot(g.OH[...], g.trig_v[k]) for k in range(3))
    segrow = jnp.zeros((1, S_), jnp.int32)
    keyrow = lax.broadcasted_iota(jnp.int32, (1, S_), 1)
    for end in ends:
        segrow += (keyrow >= end).astype(jnp.int32)
    o_ring.step(3)
    q_ring[0].step(3)
    q_ring[1].step(3)
    s_ring.step(3)

    vis8 = jnp.concatenate([AS[p, j][4:6, :] for j in range(NF)], axis=0)
    tri = (
        lax.broadcasted_iota(jnp.int32, (128, 128), 0) <= lax.broadcasted_iota(jnp.int32, (128, 128), 1)
    )
    within = dot(vis8.astype(BF), jnp.where(tri, 1.0, 0.0).astype(BF))
    base = jnp.zeros((1, 128), F32)
    pieces, vpieces = [], []
    for k in range(8):
        pieces.append(within[k : k + 1, :] + base)
        vpieces.append(vis8[k : k + 1, :])
        base = base + jnp.sum(vis8[k : k + 1, :], axis=1, keepdims=True)
    incl = jnp.concatenate(pieces, axis=1)
    visrow = jnp.concatenate(vpieces, axis=1)
    rank = jnp.where(visrow > 0.5, incl - 1.0, -1.0).astype(jnp.int32)
    SM = g.SM
    sel = lax.broadcasted_iota(jnp.int32, (VP, S_), 0) == rank
    SM[...] = jnp.where(sel, 1.0, 0.0).astype(BF)
    segv_col = jnp.sum(jnp.where(sel, segrow, 0).astype(F32), axis=1, keepdims=True).astype(jnp.int32)
    seg8 = jnp.broadcast_to(segrow.astype(F32), (8, S_)).astype(BF)
    segv_row = dot(seg8, SM[...], NT)[0:1, :].astype(jnp.int32)

    tok_ag.forward()
    s_ring.finish()
    VEC, BQ = g.VEC, g.BQ
    lane128 = lax.broadcasted_iota(jnp.int32, (n, 128), 1)
    rows0 = [AS[:, j, 0, :] for j in range(NF)]
    rows1 = [AS[:, j, 1, :] for j in range(NF)]
    rows2 = [AS[:, j, 2, :] for j in range(NF)]

    def rounded(v):
        return v.astype(BF).astype(F32)

    def turn(v, by):
        by = by % 128
        return v if by == 0 else pltpu.roll(v, by, 1)

    def put_row(k, piece):
        for q in range(n):
            VEC[k : k + 1, 128 * q : 128 * q + 128] = rounded(piece[q : q + 1, :])

    for k in range(6):
        src = rows0 if k < 4 else rows1
        piece = jnp.zeros((n, 128), F32)
        for j in range(NF):
            piece = jnp.where(lax.div(lane128, R) == j, turn(src[j], R * (j - k % 4)), piece)
        put_row(k, piece)
    for q in range(n):
        VEC[6:7, 128 * q : 128 * q + 128] = rounded(AS[q, f][3:4, :])
    t0 = jnp.where(lane128 < 96, rows2[0], turn(rows2[1], 96))
    t1 = jnp.where(lane128 < 64, turn(rows2[1], -32), turn(rows2[2], 64))
    t2 = jnp.where(lane128 < 32, turn(rows2[2], -64), turn(rows2[3], 32))
    for q in range(n):
        for k, t in enumerate((t0, t1, t2)):
            BQ[0:1, 384 * q + 128 * k : 384 * q + 128 * k + 128] = rounded(t[q : q + 1, :])

    def vec(k):
        return VEC[k : k + 1, :]

    tok_ag.finish()
    N1 = g.N1

    def norm_one(b, _):
        xhat, _inv = norm_stats(TA[b].astype(F32))
        N1[b] = (xhat * vec(0) + vec(1)).astype(BF)
        return 0

    lax.fori_loop(0, NF, norm_one, 0)
    cot_ag.forward()
    for a in got_1:
        a.wait_recv()
    w1_ring[0].step(0)
    w1_ring[1].step(0)
    for r in q_ring:
        r.finish()
    o_ring.finish()
    wo_ag = AllGather4(lambda j: WO.at[:, j])

    queue += [
        lambda: w1_ring[0].step(1),
        lambda: w1_ring[1].step(1),
        lambda: w2_ring[0].step(0),
        lambda: w1_ring[0].step(2),
        lambda: w1_ring[1].step(2),
        lambda: w2_ring[1].step(0),
        lambda: w1_ring[0].step(3),
        lambda: w1_ring[1].step(3),
        lambda: w2_ring[0].step(1),
        lambda: w2_ring[1].step(1),
        lambda: w2_ring[0].step(2),
        lambda: w2_ring[1].step(2),
        lambda: w2_ring[0].step(3),
        lambda: w2_ring[1].step(3),
    ]

    Q, K, W = g.Q, g.K, g.W
    AQf = lambda s: AQ[:, :, s].reshape(D, -1)

    def project(b, _):
        cs = g.CS[pl.ds(pl.multiple_of(b * T, T), T), :]
        for t, dst in enumerate((Q, K, W)):
            out = dot(N1[b], AQ[:, :, C * t : C * t + C].reshape(D, C))
            out = out + BQ[0:1, pl.ds(pl.multiple_of(D * t + C * f, 128), C)]
            rows = pl.ds(pl.multiple_of(b * T, T), T)
            if t == 2:
                dst[rows, :] = out.astype(BF)
                continue
            for hh in range(C // 128):
                u = out[:, 128 * hh : 128 * hh + 128]
                u = (u * cs[:, :128] + swap_halves(u) * cs[:, 128:]).astype(BF)
                dst[rows, 128 * hh : 128 * hh + 128] = u * BF(0.125) if t == 0 else u
        return 0

    lax.fori_loop(0, NF, project, 0)
    svc(2)

    QV, KV, WV = g.QV, g.KV, g.WV
    for src, dst in ((Q, QV), (K, KV), (W, WV)):
        dst[...] = dot(SM[...], src[...]).astype(BF)
    OV, PV = g.OV, g.PV
    lane_c = lax.broadcasted_iota(jnp.int32, (1, C), 1)
    hmask = [jnp.where(lax.div(lane_c, HDIM) == hd, 1.0, 0.0) for hd in range(C // HDIM)]

    def softmax(s):
        e = jnp.exp(s - jnp.max(s, axis=-1, keepdims=True))
        return e * (1.0 / jnp.sum(e, axis=-1, keepdims=True))

    same_v = segv_col == segv_row
    acc = jnp.zeros((VP, C), F32)
    for hd in range(C // HDIM):
        s = dot(QV[...] * hmask[hd].astype(BF), KV[...], NT)
        pr = softmax(jnp.where(same_v, s, FILL))
        PV[hd] = pr
        acc += dot(pr.astype(BF), WV[...]) * hmask[hd]
    OV[f] = acc.astype(BF)
    ov_ag = AllGather4(lambda j: OV.at[j])
    wo_ag.forward()
    svc(2)

    OA = g.OA

    def target_head(hd):
        def block(b, _):
            rows = pl.ds(pl.multiple_of(b * T, T), T)
            s = dot(Q[rows, :] * hmask[hd].astype(BF), K[...], NT)
            _, segq = column_segment(b * T, T, ends)
            pr = softmax(jnp.where(segq == segrow, s, FILL)).astype(BF)
            o = dot(pr, W[...])
            OA[f, rows, HDIM * hd : HDIM * hd + HDIM] = o[:, HDIM * hd : HDIM * hd + HDIM].astype(BF)
            return 0

        lax.fori_loop(0, NF, block, 0)

    cot_ag.finish()
    target_head(0)
    ov_ag.forward()
    svc(2)
    XV, N1V, DY = g.XV, g.N1V, g.DY
    for k in range(4):
        cols = slice(256 * k, 256 * k + 256)
        XV[:, cols] = dot(SM[...], TA[:, :, cols].reshape(S_, 256)).astype(BF)
        DY[:, cols] = dot(SM[...], CA[:, :, cols].reshape(S_, 256)).astype(BF)
        N1V[:, cols] = dot(SM[...], N1[:, :, cols].reshape(S_, 256)).astype(BF)
    svc(2)

    ov_ag.finish()
    wo_ag.finish()

    def out_project(parts, cols):
        return sum(
            dot(parts(j), WO[n // NF * j : n // NF * (j + 1), :, :, cols].reshape(C, -1)) for j in range(NF)
        )

    X1V, N2V = g.X1V, g.N2V
    for k in range(4):
        cols = slice(256 * k, 256 * k + 256)
        X1V[:, cols] = XV[:, cols].astype(F32) + (out_project(lambda j: OV[j], cols) + VEC[4:5, cols])
    xhat, _inv = norm_stats(X1V[...])
    N2V[...] = (xhat * vec(2) + vec(3)).astype(BF)
    svc(2)
    target_head(1)
    svc(1)
    for r in w1_ring:
        pass
    while queue and len(queue) > 6:
        svc(1)
    for r in w1_ring:
        r.finish()

    GV, GP = g.GV, g.GP

    def gelu_parts(hid):
        cdf = 0.5 * (1.0 + lax.erf(hid * (1.0 / math.sqrt(2.0))))
        return cdf

    for k in range(4):
        cols = slice(256 * k, 256 * k + 256)
        hid = dot(N2V[...], A1[:, :, cols].reshape(D, 256)) + VEC[6:7, cols]
        cdf = gelu_parts(hid)
        GV[:, cols] = (hid * cdf).astype(BF)
        GP[:, cols] = cdf + hid * (jnp.exp(-0.5 * hid * hid) * (1.0 / math.sqrt(2.0 * math.pi)))
    svc(1)
    G2, G1, GQ, GO = g.G2, g.G1, g.GQ, g.GO

    def outer(dst, lhs, rhs, width):
        def one(k, _):
            a = lhs[:, pl.ds(pl.multiple_of(128 * k, 128), 128)]
            dst[k] = dot(a, rhs[...], TN)
            return 0

        lax.fori_loop(0, n, one, 0)

    outer(G2, GV, DY, D)
    svc(1)
    hc = HC // 2
    g2_ring = [
        RingReduce(G2, 0, hc, g.st2, g.rr2, g.rl2),
        RingReduce(G2, hc, hc, g.st2, g.rr2, g.rl2),
    ]
    hr = RP // 2
    g1_ring = [
        RingReduce(G1, 0, hr, g.st1, g.rr1, g.rl1),
        RingReduce(G1, hr, hr, g.st1, g.rr1, g.rl1),
    ]
    gq_ring = [
        RingReduce(GQ, 0, hr, g.stq, g.rrq, g.rlq),
        RingReduce(GQ, hr, hr, g.stq, g.rrq, g.rlq),
    ]
    go_ring = RingReduce(GO, 0, R, g.sto, g.rro, g.rlo)
    gs_ring = RingReduce(g.VG, 0, 16, g.sts, g.rrs, g.rls, F32)
    queue += [lambda: g2_ring[0].step(0), lambda: g2_ring[1].step(0)]
    target_head(2)
    svc(2)
    target_head(3)
    oa_ag = AllGather4(lambda j: OA.at[j])
    svc(2)
    while queue:
        svc(1)
    for r in w2_ring:
        r.finish()
    queue += [
        lambda: g2_ring[0].step(1),
        lambda: g2_ring[1].step(1),
        lambda: g2_ring[0].step(2),
        lambda: g2_ring[1].step(2),
        lambda: g2_ring[0].step(3),
        lambda: g2_ring[1].step(3),
    ]

    DH, PN = g.DH, g.PN
    VG = g.VG
    zero_row = jnp.zeros((1, 128), F32)

    def put_grad(k, vrow):
        for q in range(n):
            VG[q, k : k + 1, :] = vrow[:, 128 * q : 128 * q + 128]

    for k in range(4):
        cols = slice(256 * k, 256 * k + 256)
        dg = dot(DY[...], A2[:, :, :].reshape(HF, D)[256 * k : 256 * k + 256, :], NT)
        dh = (dg * GP[:, cols]).astype(BF)
        DH[:, cols] = dh
        dc1 = jnp.sum(dh.astype(F32), axis=0, keepdims=True)
        for q in range(2):
            for j in range(NF):
                VG[2 * k + q, 9 + j : 10 + j, :] = jnp.where(f == j, dc1[:, 128 * q : 128 * q + 128], zero_row)
    svc(1)
    for k in range(4):
        cols = slice(256 * k, 256 * k + 256)
        part = dot(DH[...], A1[2 * k : 2 * k + 2, :, :].reshape(256, HF), NT).astype(BF)
        PN[:, :, cols] = part.reshape(NF, V, 256)
    n2_rs = ReduceScatter4(PN, g.PNr1, g.PNxs, g.PNr2)
    outer(G1, N2V, DH, HF)
    svc(2)
    n2_rs.forward()
    queue += [
        lambda: g1_ring[0].step(0),
        lambda: g1_ring[1].step(0),
        lambda: g1_ring[0].step(1),
        lambda: g1_ring[1].step(1),
        lambda: g1_ring[0].step(2),
        lambda: g1_ring[1].step(2),
        lambda: g1_ring[0].step(3),
        lambda: g1_ring[1].step(3),
    ]
    PF = g.PF
    for k in range(4):
        cols = slice(256 * k, 256 * k + 256)
        part = dot(GV[...], A2[:, :, cols].reshape(HF, 256)).astype(BF)
        PF[:, :, cols] = part.reshape(NF, V, 256)
    oa_ag.forward()
    svc(1)
    mine = pl.ds(pl.multiple_of(V * f, V), V)
    n2_rs.finish()
    dn2 = n2_rs.total()
    dyo = DY[mine, :].astype(F32)
    dv, dgain, dshift = norm_back(X1V[mine, :], vec(2), dn2)
    dx1 = dyo + dv
    g.DX1[...] = dx1
    dP = dx1.astype(BF)
    g.DP[f] = dP
    dp_ag = AllGather4(lambda j: g.DP.at[j])
    put_grad(2, dgain)
    put_grad(3, dshift)
    put_grad(4, jnp.sum(dP.astype(F32), axis=0, keepdims=True))
    put_grad(5, jnp.sum(dyo, axis=0, keepdims=True))
    pf_rs = ReduceScatter4(PF, g.PFr1, g.PFxs, g.PFr2)
    svc(2)
    OT = g.OT
    for j in range(NF):
        ot = OV[j].astype(F32).T.astype(BF)
        OT[n // NF * j : n // NF * (j + 1)] = ot.reshape(n // NF, NF, R, VP)
    dp_ag.forward()
    svc(1)
    pf_rs.forward()
    dp_ag.finish()
    DPv = lambda: g.DP[...].reshape(VP, D)
    go = dot(OT[:, f].reshape(n * R, VP), DPv())
    GO[...] = go.reshape(n, R, D)
    wo_heads = WO[pl.ds(n // NF * f, n // NF)].reshape(C, D)
    dO = dot(DPv(), wo_heads, NT).astype(BF)
    g.DO[...] = dO
    svc(1)
    queue += [lambda: go_ring.step(0)]

    DO = g.DO
    dq = jnp.zeros((VP, C), F32)
    dk = jnp.zeros((VP, C), F32)
    dw = jnp.zeros((VP, C), F32)
    for hd in range(C // HDIM):
        pr = PV[hd]
        dp = dot(DO[...] * hmask[hd].astype(BF), WV[...], NT)
        ds = (pr * (dp - jnp.sum(pr * dp, axis=-1, keepdims=True))).astype(BF)
        dq += dot(ds, KV[...]) * hmask[hd]
        dk += dot(ds, QV[...], TN) * hmask[hd]
        dw += dot(pr.astype(BF), DO[...], TN) * hmask[hd]
    csv = sum(dot(dot(SM[...], g.OH[...]).astype(BF), g.trig_v[k]) for k in range(3))
    DPRE = g.DPRE
    for t, (grad, scale) in enumerate(((dq, 0.125), (dk, 1.0))):
        for hh in range(C // 128):
            u = grad[:, 128 * hh : 128 * hh + 128]
            u = u * csv[:, :128] - swap_halves(u) * csv[:, 128:]
            DPRE[:, C * t + 128 * hh : C * t + 128 * hh + 128] = (u * scale).astype(BF)
    DPRE[:, 2 * C :] = dw.astype(BF)
    svc(2)
    BG = g.BG
    BG[...] = jnp.zeros(BG.shape, F32)
    db = jnp.sum(DPRE[...].astype(F32), axis=0, keepdims=True)
    for t in range(3):
        BG[0:1, pl.ds(pl.multiple_of(D * t + C * f, 128), C)] = db[:, C * t : C * t + C]
    for q in range(n):
        for t in range(3):
            VG[q, 6 + t : 7 + t, :] = BG[0:1, 384 * q + 128 * t : 384 * q + 128 * t + 128]
        VG[q, 13:16, :] = jnp.zeros((3, 128), F32)

    drain(n2_rs.ca, n2_rs.cb)
    for k in range(4):
        part = dot(DPRE[...], AQ[2 * k : 2 * k + 2, :, :].reshape(256, 3 * C), NT).astype(BF)
        PN[:, :, 256 * k : 256 * k + 256] = part.reshape(NF, V, 256)
    n1_rs = ReduceScatter4(PN, g.PMr1, g.PMxs, g.PMr2)
    outer(GQ, N1V, DPRE, 3 * C)
    svc(2)
    queue += [
        lambda: go_ring.step(1),
        lambda: gq_ring[0].step(0),
        lambda: gq_ring[1].step(0),
        lambda: go_ring.step(2),
        lambda: gq_ring[0].step(1),
        lambda: gq_ring[1].step(1),
        lambda: go_ring.step(3),
        lambda: gq_ring[0].step(2),
        lambda: gq_ring[1].step(2),
        lambda: gq_ring[0].step(3),
        lambda: gq_ring[1].step(3),
    ]
    n1_rs.forward()
    pf_rs.finish()
    out_own = X1V[mine, :] + (pf_rs.total() + vec(5))
    g.CO[f] = out_own.astype(BF)
    co_ag = AllGather4(lambda j: g.CO.at[j])
    svc(1)
    n1_rs.finish()
    dv, dgain, dshift = norm_back(XV[mine, :].astype(F32), vec(0), n1_rs.total())
    g.DX[f] = (g.DX1[...] + dv).astype(BF)
    dx_ag = AllGather4(lambda j: g.DX.at[j])
    put_grad(0, dgain)
    put_grad(1, dshift)
    gs_ring.step(0)
    co_ag.forward()
    svc(2)

    oa_ag.finish()
    N2 = g.N2

    def target_mid(b, _):
        rows = pl.ds(pl.multiple_of(b * T, T), T)
        for k in range(4):
            cols = slice(256 * k, 256 * k + 256)
            g.X1B[:, cols] = TA[b, :, cols].astype(F32) + (
                out_project(lambda j: OA[j, rows, :], cols) + VEC[4:5, cols]
            )
        x1 = g.X1B[...]
        xh, _i = norm_stats(x1)
        N2[b] = (xh * vec(2) + vec(3)).astype(BF)

        @pl.when(b == f)
        def _():
            g.X1H[...] = x1

        return 0

    lax.fori_loop(0, NF, target_mid, 0)
    dx_ag.forward()
    gs_ring.step(1)
    svc(2)
    GT, PT = g.GT, g.PT

    def target_hidden(b, _):
        for k in range(4):
            cols = slice(256 * k, 256 * k + 256)
            hid = dot(N2[b], A1[:, :, cols].reshape(D, 256)) + VEC[6:7, cols]
            GT[b, :, cols] = (hid * gelu_parts(hid)).astype(BF)
        return 0

    lax.fori_loop(0, 2, target_hidden, 0)
    gs_ring.step(2)
    svc(2)
    lax.fori_loop(2, 4, target_hidden, 0)
    gs_ring.step(3)
    svc(2)

    def target_out(b, _):
        for k in range(4):
            cols = slice(256 * k, 256 * k + 256)
            PT[b, :, cols] = dot(GT[b], A2[:, :, cols].reshape(HF, 256)).astype(BF)
        return 0

    lax.fori_loop(0, NF, target_out, 0)
    pt_rs = ReduceScatter4(PT, g.PTr1, g.PTxs, g.PTr2)
    svc(2)

    def home(src, dst):
        s = SM[:, pl.ds(pl.multiple_of(T * f, 128), T)]
        for k in range(4):
            cols = slice(256 * k, 256 * k + 256)
            dst[:, cols] = dot(s, src[:, :, cols].reshape(VP, 256), TN).astype(BF)

    outs = []

    def store(src, dst, k):
        c = pltpu.make_async_copy(src, dst, lsem.at[8 + k])
        c.start()
        outs.append(c)

    co_ag.finish()
    home(g.CO, g.CH)
    store(g.CH, g.ctx_o, 0)
    pt_rs.forward()
    svc(1)
    dx_ag.finish()
    home(g.DX, g.DXH)
    store(g.DXH, g.dx_o, 1)
    gs_ring.finish()
    SG = g.SG
    SG[f] = gs_ring.total()
    got_g = scatter(lambda j: SG.at[f], lambda j: SG.at[j])
    for k, ring in enumerate(g2_ring):
        ring.finish()
        g.D2[hc * k : hc * k + hc, :] = ring.total()
    store(g.D2, g.g2_o, 2)
    svc(1)
    E1, EQ = g.E1, g.EQ
    while queue and len(queue) > 4:
        svc(1)
    for k, ring in enumerate(g1_ring):
        ring.finish()
        E1[2 * k : 2 * k + 2] = ring.total().astype(BF).reshape(2, R, HF)
    F1 = g.F1
    F1[f] = E1[f]
    got_e1 = scatter(lambda j: E1.at[j], lambda j: F1.at[j])
    svc(2)
    pt_rs.finish()
    g.TO[...] = (g.X1H[...] + (pt_rs.total() + vec(5))).astype(BF)
    store(g.TO, g.tgt_o, 3)
    svc(2)
    go_ring.finish()
    g.DOo[...] = go_ring.total()
    store(g.DOo, g.go_o, 4)
    for a in got_e1:
        a.wait_recv()
    for j in range(NF):
        for t in range(n):
            at = HC * (NF * t + j)
            g.D1[:, at : at + HC] = F1[j, :, HC * t : HC * t + HC].astype(F32)
    store(g.D1, g.g1_o, 5)
    for a in got_g:
        a.wait_recv()
    g.SGo[...] = SG[0] + SG[1] + SG[2] + SG[3]
    store(g.SGo, g.sg_o, 6)
    while queue:
        svc(1)
    for k, ring in enumerate(gq_ring):
        ring.finish()
        EQ[2 * k : 2 * k + 2] = ring.total().astype(BF).reshape(2, R, 3 * C)
    FQ = g.FQ
    FQ[f] = EQ[f]
    got_eq = scatter(lambda j: EQ.at[j], lambda j: FQ.at[j])
    for a in got_eq:
        a.wait_recv()
    for j in range(NF):
        for t in range(3):
            g.DQo[:, D * t + C * j : D * t + C * j + C] = FQ[j, :, C * t : C * t + C].astype(F32)
    store(g.DQo, g.gq_o, 7)
    for c in outs:
        c.wait()
    for c in pending:
        c.wait_send()


def run_layer(n, tokens, cot, lengths, small, wqkv, wo, w1, w2, V):
    T, D = tokens.shape
    NF = 4
    FF = w1.shape[1]
    R = wo.shape[0]
    RP = R * NF
    HC = w2.shape[0]
    HF = HC * n
    C = D // NF
    VP = V * NF
    S_ = T * NF
    h2 = n // 2
    B, F = BF, F32
    vm = pltpu.VMEM
    scratch = dict(
        wqkv_v=vm((R, 3 * D), F), w1_v=vm((R, FF), F), wo_v=vm((R, D), F), w2_v=vm((HC, D), F),
        small_v=vm((8, 128), F), trig_v=vm((3, 128, 256), B),
        sq=vm((NF, R, 3 * C), B), s1=vm((NF, R, HF), B),
        AS=vm((n, NF, 8, 128), F), AQ=vm((n, RP, 3 * C), B), WO=vm((n, NF, R, D), B),
        A1=vm((n, RP, HF), B), A2=vm((n, HC, D), B),
        TA=vm((NF, T, D), B), CA=vm((NF, T, D), B), N1=vm((NF, T, D), B),
        OH=vm((S_, 128), B), CS=vm((S_, 256), F), SM=vm((VP, S_), B),
        VEC=vm((8, D), F), BQ=vm((8, 3 * D), F), BG=vm((8, 3 * D), F),
        Q=vm((S_, C), B), K=vm((S_, C), B), W=vm((S_, C), B),
        QV=vm((VP, C), B), KV=vm((VP, C), B), WV=vm((VP, C), B),
        OV=vm((NF, VP, C), B), PV=vm((C // HDIM, VP, VP), F), OA=vm((NF, S_, C), B),
        XV=vm((VP, D), B), N1V=vm((VP, D), B), DY=vm((VP, D), B),
        X1V=vm((VP, D), F), N2V=vm((VP, D), B), GV=vm((VP, HF), B), GP=vm((VP, HF), F),
        G2=vm((n, HC, D), F), G1=vm((n, RP, HF), F), GQ=vm((n, RP, 3 * C), F), GO=vm((n, R, D), F),
        VG=vm((n, 16, 128), F),
        st2=vm((HC, D), B), rr2=vm((h2, HC, D), B), rl2=vm((h2, HC, D), B),
        st1=vm((RP, HF), B), rr1=vm((h2, RP, HF), B), rl1=vm((h2, RP, HF), B),
        stq=vm((RP, 3 * C), B), rrq=vm((h2, RP, 3 * C), B), rlq=vm((h2, RP, 3 * C), B),
        sto=vm((R, D), B), rro=vm((h2, R, D), B), rlo=vm((h2, R, D), B),
        sts=vm((16, 128), F), rrs=vm((h2, 16, 128), F), rls=vm((h2, 16, 128), F),
        DH=vm((VP, HF), B), PN=vm((NF, V, D), B), PF=vm((NF, V, D), B),
        PNr1=vm((2, V, D), B), PNxs=vm((V, D), B), PNr2=vm((V, D), B),
        PMr1=vm((2, V, D), B), PMxs=vm((V, D), B), PMr2=vm((V, D), B),
        PFr1=vm((2, V, D), B), PFxs=vm((V, D), B), PFr2=vm((V, D), B),
        DX1=vm((V, D), F), DP=vm((NF, V, D), B), OT=vm((n, NF, R, VP), B), DO=vm((VP, C), B),
        DPRE=vm((VP, 3 * C), B), CO=vm((NF, V, D), B), DX=vm((NF, V, D), B),
        X1B=vm((T, D), F), X1H=vm((T, D), F), GT=vm((NF, T, HF), B),
        PTr1=vm((2, T, D), B), PTxs=vm((T, D), B), PTr2=vm((T, D), B),
        CH=vm((T, D), B), DXH=vm((T, D), B), TO=vm((T, D), B),
        SG=vm((NF, 16, 128), F), SGo=vm((16, 128), F),
        E1=vm((NF, R, HF), B), F1=vm((NF, R, HF), B), EQ=vm((NF, R, 3 * C), B), FQ=vm((NF, R, 3 * C), B),
        send_sems=pltpu.SemaphoreType.DMA((200,)), recv_sems=pltpu.SemaphoreType.DMA((200,)),
        local_sems=pltpu.SemaphoreType.DMA((16,)),
    )
    arr = jax.ShapeDtypeStruct
    ins = dict(
        lengths=lengths, tok=tokens, cot=cot, small=small, wqkv=wqkv, wo=wo, w1=w1, w2=w2,
        trig=jnp.asarray(trig_table()),
    )
    outs = dict(
        tgt_o=arr((T, D), B), ctx_o=arr((T, D), B), dx_o=arr((T, D), B), gq_o=arr((R, 3 * D), F),
        go_o=arr((R, D), F), g1_o=arr((R, FF), F), g2_o=arr((HC, D), F), sg_o=arr((16, 128), F),
    )
    names = [*ins, *outs, *scratch]
    any_spec = pl.BlockSpec(memory_space=pl.ANY)
    return pl.pallas_call(
        functools.partial(layer_kernel, (n, D, FF, T, V), names),
        out_shape=list(outs.values()),
        in_specs=[pl.BlockSpec(memory_space=pltpu.SMEM)] + [any_spec] * 8,
        out_specs=[any_spec] * 8,
        scratch_shapes=list(scratch.values()),
        compiler_params=pltpu.CompilerParams(
            collective_id=0, has_side_effects=True, vmem_limit_bytes=67043328
        ),
        name="layer",
    )(*ins.values())


def on_device(
    tokens, lengths, visibility_mask, visible_counts, ln1_gain, ln1_bias, qkv_weight, qkv_bias,
    out_weight, out_bias, ln2_gain, ln2_bias, fc1_weight, fc1_bias, fc2_weight, fc2_bias, context_cot,
):
    n = lax.axis_size("dp")
    f = lax.axis_index("fsdp")
    R = ln1_gain.shape[0]
    running = jnp.cumsum(visibility_mask)
    visible = (visibility_mask * (running <= visible_counts[0, 0]).astype(jnp.int32)).astype(F32)
    pad = lambda k: jnp.zeros((k,), F32)
    small = jnp.concatenate(
        [
            ln1_gain, ln1_bias, ln2_gain, ln2_bias,
            out_bias, fc2_bias, pad(64),
            qkv_bias, pad(32),
            fc1_bias,
            visible, pad(256),
        ]
    ).reshape(8, 128)
    tgt, ctx, dx, gq, go, g1, g2, sg = run_layer(
        n, tokens, context_cot, lengths, small, qkv_weight, out_weight, fc1_weight, fc2_weight, VIS_DEV
    )

    def own(k):
        return lax.dynamic_slice(sg[k], (R * f,), (R,))

    gbq = lax.dynamic_slice(sg[6:9].reshape(-1), (3 * R * f,), (3 * R,))
    gb1 = lax.dynamic_slice(sg[9:13].reshape(-1), (4 * R * f,), (4 * R,))
    return (tgt, ctx, dx, own(0), own(1), gq, gbq, go, own(4), own(2), own(3), g1, gb1, g2, own(5))


def layer_norm(inputs, scale_vec, shift_vec):
    center = inputs - jnp.mean(inputs, axis=-1, keepdims=True)
    spread = jnp.mean(center * center, axis=-1, keepdims=True)
    return center * lax.rsqrt(spread + norm_eps) * scale_vec + shift_vec


def gelu_erf(values):
    return jax.nn.gelu(values, approximate=False)


def pack_layout(seq_lens, pack_len):
    seq_ends = jnp.cumsum(seq_lens)
    places = jnp.arange(pack_len, dtype=jnp.int32)
    passed = places[:, None] >= seq_ends[None, :]
    segment = jnp.sum(passed.astype(jnp.int32), axis=1)
    before = jnp.sum(jnp.where(passed, seq_lens[None, :], 0), axis=1)
    return (segment, places - before)


def rope_tables(places):
    frame_index = (places // (GRID * GRID)).astype(jnp.float32)
    grid_row = (places // GRID % GRID).astype(jnp.float32)
    grid_col = (places % GRID).astype(jnp.float32)
    pair_index = jnp.arange(HDIM // 2, dtype=jnp.int32)
    axis_pick = jnp.minimum(pair_index // 11, 2)
    pair_order = (pair_index - 11 * axis_pick).astype(jnp.float32)
    frequency = jnp.exp(pair_order * (-math.log(10000.0) / 11.0))
    angles = (
        frame_index[:, None] * (axis_pick == 0).astype(jnp.float32)[None, :]
        + grid_row[:, None] * (axis_pick == 1).astype(jnp.float32)[None, :]
        + grid_col[:, None] * (axis_pick == 2).astype(jnp.float32)[None, :]
    ) * frequency[None, :]
    return (jnp.cos(angles), jnp.sin(angles))


def rotate(heads, cosine_table, sine_table):
    half_size = heads.shape[-1] // 2
    first_half = heads[..., :half_size]
    second_half = heads[..., half_size:]
    cosine_cols = cosine_table[:, None, :]
    sine_cols = sine_table[:, None, :]
    return jnp.concatenate(
        [
            first_half * cosine_cols - second_half * sine_cols,
            second_half * cosine_cols + first_half * sine_cols,
        ],
        axis=-1,
    )


def rotate_back(grads, cosine_table, sine_table):
    half_size = grads.shape[-1] // 2
    first_half = grads[..., :half_size]
    second_half = grads[..., half_size:]
    cosine_cols = cosine_table[:, None, :]
    sine_cols = sine_table[:, None, :]
    return jnp.concatenate(
        [
            first_half * cosine_cols + second_half * sine_cols,
            second_half * cosine_cols - first_half * sine_cols,
        ],
        axis=-1,
    )


def project(token_rows, weights, cosine_table, sine_table):
    inputs = token_rows.astype(jnp.float32)
    row_count = inputs.shape[0]
    model_width = inputs.shape[1]
    normed = layer_norm(
        inputs, weights[0].astype(jnp.float32), weights[1].astype(jnp.float32)
    ).astype(jnp.bfloat16)
    joined = jnp.dot(normed, weights[2], preferred_element_type=jnp.float32) + weights[3].astype(
        jnp.float32
    )
    query_heads = rotate(
        joined[:, :model_width].reshape(row_count, HEADS, HDIM), cosine_table, sine_table
    ).astype(jnp.bfloat16)
    key_flat = (
        rotate(
            joined[:, model_width : 2 * model_width].reshape(row_count, HEADS, HDIM),
            cosine_table,
            sine_table,
        )
        .astype(jnp.bfloat16)
        .reshape(row_count, model_width)
    )
    value_flat = joined[:, 2 * model_width :].astype(jnp.bfloat16)
    return (inputs, normed, query_heads, key_flat, value_flat)


def attend(query_heads, key_flat, value_flat, seg_query, seg_key):
    key_heads = key_flat.reshape(key_flat.shape[0], HEADS, HDIM)
    value_heads = value_flat.reshape(value_flat.shape[0], HEADS, HDIM)
    scores = jnp.einsum(
        "qhd,khd->hqk", query_heads, key_heads, preferred_element_type=jnp.float32
    ) * HDIM ** (-0.5)
    allowed = seg_query[:, None] == seg_key[None, :]
    masked = jnp.where(allowed[None], scores, masked_fill)
    row_max = jnp.max(masked, axis=-1, keepdims=True)
    raised = jnp.exp(masked - row_max)
    totals = jnp.sum(raised, axis=-1, keepdims=True)
    attn_probs = (raised / totals).astype(jnp.bfloat16)
    attended = jnp.einsum(
        "hqk,khd->qhd", attn_probs, value_heads, preferred_element_type=jnp.float32
    )
    return (
        attended.reshape(query_heads.shape[0], -1).astype(jnp.bfloat16),
        row_max + jnp.log(totals),
    )


def attend_back(query_heads, key_flat, value_flat, seg_query, seg_key, log_total, grad_att):
    key_heads = key_flat.reshape(key_flat.shape[0], HEADS, HDIM)
    value_heads = value_flat.reshape(value_flat.shape[0], HEADS, HDIM)
    scale_factor = HDIM ** (-0.5)
    scores = (
        jnp.einsum("qhd,khd->hqk", query_heads, key_heads, preferred_element_type=jnp.float32)
        * scale_factor
    )
    allowed = seg_query[:, None] == seg_key[None, :]
    masked = jnp.where(allowed[None], scores, masked_fill)
    attn_probs = jnp.exp(masked - log_total)
    grad_heads = grad_att.reshape(grad_att.shape[0], HEADS, HDIM)
    grad_probs = jnp.einsum(
        "qhd,khd->hqk", grad_heads, value_heads, preferred_element_type=jnp.float32
    )
    row_delta = jnp.sum(attn_probs * grad_probs, axis=-1, keepdims=True)
    grad_scores = (attn_probs * (grad_probs - row_delta)).astype(jnp.bfloat16)
    grad_query = (
        jnp.einsum("hqk,khd->qhd", grad_scores, key_heads, preferred_element_type=jnp.float32)
        * scale_factor
    )
    grad_key = (
        jnp.einsum("hqk,qhd->khd", grad_scores, query_heads, preferred_element_type=jnp.float32)
        * scale_factor
    )
    grad_value = jnp.einsum(
        "hqk,qhd->khd",
        attn_probs.astype(jnp.bfloat16),
        grad_heads,
        preferred_element_type=jnp.float32,
    )
    return (
        grad_query,
        grad_key.reshape(key_flat.shape[0], -1),
        grad_value.reshape(value_flat.shape[0], -1),
    )


def finish(inputs, attended, weights):
    middle = inputs + (
        jnp.dot(attended, weights[4], preferred_element_type=jnp.float32)
        + weights[5].astype(jnp.float32)
    )
    second = layer_norm(
        middle, weights[6].astype(jnp.float32), weights[7].astype(jnp.float32)
    ).astype(jnp.bfloat16)
    hidden = jnp.dot(second, weights[8], preferred_element_type=jnp.float32) + weights[9].astype(
        jnp.float32
    )
    activated = gelu_erf(hidden).astype(jnp.bfloat16)
    result = middle + (
        jnp.dot(activated, weights[10], preferred_element_type=jnp.float32)
        + weights[11].astype(jnp.float32)
    )
    return (result, middle, second, hidden, activated)


def gathered_device(
    tokens,
    lengths,
    visibility_mask,
    visible_counts,
    ln1_gain,
    ln1_bias,
    qkv_weight,
    qkv_bias,
    out_weight,
    out_bias,
    ln2_gain,
    ln2_bias,
    fc1_weight,
    fc1_bias,
    fc2_weight,
    fc2_bias,
    context_cot,
):
    tok_rows = tokens.shape[0]
    model_width = tokens.shape[1]
    groups = lax.axis_size("fsdp")
    member = lax.axis_index("fsdp")
    pack_len = tok_rows * groups
    vis_rows = VIS_DEV
    vis_pack = vis_rows * groups
    zero_low = jnp.zeros((), jnp.bfloat16)
    shards = [
        weight.astype(jnp.bfloat16)
        for weight in (
            ln1_gain,
            ln1_bias,
            qkv_weight,
            qkv_bias,
            out_weight,
            out_bias,
            ln2_gain,
            ln2_bias,
            fc1_weight,
            fc1_bias,
            fc2_weight,
            fc2_bias,
        )
    ]
    weights = (
        lax.all_gather(shards[0], ("dp", "fsdp"), axis=0, tiled=True),
        lax.all_gather(shards[1], ("dp", "fsdp"), axis=0, tiled=True),
        lax.all_gather(shards[2], ("dp", "fsdp"), axis=0, tiled=True),
        lax.all_gather(shards[3], ("dp", "fsdp"), axis=0, tiled=True),
        lax.all_gather(shards[4], ("dp", "fsdp"), axis=0, tiled=True),
        lax.all_gather(shards[5], ("dp", "fsdp"), axis=0, tiled=True),
        lax.all_gather(shards[6], ("dp", "fsdp"), axis=0, tiled=True),
        lax.all_gather(shards[7], ("dp", "fsdp"), axis=0, tiled=True),
        lax.all_gather(shards[8], ("dp", "fsdp"), axis=0, tiled=True),
        lax.all_gather(shards[9], ("dp", "fsdp"), axis=0, tiled=True),
        lax.all_gather(shards[10], ("dp", "fsdp"), axis=0, tiled=True),
        lax.all_gather(shards[11], ("dp", "fsdp"), axis=0, tiled=True),
    )
    segment, places = pack_layout(lengths[0], pack_len)
    home_rows = member * tok_rows + jnp.arange(tok_rows, dtype=jnp.int32)
    seg_home = jnp.take(segment, home_rows)
    cos_home, sin_home = rope_tables(jnp.take(places, home_rows))
    inputs, normed, query_heads, key_flat, value_flat = project(tokens, weights, cos_home, sin_home)
    key_pack, value_pack = (
        lax.all_gather(key_flat, "fsdp", axis=0, tiled=True),
        lax.all_gather(value_flat, "fsdp", axis=0, tiled=True),
    )
    attended = attend(query_heads, key_pack, value_pack, seg_home, segment)[0]
    target_out = finish(inputs, attended, weights)[0].astype(jnp.bfloat16)
    running = jnp.cumsum(visibility_mask)
    visible_here = visibility_mask * (running <= visible_counts[0, 0]).astype(jnp.int32)
    visible_all = lax.all_gather(visible_here, "fsdp", axis=0, tiled=True)
    inclusive = jnp.cumsum(visible_all)
    rank_index = jnp.arange(vis_pack, dtype=jnp.int32)
    row_of = jnp.sum((inclusive[None, :] <= rank_index[:, None]).astype(jnp.int32), axis=1)
    owner_dev = row_of // tok_rows
    local_row = row_of % tok_rows
    mine_here = (owner_dev == member)[:, None]
    send_tokens = jnp.where(mine_here, jnp.take(tokens, local_row, axis=0), zero_low)
    send_cot = jnp.where(mine_here, jnp.take(context_cot, local_row, axis=0), zero_low)
    recv_tokens, recv_cot = (
        lax.all_to_all(send_tokens, "fsdp", split_axis=0, concat_axis=0, tiled=True),
        lax.all_to_all(send_cot, "fsdp", split_axis=0, concat_axis=0, tiled=True),
    )
    slot_index = jnp.arange(vis_rows, dtype=jnp.int32)
    my_ranks = member * vis_rows + slot_index
    my_owner = jnp.take(owner_dev, my_ranks)
    my_row = jnp.take(row_of, my_ranks)
    picked = my_owner * vis_rows + slot_index
    bal_tokens = jnp.take(recv_tokens, picked, axis=0)
    bal_cot = jnp.take(recv_cot, picked, axis=0)
    seg_bal = jnp.take(segment, my_row)
    seg_keys = jnp.take(segment, row_of)
    cos_bal, sin_bal = rope_tables(jnp.take(places, my_row))
    inputs_bal, normed_bal, query_bal, key_bal, value_bal = project(
        bal_tokens, weights, cos_bal, sin_bal
    )
    key_vis, value_vis = (
        lax.all_gather(key_bal, "fsdp", axis=0, tiled=True),
        lax.all_gather(value_bal, "fsdp", axis=0, tiled=True),
    )
    attended_bal, log_total = attend(query_bal, key_vis, value_vis, seg_bal, seg_keys)
    result_bal, middle_bal, second_bal, hidden_bal, activated_bal = finish(
        inputs_bal, attended_bal, weights
    )
    grad_result = bal_cot.astype(jnp.float32)
    result_low = grad_result.astype(jnp.bfloat16)
    grad_fc2 = jnp.einsum(
        "nf,nd->fd", activated_bal, result_low, preferred_element_type=jnp.float32
    )
    grad_bfc2 = jnp.sum(result_low.astype(jnp.float32), axis=0)
    grad_activated = jnp.einsum(
        "nd,fd->nf", result_low, weights[10], preferred_element_type=jnp.float32
    )
    gelu_pull = jax.vjp(gelu_erf, hidden_bal)[1]
    hidden_low = gelu_pull(grad_activated)[0].astype(jnp.bfloat16)
    grad_fc1 = jnp.einsum("nd,nf->df", second_bal, hidden_low, preferred_element_type=jnp.float32)
    grad_bfc1 = jnp.sum(hidden_low.astype(jnp.float32), axis=0)
    grad_second = jnp.einsum(
        "nf,df->nd", hidden_low, weights[8], preferred_element_type=jnp.float32
    )
    norm_two_pull = jax.vjp(
        layer_norm, middle_bal, weights[6].astype(jnp.float32), weights[7].astype(jnp.float32)
    )[1]
    grad_mid_norm, grad_gain_two, grad_shift_two = norm_two_pull(grad_second)
    grad_middle = grad_result + grad_mid_norm
    middle_low = grad_middle.astype(jnp.bfloat16)
    grad_wout = jnp.einsum(
        "nd,ne->de", attended_bal, middle_low, preferred_element_type=jnp.float32
    )
    grad_bout = jnp.sum(middle_low.astype(jnp.float32), axis=0)
    grad_att = jnp.einsum(
        "ne,de->nd", middle_low, weights[4], preferred_element_type=jnp.float32
    ).astype(jnp.bfloat16)
    grad_query, grad_key_all, grad_value_all = attend_back(
        query_bal, key_vis, value_vis, seg_bal, seg_keys, log_total, grad_att
    )
    grad_key_own, grad_value_own = (
        lax.psum_scatter(
            grad_key_all.astype(jnp.bfloat16), "fsdp", scatter_dimension=0, tiled=True
        ).astype(jnp.float32),
        lax.psum_scatter(
            grad_value_all.astype(jnp.bfloat16), "fsdp", scatter_dimension=0, tiled=True
        ).astype(jnp.float32),
    )
    grad_query_pre = rotate_back(grad_query, cos_bal, sin_bal).reshape(vis_rows, model_width)
    grad_key_pre = rotate_back(
        grad_key_own.reshape(vis_rows, HEADS, HDIM), cos_bal, sin_bal
    ).reshape(vis_rows, model_width)
    joined_low = jnp.concatenate([grad_query_pre, grad_key_pre, grad_value_own], axis=1).astype(
        jnp.bfloat16
    )
    grad_wqkv = jnp.einsum("nd,ne->de", normed_bal, joined_low, preferred_element_type=jnp.float32)
    grad_bqkv = jnp.sum(joined_low.astype(jnp.float32), axis=0)
    grad_normed = jnp.einsum(
        "ne,de->nd", joined_low, weights[2], preferred_element_type=jnp.float32
    )
    norm_one_pull = jax.vjp(
        layer_norm, inputs_bal, weights[0].astype(jnp.float32), weights[1].astype(jnp.float32)
    )[1]
    grad_in_norm, grad_gain_one, grad_shift_one = norm_one_pull(grad_normed)
    grad_inputs = grad_middle + grad_in_norm
    destinations = jnp.arange(groups, dtype=jnp.int32)
    route_mask = (my_owner[None, :] == destinations[:, None])[:, :, None]
    send_out = jnp.where(route_mask, result_bal.astype(jnp.bfloat16)[None], zero_low).reshape(
        vis_pack, model_width
    )
    send_grad = jnp.where(route_mask, grad_inputs.astype(jnp.bfloat16)[None], zero_low).reshape(
        vis_pack, model_width
    )
    back_out, back_grad = (
        lax.all_to_all(send_out, "fsdp", split_axis=0, concat_axis=0, tiled=True),
        lax.all_to_all(send_grad, "fsdp", split_axis=0, concat_axis=0, tiled=True),
    )
    rank_home = jnp.maximum(jnp.take(inclusive, home_rows) - 1, 0)
    is_visible = (visible_here > 0)[:, None]
    context_out = jnp.where(is_visible, jnp.take(back_out, rank_home, axis=0), zero_low)
    tokens_grad = jnp.where(is_visible, jnp.take(back_grad, rank_home, axis=0), zero_low)
    grad_list = [
        grad_gain_one,
        grad_shift_one,
        grad_wqkv,
        grad_bqkv,
        grad_wout,
        grad_bout,
        grad_gain_two,
        grad_shift_two,
        grad_fc1,
        grad_bfc1,
        grad_fc2,
        grad_bfc2,
    ]
    reduced = (
        lax.psum_scatter(grad_list[0], ("dp", "fsdp"), scatter_dimension=0, tiled=True),
        lax.psum_scatter(grad_list[1], ("dp", "fsdp"), scatter_dimension=0, tiled=True),
        lax.psum_scatter(grad_list[2], ("dp", "fsdp"), scatter_dimension=0, tiled=True),
        lax.psum_scatter(grad_list[3], ("dp", "fsdp"), scatter_dimension=0, tiled=True),
        lax.psum_scatter(grad_list[4], ("dp", "fsdp"), scatter_dimension=0, tiled=True),
        lax.psum_scatter(grad_list[5], ("dp", "fsdp"), scatter_dimension=0, tiled=True),
        lax.psum_scatter(grad_list[6], ("dp", "fsdp"), scatter_dimension=0, tiled=True),
        lax.psum_scatter(grad_list[7], ("dp", "fsdp"), scatter_dimension=0, tiled=True),
        lax.psum_scatter(grad_list[8], ("dp", "fsdp"), scatter_dimension=0, tiled=True),
        lax.psum_scatter(grad_list[9], ("dp", "fsdp"), scatter_dimension=0, tiled=True),
        lax.psum_scatter(grad_list[10], ("dp", "fsdp"), scatter_dimension=0, tiled=True),
        lax.psum_scatter(grad_list[11], ("dp", "fsdp"), scatter_dimension=0, tiled=True),
    )
    return (
        target_out,
        context_out,
        tokens_grad,
        reduced[0],
        reduced[1],
        reduced[2],
        reduced[3],
        reduced[4],
        reduced[5],
        reduced[6],
        reduced[7],
        reduced[8],
        reduced[9],
        reduced[10],
        reduced[11],
    )


def per_device(tokens, *rest):
    n, group = lax.axis_size("dp"), lax.axis_size("fsdp")
    out_rows = rest[7].shape[0]
    fits = group == 4 and n == 8 and out_rows * group == 128
    return (on_device if fits else gathered_device)(tokens, *rest)


def solution(mesh):
    both = ("dp", "fsdp")
    vec, mat = P(both), P(both, None)
    return jax.shard_map(
        per_device,
        mesh=mesh,
        in_specs=(
            mat, P("dp", None), vec, P("dp", "fsdp"), vec, vec, mat, vec, mat, vec, vec, vec,
            mat, vec, mat, vec, mat,
        ),
        out_specs=(mat, mat, mat, vec, vec, mat, vec, mat, vec, vec, vec, mat, vec, mat, vec),
        check_vma=False,
    )
```

```python
import functools
import math
import types

import jax
import jax.numpy as jnp
import numpy as np
from jax import lax
from jax.experimental import pallas as pl
from jax.experimental.pallas import tpu as pltpu
from jax.sharding import PartitionSpec as P

HEADS = 16
HDIM = 64
GRID = 14
VIS_DEV = 64
norm_eps = 1e-06
masked_fill = -1e30
FRAMES = 8
EPS = 1e-06
FILL = -1e30
BF = jnp.bfloat16
F32 = jnp.float32
MESH = pl.DeviceIdType.MESH
NT = (((1,), (1,)), ((), ()))
NN = (((1,), (0,)), ((), ()))
TN = (((0,), (0,)), ((), ()))


def dot(a, b, dims=NN):
    return lax.dot_general(a, b, dims, preferred_element_type=F32)


def trig_table():
    width = FRAMES + 2 * GRID
    lane = np.arange(2 * HDIM)
    pair = lane % (HDIM // 2)
    axis = np.minimum(pair // 11, 2)
    freq = np.exp(((pair - 11 * axis).astype(np.float32)) * np.float32(-math.log(10000.0) / 11.0))
    sign = np.where(lane % HDIM < HDIM // 2, -1.0, 1.0)
    table = np.zeros((128, 4 * HDIM), np.float32)
    row = np.arange(width)
    kind = np.where(row < FRAMES, 0, np.where(row < FRAMES + GRID, 1, 2))
    coord = np.where(kind == 0, row, np.where(kind == 1, row - FRAMES, row - FRAMES - GRID))
    angle = (coord[:, None].astype(np.float32) * freq[None, :].astype(np.float32)).astype(np.float64)
    here = kind[:, None] == axis[None, :]
    table[:width, : 2 * HDIM] = np.where(here, np.cos(angle), 0.0)
    table[:width, 2 * HDIM :] = np.where(here, np.sin(angle) * sign[None, :], 0.0)
    parts = []
    rest = table
    for _ in range(3):
        part = rest.astype(jnp.bfloat16)
        parts.append(part)
        rest = rest - part.astype(np.float32)
    return np.stack(parts)


def norm_stats(v):
    center = v - jnp.mean(v, axis=-1, keepdims=True)
    inv = lax.rsqrt(jnp.mean(center * center, axis=-1, keepdims=True) + EPS)
    return center * inv, inv


def norm_back(v, gain, grad):
    xhat, inv = norm_stats(v)
    gg = grad * gain
    dv = inv * (
        gg - jnp.mean(gg, axis=-1, keepdims=True) - xhat * jnp.mean(gg * xhat, axis=-1, keepdims=True)
    )
    return (
        dv,
        jnp.sum(grad * xhat, axis=0, keepdims=True),
        jnp.sum(grad, axis=0, keepdims=True),
    )


def swap_halves(u):
    lane = lax.broadcasted_iota(jnp.int32, u.shape, 1)
    return jnp.where(
        lax.rem(lane, HDIM) < HDIM // 2,
        pltpu.roll(u, u.shape[1] - HDIM // 2, 1),
        pltpu.roll(u, HDIM // 2, 1),
    )


def column_segment(start, rows, ends):
    row = start + lax.broadcasted_iota(jnp.int32, (rows, 1), 0)
    seg = jnp.zeros((rows, 1), jnp.int32)
    for end in ends:
        seg += (row >= end).astype(jnp.int32)
    return row, seg


ALIASES = dict(N2="N1", PT="N1", D2="w2_v", D1="w1_v", DOo="wo_v", DQo="wqkv_v")


class Sems:
    def __init__(self, send, recv):
        self.send, self.recv, self.used = send, recv, 0

    def take(self):
        at = self.used
        self.used += 1
        return self.send.at[at], self.recv.at[at]


def layer_kernel(dims, names, *refs):
    n, D, FF, T, V = dims
    NF = 4
    R = D // (n * NF)
    RP = R * NF
    HC = FF // (NF * n)
    HF = FF // NF
    C = D // NF
    VP = V * NF
    S_ = T * NF
    last = n // 2 - 1
    given = dict(zip(names, refs))
    g = types.SimpleNamespace(**given, **{a: given[b] for a, b in ALIASES.items()})
    sems = Sems(g.send_sems, g.recv_sems)
    lsem = g.local_sems

    p = lax.axis_index("dp")
    f = lax.axis_index("fsdp")
    f1 = f + 1 - 2 * lax.rem(f, 2)
    f2 = lax.rem(f + 2, NF)
    f3 = NF - 1 - f
    par = lax.rem(p, 2)
    half_p = lax.div(p, 2)
    pos = (1 - par) * half_p + par * (n - 1 - half_p)

    def idx(q):
        q = lax.rem(q + 2 * n, n)
        up = lax.div(q, n // 2)
        return (1 - up) * (2 * q) + up * (2 * (n - 1 - q) + 1)

    right, left = idx(pos + 1), idx(pos - 1)

    pending = []

    def remote(src, dst, to):
        ss, rs = sems.take()
        c = pltpu.make_async_remote_copy(
            src_ref=src, dst_ref=dst, send_sem=ss, recv_sem=rs, device_id=to, device_id_type=MESH
        )
        c.start()
        pending.append(c)
        return c, ss, rs

    def drain(*copies):
        for c in copies:
            pending[:] = [d for d in pending if d is not c]
            c.wait_send()

    def arrival(dst, ss, rs, to):
        return pltpu.make_async_remote_copy(
            src_ref=dst, dst_ref=dst, send_sem=ss, recv_sem=rs, device_id=to, device_id_type=MESH
        )

    to1, to2, to3 = {"fsdp": f1}, {"fsdp": f2}, {"fsdp": f3}
    peers = ((f1, to1), (f2, to2), (f3, to3))

    loads = {}
    for i, (src, dst) in enumerate(
        (
            (g.wqkv, g.wqkv_v),
            (g.w1, g.w1_v),
            (g.wo, g.wo_v),
            (g.small, g.small_v),
            (g.tok, g.TA.at[f]),
            (g.w2, g.w2_v),
            (g.cot, g.CA.at[f]),
            (g.trig, g.trig_v),
        )
    ):
        c = pltpu.make_async_copy(src, dst, lsem.at[i])
        c.start()
        loads[i] = c

    barrier = pltpu.get_barrier_semaphore()
    for to in (to1, to2, to3, {"dp": right}, {"dp": left}):
        pl.semaphore_signal(barrier, inc=1, device_id=to, device_id_type=MESH)

    AS, AQ, WO, A1, A2 = g.AS, g.AQ, g.WO, g.A1, g.A2
    TA, CA = g.TA, g.CA

    loads[0].wait()
    for j in range(NF):
        for t in range(3):
            g.sq[j, :, C * t : C * t + C] = g.wqkv_v[:, D * t + C * j : D * t + C * j + C].astype(BF)
    AQ[p, pl.ds(pl.multiple_of(R * f, R), R), :] = g.sq[f]
    loads[3].wait()
    AS[p, f] = g.small_v[...]
    loads[5].wait()
    A2[p] = g.w2_v[...].astype(BF)
    loads[2].wait()
    WO[p, f] = g.wo_v[...].astype(BF)
    pl.semaphore_wait(barrier, 5)

    def scatter(src, dst):
        got = []
        for fj, to in peers:
            _, ss, rs = remote(src(fj), dst(f), to)
            got.append(arrival(dst(fj), ss, rs, to))
        return got

    class AllGather4:
        def __init__(self, slot):
            self.slot = slot
            _, ss, rs = remote(slot(f), slot(f), to2)
            self.across = arrival(slot(f2), ss, rs, to2)
            _, ss, rs = remote(slot(f), slot(f), to1)
            self.beside = arrival(slot(f1), ss, rs, to1)

        def forward(self):
            self.done = False
            self.across.wait_recv()
            _, ss, rs = remote(self.slot(f2), self.slot(f2), to1)
            self.passed = arrival(self.slot(f3), ss, rs, to1)

        def finish(self):
            if not self.done:
                self.done = True
                self.beside.wait_recv()
                self.passed.wait_recv()

    class ReduceScatter4:
        def __init__(self, part, r1, xs, r2):
            self.part, self.r1, self.xs, self.r2 = part, r1, xs, r2
            self.ca, ss, rs = remote(part.at[f3], r1.at[1], to1)
            self.other = arrival(r1.at[1], ss, rs, to1)
            self.cb, ss, rs = remote(part.at[f1], r1.at[0], to1)
            self.own = arrival(r1.at[0], ss, rs, to1)

        def forward(self):
            self.other.wait_recv()
            self.xs[...] = (self.part[f2].astype(F32) + self.r1[1].astype(F32)).astype(BF)
            _, ss, rs = remote(self.xs, self.r2, to2)
            self.across = arrival(self.r2, ss, rs, to2)

        def finish(self):
            self.own.wait_recv()
            self.across.wait_recv()

        def total(self):
            return self.part[f].astype(F32) + self.r1[0].astype(F32) + self.r2[...].astype(F32)

    class RingGather:
        def __init__(self, view, rows):
            self.view, self.rows = view, rows
            self.arrivals = []

        def step(self, r):
            for a in self.arrivals:
                a.wait_recv()
            self.arrivals = []
            h = self.rows // 2
            spans = ((0, self.rows), (0, self.rows)) if r < last else ((0, h), (h, h))
            for way, (s, c) in zip((1, -1), spans):
                to, frm = ({"dp": right}, {"dp": left}) if way == 1 else ({"dp": left}, {"dp": right})
                mine = self.view(idx(pos - way * r), s, c)
                _, ss, rs = remote(mine, mine, to)
                self.arrivals.append(arrival(self.view(idx(pos - way * (r + 1)), s, c), ss, rs, frm))

        def finish(self):
            for a in self.arrivals:
                a.wait_recv()
            self.arrivals = []

    def rows_view(ref, offset):
        return lambda slot, s, c: ref.at[slot, pl.ds(offset + s, c), :]

    h = RP // 2
    q_ring = [RingGather(rows_view(AQ, 0), h), RingGather(rows_view(AQ, h), h)]
    w1_ring = [RingGather(rows_view(A1, 0), h), RingGather(rows_view(A1, h), h)]
    w2_ring = [RingGather(rows_view(A2, 0), HC // 2), RingGather(rows_view(A2, HC // 2), HC // 2)]
    o_ring = RingGather(lambda slot, s, c: WO.at[slot, f, pl.ds(s, c), :], R)
    s_ring = RingGather(lambda slot, s, c: AS.at[slot, pl.ds(s, c)], NF)

    class RingReduce:
        def __init__(self, grads, start, rows, st, rr, rl, wire=BF):
            self.G, self.o, self.rows, self.st, self.rr, self.rl = grads, start, rows, st, rr, rl
            self.wire = wire
            self.arrivals = []

        def piece(self, ref, slot, s, c):
            return ref.at[slot, pl.ds(self.o + s, c), :]

        def step(self, r):
            for a in self.arrivals:
                a.wait_recv()
            self.arrivals = []
            o, rows = self.o, self.rows
            hh = rows // 2
            if r == 0:
                far = idx(pos + n // 2)
                self.st[pl.ds(o, rows), :] = self.G[far, pl.ds(o, rows), :].astype(self.wire)
                for buf, s, to, frm in (
                    (self.rr, 0, {"dp": right}, {"dp": left}),
                    (self.rl, hh, {"dp": left}, {"dp": right}),
                ):
                    dst = self.piece(buf, 0, s, hh)
                    _, ss, rs = remote(self.st.at[pl.ds(o + s, hh), :], dst, to)
                    self.arrivals.append(arrival(dst, ss, rs, frm))
                return
            for way, buf, s, to, frm in (
                (1, self.rr, 0, {"dp": right}, {"dp": left}),
                (-1, self.rl, hh, {"dp": left}, {"dp": right}),
            ):
                c = idx(pos + way * (n // 2 - r))
                if r == 1:
                    other = hh - s
                    buf[0, pl.ds(o + s, hh), :] = (
                        buf[0, pl.ds(o + s, hh), :].astype(F32) + self.G[c, pl.ds(o + s, hh), :]
                    ).astype(self.wire)
                    buf[0, pl.ds(o + other, hh), :] = self.G[c, pl.ds(o + other, hh), :].astype(self.wire)
                else:
                    buf[r - 1, pl.ds(o, rows), :] = (
                        buf[r - 1, pl.ds(o, rows), :].astype(F32) + self.G[c, pl.ds(o, rows), :]
                    ).astype(self.wire)
                src, dst = self.piece(buf, r - 1, 0, rows), self.piece(buf, r, 0, rows)
                _, ss, rs = remote(src, dst, to)
                self.arrivals.append(arrival(dst, ss, rs, frm))

        def finish(self):
            for a in self.arrivals:
                a.wait_recv()
            self.arrivals = []

        def total(self):
            o, rows = self.o, self.rows
            return (
                self.G[p, pl.ds(o, rows), :]
                + self.rr[last, pl.ds(o, rows), :].astype(F32)
                + self.rl[last, pl.ds(o, rows), :].astype(F32)
            )

    st = types.SimpleNamespace(oa=[None, None])
    N1, N2, GT, PT = g.N1, g.N2, g.GT, g.PT
    VEC, BQ, BG, VG = g.VEC, g.BQ, g.BG, g.VG
    Q, K, W, QV, KV, WV = g.Q, g.K, g.W, g.QV, g.KV, g.WV
    SM, OV, PV, OA, OT = g.SM, g.OV, g.PV, g.OA, g.OT
    XV, N1V, DY, X1V, N2V = g.XV, g.N1V, g.DY, g.X1V, g.N2V
    GV, GP, DH, PN, PF = g.GV, g.GP, g.DH, g.PN, g.PF
    G2, G1, GQ, GO = g.G2, g.G1, g.GQ, g.GO
    DO, DPRE = g.DO, g.DPRE
    E1, F1, EQ, FQ, SG = g.E1, g.F1, g.EQ, g.FQ, g.SG
    blocks = [slice(256 * k, 256 * k + 256) for k in range(D // 256)]
    mine = pl.ds(pl.multiple_of(V * f, V), V)
    hc, hr = HC // 2, RP // 2
    g2_ring = [
        RingReduce(G2, 0, hc, g.st2, g.rr2, g.rl2),
        RingReduce(G2, hc, hc, g.st2, g.rr2, g.rl2),
    ]
    g1_ring = [
        RingReduce(G1, 0, hr, g.st1, g.rr1, g.rl1),
        RingReduce(G1, hr, hr, g.st1, g.rr1, g.rl1),
    ]
    gq_ring = [
        RingReduce(GQ, 0, hr, g.stq, g.rrq, g.rlq),
        RingReduce(GQ, hr, hr, g.stq, g.rrq, g.rlq),
    ]
    go_ring = RingReduce(GO, 0, R, g.sto, g.rro, g.rlo)
    gs_ring = RingReduce(VG, 0, 16, g.sts, g.rrs, g.rls, F32)

    def finish(*rings):
        for r in rings:
            r.finish()

    def received(copies):
        for c in copies:
            c.wait_recv()

    outs = []

    def store(src, dst, k):
        c = pltpu.make_async_copy(src, dst, lsem.at[8 + k])
        c.start()
        outs.append(c)

    def vec(k):
        return VEC[k : k + 1, :]

    def start():
        st.q = scatter(lambda j: g.sq.at[j], lambda j: AQ.at[p, pl.ds(pl.multiple_of(R * j, R), R), :])
        st.s = scatter(lambda j: AS.at[p, f], lambda j: AS.at[p, j])
        q_ring[0].arrivals = list(st.q)
        s_ring.arrivals = st.s

    def cast_fc1():
        loads[1].wait()
        for j in range(NF):
            for t in range(n):
                at = HC * (NF * t + j)
                g.s1[j, :, HC * t : HC * t + HC] = g.w1_v[:, at : at + HC].astype(BF)
        A1[p, pl.ds(pl.multiple_of(R * f, R), R), :] = g.s1[f]
        st.w1 = scatter(lambda j: g.s1.at[j], lambda j: A1.at[p, pl.ds(pl.multiple_of(R * j, R), R), :])
        w1_ring[0].arrivals = list(st.w1)

    def tokens_start():
        loads[4].wait()
        st.tok = AllGather4(lambda j: TA.at[j])

    def cot_start():
        loads[6].wait()
        st.cot = AllGather4(lambda j: CA.at[j])

    def wo_start():
        o_ring.finish()
        st.wo = AllGather4(lambda j: WO.at[:, j])

    ends = []
    total_len = jnp.int32(0)
    for k in range(g.lengths.shape[1]):
        total_len = total_len + g.lengths[0, k]
        ends.append(total_len)

    def key_segments():
        keyrow = lax.broadcasted_iota(jnp.int32, (1, S_), 1)
        segrow = jnp.zeros((1, S_), jnp.int32)
        for end in ends:
            segrow += (keyrow >= end).astype(jnp.int32)
        return segrow

    def layout():
        row, _seg = column_segment(0, S_, ends)
        before = jnp.zeros((S_, 1), jnp.int32)
        for k, end in enumerate(ends):
            before += jnp.where(row >= end, g.lengths[0, k], 0)
        place = row - before
        img = GRID * GRID
        frame = jnp.zeros((S_, 1), jnp.int32)
        for t in range(1, FRAMES):
            frame += (place >= img * t).astype(jnp.int32)
        rest = place - img * frame
        grow = jnp.zeros((S_, 1), jnp.int32)
        for t in range(1, GRID):
            grow += (rest >= GRID * t).astype(jnp.int32)
        gcol = rest - GRID * grow
        lane = lax.broadcasted_iota(jnp.int32, (S_, 128), 1)
        hot = (lane == frame) | (lane == grow + FRAMES) | (lane == gcol + (FRAMES + GRID))
        g.OH[...] = jnp.where(hot, 1.0, 0.0).astype(BF)
        loads[7].wait()
        g.CS[...] = sum(dot(g.OH[...], g.trig_v[k]) for k in range(3))

    def visible():
        if s_ring.arrivals is st.s:
            received(st.s)
            s_ring.arrivals = []
        vis8 = jnp.concatenate([AS[p, j][4:6, :] for j in range(NF)], axis=0)
        above = lax.broadcasted_iota(jnp.int32, (128, 128), 0)
        tri = above <= lax.broadcasted_iota(jnp.int32, (128, 128), 1)
        within = dot(vis8.astype(BF), jnp.where(tri, 1.0, 0.0).astype(BF))
        base = jnp.zeros((1, 128), F32)
        pieces, vpieces = [], []
        for k in range(8):
            pieces.append(within[k : k + 1, :] + base)
            vpieces.append(vis8[k : k + 1, :])
            base = base + jnp.sum(vis8[k : k + 1, :], axis=1, keepdims=True)
        incl = jnp.concatenate(pieces, axis=1)
        visrow = jnp.concatenate(vpieces, axis=1)
        rank = jnp.where(visrow > 0.5, incl - 1.0, -1.0).astype(jnp.int32)
        sel = lax.broadcasted_iota(jnp.int32, (VP, S_), 0) == rank
        SM[...] = jnp.where(sel, 1.0, 0.0).astype(BF)

    def rounded(v):
        return v.astype(BF).astype(F32)

    def turn(v, by):
        by = by % 128
        return v if by == 0 else pltpu.roll(v, by, 1)

    def small_vectors():
        s_ring.finish()
        lane128 = lax.broadcasted_iota(jnp.int32, (n, 128), 1)
        rows0 = [AS[:, j, 0, :] for j in range(NF)]
        rows1 = [AS[:, j, 1, :] for j in range(NF)]
        rows2 = [AS[:, j, 2, :] for j in range(NF)]
        for k in range(6):
            src = rows0 if k < 4 else rows1
            piece = jnp.zeros((n, 128), F32)
            for j in range(NF):
                piece = jnp.where(lax.div(lane128, R) == j, turn(src[j], R * (j - k % 4)), piece)
            for q in range(n):
                VEC[k : k + 1, 128 * q : 128 * q + 128] = rounded(piece[q : q + 1, :])
        for q in range(n):
            VEC[6:7, 128 * q : 128 * q + 128] = rounded(AS[q, f][3:4, :])
        t0 = jnp.where(lane128 < 96, rows2[0], turn(rows2[1], 96))
        t1 = jnp.where(lane128 < 64, turn(rows2[1], -32), turn(rows2[2], 64))
        t2 = jnp.where(lane128 < 32, turn(rows2[2], -64), turn(rows2[3], 32))
        for q in range(n):
            for k, t in enumerate((t0, t1, t2)):
                BQ[0:1, 384 * q + 128 * k : 384 * q + 128 * k + 128] = rounded(t[q : q + 1, :])

    def first_norm():
        st.tok.finish()

        def block(b, _):
            xhat, _inv = norm_stats(TA[b].astype(F32))
            N1[b] = (xhat * vec(0) + vec(1)).astype(BF)
            return 0

        lax.fori_loop(0, NF, block, 0)

    def project_half(part):
        finish(*q_ring)

        def block(b, _):
            rows = pl.ds(pl.multiple_of(b * T, T), T)
            cs = g.CS[rows, :]
            for t, dst in enumerate((Q, K, W)):
                out = dot(N1[b], AQ[:, :, C * t : C * t + C].reshape(D, C))
                out = out + BQ[0:1, pl.ds(pl.multiple_of(D * t + C * f, 128), C)]
                if t == 2:
                    dst[rows, :] = out.astype(BF)
                    continue
                for hh in range(C // 128):
                    u = out[:, 128 * hh : 128 * hh + 128]
                    u = (u * cs[:, :128] + swap_halves(u) * cs[:, 128:]).astype(BF)
                    dst[rows, 128 * hh : 128 * hh + 128] = u * BF(0.125) if t == 0 else u
            return 0

        lax.fori_loop(NF // 2 * part, NF // 2 * (part + 1), block, 0)

    lane_c = lax.broadcasted_iota(jnp.int32, (1, C), 1)
    hmask = [jnp.where(lax.div(lane_c, HDIM) == hd, 1.0, 0.0) for hd in range(C // HDIM)]

    def softmax(s):
        e = jnp.exp(s - jnp.max(s, axis=-1, keepdims=True))
        return e * (1.0 / jnp.sum(e, axis=-1, keepdims=True))

    def context_attention():
        for src, dst in ((Q, QV), (K, KV), (W, WV)):
            dst[...] = dot(SM[...], src[...]).astype(BF)
        segrow = key_segments()
        seg8 = jnp.broadcast_to(segrow.astype(F32), (8, S_)).astype(BF)
        segv_row = dot(seg8, SM[...], NT)[0:1, :].astype(jnp.int32)
        segv_col = jnp.sum(SM[...].astype(F32) * segrow.astype(F32), axis=1, keepdims=True).astype(jnp.int32)
        same = segv_col == segv_row
        acc = jnp.zeros((VP, C), F32)
        for hd in range(C // HDIM):
            s = dot(QV[...] * hmask[hd].astype(BF), KV[...], NT)
            pr = softmax(jnp.where(same, s, FILL))
            PV[hd] = pr
            acc += dot(pr.astype(BF), WV[...]) * hmask[hd]
        OV[f] = acc.astype(BF)
        st.ov = AllGather4(lambda j: OV.at[j])

    def attend_target(b, pair):
        rows = slice(T * b, T * b + T)
        _, segq = column_segment(b * T, T, ends)
        same = segq == key_segments()
        for hd in (2 * pair, 2 * pair + 1):
            s = dot(Q[rows, :] * hmask[hd].astype(BF), K[...], NT)
            pr = softmax(jnp.where(same, s, FILL)).astype(BF)
            o = dot(pr, W[...])
            cols = slice(HDIM * hd, HDIM * hd + HDIM)
            OA[f, rows, cols] = o[:, cols].astype(BF)

    def oa_start(part):
        rows = pl.ds(S_ // 2 * part, S_ // 2)
        st.oa[part] = AllGather4(lambda j: OA.at[j, rows, :])

    def select_rows():
        for cols in blocks:
            XV[:, cols] = dot(SM[...], TA[:, :, cols].reshape(S_, 256)).astype(BF)
            N1V[:, cols] = dot(SM[...], N1[:, :, cols].reshape(S_, 256)).astype(BF)

    def select_cot():
        st.cot.finish()
        for cols in blocks:
            DY[:, cols] = dot(SM[...], CA[:, :, cols].reshape(S_, 256)).astype(BF)

    def out_project(parts, cols):
        heads = [WO[n // NF * j : n // NF * (j + 1), :, :, cols].reshape(C, -1) for j in range(NF)]
        return sum(dot(parts(j), heads[j]) for j in range(NF))

    def context_middle():
        st.wo.finish()
        st.ov.finish()
        for cols in blocks:
            X1V[:, cols] = XV[:, cols].astype(F32) + (out_project(lambda j: OV[j], cols) + VEC[4:5, cols])
        xhat, _inv = norm_stats(X1V[...])
        N2V[...] = (xhat * vec(2) + vec(3)).astype(BF)

    def normal_cdf(hid):
        return 0.5 * (1.0 + lax.erf(hid * (1.0 / math.sqrt(2.0))))

    def context_hidden():
        finish(*w1_ring)
        for cols in blocks:
            hid = dot(N2V[...], A1[:, :, cols].reshape(D, 256)) + VEC[6:7, cols]
            cdf = normal_cdf(hid)
            GV[:, cols] = (hid * cdf).astype(BF)
            GP[:, cols] = cdf + hid * (jnp.exp(-0.5 * hid * hid) * (1.0 / math.sqrt(2.0 * math.pi)))

    def outer(dst, lhs, rhs):
        def one(k, _):
            a = lhs[:, pl.ds(pl.multiple_of(128 * k, 128), 128)]
            dst[k] = dot(a, rhs[...], TN)
            return 0

        lax.fori_loop(0, n, one, 0)

    def put_grad(k, vrow):
        for q in range(n):
            VG[q, k : k + 1, :] = vrow[:, 128 * q : 128 * q + 128]

    def fc2_grad():
        outer(G2, GV, DY)

    def hidden_grad():
        finish(*w2_ring)
        for k, cols in enumerate(blocks):
            dg = dot(DY[...], A2[...].reshape(HF, D)[256 * k : 256 * k + 256, :], NT)
            dh = (dg * GP[:, cols]).astype(BF)
            DH[:, cols] = dh
            dc1 = jnp.sum(dh.astype(F32), axis=0, keepdims=True)
            for q in range(2):
                for j in range(NF):
                    piece = dc1[:, 128 * q : 128 * q + 128]
                    VG[2 * k + q, 9 + j : 10 + j, :] = jnp.where(f == j, piece, jnp.zeros((1, 128), F32))

    def second_grad():
        for k, cols in enumerate(blocks):
            part = dot(DH[...], A1[2 * k : 2 * k + 2].reshape(256, HF), NT).astype(BF)
            PN[:, :, cols] = part.reshape(NF, V, 256)
        st.n2 = ReduceScatter4(PN, g.PNr1, g.PNxs, g.PNr2)

    def fc1_grad():
        outer(G1, N2V, DH)

    def context_partial():
        for cols in blocks:
            part = dot(GV[...], A2[:, :, cols].reshape(HF, 256)).astype(BF)
            PF[:, :, cols] = part.reshape(NF, V, 256)
        st.pf = ReduceScatter4(PF, g.PFr1, g.PFxs, g.PFr2)

    def second_norm_back():
        st.n2.finish()
        dyo = DY[mine, :].astype(F32)
        dv, dgain, dshift = norm_back(X1V[mine, :], vec(2), st.n2.total())
        dx1 = dyo + dv
        g.DX1[...] = dx1
        low = dx1.astype(BF)
        g.DP[f] = low
        st.dp = AllGather4(lambda j: g.DP.at[j])
        put_grad(2, dgain)
        put_grad(3, dshift)
        put_grad(4, jnp.sum(low.astype(F32), axis=0, keepdims=True))
        put_grad(5, jnp.sum(dyo, axis=0, keepdims=True))

    def transpose_attended():
        st.ov.finish()
        for j in range(NF):
            ot = OV[j].astype(F32).T.astype(BF)
            OT[n // NF * j : n // NF * (j + 1)] = ot.reshape(n // NF, NF, R, VP)

    def out_grad():
        st.dp.finish()
        go = dot(OT[:, f].reshape(n * R, VP), g.DP[...].reshape(VP, D))
        GO[...] = go.reshape(n, R, D)

    def attended_grad():
        st.dp.finish()
        st.wo.finish()
        wo_heads = WO[pl.ds(n // NF * f, n // NF)].reshape(C, D)
        DO[...] = dot(g.DP[...].reshape(VP, D), wo_heads, NT).astype(BF)

    def attention_back():
        dq = jnp.zeros((VP, C), F32)
        dk = jnp.zeros((VP, C), F32)
        dw = jnp.zeros((VP, C), F32)
        for hd in range(C // HDIM):
            pr = PV[hd]
            dp = dot(DO[...] * hmask[hd].astype(BF), WV[...], NT)
            ds = (pr * (dp - jnp.sum(pr * dp, axis=-1, keepdims=True))).astype(BF)
            dq += dot(ds, KV[...]) * hmask[hd]
            dk += dot(ds, QV[...], TN) * hmask[hd]
            dw += dot(pr.astype(BF), DO[...], TN) * hmask[hd]
        csv = sum(dot(dot(SM[...], g.OH[...]).astype(BF), g.trig_v[k]) for k in range(3))
        for t, (grad, scale) in enumerate(((dq, 0.125), (dk, 1.0))):
            for hh in range(C // 128):
                u = grad[:, 128 * hh : 128 * hh + 128]
                u = u * csv[:, :128] - swap_halves(u) * csv[:, 128:]
                DPRE[:, C * t + 128 * hh : C * t + 128 * hh + 128] = (u * scale).astype(BF)
        DPRE[:, 2 * C :] = dw.astype(BF)

    def qkv_grad():
        outer(GQ, N1V, DPRE)

    def qkv_bias_grad():
        BG[...] = jnp.zeros(BG.shape, F32)
        db = jnp.sum(DPRE[...].astype(F32), axis=0, keepdims=True)
        for t in range(3):
            BG[0:1, pl.ds(pl.multiple_of(D * t + C * f, 128), C)] = db[:, C * t : C * t + C]
        for q in range(n):
            for t in range(3):
                VG[q, 6 + t : 7 + t, :] = BG[0:1, 384 * q + 128 * t : 384 * q + 128 * t + 128]
            VG[q, 13:16, :] = jnp.zeros((3, 128), F32)

    def first_grad():
        drain(st.n2.ca, st.n2.cb)
        for k, cols in enumerate(blocks):
            part = dot(DPRE[...], AQ[2 * k : 2 * k + 2].reshape(256, 3 * C), NT).astype(BF)
            PN[:, :, cols] = part.reshape(NF, V, 256)
        st.n1 = ReduceScatter4(PN, g.PMr1, g.PMxs, g.PMr2)

    def first_norm_back():
        st.n1.finish()
        dv, dgain, dshift = norm_back(XV[mine, :].astype(F32), vec(0), st.n1.total())
        g.DX[f] = (g.DX1[...] + dv).astype(BF)
        st.dx = AllGather4(lambda j: g.DX.at[j])
        put_grad(0, dgain)
        put_grad(1, dshift)

    def context_result():
        st.pf.finish()
        g.CO[f] = (X1V[mine, :] + (st.pf.total() + vec(5))).astype(BF)
        st.co = AllGather4(lambda j: g.CO.at[j])

    def home(src, dst):
        s = SM[:, pl.ds(pl.multiple_of(T * f, 128), T)]
        for cols in blocks:
            dst[:, cols] = dot(s, src[:, :, cols].reshape(VP, 256), TN).astype(BF)

    def home_context():
        st.co.finish()
        home(g.CO, g.CH)
        store(g.CH, g.ctx_o, 0)

    def home_grad():
        st.dx.finish()
        home(g.DX, g.DXH)
        store(g.DXH, g.dx_o, 1)

    def target_middle(b):
        st.wo.finish()
        st.oa[b // 2].finish()
        for cols in blocks:
            g.X1B[:, cols] = TA[b, :, cols].astype(F32) + (
                out_project(lambda j: OA[j, T * b : T * b + T, :], cols) + VEC[4:5, cols]
            )
        x1 = g.X1B[...]
        xh, _inv = norm_stats(x1)
        N2[b] = (xh * vec(2) + vec(3)).astype(BF)

        @pl.when(f == b)
        def _():
            g.X1H[...] = x1

    def target_hidden(b):
        finish(*w1_ring)
        for cols in blocks:
            hid = dot(N2[b], A1[:, :, cols].reshape(D, 256)) + VEC[6:7, cols]
            GT[b, :, cols] = (hid * normal_cdf(hid)).astype(BF)

    def target_out(b):
        finish(*w2_ring)
        for cols in blocks:
            PT[b, :, cols] = dot(GT[b], A2[:, :, cols].reshape(HF, 256)).astype(BF)
        if b == NF - 1:
            st.pt = ReduceScatter4(PT, g.PTr1, g.PTxs, g.PTr2)

    def target_result():
        st.pt.finish()
        g.TO[...] = (g.X1H[...] + (st.pt.total() + vec(5))).astype(BF)
        store(g.TO, g.tgt_o, 3)

    def fc2_grad_done():
        finish(*g2_ring)
        for k, ring in enumerate(g2_ring):
            g.D2[hc * k : hc * k + hc, :] = ring.total()
        store(g.D2, g.g2_o, 2)

    def fc1_grad_trade():
        finish(*g1_ring)
        for k, ring in enumerate(g1_ring):
            E1[2 * k : 2 * k + 2] = ring.total().astype(BF).reshape(2, R, HF)
        F1[f] = E1[f]
        st.e1 = scatter(lambda j: E1.at[j], lambda j: F1.at[j])

    def fc1_grad_done():
        received(st.e1)
        for j in range(NF):
            for t in range(n):
                at = HC * (NF * t + j)
                g.D1[:, at : at + HC] = F1[j, :, HC * t : HC * t + HC].astype(F32)
        store(g.D1, g.g1_o, 5)

    def out_grad_done():
        go_ring.finish()
        g.DOo[...] = go_ring.total()
        store(g.DOo, g.go_o, 4)

    def qkv_grad_trade():
        finish(*gq_ring)
        for k, ring in enumerate(gq_ring):
            EQ[2 * k : 2 * k + 2] = ring.total().astype(BF).reshape(2, R, 3 * C)
        FQ[f] = EQ[f]
        st.eq = scatter(lambda j: EQ.at[j], lambda j: FQ.at[j])

    def qkv_grad_done():
        received(st.eq)
        for j in range(NF):
            for t in range(3):
                g.DQo[:, D * t + C * j : D * t + C * j + C] = FQ[j, :, C * t : C * t + C].astype(F32)
        store(g.DQo, g.gq_o, 7)

    def small_grad_trade():
        gs_ring.finish()
        SG[f] = gs_ring.total()
        st.sg = scatter(lambda j: SG.at[f], lambda j: SG.at[j])

    def small_grad_done():
        received(st.sg)
        g.SGo[...] = SG[0] + SG[1] + SG[2] + SG[3]
        store(g.SGo, g.sg_o, 6)

    start()
    cast_fc1()
    tokens_start()
    cot_start()
    o_ring.step(0)
    w2_ring[0].step(0)
    layout()
    w2_ring[1].step(0)
    o_ring.step(1)
    q_ring[0].step(0)
    q_ring[1].step(0)
    s_ring.step(0)
    visible()
    w1_ring[0].step(0)
    o_ring.step(2)
    q_ring[0].step(1)
    q_ring[1].step(1)
    s_ring.step(1)
    w1_ring[0].step(1)
    st.tok.forward()
    o_ring.step(3)
    q_ring[0].step(2)
    q_ring[1].step(2)
    s_ring.step(2)
    w1_ring[1].step(0)
    wo_start()
    w1_ring[0].step(2)
    q_ring[0].step(3)
    st.cot.forward()
    q_ring[1].step(3)
    s_ring.step(3)
    select_cot()
    w1_ring[1].step(1)
    w1_ring[0].step(3)
    w2_ring[0].step(1)
    small_vectors()
    first_norm()
    project_half(0)
    st.wo.forward()
    w1_ring[1].step(2)
    project_half(1)
    context_attention()
    w2_ring[1].step(1)
    select_rows()
    w2_ring[0].step(2)
    attend_target(0, 0)
    w1_ring[1].step(3)
    attend_target(0, 1)
    st.ov.forward()
    attend_target(1, 0)
    w2_ring[1].step(2)
    context_middle()
    transpose_attended()
    w2_ring[0].step(3)
    attend_target(1, 1)
    oa_start(0)
    context_hidden()
    fc2_grad()
    g2_ring[0].step(0)
    g2_ring[1].step(0)
    w2_ring[1].step(3)
    attend_target(2, 0)
    attend_target(2, 1)
    g2_ring[0].step(1)
    g2_ring[1].step(1)
    st.oa[0].forward()
    attend_target(3, 0)
    hidden_grad()
    second_grad()
    g2_ring[0].step(2)
    fc1_grad()
    g1_ring[0].step(0)
    g1_ring[1].step(0)
    st.n2.forward()
    context_partial()
    target_middle(0)
    g2_ring[1].step(2)
    attend_target(3, 1)
    g2_ring[0].step(3)
    oa_start(1)
    second_norm_back()
    g1_ring[0].step(1)
    st.pf.forward()
    target_middle(1)
    target_hidden(0)
    g1_ring[1].step(1)
    target_hidden(1)
    target_out(0)
    target_out(1)
    st.oa[1].forward()
    g2_ring[1].step(3)
    target_middle(2)
    g1_ring[0].step(2)
    st.dp.forward()
    target_middle(3)
    target_hidden(2)
    g1_ring[1].step(2)
    attended_grad()
    attention_back()
    qkv_grad()
    gq_ring[0].step(0)
    gq_ring[1].step(0)
    out_grad()
    go_ring.step(0)
    g1_ring[0].step(3)
    first_grad()
    qkv_bias_grad()
    context_result()
    target_hidden(3)
    target_out(2)
    g1_ring[1].step(3)
    st.n1.forward()
    gq_ring[0].step(1)
    target_out(3)
    fc2_grad_done()
    gq_ring[1].step(1)
    go_ring.step(1)
    st.co.forward()
    st.pt.forward()
    first_norm_back()
    gs_ring.step(0)
    home_context()
    fc1_grad_trade()
    gq_ring[0].step(2)
    gq_ring[1].step(2)
    go_ring.step(2)
    gs_ring.step(1)
    gq_ring[0].step(3)
    gq_ring[1].step(3)
    target_result()
    go_ring.step(3)
    gs_ring.step(2)
    st.dx.forward()
    home_grad()
    qkv_grad_trade()
    fc1_grad_done()
    out_grad_done()
    gs_ring.step(3)
    small_grad_trade()
    qkv_grad_done()
    small_grad_done()
    for c in outs:
        c.wait()
    for c in pending:
        c.wait_send()


def run_layer(n, tokens, cot, lengths, small, wqkv, wo, w1, w2, V):
    T, D = tokens.shape
    NF = 4
    FF = w1.shape[1]
    R = wo.shape[0]
    RP = R * NF
    HC = w2.shape[0]
    HF = HC * n
    C = D // NF
    VP = V * NF
    S_ = T * NF
    h2 = n // 2
    B, F = BF, F32
    vm = pltpu.VMEM
    scratch = dict(
        wqkv_v=vm((R, 3 * D), F), w1_v=vm((R, FF), F), wo_v=vm((R, D), F), w2_v=vm((HC, D), F),
        small_v=vm((8, 128), F), trig_v=vm((3, 128, 256), B),
        sq=vm((NF, R, 3 * C), B), s1=vm((NF, R, HF), B),
        AS=vm((n, NF, 8, 128), F), AQ=vm((n, RP, 3 * C), B), WO=vm((n, NF, R, D), B),
        A1=vm((n, RP, HF), B), A2=vm((n, HC, D), B),
        TA=vm((NF, T, D), B), CA=vm((NF, T, D), B), N1=vm((NF, T, D), B),
        OH=vm((S_, 128), B), CS=vm((S_, 256), F), SM=vm((VP, S_), B),
        VEC=vm((8, D), F), BQ=vm((8, 3 * D), F), BG=vm((8, 3 * D), F),
        Q=vm((S_, C), B), K=vm((S_, C), B), W=vm((S_, C), B),
        QV=vm((VP, C), B), KV=vm((VP, C), B), WV=vm((VP, C), B),
        OV=vm((NF, VP, C), B), PV=vm((C // HDIM, VP, VP), F), OA=vm((NF, S_, C), B),
        XV=vm((VP, D), B), N1V=vm((VP, D), B), DY=vm((VP, D), B),
        X1V=vm((VP, D), F), N2V=vm((VP, D), B), GV=vm((VP, HF), B), GP=vm((VP, HF), F),
        G2=vm((n, HC, D), F), G1=vm((n, RP, HF), F), GQ=vm((n, RP, 3 * C), F), GO=vm((n, R, D), F),
        VG=vm((n, 16, 128), F),
        st2=vm((HC, D), B), rr2=vm((h2, HC, D), B), rl2=vm((h2, HC, D), B),
        st1=vm((RP, HF), B), rr1=vm((h2, RP, HF), B), rl1=vm((h2, RP, HF), B),
        stq=vm((RP, 3 * C), B), rrq=vm((h2, RP, 3 * C), B), rlq=vm((h2, RP, 3 * C), B),
        sto=vm((R, D), B), rro=vm((h2, R, D), B), rlo=vm((h2, R, D), B),
        sts=vm((16, 128), F), rrs=vm((h2, 16, 128), F), rls=vm((h2, 16, 128), F),
        DH=vm((VP, HF), B), PN=vm((NF, V, D), B), PF=vm((NF, V, D), B),
        PNr1=vm((2, V, D), B), PNxs=vm((V, D), B), PNr2=vm((V, D), B),
        PMr1=vm((2, V, D), B), PMxs=vm((V, D), B), PMr2=vm((V, D), B),
        PFr1=vm((2, V, D), B), PFxs=vm((V, D), B), PFr2=vm((V, D), B),
        DX1=vm((V, D), F), DP=vm((NF, V, D), B), OT=vm((n, NF, R, VP), B), DO=vm((VP, C), B),
        DPRE=vm((VP, 3 * C), B), CO=vm((NF, V, D), B), DX=vm((NF, V, D), B),
        X1B=vm((T, D), F), X1H=vm((T, D), F), GT=vm((NF, T, HF), B),
        PTr1=vm((2, T, D), B), PTxs=vm((T, D), B), PTr2=vm((T, D), B),
        CH=vm((T, D), B), DXH=vm((T, D), B), TO=vm((T, D), B),
        SG=vm((NF, 16, 128), F), SGo=vm((16, 128), F),
        E1=vm((NF, R, HF), B), F1=vm((NF, R, HF), B), EQ=vm((NF, R, 3 * C), B), FQ=vm((NF, R, 3 * C), B),
        send_sems=pltpu.SemaphoreType.DMA((200,)), recv_sems=pltpu.SemaphoreType.DMA((200,)),
        local_sems=pltpu.SemaphoreType.DMA((16,)),
    )
    arr = jax.ShapeDtypeStruct
    ins = dict(
        lengths=lengths, tok=tokens, cot=cot, small=small, wqkv=wqkv, wo=wo, w1=w1, w2=w2,
        trig=jnp.asarray(trig_table()),
    )
    outs = dict(
        tgt_o=arr((T, D), B), ctx_o=arr((T, D), B), dx_o=arr((T, D), B), gq_o=arr((R, 3 * D), F),
        go_o=arr((R, D), F), g1_o=arr((R, FF), F), g2_o=arr((HC, D), F), sg_o=arr((16, 128), F),
    )
    names = [*ins, *outs, *scratch]
    any_spec = pl.BlockSpec(memory_space=pl.ANY)
    return pl.pallas_call(
        functools.partial(layer_kernel, (n, D, FF, T, V), names),
        out_shape=list(outs.values()),
        in_specs=[pl.BlockSpec(memory_space=pltpu.SMEM)] + [any_spec] * 8,
        out_specs=[any_spec] * 8,
        scratch_shapes=list(scratch.values()),
        compiler_params=pltpu.CompilerParams(
            collective_id=0, has_side_effects=True, vmem_limit_bytes=67043328
        ),
        name="layer",
    )(*ins.values())


def on_device(
    tokens, lengths, visibility_mask, visible_counts, ln1_gain, ln1_bias, qkv_weight, qkv_bias,
    out_weight, out_bias, ln2_gain, ln2_bias, fc1_weight, fc1_bias, fc2_weight, fc2_bias, context_cot,
):
    n = lax.axis_size("dp")
    f = lax.axis_index("fsdp")
    R = ln1_gain.shape[0]
    running = jnp.cumsum(visibility_mask)
    visible = (visibility_mask * (running <= visible_counts[0, 0]).astype(jnp.int32)).astype(F32)
    pad = lambda k: jnp.zeros((k,), F32)
    small = jnp.concatenate(
        [
            ln1_gain, ln1_bias, ln2_gain, ln2_bias,
            out_bias, fc2_bias, pad(64),
            qkv_bias, pad(32),
            fc1_bias,
            visible, pad(256),
        ]
    ).reshape(8, 128)
    tgt, ctx, dx, gq, go, g1, g2, sg = run_layer(
        n, tokens, context_cot, lengths, small, qkv_weight, out_weight, fc1_weight, fc2_weight, VIS_DEV
    )

    def own(k):
        return lax.dynamic_slice(sg[k], (R * f,), (R,))

    gbq = lax.dynamic_slice(sg[6:9].reshape(-1), (3 * R * f,), (3 * R,))
    gb1 = lax.dynamic_slice(sg[9:13].reshape(-1), (4 * R * f,), (4 * R,))
    return (tgt, ctx, dx, own(0), own(1), gq, gbq, go, own(4), own(2), own(3), g1, gb1, g2, own(5))


def layer_norm(inputs, scale_vec, shift_vec):
    center = inputs - jnp.mean(inputs, axis=-1, keepdims=True)
    spread = jnp.mean(center * center, axis=-1, keepdims=True)
    return center * lax.rsqrt(spread + norm_eps) * scale_vec + shift_vec


def gelu_erf(values):
    return jax.nn.gelu(values, approximate=False)


def pack_layout(seq_lens, pack_len):
    seq_ends = jnp.cumsum(seq_lens)
    places = jnp.arange(pack_len, dtype=jnp.int32)
    passed = places[:, None] >= seq_ends[None, :]
    segment = jnp.sum(passed.astype(jnp.int32), axis=1)
    before = jnp.sum(jnp.where(passed, seq_lens[None, :], 0), axis=1)
    return (segment, places - before)


def rope_tables(places):
    frame_index = (places // (GRID * GRID)).astype(jnp.float32)
    grid_row = (places // GRID % GRID).astype(jnp.float32)
    grid_col = (places % GRID).astype(jnp.float32)
    pair_index = jnp.arange(HDIM // 2, dtype=jnp.int32)
    axis_pick = jnp.minimum(pair_index // 11, 2)
    pair_order = (pair_index - 11 * axis_pick).astype(jnp.float32)
    frequency = jnp.exp(pair_order * (-math.log(10000.0) / 11.0))
    angles = (
        frame_index[:, None] * (axis_pick == 0).astype(jnp.float32)[None, :]
        + grid_row[:, None] * (axis_pick == 1).astype(jnp.float32)[None, :]
        + grid_col[:, None] * (axis_pick == 2).astype(jnp.float32)[None, :]
    ) * frequency[None, :]
    return (jnp.cos(angles), jnp.sin(angles))


def rotate(heads, cosine_table, sine_table):
    half_size = heads.shape[-1] // 2
    first_half = heads[..., :half_size]
    second_half = heads[..., half_size:]
    cosine_cols = cosine_table[:, None, :]
    sine_cols = sine_table[:, None, :]
    return jnp.concatenate(
        [
            first_half * cosine_cols - second_half * sine_cols,
            second_half * cosine_cols + first_half * sine_cols,
        ],
        axis=-1,
    )


def rotate_back(grads, cosine_table, sine_table):
    half_size = grads.shape[-1] // 2
    first_half = grads[..., :half_size]
    second_half = grads[..., half_size:]
    cosine_cols = cosine_table[:, None, :]
    sine_cols = sine_table[:, None, :]
    return jnp.concatenate(
        [
            first_half * cosine_cols + second_half * sine_cols,
            second_half * cosine_cols - first_half * sine_cols,
        ],
        axis=-1,
    )


def project(token_rows, weights, cosine_table, sine_table):
    inputs = token_rows.astype(jnp.float32)
    row_count = inputs.shape[0]
    model_width = inputs.shape[1]
    normed = layer_norm(
        inputs, weights[0].astype(jnp.float32), weights[1].astype(jnp.float32)
    ).astype(jnp.bfloat16)
    joined = jnp.dot(normed, weights[2], preferred_element_type=jnp.float32) + weights[3].astype(
        jnp.float32
    )
    query_heads = rotate(
        joined[:, :model_width].reshape(row_count, HEADS, HDIM), cosine_table, sine_table
    ).astype(jnp.bfloat16)
    key_flat = (
        rotate(
            joined[:, model_width : 2 * model_width].reshape(row_count, HEADS, HDIM),
            cosine_table,
            sine_table,
        )
        .astype(jnp.bfloat16)
        .reshape(row_count, model_width)
    )
    value_flat = joined[:, 2 * model_width :].astype(jnp.bfloat16)
    return (inputs, normed, query_heads, key_flat, value_flat)


def attend(query_heads, key_flat, value_flat, seg_query, seg_key):
    key_heads = key_flat.reshape(key_flat.shape[0], HEADS, HDIM)
    value_heads = value_flat.reshape(value_flat.shape[0], HEADS, HDIM)
    scores = jnp.einsum(
        "qhd,khd->hqk", query_heads, key_heads, preferred_element_type=jnp.float32
    ) * HDIM ** (-0.5)
    allowed = seg_query[:, None] == seg_key[None, :]
    masked = jnp.where(allowed[None], scores, masked_fill)
    row_max = jnp.max(masked, axis=-1, keepdims=True)
    raised = jnp.exp(masked - row_max)
    totals = jnp.sum(raised, axis=-1, keepdims=True)
    attn_probs = (raised / totals).astype(jnp.bfloat16)
    attended = jnp.einsum(
        "hqk,khd->qhd", attn_probs, value_heads, preferred_element_type=jnp.float32
    )
    return (
        attended.reshape(query_heads.shape[0], -1).astype(jnp.bfloat16),
        row_max + jnp.log(totals),
    )


def attend_back(query_heads, key_flat, value_flat, seg_query, seg_key, log_total, grad_att):
    key_heads = key_flat.reshape(key_flat.shape[0], HEADS, HDIM)
    value_heads = value_flat.reshape(value_flat.shape[0], HEADS, HDIM)
    scale_factor = HDIM ** (-0.5)
    scores = (
        jnp.einsum("qhd,khd->hqk", query_heads, key_heads, preferred_element_type=jnp.float32)
        * scale_factor
    )
    allowed = seg_query[:, None] == seg_key[None, :]
    masked = jnp.where(allowed[None], scores, masked_fill)
    attn_probs = jnp.exp(masked - log_total)
    grad_heads = grad_att.reshape(grad_att.shape[0], HEADS, HDIM)
    grad_probs = jnp.einsum(
        "qhd,khd->hqk", grad_heads, value_heads, preferred_element_type=jnp.float32
    )
    row_delta = jnp.sum(attn_probs * grad_probs, axis=-1, keepdims=True)
    grad_scores = (attn_probs * (grad_probs - row_delta)).astype(jnp.bfloat16)
    grad_query = (
        jnp.einsum("hqk,khd->qhd", grad_scores, key_heads, preferred_element_type=jnp.float32)
        * scale_factor
    )
    grad_key = (
        jnp.einsum("hqk,qhd->khd", grad_scores, query_heads, preferred_element_type=jnp.float32)
        * scale_factor
    )
    grad_value = jnp.einsum(
        "hqk,qhd->khd",
        attn_probs.astype(jnp.bfloat16),
        grad_heads,
        preferred_element_type=jnp.float32,
    )
    return (
        grad_query,
        grad_key.reshape(key_flat.shape[0], -1),
        grad_value.reshape(value_flat.shape[0], -1),
    )


def finish(inputs, attended, weights):
    middle = inputs + (
        jnp.dot(attended, weights[4], preferred_element_type=jnp.float32)
        + weights[5].astype(jnp.float32)
    )
    second = layer_norm(
        middle, weights[6].astype(jnp.float32), weights[7].astype(jnp.float32)
    ).astype(jnp.bfloat16)
    hidden = jnp.dot(second, weights[8], preferred_element_type=jnp.float32) + weights[9].astype(
        jnp.float32
    )
    activated = gelu_erf(hidden).astype(jnp.bfloat16)
    result = middle + (
        jnp.dot(activated, weights[10], preferred_element_type=jnp.float32)
        + weights[11].astype(jnp.float32)
    )
    return (result, middle, second, hidden, activated)


def gathered_device(
    tokens,
    lengths,
    visibility_mask,
    visible_counts,
    ln1_gain,
    ln1_bias,
    qkv_weight,
    qkv_bias,
    out_weight,
    out_bias,
    ln2_gain,
    ln2_bias,
    fc1_weight,
    fc1_bias,
    fc2_weight,
    fc2_bias,
    context_cot,
):
    tok_rows = tokens.shape[0]
    model_width = tokens.shape[1]
    groups = lax.axis_size("fsdp")
    member = lax.axis_index("fsdp")
    pack_len = tok_rows * groups
    vis_rows = VIS_DEV
    vis_pack = vis_rows * groups
    zero_low = jnp.zeros((), jnp.bfloat16)
    shards = [
        weight.astype(jnp.bfloat16)
        for weight in (
            ln1_gain,
            ln1_bias,
            qkv_weight,
            qkv_bias,
            out_weight,
            out_bias,
            ln2_gain,
            ln2_bias,
            fc1_weight,
            fc1_bias,
            fc2_weight,
            fc2_bias,
        )
    ]
    weights = (
        lax.all_gather(shards[0], ("dp", "fsdp"), axis=0, tiled=True),
        lax.all_gather(shards[1], ("dp", "fsdp"), axis=0, tiled=True),
        lax.all_gather(shards[2], ("dp", "fsdp"), axis=0, tiled=True),
        lax.all_gather(shards[3], ("dp", "fsdp"), axis=0, tiled=True),
        lax.all_gather(shards[4], ("dp", "fsdp"), axis=0, tiled=True),
        lax.all_gather(shards[5], ("dp", "fsdp"), axis=0, tiled=True),
        lax.all_gather(shards[6], ("dp", "fsdp"), axis=0, tiled=True),
        lax.all_gather(shards[7], ("dp", "fsdp"), axis=0, tiled=True),
        lax.all_gather(shards[8], ("dp", "fsdp"), axis=0, tiled=True),
        lax.all_gather(shards[9], ("dp", "fsdp"), axis=0, tiled=True),
        lax.all_gather(shards[10], ("dp", "fsdp"), axis=0, tiled=True),
        lax.all_gather(shards[11], ("dp", "fsdp"), axis=0, tiled=True),
    )
    segment, places = pack_layout(lengths[0], pack_len)
    home_rows = member * tok_rows + jnp.arange(tok_rows, dtype=jnp.int32)
    seg_home = jnp.take(segment, home_rows)
    cos_home, sin_home = rope_tables(jnp.take(places, home_rows))
    inputs, normed, query_heads, key_flat, value_flat = project(tokens, weights, cos_home, sin_home)
    key_pack, value_pack = (
        lax.all_gather(key_flat, "fsdp", axis=0, tiled=True),
        lax.all_gather(value_flat, "fsdp", axis=0, tiled=True),
    )
    attended = attend(query_heads, key_pack, value_pack, seg_home, segment)[0]
    target_out = finish(inputs, attended, weights)[0].astype(jnp.bfloat16)
    running = jnp.cumsum(visibility_mask)
    visible_here = visibility_mask * (running <= visible_counts[0, 0]).astype(jnp.int32)
    visible_all = lax.all_gather(visible_here, "fsdp", axis=0, tiled=True)
    inclusive = jnp.cumsum(visible_all)
    rank_index = jnp.arange(vis_pack, dtype=jnp.int32)
    row_of = jnp.sum((inclusive[None, :] <= rank_index[:, None]).astype(jnp.int32), axis=1)
    owner_dev = row_of // tok_rows
    local_row = row_of % tok_rows
    mine_here = (owner_dev == member)[:, None]
    send_tokens = jnp.where(mine_here, jnp.take(tokens, local_row, axis=0), zero_low)
    send_cot = jnp.where(mine_here, jnp.take(context_cot, local_row, axis=0), zero_low)
    recv_tokens, recv_cot = (
        lax.all_to_all(send_tokens, "fsdp", split_axis=0, concat_axis=0, tiled=True),
        lax.all_to_all(send_cot, "fsdp", split_axis=0, concat_axis=0, tiled=True),
    )
    slot_index = jnp.arange(vis_rows, dtype=jnp.int32)
    my_ranks = member * vis_rows + slot_index
    my_owner = jnp.take(owner_dev, my_ranks)
    my_row = jnp.take(row_of, my_ranks)
    picked = my_owner * vis_rows + slot_index
    bal_tokens = jnp.take(recv_tokens, picked, axis=0)
    bal_cot = jnp.take(recv_cot, picked, axis=0)
    seg_bal = jnp.take(segment, my_row)
    seg_keys = jnp.take(segment, row_of)
    cos_bal, sin_bal = rope_tables(jnp.take(places, my_row))
    inputs_bal, normed_bal, query_bal, key_bal, value_bal = project(
        bal_tokens, weights, cos_bal, sin_bal
    )
    key_vis, value_vis = (
        lax.all_gather(key_bal, "fsdp", axis=0, tiled=True),
        lax.all_gather(value_bal, "fsdp", axis=0, tiled=True),
    )
    attended_bal, log_total = attend(query_bal, key_vis, value_vis, seg_bal, seg_keys)
    result_bal, middle_bal, second_bal, hidden_bal, activated_bal = finish(
        inputs_bal, attended_bal, weights
    )
    grad_result = bal_cot.astype(jnp.float32)
    result_low = grad_result.astype(jnp.bfloat16)
    grad_fc2 = jnp.einsum(
        "nf,nd->fd", activated_bal, result_low, preferred_element_type=jnp.float32
    )
    grad_bfc2 = jnp.sum(result_low.astype(jnp.float32), axis=0)
    grad_activated = jnp.einsum(
        "nd,fd->nf", result_low, weights[10], preferred_element_type=jnp.float32
    )
    gelu_pull = jax.vjp(gelu_erf, hidden_bal)[1]
    hidden_low = gelu_pull(grad_activated)[0].astype(jnp.bfloat16)
    grad_fc1 = jnp.einsum("nd,nf->df", second_bal, hidden_low, preferred_element_type=jnp.float32)
    grad_bfc1 = jnp.sum(hidden_low.astype(jnp.float32), axis=0)
    grad_second = jnp.einsum(
        "nf,df->nd", hidden_low, weights[8], preferred_element_type=jnp.float32
    )
    norm_two_pull = jax.vjp(
        layer_norm, middle_bal, weights[6].astype(jnp.float32), weights[7].astype(jnp.float32)
    )[1]
    grad_mid_norm, grad_gain_two, grad_shift_two = norm_two_pull(grad_second)
    grad_middle = grad_result + grad_mid_norm
    middle_low = grad_middle.astype(jnp.bfloat16)
    grad_wout = jnp.einsum(
        "nd,ne->de", attended_bal, middle_low, preferred_element_type=jnp.float32
    )
    grad_bout = jnp.sum(middle_low.astype(jnp.float32), axis=0)
    grad_att = jnp.einsum(
        "ne,de->nd", middle_low, weights[4], preferred_element_type=jnp.float32
    ).astype(jnp.bfloat16)
    grad_query, grad_key_all, grad_value_all = attend_back(
        query_bal, key_vis, value_vis, seg_bal, seg_keys, log_total, grad_att
    )
    grad_key_own, grad_value_own = (
        lax.psum_scatter(
            grad_key_all.astype(jnp.bfloat16), "fsdp", scatter_dimension=0, tiled=True
        ).astype(jnp.float32),
        lax.psum_scatter(
            grad_value_all.astype(jnp.bfloat16), "fsdp", scatter_dimension=0, tiled=True
        ).astype(jnp.float32),
    )
    grad_query_pre = rotate_back(grad_query, cos_bal, sin_bal).reshape(vis_rows, model_width)
    grad_key_pre = rotate_back(
        grad_key_own.reshape(vis_rows, HEADS, HDIM), cos_bal, sin_bal
    ).reshape(vis_rows, model_width)
    joined_low = jnp.concatenate([grad_query_pre, grad_key_pre, grad_value_own], axis=1).astype(
        jnp.bfloat16
    )
    grad_wqkv = jnp.einsum("nd,ne->de", normed_bal, joined_low, preferred_element_type=jnp.float32)
    grad_bqkv = jnp.sum(joined_low.astype(jnp.float32), axis=0)
    grad_normed = jnp.einsum(
        "ne,de->nd", joined_low, weights[2], preferred_element_type=jnp.float32
    )
    norm_one_pull = jax.vjp(
        layer_norm, inputs_bal, weights[0].astype(jnp.float32), weights[1].astype(jnp.float32)
    )[1]
    grad_in_norm, grad_gain_one, grad_shift_one = norm_one_pull(grad_normed)
    grad_inputs = grad_middle + grad_in_norm
    destinations = jnp.arange(groups, dtype=jnp.int32)
    route_mask = (my_owner[None, :] == destinations[:, None])[:, :, None]
    send_out = jnp.where(route_mask, result_bal.astype(jnp.bfloat16)[None], zero_low).reshape(
        vis_pack, model_width
    )
    send_grad = jnp.where(route_mask, grad_inputs.astype(jnp.bfloat16)[None], zero_low).reshape(
        vis_pack, model_width
    )
    back_out, back_grad = (
        lax.all_to_all(send_out, "fsdp", split_axis=0, concat_axis=0, tiled=True),
        lax.all_to_all(send_grad, "fsdp", split_axis=0, concat_axis=0, tiled=True),
    )
    rank_home = jnp.maximum(jnp.take(inclusive, home_rows) - 1, 0)
    is_visible = (visible_here > 0)[:, None]
    context_out = jnp.where(is_visible, jnp.take(back_out, rank_home, axis=0), zero_low)
    tokens_grad = jnp.where(is_visible, jnp.take(back_grad, rank_home, axis=0), zero_low)
    grad_list = [
        grad_gain_one,
        grad_shift_one,
        grad_wqkv,
        grad_bqkv,
        grad_wout,
        grad_bout,
        grad_gain_two,
        grad_shift_two,
        grad_fc1,
        grad_bfc1,
        grad_fc2,
        grad_bfc2,
    ]
    reduced = (
        lax.psum_scatter(grad_list[0], ("dp", "fsdp"), scatter_dimension=0, tiled=True),
        lax.psum_scatter(grad_list[1], ("dp", "fsdp"), scatter_dimension=0, tiled=True),
        lax.psum_scatter(grad_list[2], ("dp", "fsdp"), scatter_dimension=0, tiled=True),
        lax.psum_scatter(grad_list[3], ("dp", "fsdp"), scatter_dimension=0, tiled=True),
        lax.psum_scatter(grad_list[4], ("dp", "fsdp"), scatter_dimension=0, tiled=True),
        lax.psum_scatter(grad_list[5], ("dp", "fsdp"), scatter_dimension=0, tiled=True),
        lax.psum_scatter(grad_list[6], ("dp", "fsdp"), scatter_dimension=0, tiled=True),
        lax.psum_scatter(grad_list[7], ("dp", "fsdp"), scatter_dimension=0, tiled=True),
        lax.psum_scatter(grad_list[8], ("dp", "fsdp"), scatter_dimension=0, tiled=True),
        lax.psum_scatter(grad_list[9], ("dp", "fsdp"), scatter_dimension=0, tiled=True),
        lax.psum_scatter(grad_list[10], ("dp", "fsdp"), scatter_dimension=0, tiled=True),
        lax.psum_scatter(grad_list[11], ("dp", "fsdp"), scatter_dimension=0, tiled=True),
    )
    return (
        target_out,
        context_out,
        tokens_grad,
        reduced[0],
        reduced[1],
        reduced[2],
        reduced[3],
        reduced[4],
        reduced[5],
        reduced[6],
        reduced[7],
        reduced[8],
        reduced[9],
        reduced[10],
        reduced[11],
    )


def per_device(tokens, *rest):
    n, group = lax.axis_size("dp"), lax.axis_size("fsdp")
    out_rows = rest[7].shape[0]
    fits = group == 4 and n == 8 and out_rows * group == 128
    return (on_device if fits else gathered_device)(tokens, *rest)


def solution(mesh):
    both = ("dp", "fsdp")
    vec, mat = P(both), P(both, None)
    return jax.shard_map(
        per_device,
        mesh=mesh,
        in_specs=(
            mat, P("dp", None), vec, P("dp", "fsdp"), vec, vec, mat, vec, mat, vec, vec, vec,
            mat, vec, mat, vec, mat,
        ),
        out_specs=(mat, mat, mat, vec, vec, mat, vec, mat, vec, vec, vec, mat, vec, mat, vec),
        check_vma=False,
    )
```

```python
import functools
import math
import types

import jax
import jax.numpy as jnp
import numpy as np
from jax import lax
from jax.experimental import pallas as pl
from jax.experimental.pallas import tpu as pltpu
from jax.sharding import PartitionSpec as P

HEADS = 16
HDIM = 64
GRID = 14
VIS_DEV = 64
norm_eps = 1e-06
masked_fill = -1e30
FRAMES = 8
EPS = 1e-06
FILL = -1e30
BF = jnp.bfloat16
F32 = jnp.float32
MESH = pl.DeviceIdType.MESH
NT = (((1,), (1,)), ((), ()))
NN = (((1,), (0,)), ((), ()))
TN = (((0,), (0,)), ((), ()))


def dot(a, b, dims=NN):
    return lax.dot_general(a, b, dims, preferred_element_type=F32)


def trig_table():
    width = FRAMES + 2 * GRID
    lane = np.arange(2 * HDIM)
    pair = lane % (HDIM // 2)
    axis = np.minimum(pair // 11, 2)
    freq = np.exp(((pair - 11 * axis).astype(np.float32)) * np.float32(-math.log(10000.0) / 11.0))
    sign = np.where(lane % HDIM < HDIM // 2, -1.0, 1.0)
    table = np.zeros((128, 4 * HDIM), np.float32)
    row = np.arange(width)
    kind = np.where(row < FRAMES, 0, np.where(row < FRAMES + GRID, 1, 2))
    coord = np.where(kind == 0, row, np.where(kind == 1, row - FRAMES, row - FRAMES - GRID))
    angle = (coord[:, None].astype(np.float32) * freq[None, :].astype(np.float32)).astype(np.float64)
    here = kind[:, None] == axis[None, :]
    table[:width, : 2 * HDIM] = np.where(here, np.cos(angle), 0.0)
    table[:width, 2 * HDIM :] = np.where(here, np.sin(angle) * sign[None, :], 0.0)
    parts = []
    rest = table
    for _ in range(3):
        part = rest.astype(jnp.bfloat16)
        parts.append(part)
        rest = rest - part.astype(np.float32)
    return np.stack(parts)


def norm_stats(v):
    center = v - jnp.mean(v, axis=-1, keepdims=True)
    inv = lax.rsqrt(jnp.mean(center * center, axis=-1, keepdims=True) + EPS)
    return center * inv, inv


def norm_back(v, gain, grad):
    xhat, inv = norm_stats(v)
    gg = grad * gain
    dv = inv * (
        gg - jnp.mean(gg, axis=-1, keepdims=True) - xhat * jnp.mean(gg * xhat, axis=-1, keepdims=True)
    )
    return (
        dv,
        jnp.sum(grad * xhat, axis=0, keepdims=True),
        jnp.sum(grad, axis=0, keepdims=True),
    )


def swap_halves(u):
    lane = lax.broadcasted_iota(jnp.int32, u.shape, 1)
    return jnp.where(
        lax.rem(lane, HDIM) < HDIM // 2,
        pltpu.roll(u, u.shape[1] - HDIM // 2, 1),
        pltpu.roll(u, HDIM // 2, 1),
    )


def column_segment(start, rows, ends):
    row = start + lax.broadcasted_iota(jnp.int32, (rows, 1), 0)
    seg = jnp.zeros((rows, 1), jnp.int32)
    for end in ends:
        seg += (row >= end).astype(jnp.int32)
    return row, seg


ALIASES = dict(N2="N1", PT="N1", D2="w2_v", DOo="wo_v")


class Sems:
    def __init__(self, send, recv):
        self.send, self.recv, self.used = send, recv, 0

    def take(self):
        at = self.used
        self.used += 1
        return self.send.at[at], self.recv.at[at]


def layer_kernel(dims, names, *refs):
    n, D, FF, T, V = dims
    NF = 4
    R = D // (n * NF)
    RP = R * NF
    HC = FF // (NF * n)
    HF = FF // NF
    C = D // NF
    VP = V * NF
    S_ = T * NF
    last = n // 2 - 1
    given = dict(zip(names, refs))
    g = types.SimpleNamespace(**given, **{a: given[b] for a, b in ALIASES.items()})
    sems = Sems(g.send_sems, g.recv_sems)
    lsem = g.local_sems

    p = lax.axis_index("dp")
    f = lax.axis_index("fsdp")
    f1 = f + 1 - 2 * lax.rem(f, 2)
    f2 = lax.rem(f + 2, NF)
    f3 = NF - 1 - f
    par = lax.rem(p, 2)
    half_p = lax.div(p, 2)
    pos = (1 - par) * half_p + par * (n - 1 - half_p)

    def idx(q):
        q = lax.rem(q + 2 * n, n)
        up = lax.div(q, n // 2)
        return (1 - up) * (2 * q) + up * (2 * (n - 1 - q) + 1)

    right, left = idx(pos + 1), idx(pos - 1)

    pending = []

    def remote(src, dst, to):
        ss, rs = sems.take()
        c = pltpu.make_async_remote_copy(
            src_ref=src, dst_ref=dst, send_sem=ss, recv_sem=rs, device_id=to, device_id_type=MESH
        )
        c.start()
        pending.append(c)
        return c, ss, rs

    def drain(*copies):
        for c in copies:
            pending[:] = [d for d in pending if d is not c]
            c.wait_send()

    def arrival(dst, ss, rs, to):
        return pltpu.make_async_remote_copy(
            src_ref=dst, dst_ref=dst, send_sem=ss, recv_sem=rs, device_id=to, device_id_type=MESH
        )

    to1, to2, to3 = {"fsdp": f1}, {"fsdp": f2}, {"fsdp": f3}
    peers = ((f1, to1), (f2, to2), (f3, to3))

    loads = {}
    for i, (src, dst) in enumerate(
        (
            (g.wqkv, g.wqkv_v),
            (g.w1, g.w1_v),
            (g.wo, g.wo_v),
            (g.mask, g.mask_v),
            (g.tok, g.TA.at[f]),
            (g.w2, g.w2_v),
            (g.cot, g.CA.at[f]),
            (g.trig, g.trig_v),
        )
    ):
        c = pltpu.make_async_copy(src, dst, lsem.at[i])
        c.start()
        loads[i] = c
    vectors = []
    for k in range(8):
        vectors.append(pltpu.make_async_copy(given["in%d" % k], given["v%d" % k], lsem.at[8 + k]))
        vectors[k].start()

    barrier = pltpu.get_barrier_semaphore()
    for to in (to1, to2, to3, {"dp": right}, {"dp": left}):
        pl.semaphore_signal(barrier, inc=1, device_id=to, device_id_type=MESH)

    AS, AQ, WO, A1, A2 = g.AS, g.AQ, g.WO, g.A1, g.A2
    TA, CA = g.TA, g.CA

    loads[0].wait()
    for j in range(NF):
        for t in range(3):
            g.sq[j, :, C * t : C * t + C] = g.wqkv_v[:, D * t + C * j : D * t + C * j + C].astype(BF)
    AQ[p, pl.ds(pl.multiple_of(R * f, R), R), :] = g.sq[f]
    for c in vectors:
        c.wait()
    loads[3].wait()
    SV = g.small_v
    SV[...] = jnp.zeros(SV.shape, F32)
    for k in range(8):
        row, at = ((0, R * k), (1, R * (k - 4)), (2, 0), (3, 0))[0 if k < 4 else 1 if k < 6 else k - 4]
        value = given["v%d" % k][...]
        width = value.shape[1]
        wide = value if width == 128 else jnp.concatenate([value, jnp.zeros((1, 128 - width), F32)], axis=1)
        SV[row : row + 1, :] += wide if at == 0 else pltpu.roll(wide, at, 1)
    mask = g.mask_v[...].astype(F32)
    below = lax.broadcasted_iota(jnp.int32, (128, 128), 0) <= lax.broadcasted_iota(jnp.int32, (128, 128), 1)
    tri = jnp.where(below, 1.0, 0.0).astype(BF)
    count = g.counts[0, 0].astype(F32)
    before = jnp.zeros((1, 1), F32)
    for k in range(2):
        ones = mask[:, 128 * k : 128 * k + 128]
        running = dot(jnp.broadcast_to(ones, (8, 128)).astype(BF), tri)[0:1, :] + before
        SV[4 + k : 5 + k, :] = jnp.where(running <= count, ones, 0.0)
        before = before + jnp.sum(ones, axis=1, keepdims=True)
    AS[p, f] = SV[...]
    loads[5].wait()
    A2[p] = g.w2_v[...].astype(BF)
    loads[2].wait()
    WO[p, f] = g.wo_v[...].astype(BF)
    pl.semaphore_wait(barrier, 5)

    def scatter(src, dst):
        got = []
        for fj, to in peers:
            _, ss, rs = remote(src(fj), dst(f), to)
            got.append(arrival(dst(fj), ss, rs, to))
        return got

    class AllGather4:
        def __init__(self, slot):
            self.slot = slot
            _, ss, rs = remote(slot(f), slot(f), to2)
            self.across = arrival(slot(f2), ss, rs, to2)
            _, ss, rs = remote(slot(f), slot(f), to1)
            self.beside = arrival(slot(f1), ss, rs, to1)

        def forward(self):
            self.done = False
            self.across.wait_recv()
            _, ss, rs = remote(self.slot(f2), self.slot(f2), to1)
            self.passed = arrival(self.slot(f3), ss, rs, to1)

        def finish(self):
            if not self.done:
                self.done = True
                self.beside.wait_recv()
                self.passed.wait_recv()

    class ReduceScatter4:
        def __init__(self, part, r1, xs, r2):
            self.part, self.r1, self.xs, self.r2 = part, r1, xs, r2
            self.ca, ss, rs = remote(part.at[f3], r1.at[1], to1)
            self.other = arrival(r1.at[1], ss, rs, to1)
            self.cb, ss, rs = remote(part.at[f1], r1.at[0], to1)
            self.own = arrival(r1.at[0], ss, rs, to1)

        def forward(self):
            self.other.wait_recv()
            self.xs[...] = (self.part[f2].astype(F32) + self.r1[1].astype(F32)).astype(BF)
            _, ss, rs = remote(self.xs, self.r2, to2)
            self.across = arrival(self.r2, ss, rs, to2)

        def finish(self):
            self.own.wait_recv()
            self.across.wait_recv()

        def total(self):
            return self.part[f].astype(F32) + self.r1[0].astype(F32) + self.r2[...].astype(F32)

    class RingGather:
        def __init__(self, view, rows):
            self.view, self.rows = view, rows
            self.arrivals = []

        def step(self, r):
            for a in self.arrivals:
                a.wait_recv()
            self.arrivals = []
            h = self.rows // 2
            spans = ((0, self.rows), (0, self.rows)) if r < last else ((0, h), (h, h))
            for way, (s, c) in zip((1, -1), spans):
                to, frm = ({"dp": right}, {"dp": left}) if way == 1 else ({"dp": left}, {"dp": right})
                mine = self.view(idx(pos - way * r), s, c)
                _, ss, rs = remote(mine, mine, to)
                self.arrivals.append(arrival(self.view(idx(pos - way * (r + 1)), s, c), ss, rs, frm))

        def finish(self):
            for a in self.arrivals:
                a.wait_recv()
            self.arrivals = []

    def rows_view(ref, offset):
        return lambda slot, s, c: ref.at[slot, pl.ds(offset + s, c), :]

    h = RP // 2
    q_ring = [RingGather(rows_view(AQ, 0), h), RingGather(rows_view(AQ, h), h)]
    w1_ring = [RingGather(rows_view(A1, 0), h), RingGather(rows_view(A1, h), h)]
    w2_ring = [RingGather(rows_view(A2, 0), HC // 2), RingGather(rows_view(A2, HC // 2), HC // 2)]
    o_ring = RingGather(lambda slot, s, c: WO.at[slot, f, pl.ds(s, c), :], R)
    s_ring = RingGather(lambda slot, s, c: AS.at[slot, pl.ds(s, c)], NF)

    class RingReduce:
        def __init__(self, grads, start, rows, st, rr, rl, wire=BF):
            self.G, self.o, self.rows, self.st, self.rr, self.rl = grads, start, rows, st, rr, rl
            self.wire = wire
            self.arrivals = []

        def piece(self, ref, slot, s, c):
            return ref.at[slot, pl.ds(self.o + s, c), :]

        def step(self, r):
            for a in self.arrivals:
                a.wait_recv()
            self.arrivals = []
            o, rows = self.o, self.rows
            hh = rows // 2
            if r == 0:
                far = idx(pos + n // 2)
                self.st[pl.ds(o, rows), :] = self.G[far, pl.ds(o, rows), :].astype(self.wire)
                for buf, s, to, frm in (
                    (self.rr, 0, {"dp": right}, {"dp": left}),
                    (self.rl, hh, {"dp": left}, {"dp": right}),
                ):
                    dst = self.piece(buf, 0, s, hh)
                    _, ss, rs = remote(self.st.at[pl.ds(o + s, hh), :], dst, to)
                    self.arrivals.append(arrival(dst, ss, rs, frm))
                return
            for way, buf, s, to, frm in (
                (1, self.rr, 0, {"dp": right}, {"dp": left}),
                (-1, self.rl, hh, {"dp": left}, {"dp": right}),
            ):
                c = idx(pos + way * (n // 2 - r))
                if r == 1:
                    other = hh - s
                    buf[0, pl.ds(o + s, hh), :] = (
                        buf[0, pl.ds(o + s, hh), :].astype(F32) + self.G[c, pl.ds(o + s, hh), :]
                    ).astype(self.wire)
                    buf[0, pl.ds(o + other, hh), :] = self.G[c, pl.ds(o + other, hh), :].astype(self.wire)
                else:
                    buf[r - 1, pl.ds(o, rows), :] = (
                        buf[r - 1, pl.ds(o, rows), :].astype(F32) + self.G[c, pl.ds(o, rows), :]
                    ).astype(self.wire)
                src, dst = self.piece(buf, r - 1, 0, rows), self.piece(buf, r, 0, rows)
                _, ss, rs = remote(src, dst, to)
                self.arrivals.append(arrival(dst, ss, rs, frm))

        def finish(self):
            for a in self.arrivals:
                a.wait_recv()
            self.arrivals = []

        def total(self):
            o, rows = self.o, self.rows
            return (
                self.G[p, pl.ds(o, rows), :]
                + self.rr[last, pl.ds(o, rows), :].astype(F32)
                + self.rl[last, pl.ds(o, rows), :].astype(F32)
            )

    st = types.SimpleNamespace(oa=[None, None])
    N1, N2, GT, PT = g.N1, g.N2, g.GT, g.PT
    VEC, BQ, BG, VG = g.VEC, g.BQ, g.BG, g.VG
    Q, K, W, QV, KV, WV = g.Q, g.K, g.W, g.QV, g.KV, g.WV
    SM, OV, PV, OA, OT = g.SM, g.OV, g.PV, g.OA, g.OT
    XV, N1V, DY, X1V, N2V = g.XV, g.N1V, g.DY, g.X1V, g.N2V
    GV, GP, DH, PN, PF = g.GV, g.GP, g.DH, g.PN, g.PF
    G2, G1, GQ, GO = g.G2, g.G1, g.GQ, g.GO
    DO, DPRE = g.DO, g.DPRE
    E1, F1, EQ, FQ, SG = g.E1, g.F1, g.EQ, g.FQ, g.SG
    blocks = [slice(256 * k, 256 * k + 256) for k in range(D // 256)]
    mine = pl.ds(pl.multiple_of(V * f, V), V)
    hc, hr = HC // 2, RP // 2
    g2_ring = [
        RingReduce(G2, 0, hc, g.st2, g.rr2, g.rl2),
        RingReduce(G2, hc, hc, g.st2, g.rr2, g.rl2),
    ]
    g1_ring = [
        RingReduce(G1, 0, hr, g.st1, g.rr1, g.rl1),
        RingReduce(G1, hr, hr, g.st1, g.rr1, g.rl1),
    ]
    gq_ring = [
        RingReduce(GQ, 0, hr, g.stq, g.rrq, g.rlq),
        RingReduce(GQ, hr, hr, g.stq, g.rrq, g.rlq),
    ]
    go_ring = RingReduce(GO, 0, R, g.sto, g.rro, g.rlo)
    gs_ring = RingReduce(VG, 0, 16, g.sts, g.rrs, g.rls, F32)

    def finish(*rings):
        for r in rings:
            r.finish()

    def received(copies):
        for c in copies:
            c.wait_recv()

    outs = []

    def store(src, dst, k):
        c = pltpu.make_async_copy(src, dst, lsem.at[8 + k])
        c.start()
        outs.append(c)

    def vec(k):
        return VEC[k : k + 1, :]

    def start():
        st.q = scatter(lambda j: g.sq.at[j], lambda j: AQ.at[p, pl.ds(pl.multiple_of(R * j, R), R), :])
        st.s = scatter(lambda j: AS.at[p, f], lambda j: AS.at[p, j])
        q_ring[0].arrivals = list(st.q)
        s_ring.arrivals = st.s

    def cast_fc1():
        loads[1].wait()
        for j in range(NF):
            for t in range(n):
                at = HC * (NF * t + j)
                g.s1[j, :, HC * t : HC * t + HC] = g.w1_v[:, at : at + HC].astype(BF)
        A1[p, pl.ds(pl.multiple_of(R * f, R), R), :] = g.s1[f]
        st.w1 = scatter(lambda j: g.s1.at[j], lambda j: A1.at[p, pl.ds(pl.multiple_of(R * j, R), R), :])
        w1_ring[0].arrivals = list(st.w1)

    def tokens_start():
        loads[4].wait()
        st.tok = AllGather4(lambda j: TA.at[j])

    def cot_start():
        loads[6].wait()
        st.cot = AllGather4(lambda j: CA.at[j])

    def wo_start():
        o_ring.finish()
        st.wo = AllGather4(lambda j: WO.at[:, j])

    ends = []
    total_len = jnp.int32(0)
    for k in range(g.lengths.shape[1]):
        total_len = total_len + g.lengths[0, k]
        ends.append(total_len)

    def key_segments():
        keyrow = lax.broadcasted_iota(jnp.int32, (1, S_), 1)
        segrow = jnp.zeros((1, S_), jnp.int32)
        for end in ends:
            segrow += (keyrow >= end).astype(jnp.int32)
        return segrow

    def layout():
        row, _seg = column_segment(0, S_, ends)
        before = jnp.zeros((S_, 1), jnp.int32)
        for k, end in enumerate(ends):
            before += jnp.where(row >= end, g.lengths[0, k], 0)
        place = row - before
        img = GRID * GRID
        frame = jnp.zeros((S_, 1), jnp.int32)
        for t in range(1, FRAMES):
            frame += (place >= img * t).astype(jnp.int32)
        rest = place - img * frame
        grow = jnp.zeros((S_, 1), jnp.int32)
        for t in range(1, GRID):
            grow += (rest >= GRID * t).astype(jnp.int32)
        gcol = rest - GRID * grow
        lane = lax.broadcasted_iota(jnp.int32, (S_, 128), 1)
        hot = (lane == frame) | (lane == grow + FRAMES) | (lane == gcol + (FRAMES + GRID))
        g.OH[...] = jnp.where(hot, 1.0, 0.0).astype(BF)
        loads[7].wait()
        g.CS[...] = sum(dot(g.OH[...], g.trig_v[k]) for k in range(3))

    def visible():
        if s_ring.arrivals is st.s:
            received(st.s)
            s_ring.arrivals = []
        vis8 = jnp.concatenate([AS[p, j][4:6, :] for j in range(NF)], axis=0)
        above = lax.broadcasted_iota(jnp.int32, (128, 128), 0)
        tri = above <= lax.broadcasted_iota(jnp.int32, (128, 128), 1)
        within = dot(vis8.astype(BF), jnp.where(tri, 1.0, 0.0).astype(BF))
        base = jnp.zeros((1, 128), F32)
        pieces, vpieces = [], []
        for k in range(8):
            pieces.append(within[k : k + 1, :] + base)
            vpieces.append(vis8[k : k + 1, :])
            base = base + jnp.sum(vis8[k : k + 1, :], axis=1, keepdims=True)
        incl = jnp.concatenate(pieces, axis=1)
        visrow = jnp.concatenate(vpieces, axis=1)
        rank = jnp.where(visrow > 0.5, incl - 1.0, -1.0).astype(jnp.int32)
        sel = lax.broadcasted_iota(jnp.int32, (VP, S_), 0) == rank
        SM[...] = jnp.where(sel, 1.0, 0.0).astype(BF)

    def rounded(v):
        return v.astype(BF).astype(F32)

    def turn(v, by):
        by = by % 128
        return v if by == 0 else pltpu.roll(v, by, 1)

    def small_vectors():
        s_ring.finish()
        lane128 = lax.broadcasted_iota(jnp.int32, (n, 128), 1)
        rows0 = [AS[:, j, 0, :] for j in range(NF)]
        rows1 = [AS[:, j, 1, :] for j in range(NF)]
        rows2 = [AS[:, j, 2, :] for j in range(NF)]
        for k in range(6):
            src = rows0 if k < 4 else rows1
            piece = jnp.zeros((n, 128), F32)
            for j in range(NF):
                piece = jnp.where(lax.div(lane128, R) == j, turn(src[j], R * (j - k % 4)), piece)
            for q in range(n):
                VEC[k : k + 1, 128 * q : 128 * q + 128] = rounded(piece[q : q + 1, :])
        for q in range(n):
            VEC[6:7, 128 * q : 128 * q + 128] = rounded(AS[q, f][3:4, :])
        t0 = jnp.where(lane128 < 96, rows2[0], turn(rows2[1], 96))
        t1 = jnp.where(lane128 < 64, turn(rows2[1], -32), turn(rows2[2], 64))
        t2 = jnp.where(lane128 < 32, turn(rows2[2], -64), turn(rows2[3], 32))
        for q in range(n):
            for k, t in enumerate((t0, t1, t2)):
                BQ[0:1, 384 * q + 128 * k : 384 * q + 128 * k + 128] = rounded(t[q : q + 1, :])

    def first_norm():
        st.tok.finish()

        def block(b, _):
            xhat, _inv = norm_stats(TA[b].astype(F32))
            N1[b] = (xhat * vec(0) + vec(1)).astype(BF)
            return 0

        lax.fori_loop(0, NF, block, 0)

    def project_half(part):
        finish(*q_ring)

        def block(b, _):
            rows = pl.ds(pl.multiple_of(b * T, T), T)
            cs = g.CS[rows, :]
            for t, dst in enumerate((Q, K, W)):
                out = dot(N1[b], AQ[:, :, C * t : C * t + C].reshape(D, C))
                out = out + BQ[0:1, pl.ds(pl.multiple_of(D * t + C * f, 128), C)]
                if t == 2:
                    dst[rows, :] = out.astype(BF)
                    continue
                for hh in range(C // 128):
                    u = out[:, 128 * hh : 128 * hh + 128]
                    u = (u * cs[:, :128] + swap_halves(u) * cs[:, 128:]).astype(BF)
                    dst[rows, 128 * hh : 128 * hh + 128] = u * BF(0.125) if t == 0 else u
            return 0

        lax.fori_loop(NF // 2 * part, NF // 2 * (part + 1), block, 0)

    lane_c = lax.broadcasted_iota(jnp.int32, (1, C), 1)
    hmask = [jnp.where(lax.div(lane_c, HDIM) == hd, 1.0, 0.0) for hd in range(C // HDIM)]

    def softmax(s):
        e = jnp.exp(s - jnp.max(s, axis=-1, keepdims=True))
        return e * (1.0 / jnp.sum(e, axis=-1, keepdims=True))

    def context_attention():
        for src, dst in ((Q, QV), (K, KV), (W, WV)):
            dst[...] = dot(SM[...], src[...]).astype(BF)
        segrow = key_segments()
        seg8 = jnp.broadcast_to(segrow.astype(F32), (8, S_)).astype(BF)
        segv_row = dot(seg8, SM[...], NT)[0:1, :].astype(jnp.int32)
        segv_col = jnp.sum(SM[...].astype(F32) * segrow.astype(F32), axis=1, keepdims=True).astype(jnp.int32)
        same = segv_col == segv_row
        acc = jnp.zeros((VP, C), F32)
        for hd in range(C // HDIM):
            s = dot(QV[...] * hmask[hd].astype(BF), KV[...], NT)
            pr = softmax(jnp.where(same, s, FILL))
            PV[hd] = pr
            acc += dot(pr.astype(BF), WV[...]) * hmask[hd]
        OV[f] = acc.astype(BF)
        st.ov = AllGather4(lambda j: OV.at[j])

    def attend_target(b, pair):
        rows = slice(T * b, T * b + T)
        _, segq = column_segment(b * T, T, ends)
        same = segq == key_segments()
        for hd in (2 * pair, 2 * pair + 1):
            s = dot(Q[rows, :] * hmask[hd].astype(BF), K[...], NT)
            pr = softmax(jnp.where(same, s, FILL)).astype(BF)
            o = dot(pr, W[...])
            cols = slice(HDIM * hd, HDIM * hd + HDIM)
            OA[f, rows, cols] = o[:, cols].astype(BF)

    def oa_start(part):
        rows = pl.ds(S_ // 2 * part, S_ // 2)
        st.oa[part] = AllGather4(lambda j: OA.at[j, rows, :])

    def select_rows():
        for cols in blocks:
            XV[:, cols] = dot(SM[...], TA[:, :, cols].reshape(S_, 256)).astype(BF)
            N1V[:, cols] = dot(SM[...], N1[:, :, cols].reshape(S_, 256)).astype(BF)

    def select_cot():
        st.cot.finish()
        for cols in blocks:
            DY[:, cols] = dot(SM[...], CA[:, :, cols].reshape(S_, 256)).astype(BF)

    def out_project(parts, cols):
        heads = [WO[n // NF * j : n // NF * (j + 1), :, :, cols].reshape(C, -1) for j in range(NF)]
        return sum(dot(parts(j), heads[j]) for j in range(NF))

    def context_middle():
        st.wo.finish()
        st.ov.finish()
        for cols in blocks:
            X1V[:, cols] = XV[:, cols].astype(F32) + (out_project(lambda j: OV[j], cols) + VEC[4:5, cols])
        xhat, _inv = norm_stats(X1V[...])
        N2V[...] = (xhat * vec(2) + vec(3)).astype(BF)

    def normal_cdf(hid):
        return 0.5 * (1.0 + lax.erf(hid * (1.0 / math.sqrt(2.0))))

    def context_hidden():
        finish(*w1_ring)
        for cols in blocks:
            hid = dot(N2V[...], A1[:, :, cols].reshape(D, 256)) + VEC[6:7, cols]
            cdf = normal_cdf(hid)
            GV[:, cols] = (hid * cdf).astype(BF)
            GP[:, cols] = cdf + hid * (jnp.exp(-0.5 * hid * hid) * (1.0 / math.sqrt(2.0 * math.pi)))

    def outer(dst, lhs, rhs):
        def one(k, _):
            a = lhs[:, pl.ds(pl.multiple_of(128 * k, 128), 128)]
            dst[k] = dot(a, rhs[...], TN)
            return 0

        lax.fori_loop(0, n, one, 0)

    def put_grad(k, vrow):
        for q in range(n):
            VG[q, k : k + 1, :] = vrow[:, 128 * q : 128 * q + 128]

    def fc2_grad():
        outer(G2, GV, DY)

    def hidden_grad():
        finish(*w2_ring)
        for k, cols in enumerate(blocks):
            dg = dot(DY[...], A2[...].reshape(HF, D)[256 * k : 256 * k + 256, :], NT)
            dh = (dg * GP[:, cols]).astype(BF)
            DH[:, cols] = dh
            dc1 = jnp.sum(dh.astype(F32), axis=0, keepdims=True)
            for q in range(2):
                for j in range(NF):
                    piece = dc1[:, 128 * q : 128 * q + 128]
                    VG[2 * k + q, 9 + j : 10 + j, :] = jnp.where(f == j, piece, jnp.zeros((1, 128), F32))

    def second_grad():
        for k, cols in enumerate(blocks):
            part = dot(DH[...], A1[2 * k : 2 * k + 2].reshape(256, HF), NT).astype(BF)
            PN[:, :, cols] = part.reshape(NF, V, 256)
        st.n2 = ReduceScatter4(PN, g.PNr1, g.PNxs, g.PNr2)

    def fc1_grad():
        outer(G1, N2V, DH)

    def context_partial():
        for cols in blocks:
            part = dot(GV[...], A2[:, :, cols].reshape(HF, 256)).astype(BF)
            PF[:, :, cols] = part.reshape(NF, V, 256)
        st.pf = ReduceScatter4(PF, g.PFr1, g.PFxs, g.PFr2)

    def second_norm_back():
        st.n2.finish()
        dyo = DY[mine, :].astype(F32)
        dv, dgain, dshift = norm_back(X1V[mine, :], vec(2), st.n2.total())
        dx1 = dyo + dv
        g.DX1[...] = dx1
        low = dx1.astype(BF)
        g.DP[f] = low
        st.dp = AllGather4(lambda j: g.DP.at[j])
        put_grad(2, dgain)
        put_grad(3, dshift)
        put_grad(4, jnp.sum(low.astype(F32), axis=0, keepdims=True))
        put_grad(5, jnp.sum(dyo, axis=0, keepdims=True))

    def transpose_attended():
        st.ov.finish()
        for j in range(NF):
            ot = OV[j].astype(F32).T.astype(BF)
            OT[n // NF * j : n // NF * (j + 1)] = ot.reshape(n // NF, NF, R, VP)

    def out_grad():
        st.dp.finish()
        go = dot(OT[:, f].reshape(n * R, VP), g.DP[...].reshape(VP, D))
        GO[...] = go.reshape(n, R, D)

    def attended_grad():
        st.dp.finish()
        st.wo.finish()
        wo_heads = WO[pl.ds(n // NF * f, n // NF)].reshape(C, D)
        DO[...] = dot(g.DP[...].reshape(VP, D), wo_heads, NT).astype(BF)

    def attention_back():
        dq = jnp.zeros((VP, C), F32)
        dk = jnp.zeros((VP, C), F32)
        dw = jnp.zeros((VP, C), F32)
        for hd in range(C // HDIM):
            pr = PV[hd]
            dp = dot(DO[...] * hmask[hd].astype(BF), WV[...], NT)
            ds = (pr * (dp - jnp.sum(pr * dp, axis=-1, keepdims=True))).astype(BF)
            dq += dot(ds, KV[...]) * hmask[hd]
            dk += dot(ds, QV[...], TN) * hmask[hd]
            dw += dot(pr.astype(BF), DO[...], TN) * hmask[hd]
        csv = sum(dot(dot(SM[...], g.OH[...]).astype(BF), g.trig_v[k]) for k in range(3))
        for t, (grad, scale) in enumerate(((dq, 0.125), (dk, 1.0))):
            for hh in range(C // 128):
                u = grad[:, 128 * hh : 128 * hh + 128]
                u = u * csv[:, :128] - swap_halves(u) * csv[:, 128:]
                DPRE[:, C * t + 128 * hh : C * t + 128 * hh + 128] = (u * scale).astype(BF)
        DPRE[:, 2 * C :] = dw.astype(BF)

    def qkv_grad():
        outer(GQ, N1V, DPRE)

    def qkv_bias_grad():
        BG[...] = jnp.zeros(BG.shape, F32)
        db = jnp.sum(DPRE[...].astype(F32), axis=0, keepdims=True)
        for t in range(3):
            BG[0:1, pl.ds(pl.multiple_of(D * t + C * f, 128), C)] = db[:, C * t : C * t + C]
        for q in range(n):
            for t in range(3):
                VG[q, 6 + t : 7 + t, :] = BG[0:1, 384 * q + 128 * t : 384 * q + 128 * t + 128]
            VG[q, 13:16, :] = jnp.zeros((3, 128), F32)

    def first_grad():
        drain(st.n2.ca, st.n2.cb)
        for k, cols in enumerate(blocks):
            part = dot(DPRE[...], AQ[2 * k : 2 * k + 2].reshape(256, 3 * C), NT).astype(BF)
            PN[:, :, cols] = part.reshape(NF, V, 256)
        st.n1 = ReduceScatter4(PN, g.PMr1, g.PMxs, g.PMr2)

    def first_norm_back():
        st.n1.finish()
        dv, dgain, dshift = norm_back(XV[mine, :].astype(F32), vec(0), st.n1.total())
        g.DX[f] = (g.DX1[...] + dv).astype(BF)
        st.dx = AllGather4(lambda j: g.DX.at[j])
        put_grad(0, dgain)
        put_grad(1, dshift)

    def context_result():
        st.pf.finish()
        g.CO[f] = (X1V[mine, :] + (st.pf.total() + vec(5))).astype(BF)
        st.co = AllGather4(lambda j: g.CO.at[j])

    def home(src, dst):
        s = SM[:, pl.ds(pl.multiple_of(T * f, 128), T)]
        for cols in blocks:
            dst[:, cols] = dot(s, src[:, :, cols].reshape(VP, 256), TN).astype(BF)

    def home_context():
        st.co.finish()
        home(g.CO, g.CH)
        store(g.CH, g.ctx_o, 0)

    def home_grad():
        st.dx.finish()
        home(g.DX, g.DXH)
        store(g.DXH, g.dx_o, 1)

    def target_middle(b):
        st.wo.finish()
        st.oa[b // 2].finish()
        for cols in blocks:
            g.X1B[:, cols] = TA[b, :, cols].astype(F32) + (
                out_project(lambda j: OA[j, T * b : T * b + T, :], cols) + VEC[4:5, cols]
            )
        x1 = g.X1B[...]
        xh, _inv = norm_stats(x1)
        N2[b] = (xh * vec(2) + vec(3)).astype(BF)

        @pl.when(f == b)
        def _():
            g.X1H[...] = x1

    def target_hidden(b):
        finish(*w1_ring)
        for cols in blocks:
            hid = dot(N2[b], A1[:, :, cols].reshape(D, 256)) + VEC[6:7, cols]
            GT[b, :, cols] = (hid * normal_cdf(hid)).astype(BF)

    def target_out(b):
        finish(*w2_ring)
        for cols in blocks:
            PT[b, :, cols] = dot(GT[b], A2[:, :, cols].reshape(HF, 256)).astype(BF)
        if b == NF - 1:
            st.pt = ReduceScatter4(PT, g.PTr1, g.PTxs, g.PTr2)

    def target_result():
        st.pt.finish()
        g.TO[...] = (g.X1H[...] + (st.pt.total() + vec(5))).astype(BF)
        store(g.TO, g.tgt_o, 3)

    def fc2_grad_done():
        finish(*g2_ring)
        for k, ring in enumerate(g2_ring):
            g.D2[hc * k : hc * k + hc, :] = ring.total()
        store(g.D2, g.g2_o, 2)

    def fc1_grad_trade():
        finish(*g1_ring)
        for k, ring in enumerate(g1_ring):
            E1[2 * k : 2 * k + 2] = ring.total().astype(BF).reshape(2, R, HF)
        F1[f] = E1[f]
        st.e1 = scatter(lambda j: E1.at[j], lambda j: F1.at[j])

    def fc1_grad_done():
        received(st.e1)
        store(F1, g.g1_o, 5)

    def out_grad_done():
        go_ring.finish()
        g.DOo[...] = go_ring.total()
        store(g.DOo, g.go_o, 4)

    def qkv_grad_trade():
        finish(*gq_ring)
        for k, ring in enumerate(gq_ring):
            EQ[2 * k : 2 * k + 2] = ring.total().astype(BF).reshape(2, R, 3 * C)
        FQ[f] = EQ[f]
        st.eq = scatter(lambda j: EQ.at[j], lambda j: FQ.at[j])

    def qkv_grad_done():
        received(st.eq)
        store(FQ, g.gq_o, 7)

    def small_grad_trade():
        gs_ring.finish()
        SG[f] = gs_ring.total()
        st.sg = scatter(lambda j: SG.at[f], lambda j: SG.at[j])

    def small_grad_done():
        received(st.sg)
        g.SGo[...] = SG[0] + SG[1] + SG[2] + SG[3]
        store(g.SGo, g.sg_o, 6)

    start()
    cast_fc1()
    tokens_start()
    cot_start()
    o_ring.step(0)
    w2_ring[0].step(0)
    layout()
    w2_ring[1].step(0)
    o_ring.step(1)
    q_ring[0].step(0)
    q_ring[1].step(0)
    s_ring.step(0)
    visible()
    w1_ring[0].step(0)
    o_ring.step(2)
    q_ring[0].step(1)
    q_ring[1].step(1)
    s_ring.step(1)
    w1_ring[0].step(1)
    st.tok.forward()
    o_ring.step(3)
    q_ring[0].step(2)
    q_ring[1].step(2)
    s_ring.step(2)
    w1_ring[1].step(0)
    wo_start()
    w1_ring[0].step(2)
    q_ring[0].step(3)
    st.cot.forward()
    q_ring[1].step(3)
    s_ring.step(3)
    select_cot()
    w1_ring[1].step(1)
    w1_ring[0].step(3)
    w2_ring[0].step(1)
    small_vectors()
    first_norm()
    project_half(0)
    st.wo.forward()
    w1_ring[1].step(2)
    project_half(1)
    context_attention()
    w2_ring[1].step(1)
    select_rows()
    w2_ring[0].step(2)
    attend_target(0, 0)
    w1_ring[1].step(3)
    attend_target(0, 1)
    st.ov.forward()
    attend_target(1, 0)
    w2_ring[1].step(2)
    context_middle()
    transpose_attended()
    w2_ring[0].step(3)
    attend_target(1, 1)
    oa_start(0)
    context_hidden()
    fc2_grad()
    g2_ring[0].step(0)
    g2_ring[1].step(0)
    w2_ring[1].step(3)
    attend_target(2, 0)
    attend_target(2, 1)
    g2_ring[0].step(1)
    g2_ring[1].step(1)
    st.oa[0].forward()
    attend_target(3, 0)
    hidden_grad()
    second_grad()
    g2_ring[0].step(2)
    fc1_grad()
    g1_ring[0].step(0)
    g1_ring[1].step(0)
    st.n2.forward()
    context_partial()
    target_middle(0)
    g2_ring[1].step(2)
    attend_target(3, 1)
    g2_ring[0].step(3)
    oa_start(1)
    second_norm_back()
    g1_ring[0].step(1)
    st.pf.forward()
    target_middle(1)
    target_hidden(0)
    g1_ring[1].step(1)
    target_hidden(1)
    target_out(0)
    target_out(1)
    st.oa[1].forward()
    g2_ring[1].step(3)
    target_middle(2)
    g1_ring[0].step(2)
    st.dp.forward()
    target_middle(3)
    target_hidden(2)
    g1_ring[1].step(2)
    attended_grad()
    attention_back()
    qkv_grad()
    gq_ring[0].step(0)
    gq_ring[1].step(0)
    out_grad()
    go_ring.step(0)
    g1_ring[0].step(3)
    first_grad()
    qkv_bias_grad()
    context_result()
    target_hidden(3)
    target_out(2)
    g1_ring[1].step(3)
    st.n1.forward()
    gq_ring[0].step(1)
    target_out(3)
    fc2_grad_done()
    gq_ring[1].step(1)
    go_ring.step(1)
    st.co.forward()
    st.pt.forward()
    first_norm_back()
    gs_ring.step(0)
    home_context()
    fc1_grad_trade()
    gq_ring[0].step(2)
    gq_ring[1].step(2)
    go_ring.step(2)
    gs_ring.step(1)
    gq_ring[0].step(3)
    gq_ring[1].step(3)
    target_result()
    go_ring.step(3)
    gs_ring.step(2)
    st.dx.forward()
    home_grad()
    qkv_grad_trade()
    fc1_grad_done()
    out_grad_done()
    gs_ring.step(3)
    small_grad_trade()
    qkv_grad_done()
    small_grad_done()
    for c in outs:
        c.wait()
    for c in pending:
        c.wait_send()


def run_layer(n, tokens, cot, lengths, mask, counts, vectors, wqkv, wo, w1, w2, V):
    T, D = tokens.shape
    NF = 4
    FF = w1.shape[1]
    R = wo.shape[0]
    RP = R * NF
    HC = w2.shape[0]
    HF = HC * n
    C = D // NF
    VP = V * NF
    S_ = T * NF
    h2 = n // 2
    B, F = BF, F32
    vm = pltpu.VMEM
    scratch = dict(
        wqkv_v=vm((R, 3 * D), F), w1_v=vm((R, FF), F), wo_v=vm((R, D), F), w2_v=vm((HC, D), F),
        small_v=vm((8, 128), F), trig_v=vm((3, 128, 256), B),
        sq=vm((NF, R, 3 * C), B), s1=vm((NF, R, HF), B),
        AS=vm((n, NF, 8, 128), F), AQ=vm((n, RP, 3 * C), B), WO=vm((n, NF, R, D), B),
        A1=vm((n, RP, HF), B), A2=vm((n, HC, D), B),
        TA=vm((NF, T, D), B), CA=vm((NF, T, D), B), N1=vm((NF, T, D), B),
        OH=vm((S_, 128), B), CS=vm((S_, 256), F), SM=vm((VP, S_), B),
        VEC=vm((8, D), F), BQ=vm((8, 3 * D), F), BG=vm((8, 3 * D), F),
        Q=vm((S_, C), B), K=vm((S_, C), B), W=vm((S_, C), B),
        QV=vm((VP, C), B), KV=vm((VP, C), B), WV=vm((VP, C), B),
        OV=vm((NF, VP, C), B), PV=vm((C // HDIM, VP, VP), F), OA=vm((NF, S_, C), B),
        XV=vm((VP, D), B), N1V=vm((VP, D), B), DY=vm((VP, D), B),
        X1V=vm((VP, D), F), N2V=vm((VP, D), B), GV=vm((VP, HF), B), GP=vm((VP, HF), F),
        G2=vm((n, HC, D), F), G1=vm((n, RP, HF), F), GQ=vm((n, RP, 3 * C), F), GO=vm((n, R, D), F),
        VG=vm((n, 16, 128), F),
        st2=vm((HC, D), B), rr2=vm((h2, HC, D), B), rl2=vm((h2, HC, D), B),
        st1=vm((RP, HF), B), rr1=vm((h2, RP, HF), B), rl1=vm((h2, RP, HF), B),
        stq=vm((RP, 3 * C), B), rrq=vm((h2, RP, 3 * C), B), rlq=vm((h2, RP, 3 * C), B),
        sto=vm((R, D), B), rro=vm((h2, R, D), B), rlo=vm((h2, R, D), B),
        sts=vm((16, 128), F), rrs=vm((h2, 16, 128), F), rls=vm((h2, 16, 128), F),
        DH=vm((VP, HF), B), PN=vm((NF, V, D), B), PF=vm((NF, V, D), B),
        PNr1=vm((2, V, D), B), PNxs=vm((V, D), B), PNr2=vm((V, D), B),
        PMr1=vm((2, V, D), B), PMxs=vm((V, D), B), PMr2=vm((V, D), B),
        PFr1=vm((2, V, D), B), PFxs=vm((V, D), B), PFr2=vm((V, D), B),
        DX1=vm((V, D), F), DP=vm((NF, V, D), B), OT=vm((n, NF, R, VP), B), DO=vm((VP, C), B),
        DPRE=vm((VP, 3 * C), B), CO=vm((NF, V, D), B), DX=vm((NF, V, D), B),
        X1B=vm((T, D), F), X1H=vm((T, D), F), GT=vm((NF, T, HF), B),
        PTr1=vm((2, T, D), B), PTxs=vm((T, D), B), PTr2=vm((T, D), B),
        CH=vm((T, D), B), DXH=vm((T, D), B), TO=vm((T, D), B),
        SG=vm((NF, 16, 128), F), SGo=vm((16, 128), F),
        E1=vm((NF, R, HF), B), F1=vm((NF, R, HF), B), EQ=vm((NF, R, 3 * C), B), FQ=vm((NF, R, 3 * C), B),
        send_sems=pltpu.SemaphoreType.DMA((200,)), recv_sems=pltpu.SemaphoreType.DMA((200,)),
        local_sems=pltpu.SemaphoreType.DMA((16,)), mask_v=vm((1, T), jnp.int32),
    )
    arr = jax.ShapeDtypeStruct
    ins = dict(
        lengths=lengths, counts=counts, tok=tokens, cot=cot, mask=mask.reshape(1, T), wqkv=wqkv, wo=wo,
        w1=w1, w2=w2, trig=jnp.asarray(trig_table()),
    )
    for k, v in enumerate(vectors):
        ins["in%d" % k] = v.reshape(1, -1)
        scratch["v%d" % k] = vm((1, v.shape[0]), F)
    outs = dict(
        tgt_o=arr((T, D), B), ctx_o=arr((T, D), B), dx_o=arr((T, D), B), gq_o=arr((NF, R, 3 * C), B),
        go_o=arr((R, D), F), g1_o=arr((NF, R, HF), B), g2_o=arr((HC, D), F), sg_o=arr((16, 128), F),
    )
    names = [*ins, *outs, *scratch]
    any_spec = pl.BlockSpec(memory_space=pl.ANY)
    return pl.pallas_call(
        functools.partial(layer_kernel, (n, D, FF, T, V), names),
        out_shape=list(outs.values()),
        in_specs=[pl.BlockSpec(memory_space=pltpu.SMEM)] * 2 + [any_spec] * (len(ins) - 2),
        out_specs=[any_spec] * 8,
        scratch_shapes=list(scratch.values()),
        compiler_params=pltpu.CompilerParams(
            collective_id=0, has_side_effects=True, vmem_limit_bytes=67043328
        ),
        name="layer",
    )(*ins.values())


def outputs_kernel(dims, count, *refs):
    n, R, C, HC = dims
    NF = 4
    f = lax.axis_index("fsdp")
    tgt, ctx, dx, gq, go, g1, g2, sg = refs[:8]
    tgt_o, ctx_o, dx_o, gq_o, go_o, g1_o, g2_o = refs[8:15]
    vec_o = refs[15:23]
    bufs = refs[23:31]
    gq_w, g1_w, sem_in, sem_out = refs[31:]
    loads = []
    for k, (src, dst) in enumerate(zip((gq, g1, sg, g2, tgt, ctx, dx, go), bufs)):
        c = pltpu.make_async_copy(src, dst, sem_in.at[k])
        c.start()
        loads.append(c)
    stores = []

    def store(src, dst):
        c = pltpu.make_async_copy(src, dst, sem_out.at[len(stores)])
        c.start()
        stores.append(c)

    D = NF * C
    loads[0].wait()
    for j in range(NF):
        for t in range(3):
            gq_w[:, D * t + C * j : D * t + C * j + C] = bufs[0][j, :, C * t : C * t + C].astype(F32)
    store(gq_w, gq_o)
    loads[1].wait()
    for j in range(NF):
        for t in range(n):
            at = HC * (NF * t + j)
            g1_w[:, at : at + HC] = bufs[1][j, :, HC * t : HC * t + HC].astype(F32)
    store(g1_w, g1_o)
    for k, out in enumerate((g2_o, tgt_o, ctx_o, dx_o, go_o)):
        loads[3 + k].wait()
        store(bufs[3 + k], out)
    loads[2].wait()
    small = bufs[2]
    for k in range(6):
        vec_o[k][...] = pltpu.roll(small[k : k + 1, :], lax.rem(128 - R * f, 128), 1)[:, :R]
    rows = jnp.concatenate([small[6 + t : 7 + t, :] for t in range(3)], axis=1)
    vec_o[6][...] = pltpu.roll(rows, lax.rem(384 - 3 * R * f, 384), 1)[:, : 3 * R]
    mine = jnp.zeros((1, 128), F32)
    for j in range(NF):
        mine = jnp.where(f == j, small[9 + j : 10 + j, :], mine)
    vec_o[7][...] = mine
    for c in stores:
        c.wait()


def write_outputs(n, parts, R, D, FF, HC):
    NF = 4
    C = D // NF
    tgt = parts[0]
    arr = jax.ShapeDtypeStruct
    any_spec = pl.BlockSpec(memory_space=pl.ANY)
    order = [parts[k] for k in (3, 5, 7, 6, 0, 1, 2, 4)]
    big = [
        arr(tgt.shape, BF), arr(tgt.shape, BF), arr(tgt.shape, BF),
        arr((R, 3 * D), F32), arr((R, D), F32), arr((R, FF), F32), arr((HC, D), F32),
    ]
    small = [arr((1, w), F32) for w in (R,) * 6 + (3 * R, 4 * R)]
    return pl.pallas_call(
        functools.partial(outputs_kernel, (n, R, C, HC), 8),
        out_shape=big + small,
        in_specs=[any_spec] * 8,
        out_specs=[any_spec] * 7 + [pl.BlockSpec(memory_space=pltpu.VMEM)] * 8,
        scratch_shapes=[pltpu.VMEM(a.shape, a.dtype) for a in order]
        + [
            pltpu.VMEM((R, 3 * D), F32), pltpu.VMEM((R, FF), F32),
            pltpu.SemaphoreType.DMA((8,)), pltpu.SemaphoreType.DMA((8,)),
        ],
        name="outputs",
    )(*parts)


def on_device(
    tokens, lengths, visibility_mask, visible_counts, ln1_gain, ln1_bias, qkv_weight, qkv_bias,
    out_weight, out_bias, ln2_gain, ln2_bias, fc1_weight, fc1_bias, fc2_weight, fc2_bias, context_cot,
):
    n = lax.axis_size("dp")
    R, D = out_weight.shape
    vectors = (ln1_gain, ln1_bias, ln2_gain, ln2_bias, out_bias, fc2_bias, qkv_bias, fc1_bias)
    parts = run_layer(
        n, tokens, context_cot, lengths, visibility_mask, visible_counts, vectors,
        qkv_weight, out_weight, fc1_weight, fc2_weight, VIS_DEV,
    )
    tgt, ctx, dx, gq, go, g1, g2, *small = write_outputs(
        n, parts, R, D, fc1_weight.shape[1], fc2_weight.shape[0]
    )
    gg1, gb1, gg2, gb2, gbo, gc2, gbq, gc1 = [v.reshape(-1) for v in small]
    return (tgt, ctx, dx, gg1, gb1, gq, gbq, go, gbo, gg2, gb2, g1, gc1, g2, gc2)


def layer_norm(inputs, scale_vec, shift_vec):
    center = inputs - jnp.mean(inputs, axis=-1, keepdims=True)
    spread = jnp.mean(center * center, axis=-1, keepdims=True)
    return center * lax.rsqrt(spread + norm_eps) * scale_vec + shift_vec


def gelu_erf(values):
    return jax.nn.gelu(values, approximate=False)


def pack_layout(seq_lens, pack_len):
    seq_ends = jnp.cumsum(seq_lens)
    places = jnp.arange(pack_len, dtype=jnp.int32)
    passed = places[:, None] >= seq_ends[None, :]
    segment = jnp.sum(passed.astype(jnp.int32), axis=1)
    before = jnp.sum(jnp.where(passed, seq_lens[None, :], 0), axis=1)
    return (segment, places - before)


def rope_tables(places):
    frame_index = (places // (GRID * GRID)).astype(jnp.float32)
    grid_row = (places // GRID % GRID).astype(jnp.float32)
    grid_col = (places % GRID).astype(jnp.float32)
    pair_index = jnp.arange(HDIM // 2, dtype=jnp.int32)
    axis_pick = jnp.minimum(pair_index // 11, 2)
    pair_order = (pair_index - 11 * axis_pick).astype(jnp.float32)
    frequency = jnp.exp(pair_order * (-math.log(10000.0) / 11.0))
    angles = (
        frame_index[:, None] * (axis_pick == 0).astype(jnp.float32)[None, :]
        + grid_row[:, None] * (axis_pick == 1).astype(jnp.float32)[None, :]
        + grid_col[:, None] * (axis_pick == 2).astype(jnp.float32)[None, :]
    ) * frequency[None, :]
    return (jnp.cos(angles), jnp.sin(angles))


def rotate(heads, cosine_table, sine_table):
    half_size = heads.shape[-1] // 2
    first_half = heads[..., :half_size]
    second_half = heads[..., half_size:]
    cosine_cols = cosine_table[:, None, :]
    sine_cols = sine_table[:, None, :]
    return jnp.concatenate(
        [
            first_half * cosine_cols - second_half * sine_cols,
            second_half * cosine_cols + first_half * sine_cols,
        ],
        axis=-1,
    )


def rotate_back(grads, cosine_table, sine_table):
    half_size = grads.shape[-1] // 2
    first_half = grads[..., :half_size]
    second_half = grads[..., half_size:]
    cosine_cols = cosine_table[:, None, :]
    sine_cols = sine_table[:, None, :]
    return jnp.concatenate(
        [
            first_half * cosine_cols + second_half * sine_cols,
            second_half * cosine_cols - first_half * sine_cols,
        ],
        axis=-1,
    )


def project(token_rows, weights, cosine_table, sine_table):
    inputs = token_rows.astype(jnp.float32)
    row_count = inputs.shape[0]
    model_width = inputs.shape[1]
    normed = layer_norm(
        inputs, weights[0].astype(jnp.float32), weights[1].astype(jnp.float32)
    ).astype(jnp.bfloat16)
    joined = jnp.dot(normed, weights[2], preferred_element_type=jnp.float32) + weights[3].astype(
        jnp.float32
    )
    query_heads = rotate(
        joined[:, :model_width].reshape(row_count, HEADS, HDIM), cosine_table, sine_table
    ).astype(jnp.bfloat16)
    key_flat = (
        rotate(
            joined[:, model_width : 2 * model_width].reshape(row_count, HEADS, HDIM),
            cosine_table,
            sine_table,
        )
        .astype(jnp.bfloat16)
        .reshape(row_count, model_width)
    )
    value_flat = joined[:, 2 * model_width :].astype(jnp.bfloat16)
    return (inputs, normed, query_heads, key_flat, value_flat)


def attend(query_heads, key_flat, value_flat, seg_query, seg_key):
    key_heads = key_flat.reshape(key_flat.shape[0], HEADS, HDIM)
    value_heads = value_flat.reshape(value_flat.shape[0], HEADS, HDIM)
    scores = jnp.einsum(
        "qhd,khd->hqk", query_heads, key_heads, preferred_element_type=jnp.float32
    ) * HDIM ** (-0.5)
    allowed = seg_query[:, None] == seg_key[None, :]
    masked = jnp.where(allowed[None], scores, masked_fill)
    row_max = jnp.max(masked, axis=-1, keepdims=True)
    raised = jnp.exp(masked - row_max)
    totals = jnp.sum(raised, axis=-1, keepdims=True)
    attn_probs = (raised / totals).astype(jnp.bfloat16)
    attended = jnp.einsum(
        "hqk,khd->qhd", attn_probs, value_heads, preferred_element_type=jnp.float32
    )
    return (
        attended.reshape(query_heads.shape[0], -1).astype(jnp.bfloat16),
        row_max + jnp.log(totals),
    )


def attend_back(query_heads, key_flat, value_flat, seg_query, seg_key, log_total, grad_att):
    key_heads = key_flat.reshape(key_flat.shape[0], HEADS, HDIM)
    value_heads = value_flat.reshape(value_flat.shape[0], HEADS, HDIM)
    scale_factor = HDIM ** (-0.5)
    scores = (
        jnp.einsum("qhd,khd->hqk", query_heads, key_heads, preferred_element_type=jnp.float32)
        * scale_factor
    )
    allowed = seg_query[:, None] == seg_key[None, :]
    masked = jnp.where(allowed[None], scores, masked_fill)
    attn_probs = jnp.exp(masked - log_total)
    grad_heads = grad_att.reshape(grad_att.shape[0], HEADS, HDIM)
    grad_probs = jnp.einsum(
        "qhd,khd->hqk", grad_heads, value_heads, preferred_element_type=jnp.float32
    )
    row_delta = jnp.sum(attn_probs * grad_probs, axis=-1, keepdims=True)
    grad_scores = (attn_probs * (grad_probs - row_delta)).astype(jnp.bfloat16)
    grad_query = (
        jnp.einsum("hqk,khd->qhd", grad_scores, key_heads, preferred_element_type=jnp.float32)
        * scale_factor
    )
    grad_key = (
        jnp.einsum("hqk,qhd->khd", grad_scores, query_heads, preferred_element_type=jnp.float32)
        * scale_factor
    )
    grad_value = jnp.einsum(
        "hqk,qhd->khd",
        attn_probs.astype(jnp.bfloat16),
        grad_heads,
        preferred_element_type=jnp.float32,
    )
    return (
        grad_query,
        grad_key.reshape(key_flat.shape[0], -1),
        grad_value.reshape(value_flat.shape[0], -1),
    )


def finish(inputs, attended, weights):
    middle = inputs + (
        jnp.dot(attended, weights[4], preferred_element_type=jnp.float32)
        + weights[5].astype(jnp.float32)
    )
    second = layer_norm(
        middle, weights[6].astype(jnp.float32), weights[7].astype(jnp.float32)
    ).astype(jnp.bfloat16)
    hidden = jnp.dot(second, weights[8], preferred_element_type=jnp.float32) + weights[9].astype(
        jnp.float32
    )
    activated = gelu_erf(hidden).astype(jnp.bfloat16)
    result = middle + (
        jnp.dot(activated, weights[10], preferred_element_type=jnp.float32)
        + weights[11].astype(jnp.float32)
    )
    return (result, middle, second, hidden, activated)


def gathered_device(
    tokens,
    lengths,
    visibility_mask,
    visible_counts,
    ln1_gain,
    ln1_bias,
    qkv_weight,
    qkv_bias,
    out_weight,
    out_bias,
    ln2_gain,
    ln2_bias,
    fc1_weight,
    fc1_bias,
    fc2_weight,
    fc2_bias,
    context_cot,
):
    tok_rows = tokens.shape[0]
    model_width = tokens.shape[1]
    groups = lax.axis_size("fsdp")
    member = lax.axis_index("fsdp")
    pack_len = tok_rows * groups
    vis_rows = VIS_DEV
    vis_pack = vis_rows * groups
    zero_low = jnp.zeros((), jnp.bfloat16)
    shards = [
        weight.astype(jnp.bfloat16)
        for weight in (
            ln1_gain,
            ln1_bias,
            qkv_weight,
            qkv_bias,
            out_weight,
            out_bias,
            ln2_gain,
            ln2_bias,
            fc1_weight,
            fc1_bias,
            fc2_weight,
            fc2_bias,
        )
    ]
    weights = (
        lax.all_gather(shards[0], ("dp", "fsdp"), axis=0, tiled=True),
        lax.all_gather(shards[1], ("dp", "fsdp"), axis=0, tiled=True),
        lax.all_gather(shards[2], ("dp", "fsdp"), axis=0, tiled=True),
        lax.all_gather(shards[3], ("dp", "fsdp"), axis=0, tiled=True),
        lax.all_gather(shards[4], ("dp", "fsdp"), axis=0, tiled=True),
        lax.all_gather(shards[5], ("dp", "fsdp"), axis=0, tiled=True),
        lax.all_gather(shards[6], ("dp", "fsdp"), axis=0, tiled=True),
        lax.all_gather(shards[7], ("dp", "fsdp"), axis=0, tiled=True),
        lax.all_gather(shards[8], ("dp", "fsdp"), axis=0, tiled=True),
        lax.all_gather(shards[9], ("dp", "fsdp"), axis=0, tiled=True),
        lax.all_gather(shards[10], ("dp", "fsdp"), axis=0, tiled=True),
        lax.all_gather(shards[11], ("dp", "fsdp"), axis=0, tiled=True),
    )
    segment, places = pack_layout(lengths[0], pack_len)
    home_rows = member * tok_rows + jnp.arange(tok_rows, dtype=jnp.int32)
    seg_home = jnp.take(segment, home_rows)
    cos_home, sin_home = rope_tables(jnp.take(places, home_rows))
    inputs, normed, query_heads, key_flat, value_flat = project(tokens, weights, cos_home, sin_home)
    key_pack, value_pack = (
        lax.all_gather(key_flat, "fsdp", axis=0, tiled=True),
        lax.all_gather(value_flat, "fsdp", axis=0, tiled=True),
    )
    attended = attend(query_heads, key_pack, value_pack, seg_home, segment)[0]
    target_out = finish(inputs, attended, weights)[0].astype(jnp.bfloat16)
    running = jnp.cumsum(visibility_mask)
    visible_here = visibility_mask * (running <= visible_counts[0, 0]).astype(jnp.int32)
    visible_all = lax.all_gather(visible_here, "fsdp", axis=0, tiled=True)
    inclusive = jnp.cumsum(visible_all)
    rank_index = jnp.arange(vis_pack, dtype=jnp.int32)
    row_of = jnp.sum((inclusive[None, :] <= rank_index[:, None]).astype(jnp.int32), axis=1)
    owner_dev = row_of // tok_rows
    local_row = row_of % tok_rows
    mine_here = (owner_dev == member)[:, None]
    send_tokens = jnp.where(mine_here, jnp.take(tokens, local_row, axis=0), zero_low)
    send_cot = jnp.where(mine_here, jnp.take(context_cot, local_row, axis=0), zero_low)
    recv_tokens, recv_cot = (
        lax.all_to_all(send_tokens, "fsdp", split_axis=0, concat_axis=0, tiled=True),
        lax.all_to_all(send_cot, "fsdp", split_axis=0, concat_axis=0, tiled=True),
    )
    slot_index = jnp.arange(vis_rows, dtype=jnp.int32)
    my_ranks = member * vis_rows + slot_index
    my_owner = jnp.take(owner_dev, my_ranks)
    my_row = jnp.take(row_of, my_ranks)
    picked = my_owner * vis_rows + slot_index
    bal_tokens = jnp.take(recv_tokens, picked, axis=0)
    bal_cot = jnp.take(recv_cot, picked, axis=0)
    seg_bal = jnp.take(segment, my_row)
    seg_keys = jnp.take(segment, row_of)
    cos_bal, sin_bal = rope_tables(jnp.take(places, my_row))
    inputs_bal, normed_bal, query_bal, key_bal, value_bal = project(
        bal_tokens, weights, cos_bal, sin_bal
    )
    key_vis, value_vis = (
        lax.all_gather(key_bal, "fsdp", axis=0, tiled=True),
        lax.all_gather(value_bal, "fsdp", axis=0, tiled=True),
    )
    attended_bal, log_total = attend(query_bal, key_vis, value_vis, seg_bal, seg_keys)
    result_bal, middle_bal, second_bal, hidden_bal, activated_bal = finish(
        inputs_bal, attended_bal, weights
    )
    grad_result = bal_cot.astype(jnp.float32)
    result_low = grad_result.astype(jnp.bfloat16)
    grad_fc2 = jnp.einsum(
        "nf,nd->fd", activated_bal, result_low, preferred_element_type=jnp.float32
    )
    grad_bfc2 = jnp.sum(result_low.astype(jnp.float32), axis=0)
    grad_activated = jnp.einsum(
        "nd,fd->nf", result_low, weights[10], preferred_element_type=jnp.float32
    )
    gelu_pull = jax.vjp(gelu_erf, hidden_bal)[1]
    hidden_low = gelu_pull(grad_activated)[0].astype(jnp.bfloat16)
    grad_fc1 = jnp.einsum("nd,nf->df", second_bal, hidden_low, preferred_element_type=jnp.float32)
    grad_bfc1 = jnp.sum(hidden_low.astype(jnp.float32), axis=0)
    grad_second = jnp.einsum(
        "nf,df->nd", hidden_low, weights[8], preferred_element_type=jnp.float32
    )
    norm_two_pull = jax.vjp(
        layer_norm, middle_bal, weights[6].astype(jnp.float32), weights[7].astype(jnp.float32)
    )[1]
    grad_mid_norm, grad_gain_two, grad_shift_two = norm_two_pull(grad_second)
    grad_middle = grad_result + grad_mid_norm
    middle_low = grad_middle.astype(jnp.bfloat16)
    grad_wout = jnp.einsum(
        "nd,ne->de", attended_bal, middle_low, preferred_element_type=jnp.float32
    )
    grad_bout = jnp.sum(middle_low.astype(jnp.float32), axis=0)
    grad_att = jnp.einsum(
        "ne,de->nd", middle_low, weights[4], preferred_element_type=jnp.float32
    ).astype(jnp.bfloat16)
    grad_query, grad_key_all, grad_value_all = attend_back(
        query_bal, key_vis, value_vis, seg_bal, seg_keys, log_total, grad_att
    )
    grad_key_own, grad_value_own = (
        lax.psum_scatter(
            grad_key_all.astype(jnp.bfloat16), "fsdp", scatter_dimension=0, tiled=True
        ).astype(jnp.float32),
        lax.psum_scatter(
            grad_value_all.astype(jnp.bfloat16), "fsdp", scatter_dimension=0, tiled=True
        ).astype(jnp.float32),
    )
    grad_query_pre = rotate_back(grad_query, cos_bal, sin_bal).reshape(vis_rows, model_width)
    grad_key_pre = rotate_back(
        grad_key_own.reshape(vis_rows, HEADS, HDIM), cos_bal, sin_bal
    ).reshape(vis_rows, model_width)
    joined_low = jnp.concatenate([grad_query_pre, grad_key_pre, grad_value_own], axis=1).astype(
        jnp.bfloat16
    )
    grad_wqkv = jnp.einsum("nd,ne->de", normed_bal, joined_low, preferred_element_type=jnp.float32)
    grad_bqkv = jnp.sum(joined_low.astype(jnp.float32), axis=0)
    grad_normed = jnp.einsum(
        "ne,de->nd", joined_low, weights[2], preferred_element_type=jnp.float32
    )
    norm_one_pull = jax.vjp(
        layer_norm, inputs_bal, weights[0].astype(jnp.float32), weights[1].astype(jnp.float32)
    )[1]
    grad_in_norm, grad_gain_one, grad_shift_one = norm_one_pull(grad_normed)
    grad_inputs = grad_middle + grad_in_norm
    destinations = jnp.arange(groups, dtype=jnp.int32)
    route_mask = (my_owner[None, :] == destinations[:, None])[:, :, None]
    send_out = jnp.where(route_mask, result_bal.astype(jnp.bfloat16)[None], zero_low).reshape(
        vis_pack, model_width
    )
    send_grad = jnp.where(route_mask, grad_inputs.astype(jnp.bfloat16)[None], zero_low).reshape(
        vis_pack, model_width
    )
    back_out, back_grad = (
        lax.all_to_all(send_out, "fsdp", split_axis=0, concat_axis=0, tiled=True),
        lax.all_to_all(send_grad, "fsdp", split_axis=0, concat_axis=0, tiled=True),
    )
    rank_home = jnp.maximum(jnp.take(inclusive, home_rows) - 1, 0)
    is_visible = (visible_here > 0)[:, None]
    context_out = jnp.where(is_visible, jnp.take(back_out, rank_home, axis=0), zero_low)
    tokens_grad = jnp.where(is_visible, jnp.take(back_grad, rank_home, axis=0), zero_low)
    grad_list = [
        grad_gain_one,
        grad_shift_one,
        grad_wqkv,
        grad_bqkv,
        grad_wout,
        grad_bout,
        grad_gain_two,
        grad_shift_two,
        grad_fc1,
        grad_bfc1,
        grad_fc2,
        grad_bfc2,
    ]
    reduced = (
        lax.psum_scatter(grad_list[0], ("dp", "fsdp"), scatter_dimension=0, tiled=True),
        lax.psum_scatter(grad_list[1], ("dp", "fsdp"), scatter_dimension=0, tiled=True),
        lax.psum_scatter(grad_list[2], ("dp", "fsdp"), scatter_dimension=0, tiled=True),
        lax.psum_scatter(grad_list[3], ("dp", "fsdp"), scatter_dimension=0, tiled=True),
        lax.psum_scatter(grad_list[4], ("dp", "fsdp"), scatter_dimension=0, tiled=True),
        lax.psum_scatter(grad_list[5], ("dp", "fsdp"), scatter_dimension=0, tiled=True),
        lax.psum_scatter(grad_list[6], ("dp", "fsdp"), scatter_dimension=0, tiled=True),
        lax.psum_scatter(grad_list[7], ("dp", "fsdp"), scatter_dimension=0, tiled=True),
        lax.psum_scatter(grad_list[8], ("dp", "fsdp"), scatter_dimension=0, tiled=True),
        lax.psum_scatter(grad_list[9], ("dp", "fsdp"), scatter_dimension=0, tiled=True),
        lax.psum_scatter(grad_list[10], ("dp", "fsdp"), scatter_dimension=0, tiled=True),
        lax.psum_scatter(grad_list[11], ("dp", "fsdp"), scatter_dimension=0, tiled=True),
    )
    return (
        target_out,
        context_out,
        tokens_grad,
        reduced[0],
        reduced[1],
        reduced[2],
        reduced[3],
        reduced[4],
        reduced[5],
        reduced[6],
        reduced[7],
        reduced[8],
        reduced[9],
        reduced[10],
        reduced[11],
    )


def per_device(tokens, *rest):
    n, group = lax.axis_size("dp"), lax.axis_size("fsdp")
    out_rows = rest[7].shape[0]
    fits = group == 4 and n == 8 and out_rows * group == 128
    return (on_device if fits else gathered_device)(tokens, *rest)


def solution(mesh):
    both = ("dp", "fsdp")
    vec, mat = P(both), P(both, None)
    return jax.shard_map(
        per_device,
        mesh=mesh,
        in_specs=(
            mat, P("dp", None), vec, P("dp", "fsdp"), vec, vec, mat, vec, mat, vec, vec, vec,
            mat, vec, mat, vec, mat,
        ),
        out_specs=(mat, mat, mat, vec, vec, mat, vec, mat, vec, vec, vec, mat, vec, mat, vec),
        check_vma=False,
    )
```

```python
import functools
import math
import types

import jax
import jax.numpy as jnp
import numpy as np
from jax import lax
from jax.experimental import pallas as pl
from jax.experimental.pallas import tpu as pltpu
from jax.sharding import PartitionSpec as P

HEADS = 16
HDIM = 64
GRID = 14
VIS_DEV = 64
norm_eps = 1e-06
masked_fill = -1e30
FRAMES = 8
EPS = 1e-06
FILL = -1e30
BF = jnp.bfloat16
F32 = jnp.float32
MESH = pl.DeviceIdType.MESH
NT = (((1,), (1,)), ((), ()))
NN = (((1,), (0,)), ((), ()))
TN = (((0,), (0,)), ((), ()))


def dot(a, b, dims=NN):
    return lax.dot_general(a, b, dims, preferred_element_type=F32)


def trig_table():
    width = FRAMES + 2 * GRID
    lane = np.arange(2 * HDIM)
    pair = lane % (HDIM // 2)
    axis = np.minimum(pair // 11, 2)
    freq = np.exp(((pair - 11 * axis).astype(np.float32)) * np.float32(-math.log(10000.0) / 11.0))
    sign = np.where(lane % HDIM < HDIM // 2, -1.0, 1.0)
    table = np.zeros((128, 4 * HDIM), np.float32)
    row = np.arange(width)
    kind = np.where(row < FRAMES, 0, np.where(row < FRAMES + GRID, 1, 2))
    coord = np.where(kind == 0, row, np.where(kind == 1, row - FRAMES, row - FRAMES - GRID))
    angle = (coord[:, None].astype(np.float32) * freq[None, :].astype(np.float32)).astype(np.float64)
    here = kind[:, None] == axis[None, :]
    table[:width, : 2 * HDIM] = np.where(here, np.cos(angle), 0.0)
    table[:width, 2 * HDIM :] = np.where(here, np.sin(angle) * sign[None, :], 0.0)
    parts = []
    rest = table
    for _ in range(3):
        part = rest.astype(jnp.bfloat16)
        parts.append(part)
        rest = rest - part.astype(np.float32)
    return np.stack(parts)


def norm_stats(v):
    center = v - jnp.mean(v, axis=-1, keepdims=True)
    inv = lax.rsqrt(jnp.mean(center * center, axis=-1, keepdims=True) + EPS)
    return center * inv, inv


def norm_back(v, gain, grad):
    xhat, inv = norm_stats(v)
    gg = grad * gain
    dv = inv * (
        gg - jnp.mean(gg, axis=-1, keepdims=True) - xhat * jnp.mean(gg * xhat, axis=-1, keepdims=True)
    )
    return (
        dv,
        jnp.sum(grad * xhat, axis=0, keepdims=True),
        jnp.sum(grad, axis=0, keepdims=True),
    )


def swap_halves(u):
    lane = lax.broadcasted_iota(jnp.int32, u.shape, 1)
    return jnp.where(
        lax.rem(lane, HDIM) < HDIM // 2,
        pltpu.roll(u, u.shape[1] - HDIM // 2, 1),
        pltpu.roll(u, HDIM // 2, 1),
    )


def column_segment(start, rows, ends):
    row = start + lax.broadcasted_iota(jnp.int32, (rows, 1), 0)
    seg = jnp.zeros((rows, 1), jnp.int32)
    for end in ends:
        seg += (row >= end).astype(jnp.int32)
    return row, seg


ALIASES = dict(N2="N1", PT="N1", D2="w2_v", DOo="wo_v", X1B="GP")


class Sems:
    def __init__(self, send, recv):
        self.send, self.recv, self.sends, self.recvs = send, recv, 0, 0

    def take_send(self):
        self.sends += 1
        return self.send.at[self.sends - 1]

    def take_recv(self):
        self.recvs += 1
        return self.recv.at[self.recvs - 1]

    def take(self):
        return self.take_send(), self.take_recv()


def layer_kernel(dims, names, *refs):
    n, D, FF, T, V = dims
    NF = 4
    R = D // (n * NF)
    RP = R * NF
    HC = FF // (NF * n)
    HF = FF // NF
    C = D // NF
    VP = V * NF
    S_ = T * NF
    last = n // 2 - 1
    given = dict(zip(names, refs))
    g = types.SimpleNamespace(**given, **{a: given[b] for a, b in ALIASES.items()})
    sems = Sems(g.send_sems, g.recv_sems)
    lsem = g.local_sems

    p = lax.axis_index("dp")
    f = lax.axis_index("fsdp")
    f1 = f + 1 - 2 * lax.rem(f, 2)
    f2 = lax.rem(f + 2, NF)
    f3 = NF - 1 - f
    par = lax.rem(p, 2)
    half_p = lax.div(p, 2)
    pos = (1 - par) * half_p + par * (n - 1 - half_p)

    def idx(q):
        q = lax.rem(q + 2 * n, n)
        up = lax.div(q, n // 2)
        return (1 - up) * (2 * q) + up * (2 * (n - 1 - q) + 1)

    right, left = idx(pos + 1), idx(pos - 1)

    pending = []

    def launch(src, dst, ss, rs, to):
        c = pltpu.make_async_remote_copy(
            src_ref=src, dst_ref=dst, send_sem=ss, recv_sem=rs, device_id=to, device_id_type=MESH
        )
        c.start()
        return c

    def received(copies):
        for c in copies:
            c.wait_recv()

    def remote(src, dst, to):
        ss, rs = sems.take()
        c = launch(src, dst, ss, rs, to)
        pending.append(c)
        return c, ss, rs

    def drain(*copies):
        for c in copies:
            pending[:] = [d for d in pending if d is not c]
            c.wait_send()

    def arrival(dst, ss, rs, to):
        return pltpu.make_async_remote_copy(
            src_ref=dst, dst_ref=dst, send_sem=ss, recv_sem=rs, device_id=to, device_id_type=MESH
        )

    to1, to2, to3 = {"fsdp": f1}, {"fsdp": f2}, {"fsdp": f3}
    peers = ((f1, to1), (f2, to2), (f3, to3))

    barrier = pltpu.get_barrier_semaphore()
    for to in (to1, to2, to3, {"dp": right}, {"dp": left}):
        pl.semaphore_signal(barrier, inc=1, device_id=to, device_id_type=MESH)

    loads = {}
    for i, (src, dst) in enumerate(
        (
            (g.wqkv, g.wqkv_v),
            (g.w1, g.w1_v),
            (g.wo, g.wo_v),
            (g.mask, g.mask_v),
            (g.tok, g.TA.at[f]),
            (g.w2, g.w2_v),
            (g.cot, g.CA.at[f]),
            (g.trig, g.trig_v),
        )
    ):
        c = pltpu.make_async_copy(src, dst, lsem.at[i])
        c.start()
        loads[i] = c
    vectors = []
    for k in range(8):
        vectors.append(pltpu.make_async_copy(given["in%d" % k], given["v%d" % k], lsem.at[8 + k]))
        vectors[k].start()

    AS, AQ, WO, A1, A2 = g.AS, g.AQ, g.WO, g.A1, g.A2
    TA, CA = g.TA, g.CA

    loads[5].wait()
    A2[p] = g.w2_v[...].astype(BF)
    loads[0].wait()
    for j in range(NF):
        for t in range(3):
            g.sq[j, :, C * t : C * t + C] = g.wqkv_v[:, D * t + C * j : D * t + C * j + C].astype(BF)
    AQ[p, pl.ds(pl.multiple_of(R * f, R), R), :] = g.sq[f]
    loads[2].wait()
    WO[p, f] = g.wo_v[...].astype(BF)
    pl.semaphore_wait(barrier, 5)

    def scatter(src, dst, three):
        ss, rs = sems.take()
        for fj, to in peers:
            launch(src(fj), dst(f), ss, rs, to)
        got = arrival(three, ss, rs, to1)
        pending.append(got)
        return (got,)

    class AllGather4:
        def __init__(self, slot):
            self.slot = slot
            _, ss, rs = remote(slot(f), slot(f), to2)
            self.across = arrival(slot(f2), ss, rs, to2)
            _, ss, rs = remote(slot(f), slot(f), to1)
            self.beside = arrival(slot(f1), ss, rs, to1)

        def forward(self):
            self.done = False
            self.across.wait_recv()
            _, ss, rs = remote(self.slot(f2), self.slot(f2), to1)
            self.passed = arrival(self.slot(f3), ss, rs, to1)

        def finish(self):
            if not self.done:
                self.done = True
                self.beside.wait_recv()
                self.passed.wait_recv()

    class ReduceScatter4:
        def __init__(self, part, r1, xs, r2):
            self.part, self.r1, self.xs, self.r2 = part, r1, xs, r2
            self.ca, ss, rs = remote(part.at[f3], r1.at[1], to1)
            self.other = arrival(r1.at[1], ss, rs, to1)
            self.cb, ss, rs = remote(part.at[f1], r1.at[0], to1)
            self.own = arrival(r1.at[0], ss, rs, to1)

        def forward(self):
            self.other.wait_recv()
            self.xs[...] = (self.part[f2].astype(F32) + self.r1[1].astype(F32)).astype(BF)
            _, ss, rs = remote(self.xs, self.r2, to2)
            self.across = arrival(self.r2, ss, rs, to2)

        def finish(self):
            self.own.wait_recv()
            self.across.wait_recv()

        def total(self):
            return self.part[f].astype(F32) + self.r1[0].astype(F32) + self.r2[...].astype(F32)

    class RingGather:
        def __init__(self, view, pair, rows):
            self.view, self.pair, self.rows = view, pair, rows
            self.before, self.flight = (), None
            self.ss = sems.take_send()

        def landed(self):
            received(self.before)
            self.before = ()
            if self.flight is not None:
                self.flight.wait_recv()
                self.flight.wait_send()
                self.flight = None

        def step(self, r):
            self.landed()
            h = self.rows // 2
            spans = ((0, self.rows), (0, self.rows)) if r < last else ((0, h), (h, h))
            rs = sems.take_recv()
            for way, (s, c) in zip((1, -1), spans):
                piece = self.view(idx(pos - way * r), s, c)
                launch(piece, piece, self.ss, rs, {"dp": right if way == 1 else left})
            both = self.pair if r < last else self.view(0, 0, self.rows)
            self.flight = arrival(both, self.ss, rs, {"dp": left})

        def finish(self):
            self.landed()

    def row_rings(ref):
        h = ref.shape[1] // 2

        def ring(offset):
            view = lambda slot, s, c: ref.at[slot, pl.ds(offset + s, c), :]
            return RingGather(view, ref.at[pl.ds(0, 2), pl.ds(offset, h), :], h)

        return [ring(0), ring(h)]

    q_ring, w1_ring, w2_ring = row_rings(AQ), row_rings(A1), row_rings(A2)
    o_ring = RingGather(lambda slot, s, c: WO.at[slot, f, pl.ds(s, c), :], WO.at[pl.ds(0, 2), f], R)
    s_ring = RingGather(lambda slot, s, c: AS.at[slot, pl.ds(s, c)], AS.at[pl.ds(0, 2)], NF)

    class RingReduce:
        def __init__(self, grads, start, rows, st, rr, rl, wire=BF):
            self.G, self.o, self.rows, self.st, self.rr, self.rl = grads, start, rows, st, rr, rl
            self.wire = wire
            self.flight = None
            self.ss = sems.take_send()

        def landed(self):
            if self.flight is not None:
                self.flight.wait_recv()
                self.flight.wait_send()
                self.flight = None

        def step(self, r):
            self.landed()
            o, rows = self.o, self.rows
            hh = rows // 2
            whole = pl.ds(o, rows)
            rs = sems.take_recv()
            ways = ((1, self.rr, 0, {"dp": right}), (-1, self.rl, hh, {"dp": left}))
            if r == 0:
                far = idx(pos + n // 2)
                self.st[whole, :] = self.G[far, whole, :].astype(self.wire)
                for _, buf, s, to in ways:
                    half = pl.ds(o + s, hh)
                    launch(self.st.at[half, :], buf.at[0, half, :], self.ss, rs, to)
                self.flight = arrival(self.st.at[whole, :], self.ss, rs, {"dp": left})
                return
            for way, buf, s, to in ways:
                c = idx(pos + way * (n // 2 - r))
                if r == 1:
                    half, other = pl.ds(o + s, hh), pl.ds(o + hh - s, hh)
                    total = buf[0, half, :].astype(F32) + self.G[c, half, :]
                    buf[0, half, :] = total.astype(self.wire)
                    buf[0, other, :] = self.G[c, other, :].astype(self.wire)
                else:
                    total = buf[r - 1, whole, :].astype(F32) + self.G[c, whole, :]
                    buf[r - 1, whole, :] = total.astype(self.wire)
                launch(buf.at[r - 1, whole, :], buf.at[r, whole, :], self.ss, rs, to)
            self.flight = arrival(self.rr.at[pl.ds(0, 2), whole, :], self.ss, rs, {"dp": left})

        def finish(self):
            self.landed()

        def total(self):
            o, rows = self.o, self.rows
            return (
                self.G[p, pl.ds(o, rows), :]
                + self.rr[last, pl.ds(o, rows), :].astype(F32)
                + self.rl[last, pl.ds(o, rows), :].astype(F32)
            )

    st = types.SimpleNamespace(oa=[None, None])
    N1, N2, GT, PT = g.N1, g.N2, g.GT, g.PT
    VEC, BQ, BG, VG = g.VEC, g.BQ, g.BG, g.VG
    Q, K, W, QV, KV, WV = g.Q, g.K, g.W, g.QV, g.KV, g.WV
    SM, OV, PV, OA, OT = g.SM, g.OV, g.PV, g.OA, g.OT
    XV, N1V, DY, X1V, N2V = g.XV, g.N1V, g.DY, g.X1V, g.N2V
    GV, GP, DH, PN, PF = g.GV, g.GP, g.DH, g.PN, g.PF
    G2, G1, GQ, GO = g.G2, g.G1, g.GQ, g.GO
    DO, DPRE = g.DO, g.DPRE
    E1, F1, EQ, FQ, SG = g.E1, g.F1, g.EQ, g.FQ, g.SG
    blocks = [slice(256 * k, 256 * k + 256) for k in range(D // 256)]
    mine = pl.ds(pl.multiple_of(V * f, V), V)
    hc, hr = HC // 2, RP // 2
    g2_ring = [
        RingReduce(G2, 0, hc, g.st2, g.rr2, g.rl2),
        RingReduce(G2, hc, hc, g.st2, g.rr2, g.rl2),
    ]
    g1_ring = [
        RingReduce(G1, 0, hr, g.st1, g.rr1, g.rl1),
        RingReduce(G1, hr, hr, g.st1, g.rr1, g.rl1),
    ]
    gq_ring = [
        RingReduce(GQ, 0, hr, g.stq, g.rrq, g.rlq),
        RingReduce(GQ, hr, hr, g.stq, g.rrq, g.rlq),
    ]
    go_ring = RingReduce(GO, 0, R, g.sto, g.rro, g.rlo)
    gs_ring = RingReduce(VG, 0, 16, g.sts, g.rrs, g.rls, F32)

    def finish(*rings):
        for r in rings:
            r.finish()

    outs = []

    def store(src, dst, k):
        c = pltpu.make_async_copy(src, dst, lsem.at[8 + k])
        c.start()
        outs.append(c)

    def vec(k):
        return VEC[k : k + 1, :]

    def start():
        part = lambda j: AQ.at[p, pl.ds(pl.multiple_of(R * j, R), R), :]
        q_ring[0].before = scatter(lambda j: g.sq.at[j], part, AQ.at[0, pl.ds(0, 3 * R), :])

    def small_start():
        for c in vectors:
            c.wait()
        loads[3].wait()
        SV = g.small_v
        SV[...] = jnp.zeros(SV.shape, F32)
        for k in range(8):
            row, at = ((0, R * k), (1, R * (k - 4)), (2, 0), (3, 0))[0 if k < 4 else 1 if k < 6 else k - 4]
            value = given["v%d" % k][...]
            width = value.shape[1]
            wide = value if width == 128 else jnp.concatenate([value, jnp.zeros((1, 128 - width), F32)], axis=1)
            SV[row : row + 1, :] += wide if at == 0 else pltpu.roll(wide, at, 1)
        mask = g.mask_v[...].astype(F32)
        below = lax.broadcasted_iota(jnp.int32, (128, 128), 0) <= lax.broadcasted_iota(jnp.int32, (128, 128), 1)
        tri = jnp.where(below, 1.0, 0.0).astype(BF)
        count = g.counts[0, 0].astype(F32)
        before = jnp.zeros((1, 1), F32)
        for k in range(2):
            ones = mask[:, 128 * k : 128 * k + 128]
            running = dot(jnp.broadcast_to(ones, (8, 128)).astype(BF), tri)[0:1, :] + before
            SV[4 + k : 5 + k, :] = jnp.where(running <= count, ones, 0.0)
            before = before + jnp.sum(ones, axis=1, keepdims=True)
        AS[p, f] = SV[...]
        st.s = scatter(lambda j: AS.at[p, f], lambda j: AS.at[p, j], AS.at[0, pl.ds(0, 3)])
        s_ring.before = st.s

    def cast_fc1():
        loads[1].wait()
        for j in range(NF):
            for t in range(n):
                at = HC * (NF * t + j)
                g.s1[j, :, HC * t : HC * t + HC] = g.w1_v[:, at : at + HC].astype(BF)
        A1[p, pl.ds(pl.multiple_of(R * f, R), R), :] = g.s1[f]
        part = lambda j: A1.at[p, pl.ds(pl.multiple_of(R * j, R), R), :]
        w1_ring[0].before = scatter(lambda j: g.s1.at[j], part, A1.at[0, pl.ds(0, 3 * R), :])

    def tokens_start():
        loads[4].wait()
        st.tok = AllGather4(lambda j: TA.at[j])

    def cot_start():
        loads[6].wait()
        st.cot = AllGather4(lambda j: CA.at[j])

    def wo_start():
        o_ring.finish()
        st.wo = AllGather4(lambda j: WO.at[:, j])

    ends = []
    total_len = jnp.int32(0)
    for k in range(g.lengths.shape[1]):
        total_len = total_len + g.lengths[0, k]
        ends.append(total_len)

    def key_segments():
        keyrow = lax.broadcasted_iota(jnp.int32, (1, S_), 1)
        segrow = jnp.zeros((1, S_), jnp.int32)
        for end in ends:
            segrow += (keyrow >= end).astype(jnp.int32)
        return segrow

    def layout():
        row, _seg = column_segment(0, S_, ends)
        before = jnp.zeros((S_, 1), jnp.int32)
        for k, end in enumerate(ends):
            before += jnp.where(row >= end, g.lengths[0, k], 0)
        place = row - before
        img = GRID * GRID
        frame = jnp.zeros((S_, 1), jnp.int32)
        for t in range(1, FRAMES):
            frame += (place >= img * t).astype(jnp.int32)
        rest = place - img * frame
        grow = jnp.zeros((S_, 1), jnp.int32)
        for t in range(1, GRID):
            grow += (rest >= GRID * t).astype(jnp.int32)
        gcol = rest - GRID * grow
        lane = lax.broadcasted_iota(jnp.int32, (S_, 128), 1)
        hot = (lane == frame) | (lane == grow + FRAMES) | (lane == gcol + (FRAMES + GRID))
        g.OH[...] = jnp.where(hot, 1.0, 0.0).astype(BF)
        loads[7].wait()
        g.CS[...] = sum(dot(g.OH[...], g.trig_v[k]) for k in range(3))

    def visible():
        if s_ring.before:
            received(s_ring.before)
            s_ring.before = ()
        vis8 = jnp.concatenate([AS[p, j][4:6, :] for j in range(NF)], axis=0)
        above = lax.broadcasted_iota(jnp.int32, (128, 128), 0)
        tri = above <= lax.broadcasted_iota(jnp.int32, (128, 128), 1)
        within = dot(vis8.astype(BF), jnp.where(tri, 1.0, 0.0).astype(BF))
        base = jnp.zeros((1, 128), F32)
        pieces, vpieces = [], []
        for k in range(8):
            pieces.append(within[k : k + 1, :] + base)
            vpieces.append(vis8[k : k + 1, :])
            base = base + jnp.sum(vis8[k : k + 1, :], axis=1, keepdims=True)
        incl = jnp.concatenate(pieces, axis=1)
        visrow = jnp.concatenate(vpieces, axis=1)
        rank = jnp.where(visrow > 0.5, incl - 1.0, -1.0).astype(jnp.int32)
        sel = lax.broadcasted_iota(jnp.int32, (VP, S_), 0) == rank
        SM[...] = jnp.where(sel, 1.0, 0.0).astype(BF)

    def rounded(v):
        return v.astype(BF).astype(F32)

    def turn(v, by):
        by = by % 128
        return v if by == 0 else pltpu.roll(v, by, 1)

    def small_vectors():
        s_ring.finish()
        lane128 = lax.broadcasted_iota(jnp.int32, (n, 128), 1)
        rows0 = [AS[:, j, 0, :] for j in range(NF)]
        rows1 = [AS[:, j, 1, :] for j in range(NF)]
        rows2 = [AS[:, j, 2, :] for j in range(NF)]
        for k in range(6):
            src = rows0 if k < 4 else rows1
            piece = jnp.zeros((n, 128), F32)
            for j in range(NF):
                piece = jnp.where(lax.div(lane128, R) == j, turn(src[j], R * (j - k % 4)), piece)
            for q in range(n):
                VEC[k : k + 1, 128 * q : 128 * q + 128] = rounded(piece[q : q + 1, :])
        for q in range(n):
            VEC[6:7, 128 * q : 128 * q + 128] = rounded(AS[q, f][3:4, :])
        t0 = jnp.where(lane128 < 96, rows2[0], turn(rows2[1], 96))
        t1 = jnp.where(lane128 < 64, turn(rows2[1], -32), turn(rows2[2], 64))
        t2 = jnp.where(lane128 < 32, turn(rows2[2], -64), turn(rows2[3], 32))
        for q in range(n):
            for k, t in enumerate((t0, t1, t2)):
                BQ[0:1, 384 * q + 128 * k : 384 * q + 128 * k + 128] = rounded(t[q : q + 1, :])

    def first_norm():
        st.tok.finish()

        def block(b, _):
            xhat, _inv = norm_stats(TA[b].astype(F32))
            N1[b] = (xhat * vec(0) + vec(1)).astype(BF)
            return 0

        lax.fori_loop(0, NF, block, 0)

    def project_half(part):
        finish(*q_ring)

        def block(b, _):
            rows = pl.ds(pl.multiple_of(b * T, T), T)
            cs = g.CS[rows, :]
            for t, dst in enumerate((Q, K, W)):
                out = dot(N1[b], AQ[:, :, C * t : C * t + C].reshape(D, C))
                out = out + BQ[0:1, pl.ds(pl.multiple_of(D * t + C * f, 128), C)]
                if t == 2:
                    dst[rows, :] = out.astype(BF)
                    continue
                for hh in range(C // 128):
                    u = out[:, 128 * hh : 128 * hh + 128]
                    u = (u * cs[:, :128] + swap_halves(u) * cs[:, 128:]).astype(BF)
                    dst[rows, 128 * hh : 128 * hh + 128] = u * BF(0.125) if t == 0 else u
            return 0

        lax.fori_loop(NF // 2 * part, NF // 2 * (part + 1), block, 0)

    lane_c = lax.broadcasted_iota(jnp.int32, (1, C), 1)
    hmask = [jnp.where(lax.div(lane_c, HDIM) == hd, 1.0, 0.0) for hd in range(C // HDIM)]

    def softmax(s):
        e = jnp.exp(s - jnp.max(s, axis=-1, keepdims=True))
        return e * (1.0 / jnp.sum(e, axis=-1, keepdims=True))

    def context_attention():
        for src, dst in ((Q, QV), (K, KV), (W, WV)):
            dst[...] = dot(SM[...], src[...]).astype(BF)
        segrow = key_segments()
        seg8 = jnp.broadcast_to(segrow.astype(F32), (8, S_)).astype(BF)
        segv_row = dot(seg8, SM[...], NT)[0:1, :].astype(jnp.int32)
        segv_col = jnp.sum(SM[...].astype(F32) * segrow.astype(F32), axis=1, keepdims=True).astype(jnp.int32)
        same = segv_col == segv_row
        acc = jnp.zeros((VP, C), F32)
        for hd in range(C // HDIM):
            s = dot(QV[...] * hmask[hd].astype(BF), KV[...], NT)
            pr = softmax(jnp.where(same, s, FILL))
            PV[hd] = pr
            acc += dot(pr.astype(BF), WV[...]) * hmask[hd]
        OV[f] = acc.astype(BF)
        st.ov = AllGather4(lambda j: OV.at[j])

    def attend_target(b, pair):
        rows = slice(T * b, T * b + T)
        _, segq = column_segment(b * T, T, ends)
        same = segq == key_segments()
        for hd in (2 * pair, 2 * pair + 1):
            s = dot(Q[rows, :] * hmask[hd].astype(BF), K[...], NT)
            pr = softmax(jnp.where(same, s, FILL)).astype(BF)
            o = dot(pr, W[...])
            cols = slice(HDIM * hd, HDIM * hd + HDIM)
            OA[f, rows, cols] = o[:, cols].astype(BF)

    def oa_start(part):
        rows = pl.ds(S_ // 2 * part, S_ // 2)
        st.oa[part] = AllGather4(lambda j: OA.at[j, rows, :])

    def select_rows():
        for cols in blocks:
            XV[:, cols] = dot(SM[...], TA[:, :, cols].reshape(S_, 256)).astype(BF)
            N1V[:, cols] = dot(SM[...], N1[:, :, cols].reshape(S_, 256)).astype(BF)

    def select_cot():
        st.cot.finish()
        for cols in blocks:
            DY[:, cols] = dot(SM[...], CA[:, :, cols].reshape(S_, 256)).astype(BF)

    def out_project(parts, cols):
        heads = [WO[n // NF * j : n // NF * (j + 1), :, :, cols].reshape(C, -1) for j in range(NF)]
        return sum(dot(parts(j), heads[j]) for j in range(NF))

    def context_middle():
        st.wo.finish()
        st.ov.finish()
        for cols in blocks:
            X1V[:, cols] = XV[:, cols].astype(F32) + (out_project(lambda j: OV[j], cols) + VEC[4:5, cols])
        xhat, _inv = norm_stats(X1V[...])
        N2V[...] = (xhat * vec(2) + vec(3)).astype(BF)

    def normal_cdf(hid):
        return 0.5 * (1.0 + lax.erf(hid * (1.0 / math.sqrt(2.0))))

    def context_hidden():
        finish(*w1_ring)
        for cols in blocks:
            hid = dot(N2V[...], A1[:, :, cols].reshape(D, 256)) + VEC[6:7, cols]
            cdf = normal_cdf(hid)
            GV[:, cols] = (hid * cdf).astype(BF)
            GP[:, cols] = cdf + hid * (jnp.exp(-0.5 * hid * hid) * (1.0 / math.sqrt(2.0 * math.pi)))

    def outer(dst, lhs, rhs):
        for k, cols in enumerate(blocks):
            g.LT[cols, :] = lhs[:, cols].astype(F32).T.astype(BF)

        def one(k, _):
            rows = pl.ds(pl.multiple_of(512 * k, 512), 512)
            for c in range(dst.shape[2] // 256):
                cols = slice(256 * c, 256 * c + 256)
                dst[pl.ds(4 * k, 4), :, cols] = dot(g.LT[rows, :], rhs[:, cols]).reshape(4, 128, 256)
            return 0

        lax.fori_loop(0, n // 4, one, 0)

    def put_grad(k, vrow):
        for q in range(n):
            VG[q, k : k + 1, :] = vrow[:, 128 * q : 128 * q + 128]

    def fc2_grad():
        outer(G2, GV, DY)

    def hidden_grad():
        finish(*w2_ring)
        for k, cols in enumerate(blocks):
            dg = dot(DY[...], A2[...].reshape(HF, D)[256 * k : 256 * k + 256, :], NT)
            dh = (dg * GP[:, cols]).astype(BF)
            DH[:, cols] = dh
            dc1 = jnp.sum(dh.astype(F32), axis=0, keepdims=True)
            for q in range(2):
                for j in range(NF):
                    piece = dc1[:, 128 * q : 128 * q + 128]
                    VG[2 * k + q, 9 + j : 10 + j, :] = jnp.where(f == j, piece, jnp.zeros((1, 128), F32))

    def second_grad():
        for k, cols in enumerate(blocks):
            part = dot(DH[...], A1[2 * k : 2 * k + 2].reshape(256, HF), NT).astype(BF)
            PN[:, :, cols] = part.reshape(NF, V, 256)
        st.n2 = ReduceScatter4(PN, g.PNr1, g.PNxs, g.PNr2)

    def fc1_grad():
        outer(G1, N2V, DH)

    def context_partial():
        for cols in blocks:
            part = dot(GV[...], A2[:, :, cols].reshape(HF, 256)).astype(BF)
            PF[:, :, cols] = part.reshape(NF, V, 256)
        st.pf = ReduceScatter4(PF, g.PFr1, g.PFxs, g.PFr2)

    def second_norm_back():
        st.n2.finish()
        dyo = DY[mine, :].astype(F32)
        dv, dgain, dshift = norm_back(X1V[mine, :], vec(2), st.n2.total())
        dx1 = dyo + dv
        g.DX1[...] = dx1
        low = dx1.astype(BF)
        g.DP[f] = low
        st.dp = AllGather4(lambda j: g.DP.at[j])
        put_grad(2, dgain)
        put_grad(3, dshift)
        put_grad(4, jnp.sum(low.astype(F32), axis=0, keepdims=True))
        put_grad(5, jnp.sum(dyo, axis=0, keepdims=True))

    def transpose_attended():
        st.ov.finish()
        for j in range(NF):
            ot = OV[j].astype(F32).T.astype(BF)
            OT[n // NF * j : n // NF * (j + 1)] = ot.reshape(n // NF, NF, R, VP)

    def out_grad():
        st.dp.finish()
        go = dot(OT[:, f].reshape(n * R, VP), g.DP[...].reshape(VP, D))
        GO[...] = go.reshape(n, R, D)

    def attended_grad():
        st.dp.finish()
        st.wo.finish()
        wo_heads = WO[pl.ds(n // NF * f, n // NF)].reshape(C, D)
        DO[...] = dot(g.DP[...].reshape(VP, D), wo_heads, NT).astype(BF)

    def attention_back():
        dq = jnp.zeros((VP, C), F32)
        dk = jnp.zeros((VP, C), F32)
        dw = jnp.zeros((VP, C), F32)
        for hd in range(C // HDIM):
            pr = PV[hd]
            dp = dot(DO[...] * hmask[hd].astype(BF), WV[...], NT)
            ds = (pr * (dp - jnp.sum(pr * dp, axis=-1, keepdims=True))).astype(BF)
            dq += dot(ds, KV[...]) * hmask[hd]
            dk += dot(ds, QV[...], TN) * hmask[hd]
            dw += dot(pr.astype(BF), DO[...], TN) * hmask[hd]
        csv = sum(dot(dot(SM[...], g.OH[...]).astype(BF), g.trig_v[k]) for k in range(3))
        for t, (grad, scale) in enumerate(((dq, 0.125), (dk, 1.0))):
            for hh in range(C // 128):
                u = grad[:, 128 * hh : 128 * hh + 128]
                u = u * csv[:, :128] - swap_halves(u) * csv[:, 128:]
                DPRE[:, C * t + 128 * hh : C * t + 128 * hh + 128] = (u * scale).astype(BF)
        DPRE[:, 2 * C :] = dw.astype(BF)

    def qkv_grad():
        outer(GQ, N1V, DPRE)

    def qkv_bias_grad():
        BG[...] = jnp.zeros(BG.shape, F32)
        db = jnp.sum(DPRE[...].astype(F32), axis=0, keepdims=True)
        for t in range(3):
            BG[0:1, pl.ds(pl.multiple_of(D * t + C * f, 128), C)] = db[:, C * t : C * t + C]
        for q in range(n):
            for t in range(3):
                VG[q, 6 + t : 7 + t, :] = BG[0:1, 384 * q + 128 * t : 384 * q + 128 * t + 128]
            VG[q, 13:16, :] = jnp.zeros((3, 128), F32)

    def first_grad():
        drain(st.n2.ca, st.n2.cb)
        for k, cols in enumerate(blocks):
            part = dot(DPRE[...], AQ[2 * k : 2 * k + 2].reshape(256, 3 * C), NT).astype(BF)
            PN[:, :, cols] = part.reshape(NF, V, 256)
        st.n1 = ReduceScatter4(PN, g.PMr1, g.PMxs, g.PMr2)

    def first_norm_back():
        st.n1.finish()
        dv, dgain, dshift = norm_back(XV[mine, :].astype(F32), vec(0), st.n1.total())
        g.DX[f] = (g.DX1[...] + dv).astype(BF)
        st.dx = AllGather4(lambda j: g.DX.at[j])
        put_grad(0, dgain)
        put_grad(1, dshift)

    def context_result():
        st.pf.finish()
        g.CO[f] = (X1V[mine, :] + (st.pf.total() + vec(5))).astype(BF)
        st.co = AllGather4(lambda j: g.CO.at[j])

    def home(src, dst):
        s = SM[:, pl.ds(pl.multiple_of(T * f, 128), T)]
        for cols in blocks:
            dst[:, cols] = dot(s, src[:, :, cols].reshape(VP, 256), TN).astype(BF)

    def home_context():
        st.co.finish()
        home(g.CO, g.CH)
        store(g.CH, g.ctx_o, 0)

    def home_grad():
        st.dx.finish()
        home(g.DX, g.DXH)
        store(g.DXH, g.dx_o, 1)

    def target_middle(b):
        st.wo.finish()
        st.oa[b // 2].finish()
        for cols in blocks:
            g.X1B[:, cols] = TA[b, :, cols].astype(F32) + (
                out_project(lambda j: OA[j, T * b : T * b + T, :], cols) + VEC[4:5, cols]
            )
        x1 = g.X1B[...]
        xh, _inv = norm_stats(x1)
        N2[b] = (xh * vec(2) + vec(3)).astype(BF)

        @pl.when(f == b)
        def _():
            g.X1H[...] = x1

    def target_hidden(b):
        finish(*w1_ring)
        for cols in blocks:
            hid = dot(N2[b], A1[:, :, cols].reshape(D, 256)) + VEC[6:7, cols]
            GT[b, :, cols] = (hid * normal_cdf(hid)).astype(BF)

    def target_out(b):
        finish(*w2_ring)
        for cols in blocks:
            PT[b, :, cols] = dot(GT[b], A2[:, :, cols].reshape(HF, 256)).astype(BF)
        if b == NF - 1:
            st.pt = ReduceScatter4(PT, g.PTr1, g.PTxs, g.PTr2)

    def target_result():
        st.pt.finish()
        g.TO[...] = (g.X1H[...] + (st.pt.total() + vec(5))).astype(BF)
        store(g.TO, g.tgt_o, 3)

    def fc2_grad_done():
        finish(*g2_ring)
        for k, ring in enumerate(g2_ring):
            g.D2[hc * k : hc * k + hc, :] = ring.total()
        store(g.D2, g.g2_o, 2)

    def fc1_grad_trade():
        finish(*g1_ring)
        for k, ring in enumerate(g1_ring):
            E1[2 * k : 2 * k + 2] = ring.total().astype(BF).reshape(2, R, HF)
        F1[f] = E1[f]
        st.e1 = scatter(lambda j: E1.at[j], lambda j: F1.at[j], F1.at[pl.ds(0, 3)])

    def fc1_grad_done():
        received(st.e1)
        store(F1, g.g1_o, 5)

    def out_grad_done():
        go_ring.finish()
        g.DOo[...] = go_ring.total()
        store(g.DOo, g.go_o, 4)

    def qkv_grad_trade():
        finish(*gq_ring)
        for k, ring in enumerate(gq_ring):
            EQ[2 * k : 2 * k + 2] = ring.total().astype(BF).reshape(2, R, 3 * C)
        FQ[f] = EQ[f]
        st.eq = scatter(lambda j: EQ.at[j], lambda j: FQ.at[j], FQ.at[pl.ds(0, 3)])

    def qkv_grad_done():
        received(st.eq)
        store(FQ, g.gq_o, 7)

    def small_grad_trade():
        gs_ring.finish()
        SG[f] = gs_ring.total()
        st.sg = scatter(lambda j: SG.at[f], lambda j: SG.at[j], SG.at[pl.ds(0, 3)])

    def small_grad_done():
        received(st.sg)
        g.SGo[...] = SG[0] + SG[1] + SG[2] + SG[3]
        store(g.SGo, g.sg_o, 6)

    start()
    small_start()
    cast_fc1()
    tokens_start()
    cot_start()
    w2_ring[0].step(0)
    o_ring.step(0)
    layout()
    q_ring[0].step(0)
    q_ring[1].step(0)
    s_ring.step(0)
    visible()
    w1_ring[0].step(0)
    o_ring.step(1)
    q_ring[0].step(1)
    q_ring[1].step(1)
    s_ring.step(1)
    w1_ring[0].step(1)
    o_ring.step(2)
    q_ring[0].step(2)
    st.tok.forward()
    q_ring[1].step(2)
    s_ring.step(2)
    w1_ring[0].step(2)
    o_ring.step(3)
    q_ring[0].step(3)
    q_ring[1].step(3)
    s_ring.step(3)
    st.cot.forward()
    w1_ring[1].step(0)
    w1_ring[0].step(3)
    wo_start()
    select_cot()
    small_vectors()
    first_norm()
    w2_ring[1].step(0)
    project_half(0)
    w1_ring[1].step(1)
    project_half(1)
    select_rows()
    context_attention()
    w2_ring[1].step(1)
    attend_target(2, 0)
    w2_ring[0].step(1)
    attend_target(1, 0)
    w1_ring[1].step(2)
    st.wo.forward()
    attend_target(1, 1)
    attend_target(0, 0)
    st.ov.forward()
    attend_target(0, 1)
    w2_ring[0].step(2)
    context_middle()
    transpose_attended()
    oa_start(0)
    attend_target(2, 1)
    w1_ring[1].step(3)
    attend_target(3, 0)
    w2_ring[1].step(2)
    attend_target(3, 1)
    oa_start(1)
    w2_ring[0].step(3)
    context_hidden()
    fc2_grad()
    g2_ring[0].step(0)
    g2_ring[1].step(0)
    st.oa[0].forward()
    w2_ring[1].step(3)
    g2_ring[0].step(1)
    g2_ring[1].step(1)
    st.oa[1].forward()
    hidden_grad()
    second_grad()
    fc1_grad()
    g1_ring[0].step(0)
    g1_ring[1].step(0)
    context_partial()
    st.n2.forward()
    target_middle(0)
    target_middle(1)
    g2_ring[0].step(2)
    st.pf.forward()
    g2_ring[1].step(2)
    target_hidden(0)
    target_middle(2)
    g1_ring[0].step(1)
    target_middle(3)
    second_norm_back()
    target_hidden(2)
    target_hidden(3)
    context_result()
    target_hidden(1)
    g1_ring[1].step(1)
    target_out(0)
    target_out(1)
    g2_ring[1].step(3)
    st.dp.forward()
    target_out(2)
    target_out(3)
    attended_grad()
    g1_ring[0].step(2)
    attention_back()
    first_grad()
    qkv_grad()
    gq_ring[0].step(0)
    gq_ring[1].step(0)
    out_grad()
    go_ring.step(0)
    qkv_bias_grad()
    st.n1.forward()
    st.co.forward()
    st.pt.forward()
    g1_ring[1].step(2)
    home_context()
    g1_ring[0].step(3)
    gq_ring[0].step(1)
    first_norm_back()
    gs_ring.step(0)
    gq_ring[1].step(1)
    go_ring.step(1)
    g1_ring[1].step(3)
    gq_ring[0].step(2)
    gs_ring.step(1)
    gq_ring[1].step(2)
    target_result()
    go_ring.step(2)
    st.dx.forward()
    fc1_grad_trade()
    home_grad()
    gq_ring[0].step(3)
    gs_ring.step(2)
    gq_ring[1].step(3)
    fc1_grad_done()
    go_ring.step(3)
    gs_ring.step(3)
    g2_ring[0].step(3)
    qkv_grad_trade()
    out_grad_done()
    small_grad_trade()
    fc2_grad_done()
    qkv_grad_done()
    small_grad_done()
    for c in outs:
        c.wait()
    for c in pending:
        c.wait_send()


def run_layer(n, tokens, cot, lengths, mask, counts, vectors, wqkv, wo, w1, w2, V):
    T, D = tokens.shape
    NF = 4
    FF = w1.shape[1]
    R = wo.shape[0]
    RP = R * NF
    HC = w2.shape[0]
    HF = HC * n
    C = D // NF
    VP = V * NF
    S_ = T * NF
    h2 = n // 2
    B, F = BF, F32
    vm = pltpu.VMEM
    scratch = dict(
        wqkv_v=vm((R, 3 * D), F), w1_v=vm((R, FF), F), wo_v=vm((R, D), F), w2_v=vm((HC, D), F),
        small_v=vm((8, 128), F), trig_v=vm((3, 128, 256), B),
        sq=vm((NF, R, 3 * C), B), s1=vm((NF, R, HF), B),
        AS=vm((n, NF, 8, 128), F), AQ=vm((n, RP, 3 * C), B), WO=vm((n, NF, R, D), B),
        A1=vm((n, RP, HF), B), A2=vm((n, HC, D), B),
        TA=vm((NF, T, D), B), CA=vm((NF, T, D), B), N1=vm((NF, T, D), B),
        OH=vm((S_, 128), B), CS=vm((S_, 256), F), SM=vm((VP, S_), B),
        VEC=vm((8, D), F), BQ=vm((8, 3 * D), F), BG=vm((8, 3 * D), F),
        Q=vm((S_, C), B), K=vm((S_, C), B), W=vm((S_, C), B),
        QV=vm((VP, C), B), KV=vm((VP, C), B), WV=vm((VP, C), B),
        OV=vm((NF, VP, C), B), PV=vm((C // HDIM, VP, VP), F), OA=vm((NF, S_, C), B),
        XV=vm((VP, D), B), N1V=vm((VP, D), B), DY=vm((VP, D), B),
        X1V=vm((VP, D), F), N2V=vm((VP, D), B), GV=vm((VP, HF), B), GP=vm((VP, HF), F),
        G2=vm((n, HC, D), F), G1=vm((n, RP, HF), F), GQ=vm((n, RP, 3 * C), F), GO=vm((n, R, D), F),
        VG=vm((n, 16, 128), F),
        st2=vm((HC, D), B), rr2=vm((h2, HC, D), B), rl2=vm((h2, HC, D), B),
        st1=vm((RP, HF), B), rr1=vm((h2, RP, HF), B), rl1=vm((h2, RP, HF), B),
        stq=vm((RP, 3 * C), B), rrq=vm((h2, RP, 3 * C), B), rlq=vm((h2, RP, 3 * C), B),
        sto=vm((R, D), B), rro=vm((h2, R, D), B), rlo=vm((h2, R, D), B),
        sts=vm((16, 128), F), rrs=vm((h2, 16, 128), F), rls=vm((h2, 16, 128), F),
        DH=vm((VP, HF), B), PN=vm((NF, V, D), B), PF=vm((NF, V, D), B),
        PNr1=vm((2, V, D), B), PNxs=vm((V, D), B), PNr2=vm((V, D), B),
        PMr1=vm((2, V, D), B), PMxs=vm((V, D), B), PMr2=vm((V, D), B),
        PFr1=vm((2, V, D), B), PFxs=vm((V, D), B), PFr2=vm((V, D), B),
        DX1=vm((V, D), F), DP=vm((NF, V, D), B), OT=vm((n, NF, R, VP), B), DO=vm((VP, C), B),
        DPRE=vm((VP, 3 * C), B), CO=vm((NF, V, D), B), DX=vm((NF, V, D), B),
        X1H=vm((T, D), F), GT=vm((NF, T, HF), B),
        PTr1=vm((2, T, D), B), PTxs=vm((T, D), B), PTr2=vm((T, D), B),
        CH=vm((T, D), B), DXH=vm((T, D), B), TO=vm((T, D), B),
        SG=vm((NF, 16, 128), F), SGo=vm((16, 128), F),
        E1=vm((NF, R, HF), B), F1=vm((NF, R, HF), B), EQ=vm((NF, R, 3 * C), B), FQ=vm((NF, R, 3 * C), B),
        send_sems=pltpu.SemaphoreType.DMA((61,)), recv_sems=pltpu.SemaphoreType.DMA((109,)),
        local_sems=pltpu.SemaphoreType.DMA((16,)), mask_v=vm((1, T), jnp.int32), LT=vm((D, VP), B),
    )
    arr = jax.ShapeDtypeStruct
    ins = dict(
        lengths=lengths, counts=counts, tok=tokens, cot=cot, mask=mask.reshape(1, T), wqkv=wqkv, wo=wo,
        w1=w1, w2=w2, trig=jnp.asarray(trig_table()),
    )
    for k, v in enumerate(vectors):
        ins["in%d" % k] = v.reshape(1, -1)
        scratch["v%d" % k] = vm((1, v.shape[0]), F)
    outs = dict(
        tgt_o=arr((T, D), B), ctx_o=arr((T, D), B), dx_o=arr((T, D), B), gq_o=arr((NF, R, 3 * C), B),
        go_o=arr((R, D), F), g1_o=arr((NF, R, HF), B), g2_o=arr((HC, D), F), sg_o=arr((16, 128), F),
    )
    names = [*ins, *outs, *scratch]
    any_spec = pl.BlockSpec(memory_space=pl.ANY)
    return pl.pallas_call(
        functools.partial(layer_kernel, (n, D, FF, T, V), names),
        out_shape=list(outs.values()),
        in_specs=[pl.BlockSpec(memory_space=pltpu.SMEM)] * 2 + [any_spec] * (len(ins) - 2),
        out_specs=[any_spec] * 8,
        scratch_shapes=list(scratch.values()),
        compiler_params=pltpu.CompilerParams(
            collective_id=0, has_side_effects=True, vmem_limit_bytes=67043328
        ),
        name="layer",
    )(*ins.values())


def outputs_kernel(dims, count, *refs):
    n, R, C, HC = dims
    NF = 4
    f = lax.axis_index("fsdp")
    tgt, ctx, dx, gq, go, g1, g2, sg = refs[:8]
    tgt_o, ctx_o, dx_o, gq_o, go_o, g1_o, g2_o = refs[8:15]
    vec_o = refs[15:23]
    bufs = refs[23:31]
    gq_w, g1_w, sem_in, sem_out = refs[31:]
    loads = []
    for k, (src, dst) in enumerate(zip((gq, g1, sg, g2, tgt, ctx, dx, go), bufs)):
        c = pltpu.make_async_copy(src, dst, sem_in.at[k])
        c.start()
        loads.append(c)
    stores = []

    def store(src, dst):
        c = pltpu.make_async_copy(src, dst, sem_out.at[len(stores)])
        c.start()
        stores.append(c)

    D = NF * C
    loads[0].wait()
    for j in range(NF):
        for t in range(3):
            gq_w[:, D * t + C * j : D * t + C * j + C] = bufs[0][j, :, C * t : C * t + C].astype(F32)
    store(gq_w, gq_o)
    loads[1].wait()
    for j in range(NF):
        for t in range(n):
            at = HC * (NF * t + j)
            g1_w[:, at : at + HC] = bufs[1][j, :, HC * t : HC * t + HC].astype(F32)
    store(g1_w, g1_o)
    for k, out in enumerate((g2_o, tgt_o, ctx_o, dx_o, go_o)):
        loads[3 + k].wait()
        store(bufs[3 + k], out)
    loads[2].wait()
    small = bufs[2]
    for k in range(6):
        vec_o[k][...] = pltpu.roll(small[k : k + 1, :], lax.rem(128 - R * f, 128), 1)[:, :R]
    rows = jnp.concatenate([small[6 + t : 7 + t, :] for t in range(3)], axis=1)
    vec_o[6][...] = pltpu.roll(rows, lax.rem(384 - 3 * R * f, 384), 1)[:, : 3 * R]
    mine = jnp.zeros((1, 128), F32)
    for j in range(NF):
        mine = jnp.where(f == j, small[9 + j : 10 + j, :], mine)
    vec_o[7][...] = mine
    for c in stores:
        c.wait()


def write_outputs(n, parts, R, D, FF, HC):
    NF = 4
    C = D // NF
    tgt = parts[0]
    arr = jax.ShapeDtypeStruct
    any_spec = pl.BlockSpec(memory_space=pl.ANY)
    order = [parts[k] for k in (3, 5, 7, 6, 0, 1, 2, 4)]
    big = [
        arr(tgt.shape, BF), arr(tgt.shape, BF), arr(tgt.shape, BF),
        arr((R, 3 * D), F32), arr((R, D), F32), arr((R, FF), F32), arr((HC, D), F32),
    ]
    small = [arr((1, w), F32) for w in (R,) * 6 + (3 * R, 4 * R)]
    return pl.pallas_call(
        functools.partial(outputs_kernel, (n, R, C, HC), 8),
        out_shape=big + small,
        in_specs=[any_spec] * 8,
        out_specs=[any_spec] * 7 + [pl.BlockSpec(memory_space=pltpu.VMEM)] * 8,
        scratch_shapes=[pltpu.VMEM(a.shape, a.dtype) for a in order]
        + [
            pltpu.VMEM((R, 3 * D), F32), pltpu.VMEM((R, FF), F32),
            pltpu.SemaphoreType.DMA((8,)), pltpu.SemaphoreType.DMA((8,)),
        ],
        name="outputs",
    )(*parts)


def on_device(
    tokens, lengths, visibility_mask, visible_counts, ln1_gain, ln1_bias, qkv_weight, qkv_bias,
    out_weight, out_bias, ln2_gain, ln2_bias, fc1_weight, fc1_bias, fc2_weight, fc2_bias, context_cot,
):
    n = lax.axis_size("dp")
    R, D = out_weight.shape
    vectors = (ln1_gain, ln1_bias, ln2_gain, ln2_bias, out_bias, fc2_bias, qkv_bias, fc1_bias)
    parts = run_layer(
        n, tokens, context_cot, lengths, visibility_mask, visible_counts, vectors,
        qkv_weight, out_weight, fc1_weight, fc2_weight, VIS_DEV,
    )
    tgt, ctx, dx, gq, go, g1, g2, *small = write_outputs(
        n, parts, R, D, fc1_weight.shape[1], fc2_weight.shape[0]
    )
    gg1, gb1, gg2, gb2, gbo, gc2, gbq, gc1 = [v.reshape(-1) for v in small]
    return (tgt, ctx, dx, gg1, gb1, gq, gbq, go, gbo, gg2, gb2, g1, gc1, g2, gc2)


def layer_norm(inputs, scale_vec, shift_vec):
    center = inputs - jnp.mean(inputs, axis=-1, keepdims=True)
    spread = jnp.mean(center * center, axis=-1, keepdims=True)
    return center * lax.rsqrt(spread + norm_eps) * scale_vec + shift_vec


def gelu_erf(values):
    return jax.nn.gelu(values, approximate=False)


def pack_layout(seq_lens, pack_len):
    seq_ends = jnp.cumsum(seq_lens)
    places = jnp.arange(pack_len, dtype=jnp.int32)
    passed = places[:, None] >= seq_ends[None, :]
    segment = jnp.sum(passed.astype(jnp.int32), axis=1)
    before = jnp.sum(jnp.where(passed, seq_lens[None, :], 0), axis=1)
    return (segment, places - before)


def rope_tables(places):
    frame_index = (places // (GRID * GRID)).astype(jnp.float32)
    grid_row = (places // GRID % GRID).astype(jnp.float32)
    grid_col = (places % GRID).astype(jnp.float32)
    pair_index = jnp.arange(HDIM // 2, dtype=jnp.int32)
    axis_pick = jnp.minimum(pair_index // 11, 2)
    pair_order = (pair_index - 11 * axis_pick).astype(jnp.float32)
    frequency = jnp.exp(pair_order * (-math.log(10000.0) / 11.0))
    angles = (
        frame_index[:, None] * (axis_pick == 0).astype(jnp.float32)[None, :]
        + grid_row[:, None] * (axis_pick == 1).astype(jnp.float32)[None, :]
        + grid_col[:, None] * (axis_pick == 2).astype(jnp.float32)[None, :]
    ) * frequency[None, :]
    return (jnp.cos(angles), jnp.sin(angles))


def rotate(heads, cosine_table, sine_table):
    half_size = heads.shape[-1] // 2
    first_half = heads[..., :half_size]
    second_half = heads[..., half_size:]
    cosine_cols = cosine_table[:, None, :]
    sine_cols = sine_table[:, None, :]
    return jnp.concatenate(
        [
            first_half * cosine_cols - second_half * sine_cols,
            second_half * cosine_cols + first_half * sine_cols,
        ],
        axis=-1,
    )


def rotate_back(grads, cosine_table, sine_table):
    half_size = grads.shape[-1] // 2
    first_half = grads[..., :half_size]
    second_half = grads[..., half_size:]
    cosine_cols = cosine_table[:, None, :]
    sine_cols = sine_table[:, None, :]
    return jnp.concatenate(
        [
            first_half * cosine_cols + second_half * sine_cols,
            second_half * cosine_cols - first_half * sine_cols,
        ],
        axis=-1,
    )


def project(token_rows, weights, cosine_table, sine_table):
    inputs = token_rows.astype(jnp.float32)
    row_count = inputs.shape[0]
    model_width = inputs.shape[1]
    normed = layer_norm(
        inputs, weights[0].astype(jnp.float32), weights[1].astype(jnp.float32)
    ).astype(jnp.bfloat16)
    joined = jnp.dot(normed, weights[2], preferred_element_type=jnp.float32) + weights[3].astype(
        jnp.float32
    )
    query_heads = rotate(
        joined[:, :model_width].reshape(row_count, HEADS, HDIM), cosine_table, sine_table
    ).astype(jnp.bfloat16)
    key_flat = (
        rotate(
            joined[:, model_width : 2 * model_width].reshape(row_count, HEADS, HDIM),
            cosine_table,
            sine_table,
        )
        .astype(jnp.bfloat16)
        .reshape(row_count, model_width)
    )
    value_flat = joined[:, 2 * model_width :].astype(jnp.bfloat16)
    return (inputs, normed, query_heads, key_flat, value_flat)


def attend(query_heads, key_flat, value_flat, seg_query, seg_key):
    key_heads = key_flat.reshape(key_flat.shape[0], HEADS, HDIM)
    value_heads = value_flat.reshape(value_flat.shape[0], HEADS, HDIM)
    scores = jnp.einsum(
        "qhd,khd->hqk", query_heads, key_heads, preferred_element_type=jnp.float32
    ) * HDIM ** (-0.5)
    allowed = seg_query[:, None] == seg_key[None, :]
    masked = jnp.where(allowed[None], scores, masked_fill)
    row_max = jnp.max(masked, axis=-1, keepdims=True)
    raised = jnp.exp(masked - row_max)
    totals = jnp.sum(raised, axis=-1, keepdims=True)
    attn_probs = (raised / totals).astype(jnp.bfloat16)
    attended = jnp.einsum(
        "hqk,khd->qhd", attn_probs, value_heads, preferred_element_type=jnp.float32
    )
    return (
        attended.reshape(query_heads.shape[0], -1).astype(jnp.bfloat16),
        row_max + jnp.log(totals),
    )


def attend_back(query_heads, key_flat, value_flat, seg_query, seg_key, log_total, grad_att):
    key_heads = key_flat.reshape(key_flat.shape[0], HEADS, HDIM)
    value_heads = value_flat.reshape(value_flat.shape[0], HEADS, HDIM)
    scale_factor = HDIM ** (-0.5)
    scores = (
        jnp.einsum("qhd,khd->hqk", query_heads, key_heads, preferred_element_type=jnp.float32)
        * scale_factor
    )
    allowed = seg_query[:, None] == seg_key[None, :]
    masked = jnp.where(allowed[None], scores, masked_fill)
    attn_probs = jnp.exp(masked - log_total)
    grad_heads = grad_att.reshape(grad_att.shape[0], HEADS, HDIM)
    grad_probs = jnp.einsum(
        "qhd,khd->hqk", grad_heads, value_heads, preferred_element_type=jnp.float32
    )
    row_delta = jnp.sum(attn_probs * grad_probs, axis=-1, keepdims=True)
    grad_scores = (attn_probs * (grad_probs - row_delta)).astype(jnp.bfloat16)
    grad_query = (
        jnp.einsum("hqk,khd->qhd", grad_scores, key_heads, preferred_element_type=jnp.float32)
        * scale_factor
    )
    grad_key = (
        jnp.einsum("hqk,qhd->khd", grad_scores, query_heads, preferred_element_type=jnp.float32)
        * scale_factor
    )
    grad_value = jnp.einsum(
        "hqk,qhd->khd",
        attn_probs.astype(jnp.bfloat16),
        grad_heads,
        preferred_element_type=jnp.float32,
    )
    return (
        grad_query,
        grad_key.reshape(key_flat.shape[0], -1),
        grad_value.reshape(value_flat.shape[0], -1),
    )


def finish(inputs, attended, weights):
    middle = inputs + (
        jnp.dot(attended, weights[4], preferred_element_type=jnp.float32)
        + weights[5].astype(jnp.float32)
    )
    second = layer_norm(
        middle, weights[6].astype(jnp.float32), weights[7].astype(jnp.float32)
    ).astype(jnp.bfloat16)
    hidden = jnp.dot(second, weights[8], preferred_element_type=jnp.float32) + weights[9].astype(
        jnp.float32
    )
    activated = gelu_erf(hidden).astype(jnp.bfloat16)
    result = middle + (
        jnp.dot(activated, weights[10], preferred_element_type=jnp.float32)
        + weights[11].astype(jnp.float32)
    )
    return (result, middle, second, hidden, activated)


def gathered_device(
    tokens,
    lengths,
    visibility_mask,
    visible_counts,
    ln1_gain,
    ln1_bias,
    qkv_weight,
    qkv_bias,
    out_weight,
    out_bias,
    ln2_gain,
    ln2_bias,
    fc1_weight,
    fc1_bias,
    fc2_weight,
    fc2_bias,
    context_cot,
):
    tok_rows = tokens.shape[0]
    model_width = tokens.shape[1]
    groups = lax.axis_size("fsdp")
    member = lax.axis_index("fsdp")
    pack_len = tok_rows * groups
    vis_rows = VIS_DEV
    vis_pack = vis_rows * groups
    zero_low = jnp.zeros((), jnp.bfloat16)
    shards = [
        weight.astype(jnp.bfloat16)
        for weight in (
            ln1_gain,
            ln1_bias,
            qkv_weight,
            qkv_bias,
            out_weight,
            out_bias,
            ln2_gain,
            ln2_bias,
            fc1_weight,
            fc1_bias,
            fc2_weight,
            fc2_bias,
        )
    ]
    weights = (
        lax.all_gather(shards[0], ("dp", "fsdp"), axis=0, tiled=True),
        lax.all_gather(shards[1], ("dp", "fsdp"), axis=0, tiled=True),
        lax.all_gather(shards[2], ("dp", "fsdp"), axis=0, tiled=True),
        lax.all_gather(shards[3], ("dp", "fsdp"), axis=0, tiled=True),
        lax.all_gather(shards[4], ("dp", "fsdp"), axis=0, tiled=True),
        lax.all_gather(shards[5], ("dp", "fsdp"), axis=0, tiled=True),
        lax.all_gather(shards[6], ("dp", "fsdp"), axis=0, tiled=True),
        lax.all_gather(shards[7], ("dp", "fsdp"), axis=0, tiled=True),
        lax.all_gather(shards[8], ("dp", "fsdp"), axis=0, tiled=True),
        lax.all_gather(shards[9], ("dp", "fsdp"), axis=0, tiled=True),
        lax.all_gather(shards[10], ("dp", "fsdp"), axis=0, tiled=True),
        lax.all_gather(shards[11], ("dp", "fsdp"), axis=0, tiled=True),
    )
    segment, places = pack_layout(lengths[0], pack_len)
    home_rows = member * tok_rows + jnp.arange(tok_rows, dtype=jnp.int32)
    seg_home = jnp.take(segment, home_rows)
    cos_home, sin_home = rope_tables(jnp.take(places, home_rows))
    inputs, normed, query_heads, key_flat, value_flat = project(tokens, weights, cos_home, sin_home)
    key_pack, value_pack = (
        lax.all_gather(key_flat, "fsdp", axis=0, tiled=True),
        lax.all_gather(value_flat, "fsdp", axis=0, tiled=True),
    )
    attended = attend(query_heads, key_pack, value_pack, seg_home, segment)[0]
    target_out = finish(inputs, attended, weights)[0].astype(jnp.bfloat16)
    running = jnp.cumsum(visibility_mask)
    visible_here = visibility_mask * (running <= visible_counts[0, 0]).astype(jnp.int32)
    visible_all = lax.all_gather(visible_here, "fsdp", axis=0, tiled=True)
    inclusive = jnp.cumsum(visible_all)
    rank_index = jnp.arange(vis_pack, dtype=jnp.int32)
    row_of = jnp.sum((inclusive[None, :] <= rank_index[:, None]).astype(jnp.int32), axis=1)
    owner_dev = row_of // tok_rows
    local_row = row_of % tok_rows
    mine_here = (owner_dev == member)[:, None]
    send_tokens = jnp.where(mine_here, jnp.take(tokens, local_row, axis=0), zero_low)
    send_cot = jnp.where(mine_here, jnp.take(context_cot, local_row, axis=0), zero_low)
    recv_tokens, recv_cot = (
        lax.all_to_all(send_tokens, "fsdp", split_axis=0, concat_axis=0, tiled=True),
        lax.all_to_all(send_cot, "fsdp", split_axis=0, concat_axis=0, tiled=True),
    )
    slot_index = jnp.arange(vis_rows, dtype=jnp.int32)
    my_ranks = member * vis_rows + slot_index
    my_owner = jnp.take(owner_dev, my_ranks)
    my_row = jnp.take(row_of, my_ranks)
    picked = my_owner * vis_rows + slot_index
    bal_tokens = jnp.take(recv_tokens, picked, axis=0)
    bal_cot = jnp.take(recv_cot, picked, axis=0)
    seg_bal = jnp.take(segment, my_row)
    seg_keys = jnp.take(segment, row_of)
    cos_bal, sin_bal = rope_tables(jnp.take(places, my_row))
    inputs_bal, normed_bal, query_bal, key_bal, value_bal = project(
        bal_tokens, weights, cos_bal, sin_bal
    )
    key_vis, value_vis = (
        lax.all_gather(key_bal, "fsdp", axis=0, tiled=True),
        lax.all_gather(value_bal, "fsdp", axis=0, tiled=True),
    )
    attended_bal, log_total = attend(query_bal, key_vis, value_vis, seg_bal, seg_keys)
    result_bal, middle_bal, second_bal, hidden_bal, activated_bal = finish(
        inputs_bal, attended_bal, weights
    )
    grad_result = bal_cot.astype(jnp.float32)
    result_low = grad_result.astype(jnp.bfloat16)
    grad_fc2 = jnp.einsum(
        "nf,nd->fd", activated_bal, result_low, preferred_element_type=jnp.float32
    )
    grad_bfc2 = jnp.sum(result_low.astype(jnp.float32), axis=0)
    grad_activated = jnp.einsum(
        "nd,fd->nf", result_low, weights[10], preferred_element_type=jnp.float32
    )
    gelu_pull = jax.vjp(gelu_erf, hidden_bal)[1]
    hidden_low = gelu_pull(grad_activated)[0].astype(jnp.bfloat16)
    grad_fc1 = jnp.einsum("nd,nf->df", second_bal, hidden_low, preferred_element_type=jnp.float32)
    grad_bfc1 = jnp.sum(hidden_low.astype(jnp.float32), axis=0)
    grad_second = jnp.einsum(
        "nf,df->nd", hidden_low, weights[8], preferred_element_type=jnp.float32
    )
    norm_two_pull = jax.vjp(
        layer_norm, middle_bal, weights[6].astype(jnp.float32), weights[7].astype(jnp.float32)
    )[1]
    grad_mid_norm, grad_gain_two, grad_shift_two = norm_two_pull(grad_second)
    grad_middle = grad_result + grad_mid_norm
    middle_low = grad_middle.astype(jnp.bfloat16)
    grad_wout = jnp.einsum(
        "nd,ne->de", attended_bal, middle_low, preferred_element_type=jnp.float32
    )
    grad_bout = jnp.sum(middle_low.astype(jnp.float32), axis=0)
    grad_att = jnp.einsum(
        "ne,de->nd", middle_low, weights[4], preferred_element_type=jnp.float32
    ).astype(jnp.bfloat16)
    grad_query, grad_key_all, grad_value_all = attend_back(
        query_bal, key_vis, value_vis, seg_bal, seg_keys, log_total, grad_att
    )
    grad_key_own, grad_value_own = (
        lax.psum_scatter(
            grad_key_all.astype(jnp.bfloat16), "fsdp", scatter_dimension=0, tiled=True
        ).astype(jnp.float32),
        lax.psum_scatter(
            grad_value_all.astype(jnp.bfloat16), "fsdp", scatter_dimension=0, tiled=True
        ).astype(jnp.float32),
    )
    grad_query_pre = rotate_back(grad_query, cos_bal, sin_bal).reshape(vis_rows, model_width)
    grad_key_pre = rotate_back(
        grad_key_own.reshape(vis_rows, HEADS, HDIM), cos_bal, sin_bal
    ).reshape(vis_rows, model_width)
    joined_low = jnp.concatenate([grad_query_pre, grad_key_pre, grad_value_own], axis=1).astype(
        jnp.bfloat16
    )
    grad_wqkv = jnp.einsum("nd,ne->de", normed_bal, joined_low, preferred_element_type=jnp.float32)
    grad_bqkv = jnp.sum(joined_low.astype(jnp.float32), axis=0)
    grad_normed = jnp.einsum(
        "ne,de->nd", joined_low, weights[2], preferred_element_type=jnp.float32
    )
    norm_one_pull = jax.vjp(
        layer_norm, inputs_bal, weights[0].astype(jnp.float32), weights[1].astype(jnp.float32)
    )[1]
    grad_in_norm, grad_gain_one, grad_shift_one = norm_one_pull(grad_normed)
    grad_inputs = grad_middle + grad_in_norm
    destinations = jnp.arange(groups, dtype=jnp.int32)
    route_mask = (my_owner[None, :] == destinations[:, None])[:, :, None]
    send_out = jnp.where(route_mask, result_bal.astype(jnp.bfloat16)[None], zero_low).reshape(
        vis_pack, model_width
    )
    send_grad = jnp.where(route_mask, grad_inputs.astype(jnp.bfloat16)[None], zero_low).reshape(
        vis_pack, model_width
    )
    back_out, back_grad = (
        lax.all_to_all(send_out, "fsdp", split_axis=0, concat_axis=0, tiled=True),
        lax.all_to_all(send_grad, "fsdp", split_axis=0, concat_axis=0, tiled=True),
    )
    rank_home = jnp.maximum(jnp.take(inclusive, home_rows) - 1, 0)
    is_visible = (visible_here > 0)[:, None]
    context_out = jnp.where(is_visible, jnp.take(back_out, rank_home, axis=0), zero_low)
    tokens_grad = jnp.where(is_visible, jnp.take(back_grad, rank_home, axis=0), zero_low)
    grad_list = [
        grad_gain_one,
        grad_shift_one,
        grad_wqkv,
        grad_bqkv,
        grad_wout,
        grad_bout,
        grad_gain_two,
        grad_shift_two,
        grad_fc1,
        grad_bfc1,
        grad_fc2,
        grad_bfc2,
    ]
    reduced = (
        lax.psum_scatter(grad_list[0], ("dp", "fsdp"), scatter_dimension=0, tiled=True),
        lax.psum_scatter(grad_list[1], ("dp", "fsdp"), scatter_dimension=0, tiled=True),
        lax.psum_scatter(grad_list[2], ("dp", "fsdp"), scatter_dimension=0, tiled=True),
        lax.psum_scatter(grad_list[3], ("dp", "fsdp"), scatter_dimension=0, tiled=True),
        lax.psum_scatter(grad_list[4], ("dp", "fsdp"), scatter_dimension=0, tiled=True),
        lax.psum_scatter(grad_list[5], ("dp", "fsdp"), scatter_dimension=0, tiled=True),
        lax.psum_scatter(grad_list[6], ("dp", "fsdp"), scatter_dimension=0, tiled=True),
        lax.psum_scatter(grad_list[7], ("dp", "fsdp"), scatter_dimension=0, tiled=True),
        lax.psum_scatter(grad_list[8], ("dp", "fsdp"), scatter_dimension=0, tiled=True),
        lax.psum_scatter(grad_list[9], ("dp", "fsdp"), scatter_dimension=0, tiled=True),
        lax.psum_scatter(grad_list[10], ("dp", "fsdp"), scatter_dimension=0, tiled=True),
        lax.psum_scatter(grad_list[11], ("dp", "fsdp"), scatter_dimension=0, tiled=True),
    )
    return (
        target_out,
        context_out,
        tokens_grad,
        reduced[0],
        reduced[1],
        reduced[2],
        reduced[3],
        reduced[4],
        reduced[5],
        reduced[6],
        reduced[7],
        reduced[8],
        reduced[9],
        reduced[10],
        reduced[11],
    )


def per_device(tokens, *rest):
    n, group = lax.axis_size("dp"), lax.axis_size("fsdp")
    out_rows = rest[7].shape[0]
    fits = group == 4 and n == 8 and out_rows * group == 128
    return (on_device if fits else gathered_device)(tokens, *rest)


def solution(mesh):
    both = ("dp", "fsdp")
    vec, mat = P(both), P(both, None)
    return jax.shard_map(
        per_device,
        mesh=mesh,
        in_specs=(
            mat, P("dp", None), vec, P("dp", "fsdp"), vec, vec, mat, vec, mat, vec, vec, vec,
            mat, vec, mat, vec, mat,
        ),
        out_specs=(mat, mat, mat, vec, vec, mat, vec, mat, vec, vec, vec, mat, vec, mat, vec),
        check_vma=False,
    )
```

```python
import functools
import math
import types

import jax
import jax.numpy as jnp
import numpy as np
from jax import lax
from jax.experimental import pallas as pl
from jax.experimental.pallas import tpu as pltpu
from jax.sharding import PartitionSpec as P

HEADS = 16
HDIM = 64
GRID = 14
VIS_DEV = 64
norm_eps = 1e-06
masked_fill = -1e30
FRAMES = 8
EPS = 1e-06
FILL = -1e30
BF = jnp.bfloat16
F32 = jnp.float32
MESH = pl.DeviceIdType.MESH
NT = (((1,), (1,)), ((), ()))
NN = (((1,), (0,)), ((), ()))
TN = (((0,), (0,)), ((), ()))


def dot(a, b, dims=NN):
    return lax.dot_general(a, b, dims, preferred_element_type=F32)


def trig_table():
    width = FRAMES + 2 * GRID
    lane = np.arange(2 * HDIM)
    pair = lane % (HDIM // 2)
    axis = np.minimum(pair // 11, 2)
    freq = np.exp(((pair - 11 * axis).astype(np.float32)) * np.float32(-math.log(10000.0) / 11.0))
    sign = np.where(lane % HDIM < HDIM // 2, -1.0, 1.0)
    table = np.zeros((128, 4 * HDIM), np.float32)
    row = np.arange(width)
    kind = np.where(row < FRAMES, 0, np.where(row < FRAMES + GRID, 1, 2))
    coord = np.where(kind == 0, row, np.where(kind == 1, row - FRAMES, row - FRAMES - GRID))
    angle = (coord[:, None].astype(np.float32) * freq[None, :].astype(np.float32)).astype(np.float64)
    here = kind[:, None] == axis[None, :]
    table[:width, : 2 * HDIM] = np.where(here, np.cos(angle), 0.0)
    table[:width, 2 * HDIM :] = np.where(here, np.sin(angle) * sign[None, :], 0.0)
    parts = []
    rest = table
    for _ in range(3):
        part = rest.astype(jnp.bfloat16)
        parts.append(part)
        rest = rest - part.astype(np.float32)
    return np.stack(parts)


def norm_stats(v):
    center = v - jnp.mean(v, axis=-1, keepdims=True)
    inv = lax.rsqrt(jnp.mean(center * center, axis=-1, keepdims=True) + EPS)
    return center * inv, inv


def norm_back(v, gain, grad):
    xhat, inv = norm_stats(v)
    gg = grad * gain
    dv = inv * (
        gg - jnp.mean(gg, axis=-1, keepdims=True) - xhat * jnp.mean(gg * xhat, axis=-1, keepdims=True)
    )
    return (
        dv,
        jnp.sum(grad * xhat, axis=0, keepdims=True),
        jnp.sum(grad, axis=0, keepdims=True),
    )


def swap_halves(u):
    lane = lax.broadcasted_iota(jnp.int32, u.shape, 1)
    return jnp.where(
        lax.rem(lane, HDIM) < HDIM // 2,
        pltpu.roll(u, u.shape[1] - HDIM // 2, 1),
        pltpu.roll(u, HDIM // 2, 1),
    )


def column_segment(start, rows, ends):
    row = start + lax.broadcasted_iota(jnp.int32, (rows, 1), 0)
    seg = jnp.zeros((rows, 1), jnp.int32)
    for end in ends:
        seg += (row >= end).astype(jnp.int32)
    return row, seg


ALIASES = dict(N2="N1", PT="N1", D2="w2_v", DOo="wo_v", X1B="GP")


class Sems:
    def __init__(self, send, recv):
        self.send, self.recv = send, recv
        self.sends = self.recvs = self.clock = 0
        self.idle_sends, self.idle_recvs, self.waited = [], [], []

    def take_send(self):
        if self.idle_sends:
            return self.idle_sends.pop()
        self.sends += 1
        return self.send.at[self.sends - 1]

    def give_send(self, sem):
        self.idle_sends.append(sem)

    def take_recv(self):
        self.recvs += 1
        return self.recv.at[self.recvs - 1]

    def ring_sent(self):
        rs = self.idle_recvs.pop() if self.idle_recvs else self.take_recv()
        self.clock += 1
        return rs, self.clock

    def ring_landed(self, sem, sent):
        self.idle_recvs += [old for at, old in self.waited if at < sent]
        self.waited = [(at, old) for at, old in self.waited if at >= sent]
        self.waited.append((self.clock, sem))


def layer_kernel(dims, names, *refs):
    n, D, FF, T, V = dims
    NF = 4
    R = D // (n * NF)
    RP = R * NF
    HC = FF // (NF * n)
    HF = FF // NF
    C = D // NF
    VP = V * NF
    S_ = T * NF
    last = n // 2 - 1
    given = dict(zip(names, refs))
    g = types.SimpleNamespace(**given, **{a: given[b] for a, b in ALIASES.items()})
    sems = Sems(g.send_sems, g.recv_sems)
    lsem = g.local_sems

    p = lax.axis_index("dp")
    f = lax.axis_index("fsdp")
    f1 = f + 1 - 2 * lax.rem(f, 2)
    f2 = lax.rem(f + 2, NF)
    f3 = NF - 1 - f
    par = lax.rem(p, 2)
    half_p = lax.div(p, 2)
    pos = (1 - par) * half_p + par * (n - 1 - half_p)

    def idx(q):
        q = lax.rem(q + 2 * n, n)
        up = lax.div(q, n // 2)
        return (1 - up) * (2 * q) + up * (2 * (n - 1 - q) + 1)

    right, left = idx(pos + 1), idx(pos - 1)

    def launch(src, dst, ss, rs, to):
        c = pltpu.make_async_remote_copy(
            src_ref=src, dst_ref=dst, send_sem=ss, recv_sem=rs, device_id=to, device_id_type=MESH
        )
        c.start()
        return c

    def sent(copies):
        for c in copies:
            c.wait_send()
            sems.give_send(c.src_sem)

    def received(copies):
        for c in copies:
            c.wait_recv()
        sent(copies)

    def remote(src, dst, to):
        ss, rs = sems.take_send(), sems.take_recv()
        return launch(src, dst, ss, rs, to), ss, rs

    def arrival(dst, ss, rs, to):
        return pltpu.make_async_remote_copy(
            src_ref=dst, dst_ref=dst, send_sem=ss, recv_sem=rs, device_id=to, device_id_type=MESH
        )

    to1, to2, to3 = {"fsdp": f1}, {"fsdp": f2}, {"fsdp": f3}
    peers = ((f1, to1), (f2, to2), (f3, to3))

    barrier = pltpu.get_barrier_semaphore()
    for to in (to1, to2, to3, {"dp": right}, {"dp": left}):
        pl.semaphore_signal(barrier, inc=1, device_id=to, device_id_type=MESH)

    loads = {}
    for i, (src, dst) in enumerate(
        (
            (g.wqkv, g.wqkv_v),
            (g.w1, g.w1_v),
            (g.wo, g.wo_v),
            (g.mask, g.mask_v),
            (g.tok, g.TA.at[f]),
            (g.w2, g.w2_v),
            (g.cot, g.CA.at[f]),
            (g.trig, g.trig_v),
        )
    ):
        c = pltpu.make_async_copy(src, dst, lsem.at[i])
        c.start()
        loads[i] = c
    vectors = []
    for k in range(8):
        vectors.append(pltpu.make_async_copy(given["in%d" % k], given["v%d" % k], lsem.at[8 + k]))
        vectors[k].start()

    AS, AQ, WO, A1, A2 = g.AS, g.AQ, g.WO, g.A1, g.A2
    TA, CA = g.TA, g.CA

    loads[5].wait()
    A2[p] = g.w2_v[...].astype(BF)
    loads[0].wait()
    for j in range(NF):
        for t in range(3):
            g.sq[j, :, C * t : C * t + C] = g.wqkv_v[:, D * t + C * j : D * t + C * j + C].astype(BF)
    AQ[p, pl.ds(pl.multiple_of(R * f, R), R), :] = g.sq[f]
    loads[2].wait()
    WO[p, f] = g.wo_v[...].astype(BF)
    pl.semaphore_wait(barrier, 5)

    def scatter(src, dst, three):
        ss, rs = sems.take_send(), sems.take_recv()
        for fj, to in peers:
            launch(src(fj), dst(f), ss, rs, to)
        return (arrival(three, ss, rs, to1),)

    class AllGather4:
        def __init__(self, slot):
            self.slot = slot
            self.done = False
            c, ss, rs = remote(slot(f), slot(f), to2)
            d, sd, rd = remote(slot(f), slot(f), to1)
            self.across = arrival(slot(f2), ss, rs, to2)
            self.beside = arrival(slot(f1), sd, rd, to1)
            self.copies = [c, d]

        def forward(self):
            self.across.wait_recv()
            c, ss, rs = remote(self.slot(f2), self.slot(f2), to1)
            self.passed = arrival(self.slot(f3), ss, rs, to1)
            self.copies.append(c)

        def finish(self):
            if not self.done:
                self.done = True
                self.beside.wait_recv()
                self.passed.wait_recv()
                sent(self.copies)

    class ReduceScatter4:
        def __init__(self, part, r1, xs, r2):
            self.part, self.r1, self.xs, self.r2 = part, r1, xs, r2
            c, ss, rs = remote(part.at[f3], r1.at[1], to1)
            d, sd, rd = remote(part.at[f1], r1.at[0], to1)
            self.other = arrival(r1.at[1], ss, rs, to1)
            self.own = arrival(r1.at[0], sd, rd, to1)
            self.copies = [c, d]

        def forward(self):
            self.other.wait_recv()
            self.xs[...] = (self.part[f2].astype(F32) + self.r1[1].astype(F32)).astype(BF)
            c, ss, rs = remote(self.xs, self.r2, to2)
            self.across = arrival(self.r2, ss, rs, to2)
            self.copies.append(c)

        def finish(self):
            self.own.wait_recv()
            self.across.wait_recv()
            sent(self.copies)

        def total(self):
            return self.part[f].astype(F32) + self.r1[0].astype(F32) + self.r2[...].astype(F32)

    class RingGather:
        def __init__(self, view, pair, rows):
            self.view, self.pair, self.rows = view, pair, rows
            self.before, self.flight = (), None

        def landed(self):
            received(self.before)
            self.before = ()
            if self.flight is not None:
                received([self.flight])
                sems.ring_landed(self.flight.dst_sem, self.at)
                self.flight = None

        def step(self, r):
            self.landed()
            h = self.rows // 2
            spans = ((0, self.rows), (0, self.rows)) if r < last else ((0, h), (h, h))
            ss = sems.take_send()
            rs, self.at = sems.ring_sent()
            for way, (s, c) in zip((1, -1), spans):
                piece = self.view(idx(pos - way * r), s, c)
                launch(piece, piece, ss, rs, {"dp": right if way == 1 else left})
            both = self.pair if r < last else self.view(0, 0, self.rows)
            self.flight = arrival(both, ss, rs, {"dp": left})

        def finish(self):
            self.landed()

    def row_rings(ref):
        h = ref.shape[1] // 2

        def ring(offset):
            view = lambda slot, s, c: ref.at[slot, pl.ds(offset + s, c), :]
            return RingGather(view, ref.at[pl.ds(0, 2), pl.ds(offset, h), :], h)

        return [ring(0), ring(h)]

    q_ring, w1_ring, w2_ring = row_rings(AQ), row_rings(A1), row_rings(A2)
    o_ring = RingGather(lambda slot, s, c: WO.at[slot, f, pl.ds(s, c), :], WO.at[pl.ds(0, 2), f], R)
    s_ring = RingGather(lambda slot, s, c: AS.at[slot, pl.ds(s, c)], AS.at[pl.ds(0, 2)], NF)

    class RingReduce:
        def __init__(self, grads, start, rows, st, rr, rl, wire=BF):
            self.G, self.o, self.rows, self.st, self.rr, self.rl = grads, start, rows, st, rr, rl
            self.wire = wire
            self.flight = None

        def landed(self):
            if self.flight is not None:
                received([self.flight])
                sems.ring_landed(self.flight.dst_sem, self.at)
                self.flight = None

        def step(self, r):
            self.landed()
            o, rows = self.o, self.rows
            hh = rows // 2
            whole = pl.ds(o, rows)
            ss = sems.take_send()
            rs, self.at = sems.ring_sent()
            ways = ((1, self.rr, 0, {"dp": right}), (-1, self.rl, hh, {"dp": left}))
            if r == 0:
                far = idx(pos + n // 2)
                self.st[whole, :] = self.G[far, whole, :].astype(self.wire)
                for _, buf, s, to in ways:
                    half = pl.ds(o + s, hh)
                    launch(self.st.at[half, :], buf.at[0, half, :], ss, rs, to)
                self.flight = arrival(self.st.at[whole, :], ss, rs, {"dp": left})
                return
            for way, buf, s, to in ways:
                c = idx(pos + way * (n // 2 - r))
                if r == 1:
                    half, other = pl.ds(o + s, hh), pl.ds(o + hh - s, hh)
                    total = buf[0, half, :].astype(F32) + self.G[c, half, :]
                    buf[0, half, :] = total.astype(self.wire)
                    buf[0, other, :] = self.G[c, other, :].astype(self.wire)
                else:
                    total = buf[r - 1, whole, :].astype(F32) + self.G[c, whole, :]
                    buf[r - 1, whole, :] = total.astype(self.wire)
                launch(buf.at[r - 1, whole, :], buf.at[r, whole, :], ss, rs, to)
            self.flight = arrival(self.rr.at[pl.ds(0, 2), whole, :], ss, rs, {"dp": left})

        def finish(self):
            self.landed()

        def total(self):
            o, rows = self.o, self.rows
            return (
                self.G[p, pl.ds(o, rows), :]
                + self.rr[last, pl.ds(o, rows), :].astype(F32)
                + self.rl[last, pl.ds(o, rows), :].astype(F32)
            )

    st = types.SimpleNamespace(oa=[None, None])
    N1, N2, GT, PT = g.N1, g.N2, g.GT, g.PT
    VEC, BQ, BG, VG = g.VEC, g.BQ, g.BG, g.VG
    Q, K, W, QV, KV, WV = g.Q, g.K, g.W, g.QV, g.KV, g.WV
    SM, OV, PV, OA, OT = g.SM, g.OV, g.PV, g.OA, g.OT
    XV, N1V, DY, X1V, N2V = g.XV, g.N1V, g.DY, g.X1V, g.N2V
    GV, GP, DH, PN, PF = g.GV, g.GP, g.DH, g.PN, g.PF
    G2, G1, GQ, GO = g.G2, g.G1, g.GQ, g.GO
    DO, DPRE = g.DO, g.DPRE
    E1, F1, EQ, FQ, SG = g.E1, g.F1, g.EQ, g.FQ, g.SG
    blocks = [slice(256 * k, 256 * k + 256) for k in range(D // 256)]
    mine = pl.ds(pl.multiple_of(V * f, V), V)
    hc, hr = HC // 2, RP // 2
    g2_ring = [
        RingReduce(G2, 0, hc, g.st2, g.rr2, g.rl2),
        RingReduce(G2, hc, hc, g.st2, g.rr2, g.rl2),
    ]
    g1_ring = [
        RingReduce(G1, 0, hr, g.st1, g.rr1, g.rl1),
        RingReduce(G1, hr, hr, g.st1, g.rr1, g.rl1),
    ]
    gq_ring = [
        RingReduce(GQ, 0, hr, g.stq, g.rrq, g.rlq),
        RingReduce(GQ, hr, hr, g.stq, g.rrq, g.rlq),
    ]
    go_ring = RingReduce(GO, 0, R, g.sto, g.rro, g.rlo)
    gs_ring = RingReduce(VG, 0, 16, g.sts, g.rrs, g.rls, F32)

    def finish(*rings):
        for r in rings:
            r.finish()

    outs = []

    def store(src, dst, k):
        c = pltpu.make_async_copy(src, dst, lsem.at[8 + k])
        c.start()
        outs.append(c)

    def vec(k):
        return VEC[k : k + 1, :]

    def start():
        part = lambda j: AQ.at[p, pl.ds(pl.multiple_of(R * j, R), R), :]
        q_ring[0].before = scatter(lambda j: g.sq.at[j], part, AQ.at[0, pl.ds(0, 3 * R), :])

    def small_start():
        for c in vectors:
            c.wait()
        loads[3].wait()
        SV = g.small_v
        SV[...] = jnp.zeros(SV.shape, F32)
        for k in range(8):
            row, at = ((0, R * k), (1, R * (k - 4)), (2, 0), (3, 0))[0 if k < 4 else 1 if k < 6 else k - 4]
            value = given["v%d" % k][...]
            width = value.shape[1]
            wide = value if width == 128 else jnp.concatenate([value, jnp.zeros((1, 128 - width), F32)], axis=1)
            SV[row : row + 1, :] += wide if at == 0 else pltpu.roll(wide, at, 1)
        mask = g.mask_v[...].astype(F32)
        below = lax.broadcasted_iota(jnp.int32, (128, 128), 0) <= lax.broadcasted_iota(jnp.int32, (128, 128), 1)
        tri = jnp.where(below, 1.0, 0.0).astype(BF)
        count = g.counts[0, 0].astype(F32)
        before = jnp.zeros((1, 1), F32)
        for k in range(2):
            ones = mask[:, 128 * k : 128 * k + 128]
            running = dot(jnp.broadcast_to(ones, (8, 128)).astype(BF), tri)[0:1, :] + before
            SV[4 + k : 5 + k, :] = jnp.where(running <= count, ones, 0.0)
            before = before + jnp.sum(ones, axis=1, keepdims=True)
        AS[p, f] = SV[...]
        st.s = scatter(lambda j: AS.at[p, f], lambda j: AS.at[p, j], AS.at[0, pl.ds(0, 3)])
        s_ring.before = st.s

    def cast_fc1():
        loads[1].wait()
        for j in range(NF):
            for t in range(n):
                at = HC * (NF * t + j)
                g.s1[j, :, HC * t : HC * t + HC] = g.w1_v[:, at : at + HC].astype(BF)
        A1[p, pl.ds(pl.multiple_of(R * f, R), R), :] = g.s1[f]
        part = lambda j: A1.at[p, pl.ds(pl.multiple_of(R * j, R), R), :]
        w1_ring[0].before = scatter(lambda j: g.s1.at[j], part, A1.at[0, pl.ds(0, 3 * R), :])

    def tokens_start():
        loads[4].wait()
        st.tok = AllGather4(lambda j: TA.at[j])

    def cot_start():
        loads[6].wait()
        st.cot = AllGather4(lambda j: CA.at[j])

    def wo_start():
        o_ring.finish()
        st.wo = AllGather4(lambda j: WO.at[:, j])

    ends = []
    total_len = jnp.int32(0)
    for k in range(g.lengths.shape[1]):
        total_len = total_len + g.lengths[0, k]
        ends.append(total_len)

    def key_segments():
        keyrow = lax.broadcasted_iota(jnp.int32, (1, S_), 1)
        segrow = jnp.zeros((1, S_), jnp.int32)
        for end in ends:
            segrow += (keyrow >= end).astype(jnp.int32)
        return segrow

    def layout():
        row, _seg = column_segment(0, S_, ends)
        before = jnp.zeros((S_, 1), jnp.int32)
        for k, end in enumerate(ends):
            before += jnp.where(row >= end, g.lengths[0, k], 0)
        place = row - before
        img = GRID * GRID
        frame = jnp.zeros((S_, 1), jnp.int32)
        for t in range(1, FRAMES):
            frame += (place >= img * t).astype(jnp.int32)
        rest = place - img * frame
        grow = jnp.zeros((S_, 1), jnp.int32)
        for t in range(1, GRID):
            grow += (rest >= GRID * t).astype(jnp.int32)
        gcol = rest - GRID * grow
        lane = lax.broadcasted_iota(jnp.int32, (S_, 128), 1)
        hot = (lane == frame) | (lane == grow + FRAMES) | (lane == gcol + (FRAMES + GRID))
        g.OH[...] = jnp.where(hot, 1.0, 0.0).astype(BF)
        loads[7].wait()
        g.CS[...] = sum(dot(g.OH[...], g.trig_v[k]) for k in range(3))

    def visible():
        if s_ring.before:
            received(s_ring.before)
            s_ring.before = ()
        vis8 = jnp.concatenate([AS[p, j][4:6, :] for j in range(NF)], axis=0)
        above = lax.broadcasted_iota(jnp.int32, (128, 128), 0)
        tri = above <= lax.broadcasted_iota(jnp.int32, (128, 128), 1)
        within = dot(vis8.astype(BF), jnp.where(tri, 1.0, 0.0).astype(BF))
        base = jnp.zeros((1, 128), F32)
        pieces, vpieces = [], []
        for k in range(8):
            pieces.append(within[k : k + 1, :] + base)
            vpieces.append(vis8[k : k + 1, :])
            base = base + jnp.sum(vis8[k : k + 1, :], axis=1, keepdims=True)
        incl = jnp.concatenate(pieces, axis=1)
        visrow = jnp.concatenate(vpieces, axis=1)
        rank = jnp.where(visrow > 0.5, incl - 1.0, -1.0).astype(jnp.int32)
        sel = lax.broadcasted_iota(jnp.int32, (VP, S_), 0) == rank
        SM[...] = jnp.where(sel, 1.0, 0.0).astype(BF)

    def rounded(v):
        return v.astype(BF).astype(F32)

    def turn(v, by):
        by = by % 128
        return v if by == 0 else pltpu.roll(v, by, 1)

    def small_vectors():
        s_ring.finish()
        lane128 = lax.broadcasted_iota(jnp.int32, (n, 128), 1)
        rows0 = [AS[:, j, 0, :] for j in range(NF)]
        rows1 = [AS[:, j, 1, :] for j in range(NF)]
        rows2 = [AS[:, j, 2, :] for j in range(NF)]
        for k in range(6):
            src = rows0 if k < 4 else rows1
            piece = jnp.zeros((n, 128), F32)
            for j in range(NF):
                piece = jnp.where(lax.div(lane128, R) == j, turn(src[j], R * (j - k % 4)), piece)
            for q in range(n):
                VEC[k : k + 1, 128 * q : 128 * q + 128] = rounded(piece[q : q + 1, :])
        for q in range(n):
            VEC[6:7, 128 * q : 128 * q + 128] = rounded(AS[q, f][3:4, :])
        t0 = jnp.where(lane128 < 96, rows2[0], turn(rows2[1], 96))
        t1 = jnp.where(lane128 < 64, turn(rows2[1], -32), turn(rows2[2], 64))
        t2 = jnp.where(lane128 < 32, turn(rows2[2], -64), turn(rows2[3], 32))
        for q in range(n):
            for k, t in enumerate((t0, t1, t2)):
                BQ[0:1, 384 * q + 128 * k : 384 * q + 128 * k + 128] = rounded(t[q : q + 1, :])

    def first_norm():
        st.tok.finish()

        def block(b, _):
            xhat, _inv = norm_stats(TA[b].astype(F32))
            N1[b] = (xhat * vec(0) + vec(1)).astype(BF)
            return 0

        lax.fori_loop(0, NF, block, 0)

    def project_half(part):
        finish(*q_ring)

        def block(b, _):
            rows = pl.ds(pl.multiple_of(b * T, T), T)
            cs = g.CS[rows, :]
            for t, dst in enumerate((Q, K, W)):
                out = dot(N1[b], AQ[:, :, C * t : C * t + C].reshape(D, C))
                out = out + BQ[0:1, pl.ds(pl.multiple_of(D * t + C * f, 128), C)]
                if t == 2:
                    dst[rows, :] = out.astype(BF)
                    continue
                for hh in range(C // 128):
                    u = out[:, 128 * hh : 128 * hh + 128]
                    u = (u * cs[:, :128] + swap_halves(u) * cs[:, 128:]).astype(BF)
                    dst[rows, 128 * hh : 128 * hh + 128] = u * BF(0.125) if t == 0 else u
            return 0

        lax.fori_loop(NF // 2 * part, NF // 2 * (part + 1), block, 0)

    lane_c = lax.broadcasted_iota(jnp.int32, (1, C), 1)
    hmask = [jnp.where(lax.div(lane_c, HDIM) == hd, 1.0, 0.0) for hd in range(C // HDIM)]

    def softmax(s):
        e = jnp.exp(s - jnp.max(s, axis=-1, keepdims=True))
        return e * (1.0 / jnp.sum(e, axis=-1, keepdims=True))

    def context_attention():
        for src, dst in ((Q, QV), (K, KV), (W, WV)):
            dst[...] = dot(SM[...], src[...]).astype(BF)
        segrow = key_segments()
        seg8 = jnp.broadcast_to(segrow.astype(F32), (8, S_)).astype(BF)
        segv_row = dot(seg8, SM[...], NT)[0:1, :].astype(jnp.int32)
        segv_col = jnp.sum(SM[...].astype(F32) * segrow.astype(F32), axis=1, keepdims=True).astype(jnp.int32)
        same = segv_col == segv_row
        acc = jnp.zeros((VP, C), F32)
        for hd in range(C // HDIM):
            s = dot(QV[...] * hmask[hd].astype(BF), KV[...], NT)
            pr = softmax(jnp.where(same, s, FILL))
            PV[hd] = pr
            acc += dot(pr.astype(BF), WV[...]) * hmask[hd]
        OV[f] = acc.astype(BF)
        st.ov = AllGather4(lambda j: OV.at[j])

    def attend_target(b, pair):
        rows = slice(T * b, T * b + T)
        _, segq = column_segment(b * T, T, ends)
        same = segq == key_segments()
        for hd in (2 * pair, 2 * pair + 1):
            s = dot(Q[rows, :] * hmask[hd].astype(BF), K[...], NT)
            pr = softmax(jnp.where(same, s, FILL)).astype(BF)
            o = dot(pr, W[...])
            cols = slice(HDIM * hd, HDIM * hd + HDIM)
            OA[f, rows, cols] = o[:, cols].astype(BF)

    def oa_start(part):
        rows = pl.ds(S_ // 2 * part, S_ // 2)
        st.oa[part] = AllGather4(lambda j: OA.at[j, rows, :])

    def select_rows():
        for cols in blocks:
            XV[:, cols] = dot(SM[...], TA[:, :, cols].reshape(S_, 256)).astype(BF)
            N1V[:, cols] = dot(SM[...], N1[:, :, cols].reshape(S_, 256)).astype(BF)

    def select_cot():
        st.cot.finish()
        for cols in blocks:
            DY[:, cols] = dot(SM[...], CA[:, :, cols].reshape(S_, 256)).astype(BF)

    def out_project(parts, cols):
        heads = [WO[n // NF * j : n // NF * (j + 1), :, :, cols].reshape(C, -1) for j in range(NF)]
        return sum(dot(parts(j), heads[j]) for j in range(NF))

    def context_middle():
        st.wo.finish()
        st.ov.finish()
        for cols in blocks:
            X1V[:, cols] = XV[:, cols].astype(F32) + (out_project(lambda j: OV[j], cols) + VEC[4:5, cols])
        xhat, _inv = norm_stats(X1V[...])
        N2V[...] = (xhat * vec(2) + vec(3)).astype(BF)

    def normal_cdf(hid):
        return 0.5 * (1.0 + lax.erf(hid * (1.0 / math.sqrt(2.0))))

    def context_hidden():
        finish(*w1_ring)
        for cols in blocks:
            hid = dot(N2V[...], A1[:, :, cols].reshape(D, 256)) + VEC[6:7, cols]
            cdf = normal_cdf(hid)
            GV[:, cols] = (hid * cdf).astype(BF)
            GP[:, cols] = cdf + hid * (jnp.exp(-0.5 * hid * hid) * (1.0 / math.sqrt(2.0 * math.pi)))

    def outer(dst, lhs, rhs):
        for k, cols in enumerate(blocks):
            g.LT[cols, :] = lhs[:, cols].astype(F32).T.astype(BF)

        def one(k, _):
            rows = pl.ds(pl.multiple_of(512 * k, 512), 512)
            for c in range(dst.shape[2] // 256):
                cols = slice(256 * c, 256 * c + 256)
                dst[pl.ds(4 * k, 4), :, cols] = dot(g.LT[rows, :], rhs[:, cols]).reshape(4, 128, 256)
            return 0

        lax.fori_loop(0, n // 4, one, 0)

    def put_grad(k, vrow):
        for q in range(n):
            VG[q, k : k + 1, :] = vrow[:, 128 * q : 128 * q + 128]

    def fc2_grad():
        outer(G2, GV, DY)

    def hidden_grad():
        finish(*w2_ring)
        for k, cols in enumerate(blocks):
            dg = dot(DY[...], A2[...].reshape(HF, D)[256 * k : 256 * k + 256, :], NT)
            dh = (dg * GP[:, cols]).astype(BF)
            DH[:, cols] = dh
            dc1 = jnp.sum(dh.astype(F32), axis=0, keepdims=True)
            for q in range(2):
                for j in range(NF):
                    piece = dc1[:, 128 * q : 128 * q + 128]
                    VG[2 * k + q, 9 + j : 10 + j, :] = jnp.where(f == j, piece, jnp.zeros((1, 128), F32))

    def second_grad():
        for k, cols in enumerate(blocks):
            part = dot(DH[...], A1[2 * k : 2 * k + 2].reshape(256, HF), NT).astype(BF)
            PN[:, :, cols] = part.reshape(NF, V, 256)
        st.n2 = ReduceScatter4(PN, g.PNr1, g.PNxs, g.PNr2)

    def fc1_grad():
        outer(G1, N2V, DH)

    def context_partial():
        for cols in blocks:
            part = dot(GV[...], A2[:, :, cols].reshape(HF, 256)).astype(BF)
            PF[:, :, cols] = part.reshape(NF, V, 256)
        st.pf = ReduceScatter4(PF, g.PFr1, g.PFxs, g.PFr2)

    def second_norm_back():
        st.n2.finish()
        dyo = DY[mine, :].astype(F32)
        dv, dgain, dshift = norm_back(X1V[mine, :], vec(2), st.n2.total())
        dx1 = dyo + dv
        g.DX1[...] = dx1
        low = dx1.astype(BF)
        g.DP[f] = low
        st.dp = AllGather4(lambda j: g.DP.at[j])
        put_grad(2, dgain)
        put_grad(3, dshift)
        put_grad(4, jnp.sum(low.astype(F32), axis=0, keepdims=True))
        put_grad(5, jnp.sum(dyo, axis=0, keepdims=True))

    def transpose_attended():
        st.ov.finish()
        for j in range(NF):
            ot = OV[j].astype(F32).T.astype(BF)
            OT[n // NF * j : n // NF * (j + 1)] = ot.reshape(n // NF, NF, R, VP)

    def out_grad():
        st.dp.finish()
        go = dot(OT[:, f].reshape(n * R, VP), g.DP[...].reshape(VP, D))
        GO[...] = go.reshape(n, R, D)

    def attended_grad():
        st.dp.finish()
        st.wo.finish()
        wo_heads = WO[pl.ds(n // NF * f, n // NF)].reshape(C, D)
        DO[...] = dot(g.DP[...].reshape(VP, D), wo_heads, NT).astype(BF)

    def attention_back():
        dq = jnp.zeros((VP, C), F32)
        dk = jnp.zeros((VP, C), F32)
        dw = jnp.zeros((VP, C), F32)
        for hd in range(C // HDIM):
            pr = PV[hd]
            dp = dot(DO[...] * hmask[hd].astype(BF), WV[...], NT)
            ds = (pr * (dp - jnp.sum(pr * dp, axis=-1, keepdims=True))).astype(BF)
            dq += dot(ds, KV[...]) * hmask[hd]
            dk += dot(ds, QV[...], TN) * hmask[hd]
            dw += dot(pr.astype(BF), DO[...], TN) * hmask[hd]
        csv = sum(dot(dot(SM[...], g.OH[...]).astype(BF), g.trig_v[k]) for k in range(3))
        for t, (grad, scale) in enumerate(((dq, 0.125), (dk, 1.0))):
            for hh in range(C // 128):
                u = grad[:, 128 * hh : 128 * hh + 128]
                u = u * csv[:, :128] - swap_halves(u) * csv[:, 128:]
                DPRE[:, C * t + 128 * hh : C * t + 128 * hh + 128] = (u * scale).astype(BF)
        DPRE[:, 2 * C :] = dw.astype(BF)

    def qkv_grad():
        outer(GQ, N1V, DPRE)

    def qkv_bias_grad():
        BG[...] = jnp.zeros(BG.shape, F32)
        db = jnp.sum(DPRE[...].astype(F32), axis=0, keepdims=True)
        for t in range(3):
            BG[0:1, pl.ds(pl.multiple_of(D * t + C * f, 128), C)] = db[:, C * t : C * t + C]
        for q in range(n):
            for t in range(3):
                VG[q, 6 + t : 7 + t, :] = BG[0:1, 384 * q + 128 * t : 384 * q + 128 * t + 128]
            VG[q, 13:16, :] = jnp.zeros((3, 128), F32)

    def first_grad():
        for k, cols in enumerate(blocks):
            part = dot(DPRE[...], AQ[2 * k : 2 * k + 2].reshape(256, 3 * C), NT).astype(BF)
            PN[:, :, cols] = part.reshape(NF, V, 256)
        st.n1 = ReduceScatter4(PN, g.PMr1, g.PMxs, g.PMr2)

    def first_norm_back():
        st.n1.finish()
        dv, dgain, dshift = norm_back(XV[mine, :].astype(F32), vec(0), st.n1.total())
        g.DX[f] = (g.DX1[...] + dv).astype(BF)
        st.dx = AllGather4(lambda j: g.DX.at[j])
        put_grad(0, dgain)
        put_grad(1, dshift)

    def context_result():
        st.pf.finish()
        g.CO[f] = (X1V[mine, :] + (st.pf.total() + vec(5))).astype(BF)
        st.co = AllGather4(lambda j: g.CO.at[j])

    def home(src, dst):
        s = SM[:, pl.ds(pl.multiple_of(T * f, 128), T)]
        for cols in blocks:
            dst[:, cols] = dot(s, src[:, :, cols].reshape(VP, 256), TN).astype(BF)

    def home_context():
        st.co.finish()
        home(g.CO, g.CH)
        store(g.CH, g.ctx_o, 0)

    def home_grad():
        st.dx.finish()
        home(g.DX, g.DXH)
        store(g.DXH, g.dx_o, 1)

    def target_middle(b):
        st.wo.finish()
        st.oa[b // 2].finish()
        for cols in blocks:
            g.X1B[:, cols] = TA[b, :, cols].astype(F32) + (
                out_project(lambda j: OA[j, T * b : T * b + T, :], cols) + VEC[4:5, cols]
            )
        x1 = g.X1B[...]
        xh, _inv = norm_stats(x1)
        N2[b] = (xh * vec(2) + vec(3)).astype(BF)

        @pl.when(f == b)
        def _():
            g.X1H[...] = x1

    def target_hidden(b):
        finish(*w1_ring)
        for cols in blocks:
            hid = dot(N2[b], A1[:, :, cols].reshape(D, 256)) + VEC[6:7, cols]
            GT[b, :, cols] = (hid * normal_cdf(hid)).astype(BF)

    def target_out(b):
        finish(*w2_ring)
        for cols in blocks:
            PT[b, :, cols] = dot(GT[b], A2[:, :, cols].reshape(HF, 256)).astype(BF)
        if b == NF - 1:
            st.pt = ReduceScatter4(PT, g.PTr1, g.PTxs, g.PTr2)

    def target_result():
        st.pt.finish()
        g.TO[...] = (g.X1H[...] + (st.pt.total() + vec(5))).astype(BF)
        store(g.TO, g.tgt_o, 3)

    def fc2_grad_done():
        finish(*g2_ring)
        for k, ring in enumerate(g2_ring):
            g.D2[hc * k : hc * k + hc, :] = ring.total()
        store(g.D2, g.g2_o, 2)

    def fc1_grad_trade():
        finish(*g1_ring)
        for k, ring in enumerate(g1_ring):
            E1[2 * k : 2 * k + 2] = ring.total().astype(BF).reshape(2, R, HF)
        F1[f] = E1[f]
        st.e1 = scatter(lambda j: E1.at[j], lambda j: F1.at[j], F1.at[pl.ds(0, 3)])

    def fc1_grad_done():
        received(st.e1)
        store(F1, g.g1_o, 5)

    def out_grad_done():
        go_ring.finish()
        g.DOo[...] = go_ring.total()
        store(g.DOo, g.go_o, 4)

    def qkv_grad_trade():
        finish(*gq_ring)
        for k, ring in enumerate(gq_ring):
            EQ[2 * k : 2 * k + 2] = ring.total().astype(BF).reshape(2, R, 3 * C)
        FQ[f] = EQ[f]
        st.eq = scatter(lambda j: EQ.at[j], lambda j: FQ.at[j], FQ.at[pl.ds(0, 3)])

    def qkv_grad_done():
        received(st.eq)
        store(FQ, g.gq_o, 7)

    def small_grad_trade():
        gs_ring.finish()
        SG[f] = gs_ring.total()
        st.sg = scatter(lambda j: SG.at[f], lambda j: SG.at[j], SG.at[pl.ds(0, 3)])

    def small_grad_done():
        received(st.sg)
        g.SGo[...] = SG[0] + SG[1] + SG[2] + SG[3]
        store(g.SGo, g.sg_o, 6)

    start()
    o_ring.step(0)
    w2_ring[0].step(0)
    small_start()
    layout()
    cast_fc1()
    w2_ring[1].step(0)
    tokens_start()
    o_ring.step(1)
    cot_start()
    q_ring[0].step(0)
    visible()
    s_ring.step(0)
    q_ring[1].step(0)
    w1_ring[0].step(0)
    o_ring.step(2)
    q_ring[0].step(1)
    s_ring.step(1)
    q_ring[1].step(1)
    w1_ring[1].step(0)
    o_ring.step(3)
    st.tok.forward()
    q_ring[0].step(2)
    s_ring.step(2)
    q_ring[1].step(2)
    w1_ring[0].step(1)
    wo_start()
    w1_ring[1].step(1)
    s_ring.step(3)
    q_ring[0].step(3)
    st.cot.forward()
    q_ring[1].step(3)
    select_cot()
    w2_ring[0].step(1)
    w1_ring[0].step(2)
    small_vectors()
    first_norm()
    select_rows()
    w1_ring[1].step(2)
    project_half(0)
    project_half(1)
    context_attention()
    w1_ring[0].step(3)
    st.wo.forward()
    attend_target(3, 0)
    w2_ring[1].step(1)
    attend_target(0, 0)
    w1_ring[1].step(3)
    attend_target(3, 1)
    w2_ring[0].step(2)
    st.ov.forward()
    attend_target(2, 0)
    attend_target(2, 1)
    oa_start(1)
    context_middle()
    w2_ring[1].step(2)
    context_hidden()
    fc2_grad()
    g2_ring[1].step(0)
    attend_target(1, 0)
    w2_ring[0].step(3)
    attend_target(1, 1)
    transpose_attended()
    w2_ring[1].step(3)
    g2_ring[0].step(0)
    attend_target(0, 1)
    oa_start(0)
    st.oa[1].forward()
    g2_ring[1].step(1)
    hidden_grad()
    fc1_grad()
    g1_ring[0].step(0)
    context_partial()
    g2_ring[0].step(1)
    second_grad()
    g1_ring[1].step(0)
    st.pf.forward()
    st.n2.forward()
    g1_ring[0].step(1)
    st.oa[0].forward()
    target_middle(0)
    g2_ring[0].step(2)
    target_hidden(0)
    context_result()
    target_out(0)
    g1_ring[1].step(1)
    target_middle(1)
    target_hidden(1)
    second_norm_back()
    g1_ring[0].step(2)
    target_middle(2)
    target_middle(3)
    st.co.forward()
    target_hidden(2)
    target_out(2)
    g2_ring[0].step(3)
    home_context()
    g1_ring[1].step(2)
    st.dp.forward()
    target_hidden(3)
    target_out(1)
    attended_grad()
    attention_back()
    g1_ring[0].step(3)
    first_grad()
    target_out(3)
    qkv_grad()
    gq_ring[1].step(0)
    st.n1.forward()
    gq_ring[0].step(0)
    qkv_bias_grad()
    out_grad()
    g1_ring[1].step(3)
    st.pt.forward()
    gq_ring[1].step(1)
    first_norm_back()
    gs_ring.step(0)
    gq_ring[0].step(1)
    fc1_grad_trade()
    go_ring.step(0)
    g2_ring[1].step(2)
    gq_ring[1].step(2)
    gs_ring.step(1)
    gq_ring[0].step(2)
    target_result()
    go_ring.step(1)
    gq_ring[1].step(3)
    gs_ring.step(2)
    st.dx.forward()
    gq_ring[0].step(3)
    home_grad()
    fc1_grad_done()
    go_ring.step(2)
    gs_ring.step(3)
    g2_ring[1].step(3)
    qkv_grad_trade()
    go_ring.step(3)
    small_grad_trade()
    fc2_grad_done()
    qkv_grad_done()
    small_grad_done()
    out_grad_done()
    for c in outs:
        c.wait()


def run_layer(n, tokens, cot, lengths, mask, counts, vectors, wqkv, wo, w1, w2, V):
    T, D = tokens.shape
    NF = 4
    FF = w1.shape[1]
    R = wo.shape[0]
    RP = R * NF
    HC = w2.shape[0]
    HF = HC * n
    C = D // NF
    VP = V * NF
    S_ = T * NF
    h2 = n // 2
    B, F = BF, F32
    vm = pltpu.VMEM
    scratch = dict(
        wqkv_v=vm((R, 3 * D), F), w1_v=vm((R, FF), F), wo_v=vm((R, D), F), w2_v=vm((HC, D), F),
        small_v=vm((8, 128), F), trig_v=vm((3, 128, 256), B),
        sq=vm((NF, R, 3 * C), B), s1=vm((NF, R, HF), B),
        AS=vm((n, NF, 8, 128), F), AQ=vm((n, RP, 3 * C), B), WO=vm((n, NF, R, D), B),
        A1=vm((n, RP, HF), B), A2=vm((n, HC, D), B),
        TA=vm((NF, T, D), B), CA=vm((NF, T, D), B), N1=vm((NF, T, D), B),
        OH=vm((S_, 128), B), CS=vm((S_, 256), F), SM=vm((VP, S_), B),
        VEC=vm((8, D), F), BQ=vm((8, 3 * D), F), BG=vm((8, 3 * D), F),
        Q=vm((S_, C), B), K=vm((S_, C), B), W=vm((S_, C), B),
        QV=vm((VP, C), B), KV=vm((VP, C), B), WV=vm((VP, C), B),
        OV=vm((NF, VP, C), B), PV=vm((C // HDIM, VP, VP), F), OA=vm((NF, S_, C), B),
        XV=vm((VP, D), B), N1V=vm((VP, D), B), DY=vm((VP, D), B),
        X1V=vm((VP, D), F), N2V=vm((VP, D), B), GV=vm((VP, HF), B), GP=vm((VP, HF), F),
        G2=vm((n, HC, D), F), G1=vm((n, RP, HF), F), GQ=vm((n, RP, 3 * C), F), GO=vm((n, R, D), F),
        VG=vm((n, 16, 128), F),
        st2=vm((HC, D), B), rr2=vm((h2, HC, D), B), rl2=vm((h2, HC, D), B),
        st1=vm((RP, HF), B), rr1=vm((h2, RP, HF), B), rl1=vm((h2, RP, HF), B),
        stq=vm((RP, 3 * C), B), rrq=vm((h2, RP, 3 * C), B), rlq=vm((h2, RP, 3 * C), B),
        sto=vm((R, D), B), rro=vm((h2, R, D), B), rlo=vm((h2, R, D), B),
        sts=vm((16, 128), F), rrs=vm((h2, 16, 128), F), rls=vm((h2, 16, 128), F),
        DH=vm((VP, HF), B), PN=vm((NF, V, D), B), PF=vm((NF, V, D), B),
        PNr1=vm((2, V, D), B), PNxs=vm((V, D), B), PNr2=vm((V, D), B),
        PMr1=vm((2, V, D), B), PMxs=vm((V, D), B), PMr2=vm((V, D), B),
        PFr1=vm((2, V, D), B), PFxs=vm((V, D), B), PFr2=vm((V, D), B),
        DX1=vm((V, D), F), DP=vm((NF, V, D), B), OT=vm((n, NF, R, VP), B), DO=vm((VP, C), B),
        DPRE=vm((VP, 3 * C), B), CO=vm((NF, V, D), B), DX=vm((NF, V, D), B),
        X1H=vm((T, D), F), GT=vm((NF, T, HF), B),
        PTr1=vm((2, T, D), B), PTxs=vm((T, D), B), PTr2=vm((T, D), B),
        CH=vm((T, D), B), DXH=vm((T, D), B), TO=vm((T, D), B),
        SG=vm((NF, 16, 128), F), SGo=vm((16, 128), F),
        E1=vm((NF, R, HF), B), F1=vm((NF, R, HF), B), EQ=vm((NF, R, 3 * C), B), FQ=vm((NF, R, 3 * C), B),
        send_sems=pltpu.SemaphoreType.DMA((16,)), recv_sems=pltpu.SemaphoreType.DMA((59,)),
        local_sems=pltpu.SemaphoreType.DMA((16,)), mask_v=vm((1, T), jnp.int32), LT=vm((D, VP), B),
    )
    arr = jax.ShapeDtypeStruct
    ins = dict(
        lengths=lengths, counts=counts, tok=tokens, cot=cot, mask=mask.reshape(1, T), wqkv=wqkv, wo=wo,
        w1=w1, w2=w2, trig=jnp.asarray(trig_table()),
    )
    for k, v in enumerate(vectors):
        ins["in%d" % k] = v.reshape(1, -1)
        scratch["v%d" % k] = vm((1, v.shape[0]), F)
    outs = dict(
        tgt_o=arr((T, D), B), ctx_o=arr((T, D), B), dx_o=arr((T, D), B), gq_o=arr((NF, R, 3 * C), B),
        go_o=arr((R, D), F), g1_o=arr((NF, R, HF), B), g2_o=arr((HC, D), F), sg_o=arr((16, 128), F),
    )
    names = [*ins, *outs, *scratch]
    any_spec = pl.BlockSpec(memory_space=pl.ANY)
    return pl.pallas_call(
        functools.partial(layer_kernel, (n, D, FF, T, V), names),
        out_shape=list(outs.values()),
        in_specs=[pl.BlockSpec(memory_space=pltpu.SMEM)] * 2 + [any_spec] * (len(ins) - 2),
        out_specs=[any_spec] * 8,
        scratch_shapes=list(scratch.values()),
        compiler_params=pltpu.CompilerParams(
            collective_id=0, has_side_effects=True, vmem_limit_bytes=67043328
        ),
        name="layer",
    )(*ins.values())


def outputs_kernel(dims, count, *refs):
    n, R, C, HC = dims
    NF = 4
    f = lax.axis_index("fsdp")
    tgt, ctx, dx, gq, go, g1, g2, sg = refs[:8]
    tgt_o, ctx_o, dx_o, gq_o, go_o, g1_o, g2_o = refs[8:15]
    vec_o = refs[15:23]
    bufs = refs[23:31]
    gq_w, g1_w, sem_in, sem_out = refs[31:]
    loads = []
    for k, (src, dst) in enumerate(zip((g2, tgt, ctx, dx, go, gq, g1, sg), bufs)):
        c = pltpu.make_async_copy(src, dst, sem_in.at[k])
        c.start()
        loads.append(c)
    stores = []

    def store(src, dst):
        c = pltpu.make_async_copy(src, dst, sem_out.at[len(stores)])
        c.start()
        stores.append(c)

    for k, out in enumerate((g2_o, tgt_o, ctx_o, dx_o, go_o)):
        loads[k].wait()
        store(bufs[k], out)
    D = NF * C
    loads[5].wait()
    for j in range(NF):
        for t in range(3):
            gq_w[:, D * t + C * j : D * t + C * j + C] = bufs[5][j, :, C * t : C * t + C].astype(F32)
    store(gq_w, gq_o)
    loads[6].wait()
    for j in range(NF):
        for t in range(n):
            at = HC * (NF * t + j)
            g1_w[:, at : at + HC] = bufs[6][j, :, HC * t : HC * t + HC].astype(F32)
    store(g1_w, g1_o)
    loads[7].wait()
    small = bufs[7]
    for k in range(6):
        vec_o[k][...] = pltpu.roll(small[k : k + 1, :], lax.rem(128 - R * f, 128), 1)[:, :R]
    rows = jnp.concatenate([small[6 + t : 7 + t, :] for t in range(3)], axis=1)
    vec_o[6][...] = pltpu.roll(rows, lax.rem(384 - 3 * R * f, 384), 1)[:, : 3 * R]
    mine = jnp.zeros((1, 128), F32)
    for j in range(NF):
        mine = jnp.where(f == j, small[9 + j : 10 + j, :], mine)
    vec_o[7][...] = mine
    for c in stores:
        c.wait()


def write_outputs(n, parts, R, D, FF, HC):
    NF = 4
    C = D // NF
    tgt = parts[0]
    arr = jax.ShapeDtypeStruct
    any_spec = pl.BlockSpec(memory_space=pl.ANY)
    order = [parts[k] for k in (6, 0, 1, 2, 4, 3, 5, 7)]
    big = [
        arr(tgt.shape, BF), arr(tgt.shape, BF), arr(tgt.shape, BF),
        arr((R, 3 * D), F32), arr((R, D), F32), arr((R, FF), F32), arr((HC, D), F32),
    ]
    small = [arr((1, w), F32) for w in (R,) * 6 + (3 * R, 4 * R)]
    return pl.pallas_call(
        functools.partial(outputs_kernel, (n, R, C, HC), 8),
        out_shape=big + small,
        in_specs=[any_spec] * 8,
        out_specs=[any_spec] * 7 + [pl.BlockSpec(memory_space=pltpu.VMEM)] * 8,
        scratch_shapes=[pltpu.VMEM(a.shape, a.dtype) for a in order]
        + [
            pltpu.VMEM((R, 3 * D), F32), pltpu.VMEM((R, FF), F32),
            pltpu.SemaphoreType.DMA((8,)), pltpu.SemaphoreType.DMA((8,)),
        ],
        name="outputs",
    )(*parts)


def on_device(
    tokens, lengths, visibility_mask, visible_counts, ln1_gain, ln1_bias, qkv_weight, qkv_bias,
    out_weight, out_bias, ln2_gain, ln2_bias, fc1_weight, fc1_bias, fc2_weight, fc2_bias, context_cot,
):
    n = lax.axis_size("dp")
    R, D = out_weight.shape
    vectors = (ln1_gain, ln1_bias, ln2_gain, ln2_bias, out_bias, fc2_bias, qkv_bias, fc1_bias)
    parts = run_layer(
        n, tokens, context_cot, lengths, visibility_mask, visible_counts, vectors,
        qkv_weight, out_weight, fc1_weight, fc2_weight, VIS_DEV,
    )
    tgt, ctx, dx, gq, go, g1, g2, *small = write_outputs(
        n, parts, R, D, fc1_weight.shape[1], fc2_weight.shape[0]
    )
    gg1, gb1, gg2, gb2, gbo, gc2, gbq, gc1 = [v.reshape(-1) for v in small]
    return (tgt, ctx, dx, gg1, gb1, gq, gbq, go, gbo, gg2, gb2, g1, gc1, g2, gc2)


def layer_norm(inputs, scale_vec, shift_vec):
    center = inputs - jnp.mean(inputs, axis=-1, keepdims=True)
    spread = jnp.mean(center * center, axis=-1, keepdims=True)
    return center * lax.rsqrt(spread + norm_eps) * scale_vec + shift_vec


def gelu_erf(values):
    return jax.nn.gelu(values, approximate=False)


def pack_layout(seq_lens, pack_len):
    seq_ends = jnp.cumsum(seq_lens)
    places = jnp.arange(pack_len, dtype=jnp.int32)
    passed = places[:, None] >= seq_ends[None, :]
    segment = jnp.sum(passed.astype(jnp.int32), axis=1)
    before = jnp.sum(jnp.where(passed, seq_lens[None, :], 0), axis=1)
    return (segment, places - before)


def rope_tables(places):
    frame_index = (places // (GRID * GRID)).astype(jnp.float32)
    grid_row = (places // GRID % GRID).astype(jnp.float32)
    grid_col = (places % GRID).astype(jnp.float32)
    pair_index = jnp.arange(HDIM // 2, dtype=jnp.int32)
    axis_pick = jnp.minimum(pair_index // 11, 2)
    pair_order = (pair_index - 11 * axis_pick).astype(jnp.float32)
    frequency = jnp.exp(pair_order * (-math.log(10000.0) / 11.0))
    angles = (
        frame_index[:, None] * (axis_pick == 0).astype(jnp.float32)[None, :]
        + grid_row[:, None] * (axis_pick == 1).astype(jnp.float32)[None, :]
        + grid_col[:, None] * (axis_pick == 2).astype(jnp.float32)[None, :]
    ) * frequency[None, :]
    return (jnp.cos(angles), jnp.sin(angles))


def rotate(heads, cosine_table, sine_table):
    half_size = heads.shape[-1] // 2
    first_half = heads[..., :half_size]
    second_half = heads[..., half_size:]
    cosine_cols = cosine_table[:, None, :]
    sine_cols = sine_table[:, None, :]
    return jnp.concatenate(
        [
            first_half * cosine_cols - second_half * sine_cols,
            second_half * cosine_cols + first_half * sine_cols,
        ],
        axis=-1,
    )


def rotate_back(grads, cosine_table, sine_table):
    half_size = grads.shape[-1] // 2
    first_half = grads[..., :half_size]
    second_half = grads[..., half_size:]
    cosine_cols = cosine_table[:, None, :]
    sine_cols = sine_table[:, None, :]
    return jnp.concatenate(
        [
            first_half * cosine_cols + second_half * sine_cols,
            second_half * cosine_cols - first_half * sine_cols,
        ],
        axis=-1,
    )


def project(token_rows, weights, cosine_table, sine_table):
    inputs = token_rows.astype(jnp.float32)
    row_count = inputs.shape[0]
    model_width = inputs.shape[1]
    normed = layer_norm(
        inputs, weights[0].astype(jnp.float32), weights[1].astype(jnp.float32)
    ).astype(jnp.bfloat16)
    joined = jnp.dot(normed, weights[2], preferred_element_type=jnp.float32) + weights[3].astype(
        jnp.float32
    )
    query_heads = rotate(
        joined[:, :model_width].reshape(row_count, HEADS, HDIM), cosine_table, sine_table
    ).astype(jnp.bfloat16)
    key_flat = (
        rotate(
            joined[:, model_width : 2 * model_width].reshape(row_count, HEADS, HDIM),
            cosine_table,
            sine_table,
        )
        .astype(jnp.bfloat16)
        .reshape(row_count, model_width)
    )
    value_flat = joined[:, 2 * model_width :].astype(jnp.bfloat16)
    return (inputs, normed, query_heads, key_flat, value_flat)


def attend(query_heads, key_flat, value_flat, seg_query, seg_key):
    key_heads = key_flat.reshape(key_flat.shape[0], HEADS, HDIM)
    value_heads = value_flat.reshape(value_flat.shape[0], HEADS, HDIM)
    scores = jnp.einsum(
        "qhd,khd->hqk", query_heads, key_heads, preferred_element_type=jnp.float32
    ) * HDIM ** (-0.5)
    allowed = seg_query[:, None] == seg_key[None, :]
    masked = jnp.where(allowed[None], scores, masked_fill)
    row_max = jnp.max(masked, axis=-1, keepdims=True)
    raised = jnp.exp(masked - row_max)
    totals = jnp.sum(raised, axis=-1, keepdims=True)
    attn_probs = (raised / totals).astype(jnp.bfloat16)
    attended = jnp.einsum(
        "hqk,khd->qhd", attn_probs, value_heads, preferred_element_type=jnp.float32
    )
    return (
        attended.reshape(query_heads.shape[0], -1).astype(jnp.bfloat16),
        row_max + jnp.log(totals),
    )


def attend_back(query_heads, key_flat, value_flat, seg_query, seg_key, log_total, grad_att):
    key_heads = key_flat.reshape(key_flat.shape[0], HEADS, HDIM)
    value_heads = value_flat.reshape(value_flat.shape[0], HEADS, HDIM)
    scale_factor = HDIM ** (-0.5)
    scores = (
        jnp.einsum("qhd,khd->hqk", query_heads, key_heads, preferred_element_type=jnp.float32)
        * scale_factor
    )
    allowed = seg_query[:, None] == seg_key[None, :]
    masked = jnp.where(allowed[None], scores, masked_fill)
    attn_probs = jnp.exp(masked - log_total)
    grad_heads = grad_att.reshape(grad_att.shape[0], HEADS, HDIM)
    grad_probs = jnp.einsum(
        "qhd,khd->hqk", grad_heads, value_heads, preferred_element_type=jnp.float32
    )
    row_delta = jnp.sum(attn_probs * grad_probs, axis=-1, keepdims=True)
    grad_scores = (attn_probs * (grad_probs - row_delta)).astype(jnp.bfloat16)
    grad_query = (
        jnp.einsum("hqk,khd->qhd", grad_scores, key_heads, preferred_element_type=jnp.float32)
        * scale_factor
    )
    grad_key = (
        jnp.einsum("hqk,qhd->khd", grad_scores, query_heads, preferred_element_type=jnp.float32)
        * scale_factor
    )
    grad_value = jnp.einsum(
        "hqk,qhd->khd",
        attn_probs.astype(jnp.bfloat16),
        grad_heads,
        preferred_element_type=jnp.float32,
    )
    return (
        grad_query,
        grad_key.reshape(key_flat.shape[0], -1),
        grad_value.reshape(value_flat.shape[0], -1),
    )


def finish(inputs, attended, weights):
    middle = inputs + (
        jnp.dot(attended, weights[4], preferred_element_type=jnp.float32)
        + weights[5].astype(jnp.float32)
    )
    second = layer_norm(
        middle, weights[6].astype(jnp.float32), weights[7].astype(jnp.float32)
    ).astype(jnp.bfloat16)
    hidden = jnp.dot(second, weights[8], preferred_element_type=jnp.float32) + weights[9].astype(
        jnp.float32
    )
    activated = gelu_erf(hidden).astype(jnp.bfloat16)
    result = middle + (
        jnp.dot(activated, weights[10], preferred_element_type=jnp.float32)
        + weights[11].astype(jnp.float32)
    )
    return (result, middle, second, hidden, activated)


def gathered_device(
    tokens,
    lengths,
    visibility_mask,
    visible_counts,
    ln1_gain,
    ln1_bias,
    qkv_weight,
    qkv_bias,
    out_weight,
    out_bias,
    ln2_gain,
    ln2_bias,
    fc1_weight,
    fc1_bias,
    fc2_weight,
    fc2_bias,
    context_cot,
):
    tok_rows = tokens.shape[0]
    model_width = tokens.shape[1]
    groups = lax.axis_size("fsdp")
    member = lax.axis_index("fsdp")
    pack_len = tok_rows * groups
    vis_rows = VIS_DEV
    vis_pack = vis_rows * groups
    zero_low = jnp.zeros((), jnp.bfloat16)
    shards = [
        weight.astype(jnp.bfloat16)
        for weight in (
            ln1_gain,
            ln1_bias,
            qkv_weight,
            qkv_bias,
            out_weight,
            out_bias,
            ln2_gain,
            ln2_bias,
            fc1_weight,
            fc1_bias,
            fc2_weight,
            fc2_bias,
        )
    ]
    weights = (
        lax.all_gather(shards[0], ("dp", "fsdp"), axis=0, tiled=True),
        lax.all_gather(shards[1], ("dp", "fsdp"), axis=0, tiled=True),
        lax.all_gather(shards[2], ("dp", "fsdp"), axis=0, tiled=True),
        lax.all_gather(shards[3], ("dp", "fsdp"), axis=0, tiled=True),
        lax.all_gather(shards[4], ("dp", "fsdp"), axis=0, tiled=True),
        lax.all_gather(shards[5], ("dp", "fsdp"), axis=0, tiled=True),
        lax.all_gather(shards[6], ("dp", "fsdp"), axis=0, tiled=True),
        lax.all_gather(shards[7], ("dp", "fsdp"), axis=0, tiled=True),
        lax.all_gather(shards[8], ("dp", "fsdp"), axis=0, tiled=True),
        lax.all_gather(shards[9], ("dp", "fsdp"), axis=0, tiled=True),
        lax.all_gather(shards[10], ("dp", "fsdp"), axis=0, tiled=True),
        lax.all_gather(shards[11], ("dp", "fsdp"), axis=0, tiled=True),
    )
    segment, places = pack_layout(lengths[0], pack_len)
    home_rows = member * tok_rows + jnp.arange(tok_rows, dtype=jnp.int32)
    seg_home = jnp.take(segment, home_rows)
    cos_home, sin_home = rope_tables(jnp.take(places, home_rows))
    inputs, normed, query_heads, key_flat, value_flat = project(tokens, weights, cos_home, sin_home)
    key_pack, value_pack = (
        lax.all_gather(key_flat, "fsdp", axis=0, tiled=True),
        lax.all_gather(value_flat, "fsdp", axis=0, tiled=True),
    )
    attended = attend(query_heads, key_pack, value_pack, seg_home, segment)[0]
    target_out = finish(inputs, attended, weights)[0].astype(jnp.bfloat16)
    running = jnp.cumsum(visibility_mask)
    visible_here = visibility_mask * (running <= visible_counts[0, 0]).astype(jnp.int32)
    visible_all = lax.all_gather(visible_here, "fsdp", axis=0, tiled=True)
    inclusive = jnp.cumsum(visible_all)
    rank_index = jnp.arange(vis_pack, dtype=jnp.int32)
    row_of = jnp.sum((inclusive[None, :] <= rank_index[:, None]).astype(jnp.int32), axis=1)
    owner_dev = row_of // tok_rows
    local_row = row_of % tok_rows
    mine_here = (owner_dev == member)[:, None]
    send_tokens = jnp.where(mine_here, jnp.take(tokens, local_row, axis=0), zero_low)
    send_cot = jnp.where(mine_here, jnp.take(context_cot, local_row, axis=0), zero_low)
    recv_tokens, recv_cot = (
        lax.all_to_all(send_tokens, "fsdp", split_axis=0, concat_axis=0, tiled=True),
        lax.all_to_all(send_cot, "fsdp", split_axis=0, concat_axis=0, tiled=True),
    )
    slot_index = jnp.arange(vis_rows, dtype=jnp.int32)
    my_ranks = member * vis_rows + slot_index
    my_owner = jnp.take(owner_dev, my_ranks)
    my_row = jnp.take(row_of, my_ranks)
    picked = my_owner * vis_rows + slot_index
    bal_tokens = jnp.take(recv_tokens, picked, axis=0)
    bal_cot = jnp.take(recv_cot, picked, axis=0)
    seg_bal = jnp.take(segment, my_row)
    seg_keys = jnp.take(segment, row_of)
    cos_bal, sin_bal = rope_tables(jnp.take(places, my_row))
    inputs_bal, normed_bal, query_bal, key_bal, value_bal = project(
        bal_tokens, weights, cos_bal, sin_bal
    )
    key_vis, value_vis = (
        lax.all_gather(key_bal, "fsdp", axis=0, tiled=True),
        lax.all_gather(value_bal, "fsdp", axis=0, tiled=True),
    )
    attended_bal, log_total = attend(query_bal, key_vis, value_vis, seg_bal, seg_keys)
    result_bal, middle_bal, second_bal, hidden_bal, activated_bal = finish(
        inputs_bal, attended_bal, weights
    )
    grad_result = bal_cot.astype(jnp.float32)
    result_low = grad_result.astype(jnp.bfloat16)
    grad_fc2 = jnp.einsum(
        "nf,nd->fd", activated_bal, result_low, preferred_element_type=jnp.float32
    )
    grad_bfc2 = jnp.sum(result_low.astype(jnp.float32), axis=0)
    grad_activated = jnp.einsum(
        "nd,fd->nf", result_low, weights[10], preferred_element_type=jnp.float32
    )
    gelu_pull = jax.vjp(gelu_erf, hidden_bal)[1]
    hidden_low = gelu_pull(grad_activated)[0].astype(jnp.bfloat16)
    grad_fc1 = jnp.einsum("nd,nf->df", second_bal, hidden_low, preferred_element_type=jnp.float32)
    grad_bfc1 = jnp.sum(hidden_low.astype(jnp.float32), axis=0)
    grad_second = jnp.einsum(
        "nf,df->nd", hidden_low, weights[8], preferred_element_type=jnp.float32
    )
    norm_two_pull = jax.vjp(
        layer_norm, middle_bal, weights[6].astype(jnp.float32), weights[7].astype(jnp.float32)
    )[1]
    grad_mid_norm, grad_gain_two, grad_shift_two = norm_two_pull(grad_second)
    grad_middle = grad_result + grad_mid_norm
    middle_low = grad_middle.astype(jnp.bfloat16)
    grad_wout = jnp.einsum(
        "nd,ne->de", attended_bal, middle_low, preferred_element_type=jnp.float32
    )
    grad_bout = jnp.sum(middle_low.astype(jnp.float32), axis=0)
    grad_att = jnp.einsum(
        "ne,de->nd", middle_low, weights[4], preferred_element_type=jnp.float32
    ).astype(jnp.bfloat16)
    grad_query, grad_key_all, grad_value_all = attend_back(
        query_bal, key_vis, value_vis, seg_bal, seg_keys, log_total, grad_att
    )
    grad_key_own, grad_value_own = (
        lax.psum_scatter(
            grad_key_all.astype(jnp.bfloat16), "fsdp", scatter_dimension=0, tiled=True
        ).astype(jnp.float32),
        lax.psum_scatter(
            grad_value_all.astype(jnp.bfloat16), "fsdp", scatter_dimension=0, tiled=True
        ).astype(jnp.float32),
    )
    grad_query_pre = rotate_back(grad_query, cos_bal, sin_bal).reshape(vis_rows, model_width)
    grad_key_pre = rotate_back(
        grad_key_own.reshape(vis_rows, HEADS, HDIM), cos_bal, sin_bal
    ).reshape(vis_rows, model_width)
    joined_low = jnp.concatenate([grad_query_pre, grad_key_pre, grad_value_own], axis=1).astype(
        jnp.bfloat16
    )
    grad_wqkv = jnp.einsum("nd,ne->de", normed_bal, joined_low, preferred_element_type=jnp.float32)
    grad_bqkv = jnp.sum(joined_low.astype(jnp.float32), axis=0)
    grad_normed = jnp.einsum(
        "ne,de->nd", joined_low, weights[2], preferred_element_type=jnp.float32
    )
    norm_one_pull = jax.vjp(
        layer_norm, inputs_bal, weights[0].astype(jnp.float32), weights[1].astype(jnp.float32)
    )[1]
    grad_in_norm, grad_gain_one, grad_shift_one = norm_one_pull(grad_normed)
    grad_inputs = grad_middle + grad_in_norm
    destinations = jnp.arange(groups, dtype=jnp.int32)
    route_mask = (my_owner[None, :] == destinations[:, None])[:, :, None]
    send_out = jnp.where(route_mask, result_bal.astype(jnp.bfloat16)[None], zero_low).reshape(
        vis_pack, model_width
    )
    send_grad = jnp.where(route_mask, grad_inputs.astype(jnp.bfloat16)[None], zero_low).reshape(
        vis_pack, model_width
    )
    back_out, back_grad = (
        lax.all_to_all(send_out, "fsdp", split_axis=0, concat_axis=0, tiled=True),
        lax.all_to_all(send_grad, "fsdp", split_axis=0, concat_axis=0, tiled=True),
    )
    rank_home = jnp.maximum(jnp.take(inclusive, home_rows) - 1, 0)
    is_visible = (visible_here > 0)[:, None]
    context_out = jnp.where(is_visible, jnp.take(back_out, rank_home, axis=0), zero_low)
    tokens_grad = jnp.where(is_visible, jnp.take(back_grad, rank_home, axis=0), zero_low)
    grad_list = [
        grad_gain_one,
        grad_shift_one,
        grad_wqkv,
        grad_bqkv,
        grad_wout,
        grad_bout,
        grad_gain_two,
        grad_shift_two,
        grad_fc1,
        grad_bfc1,
        grad_fc2,
        grad_bfc2,
    ]
    reduced = (
        lax.psum_scatter(grad_list[0], ("dp", "fsdp"), scatter_dimension=0, tiled=True),
        lax.psum_scatter(grad_list[1], ("dp", "fsdp"), scatter_dimension=0, tiled=True),
        lax.psum_scatter(grad_list[2], ("dp", "fsdp"), scatter_dimension=0, tiled=True),
        lax.psum_scatter(grad_list[3], ("dp", "fsdp"), scatter_dimension=0, tiled=True),
        lax.psum_scatter(grad_list[4], ("dp", "fsdp"), scatter_dimension=0, tiled=True),
        lax.psum_scatter(grad_list[5], ("dp", "fsdp"), scatter_dimension=0, tiled=True),
        lax.psum_scatter(grad_list[6], ("dp", "fsdp"), scatter_dimension=0, tiled=True),
        lax.psum_scatter(grad_list[7], ("dp", "fsdp"), scatter_dimension=0, tiled=True),
        lax.psum_scatter(grad_list[8], ("dp", "fsdp"), scatter_dimension=0, tiled=True),
        lax.psum_scatter(grad_list[9], ("dp", "fsdp"), scatter_dimension=0, tiled=True),
        lax.psum_scatter(grad_list[10], ("dp", "fsdp"), scatter_dimension=0, tiled=True),
        lax.psum_scatter(grad_list[11], ("dp", "fsdp"), scatter_dimension=0, tiled=True),
    )
    return (
        target_out,
        context_out,
        tokens_grad,
        reduced[0],
        reduced[1],
        reduced[2],
        reduced[3],
        reduced[4],
        reduced[5],
        reduced[6],
        reduced[7],
        reduced[8],
        reduced[9],
        reduced[10],
        reduced[11],
    )


def per_device(tokens, *rest):
    n, group = lax.axis_size("dp"), lax.axis_size("fsdp")
    out_rows = rest[7].shape[0]
    fits = group == 4 and n == 8 and out_rows * group == 128
    return (on_device if fits else gathered_device)(tokens, *rest)


def solution(mesh):
    both = ("dp", "fsdp")
    vec, mat = P(both), P(both, None)
    return jax.shard_map(
        per_device,
        mesh=mesh,
        in_specs=(
            mat, P("dp", None), vec, P("dp", "fsdp"), vec, vec, mat, vec, mat, vec, vec, vec,
            mat, vec, mat, vec, mat,
        ),
        out_specs=(mat, mat, mat, vec, vec, mat, vec, mat, vec, vec, vec, mat, vec, mat, vec),
        check_vma=False,
    )
```

```python
import functools
import math
import types

import jax
import jax.numpy as jnp
import numpy as np
from jax import lax
from jax.experimental import pallas as pl
from jax.experimental.pallas import tpu as pltpu
from jax.sharding import PartitionSpec as P

HEADS = 16
HDIM = 64
GRID = 14
VIS_DEV = 64
norm_eps = 1e-06
masked_fill = -1e30
FRAMES = 8
EPS = 1e-06
FILL = -1e30
BF = jnp.bfloat16
F32 = jnp.float32
MESH = pl.DeviceIdType.MESH
NT = (((1,), (1,)), ((), ()))
NN = (((1,), (0,)), ((), ()))
TN = (((0,), (0,)), ((), ()))


def dot(a, b, dims=NN):
    return lax.dot_general(a, b, dims, preferred_element_type=F32)


def trig_table():
    width = FRAMES + 2 * GRID
    lane = np.arange(2 * HDIM)
    pair = lane % (HDIM // 2)
    axis = np.minimum(pair // 11, 2)
    freq = np.exp(((pair - 11 * axis).astype(np.float32)) * np.float32(-math.log(10000.0) / 11.0))
    sign = np.where(lane % HDIM < HDIM // 2, -1.0, 1.0)
    table = np.zeros((128, 4 * HDIM), np.float32)
    row = np.arange(width)
    kind = np.where(row < FRAMES, 0, np.where(row < FRAMES + GRID, 1, 2))
    coord = np.where(kind == 0, row, np.where(kind == 1, row - FRAMES, row - FRAMES - GRID))
    angle = (coord[:, None].astype(np.float32) * freq[None, :].astype(np.float32)).astype(np.float64)
    here = kind[:, None] == axis[None, :]
    table[:width, : 2 * HDIM] = np.where(here, np.cos(angle), 0.0)
    table[:width, 2 * HDIM :] = np.where(here, np.sin(angle) * sign[None, :], 0.0)
    parts = []
    rest = table
    for _ in range(3):
        part = rest.astype(jnp.bfloat16)
        parts.append(part)
        rest = rest - part.astype(np.float32)
    return np.stack(parts)


def norm_stats(v):
    center = v - jnp.mean(v, axis=-1, keepdims=True)
    inv = lax.rsqrt(jnp.mean(center * center, axis=-1, keepdims=True) + EPS)
    return center * inv, inv


def norm_back(v, gain, grad):
    xhat, inv = norm_stats(v)
    gg = grad * gain
    dv = inv * (
        gg - jnp.mean(gg, axis=-1, keepdims=True) - xhat * jnp.mean(gg * xhat, axis=-1, keepdims=True)
    )
    return (
        dv,
        jnp.sum(grad * xhat, axis=0, keepdims=True),
        jnp.sum(grad, axis=0, keepdims=True),
    )


def swap_halves(u):
    lane = lax.broadcasted_iota(jnp.int32, u.shape, 1)
    return jnp.where(
        lax.rem(lane, HDIM) < HDIM // 2,
        pltpu.roll(u, u.shape[1] - HDIM // 2, 1),
        pltpu.roll(u, HDIM // 2, 1),
    )


def column_segment(start, rows, ends):
    row = start + lax.broadcasted_iota(jnp.int32, (rows, 1), 0)
    seg = jnp.zeros((rows, 1), jnp.int32)
    for end in ends:
        seg += (row >= end).astype(jnp.int32)
    return row, seg


ALIASES = dict(N2="N1", PT="N1", X1B="GP")


class Sems:
    def __init__(self, send, recv):
        self.send, self.recv = send, recv
        self.sends = self.recvs = self.clock = 0
        self.idle_sends, self.idle_recvs, self.waited = [], [], []

    def take_send(self):
        if self.idle_sends:
            return self.idle_sends.pop()
        self.sends += 1
        return self.send.at[self.sends - 1]

    def give_send(self, sem):
        self.idle_sends.append(sem)

    def take_recv(self):
        self.recvs += 1
        return self.recv.at[self.recvs - 1]

    def ring_sent(self):
        rs = self.idle_recvs.pop() if self.idle_recvs else self.take_recv()
        self.clock += 1
        return rs, self.clock

    def ring_landed(self, sem, sent):
        self.idle_recvs += [old for at, old in self.waited if at < sent]
        self.waited = [(at, old) for at, old in self.waited if at >= sent]
        self.waited.append((self.clock, sem))


def layer_kernel(dims, names, *refs):
    n, D, FF, T, V = dims
    NF = 4
    R = D // (n * NF)
    RP = R * NF
    HC = FF // (NF * n)
    HF = FF // NF
    C = D // NF
    VP = V * NF
    S_ = T * NF
    last = n // 2 - 1
    given = dict(zip(names, refs))
    g = types.SimpleNamespace(**given, **{a: given[b] for a, b in ALIASES.items()})
    sems = Sems(g.send_sems, g.recv_sems)
    lsem = g.local_sems

    p = lax.axis_index("dp")
    f = lax.axis_index("fsdp")
    f1 = f + 1 - 2 * lax.rem(f, 2)
    f2 = lax.rem(f + 2, NF)
    f3 = NF - 1 - f
    par = lax.rem(p, 2)
    half_p = lax.div(p, 2)
    pos = (1 - par) * half_p + par * (n - 1 - half_p)

    def idx(q):
        q = lax.rem(q + 2 * n, n)
        up = lax.div(q, n // 2)
        return (1 - up) * (2 * q) + up * (2 * (n - 1 - q) + 1)

    right, left = idx(pos + 1), idx(pos - 1)

    def launch(src, dst, ss, rs, to):
        c = pltpu.make_async_remote_copy(
            src_ref=src, dst_ref=dst, send_sem=ss, recv_sem=rs, device_id=to, device_id_type=MESH
        )
        c.start()
        return c

    def sent(copies):
        for c in copies:
            c.wait_send()
            sems.give_send(c.src_sem)

    def received(copies):
        for c in copies:
            c.wait_recv()
        sent(copies)

    def remote(src, dst, to):
        ss, rs = sems.take_send(), sems.take_recv()
        return launch(src, dst, ss, rs, to), ss, rs

    def arrival(dst, ss, rs, to):
        return pltpu.make_async_remote_copy(
            src_ref=dst, dst_ref=dst, send_sem=ss, recv_sem=rs, device_id=to, device_id_type=MESH
        )

    to1, to2, to3 = {"fsdp": f1}, {"fsdp": f2}, {"fsdp": f3}
    peers = ((f1, to1), (f2, to2), (f3, to3))

    barrier = pltpu.get_barrier_semaphore()
    for to in (to1, to2, to3, {"dp": right}, {"dp": left}):
        pl.semaphore_signal(barrier, inc=1, device_id=to, device_id_type=MESH)

    loads = {}
    for i, (src, dst) in enumerate(
        (
            (g.wqkv, g.wqkv_v),
            (g.w1, g.w1_v),
            (g.wo, g.wo_v),
            (g.mask, g.mask_v),
            (g.tok, g.TA.at[f]),
            (g.w2, g.w2_v),
            (g.cot, g.CA.at[f]),
            (g.trig, g.trig_v),
        )
    ):
        c = pltpu.make_async_copy(src, dst, lsem.at[i])
        c.start()
        loads[i] = c
    vectors = []
    for k in range(8):
        vectors.append(pltpu.make_async_copy(given["in%d" % k], given["v%d" % k], lsem.at[8 + k]))
        vectors[k].start()

    AS, AQ, WO, A1, A2 = g.AS, g.AQ, g.WO, g.A1, g.A2
    TA, CA = g.TA, g.CA

    loads[5].wait()
    A2[p] = g.w2_v[...].astype(BF)
    loads[0].wait()
    for j in range(NF):
        for t in range(3):
            g.sq[j, :, C * t : C * t + C] = g.wqkv_v[:, D * t + C * j : D * t + C * j + C].astype(BF)
    AQ[p, pl.ds(pl.multiple_of(R * f, R), R), :] = g.sq[f]
    loads[2].wait()
    WO[p, f] = g.wo_v[...].astype(BF)
    pl.semaphore_wait(barrier, 5)

    def scatter(src, dst, three):
        ss, rs = sems.take_send(), sems.take_recv()
        for fj, to in peers:
            launch(src(fj), dst(f), ss, rs, to)
        return (arrival(three, ss, rs, to1),)

    class AllGather4:
        def __init__(self, slot):
            self.slot = slot
            self.done = False
            c, ss, rs = remote(slot(f), slot(f), to2)
            d, sd, rd = remote(slot(f), slot(f), to1)
            self.across = arrival(slot(f2), ss, rs, to2)
            self.beside = arrival(slot(f1), sd, rd, to1)
            self.copies = [c, d]

        def forward(self):
            self.across.wait_recv()
            c, ss, rs = remote(self.slot(f2), self.slot(f2), to1)
            self.passed = arrival(self.slot(f3), ss, rs, to1)
            self.copies.append(c)

        def finish(self):
            if not self.done:
                self.done = True
                self.beside.wait_recv()
                self.passed.wait_recv()
                sent(self.copies)

    class ReduceScatter4:
        def __init__(self, part, r1, xs, r2):
            self.part, self.r1, self.xs, self.r2 = part, r1, xs, r2
            c, ss, rs = remote(part.at[f3], r1.at[1], to1)
            d, sd, rd = remote(part.at[f1], r1.at[0], to1)
            self.other = arrival(r1.at[1], ss, rs, to1)
            self.own = arrival(r1.at[0], sd, rd, to1)
            self.copies = [c, d]

        def forward(self):
            self.other.wait_recv()
            self.xs[...] = (self.part[f2].astype(F32) + self.r1[1].astype(F32)).astype(BF)
            c, ss, rs = remote(self.xs, self.r2, to2)
            self.across = arrival(self.r2, ss, rs, to2)
            self.copies.append(c)

        def finish(self):
            self.own.wait_recv()
            self.across.wait_recv()
            sent(self.copies)

        def total(self):
            return self.part[f].astype(F32) + self.r1[0].astype(F32) + self.r2[...].astype(F32)

    class RingGather:
        def __init__(self, view, pair, rows):
            self.view, self.pair, self.rows = view, pair, rows
            self.before, self.flight = (), None

        def landed(self):
            received(self.before)
            self.before = ()
            if self.flight is not None:
                received([self.flight])
                sems.ring_landed(self.flight.dst_sem, self.at)
                self.flight = None

        def step(self, r):
            self.landed()
            h = self.rows // 2
            spans = ((0, self.rows), (0, self.rows)) if r < last else ((0, h), (h, h))
            ss = sems.take_send()
            rs, self.at = sems.ring_sent()
            for way, (s, c) in zip((1, -1), spans):
                piece = self.view(idx(pos - way * r), s, c)
                launch(piece, piece, ss, rs, {"dp": right if way == 1 else left})
            both = self.pair if r < last else self.view(0, 0, self.rows)
            self.flight = arrival(both, ss, rs, {"dp": left})

        def finish(self):
            self.landed()

    def row_rings(ref):
        h = ref.shape[1] // 2

        def ring(offset):
            view = lambda slot, s, c: ref.at[slot, pl.ds(offset + s, c), :]
            return RingGather(view, ref.at[pl.ds(0, 2), pl.ds(offset, h), :], h)

        return [ring(0), ring(h)]

    q_ring, w1_ring, w2_ring = row_rings(AQ), row_rings(A1), row_rings(A2)
    o_ring = RingGather(lambda slot, s, c: WO.at[slot, f, pl.ds(s, c), :], WO.at[pl.ds(0, 2), f], R)
    s_ring = RingGather(lambda slot, s, c: AS.at[slot, pl.ds(s, c)], AS.at[pl.ds(0, 2)], NF)

    class RingReduce:
        def __init__(self, grads, start, rows, st, rr, rl, wire=BF):
            self.G, self.o, self.rows, self.st, self.rr, self.rl = grads, start, rows, st, rr, rl
            self.wire = wire
            self.flight = None

        def landed(self):
            if self.flight is not None:
                received([self.flight])
                sems.ring_landed(self.flight.dst_sem, self.at)
                self.flight = None

        def step(self, r):
            self.landed()
            o, rows = self.o, self.rows
            hh = rows // 2
            whole = pl.ds(o, rows)
            ss = sems.take_send()
            rs, self.at = sems.ring_sent()
            ways = ((1, self.rr, 0, {"dp": right}), (-1, self.rl, hh, {"dp": left}))
            if r == 0:
                far = idx(pos + n // 2)
                self.st[whole, :] = self.G[far, whole, :].astype(self.wire)
                for _, buf, s, to in ways:
                    half = pl.ds(o + s, hh)
                    launch(self.st.at[half, :], buf.at[0, half, :], ss, rs, to)
                self.flight = arrival(self.st.at[whole, :], ss, rs, {"dp": left})
                return
            for way, buf, s, to in ways:
                c = idx(pos + way * (n // 2 - r))
                if r == 1:
                    half, other = pl.ds(o + s, hh), pl.ds(o + hh - s, hh)
                    total = buf[0, half, :].astype(F32) + self.G[c, half, :].astype(F32)
                    buf[0, half, :] = total.astype(self.wire)
                    buf[0, other, :] = self.G[c, other, :].astype(self.wire)
                else:
                    total = buf[r - 1, whole, :].astype(F32) + self.G[c, whole, :].astype(F32)
                    buf[r - 1, whole, :] = total.astype(self.wire)
                launch(buf.at[r - 1, whole, :], buf.at[r, whole, :], ss, rs, to)
            self.flight = arrival(self.rr.at[pl.ds(0, 2), whole, :], ss, rs, {"dp": left})

        def finish(self):
            self.landed()

        def total(self):
            o, rows = self.o, self.rows
            return (
                self.G[p, pl.ds(o, rows), :].astype(F32)
                + self.rr[last, pl.ds(o, rows), :].astype(F32)
                + self.rl[last, pl.ds(o, rows), :].astype(F32)
            )

    st = types.SimpleNamespace(oa=[None, None])
    N1, N2, GT, PT = g.N1, g.N2, g.GT, g.PT
    VEC, BQ, BG, VG = g.VEC, g.BQ, g.BG, g.VG
    Q, K, W, QV, KV, WV = g.Q, g.K, g.W, g.QV, g.KV, g.WV
    SM, OV, PV, OA, OT = g.SM, g.OV, g.PV, g.OA, g.OT
    XV, N1V, DY, X1V, N2V = g.XV, g.N1V, g.DY, g.X1V, g.N2V
    GV, GP, DH, PN, PF = g.GV, g.GP, g.DH, g.PN, g.PF
    G2, G1, GQ, GO = g.G2, g.G1, g.GQ, g.GO
    DO, DPRE = g.DO, g.DPRE
    E1, F1, EQ, FQ, SG = g.E1, g.g1_o, g.EQ, g.gq_o, g.SG
    blocks = [slice(256 * k, 256 * k + 256) for k in range(D // 256)]
    mine = pl.ds(pl.multiple_of(V * f, V), V)
    hc, hr = HC // 2, RP // 2
    g2_ring = [
        RingReduce(G2, 0, hc, g.st2, g.rr2, g.rl2),
        RingReduce(G2, hc, hc, g.st2, g.rr2, g.rl2),
    ]
    g1_ring = [
        RingReduce(G1, 0, hr, g.st1, g.rr1, g.rl1),
        RingReduce(G1, hr, hr, g.st1, g.rr1, g.rl1),
    ]
    gq_ring = [
        RingReduce(GQ, 0, hr, g.stq, g.rrq, g.rlq),
        RingReduce(GQ, hr, hr, g.stq, g.rrq, g.rlq),
    ]
    go_ring = RingReduce(GO, 0, R, g.sto, g.rro, g.rlo)
    gs_ring = RingReduce(VG, 0, 16, g.sts, g.rrs, g.rls, F32)

    def finish(*rings):
        for r in rings:
            r.finish()

    def vec(k):
        return VEC[k : k + 1, :]

    def start():
        part = lambda j: AQ.at[p, pl.ds(pl.multiple_of(R * j, R), R), :]
        q_ring[0].before = scatter(lambda j: g.sq.at[j], part, AQ.at[0, pl.ds(0, 3 * R), :])

    def small_start():
        for c in vectors:
            c.wait()
        loads[3].wait()
        SV = g.small_v
        SV[...] = jnp.zeros(SV.shape, F32)
        for k in range(8):
            row, at = ((0, R * k), (1, R * (k - 4)), (2, 0), (3, 0))[0 if k < 4 else 1 if k < 6 else k - 4]
            value = given["v%d" % k][...]
            width = value.shape[1]
            wide = value if width == 128 else jnp.concatenate([value, jnp.zeros((1, 128 - width), F32)], axis=1)
            SV[row : row + 1, :] += wide if at == 0 else pltpu.roll(wide, at, 1)
        mask = g.mask_v[...].astype(F32)
        below = lax.broadcasted_iota(jnp.int32, (128, 128), 0) <= lax.broadcasted_iota(jnp.int32, (128, 128), 1)
        tri = jnp.where(below, 1.0, 0.0).astype(BF)
        count = g.counts[0, 0].astype(F32)
        before = jnp.zeros((1, 1), F32)
        for k in range(2):
            ones = mask[:, 128 * k : 128 * k + 128]
            running = dot(jnp.broadcast_to(ones, (8, 128)).astype(BF), tri)[0:1, :] + before
            SV[4 + k : 5 + k, :] = jnp.where(running <= count, ones, 0.0)
            before = before + jnp.sum(ones, axis=1, keepdims=True)
        AS[p, f] = SV[...]
        st.s = scatter(lambda j: AS.at[p, f], lambda j: AS.at[p, j], AS.at[0, pl.ds(0, 3)])
        s_ring.before = st.s

    def cast_fc1():
        loads[1].wait()
        for j in range(NF):
            for t in range(n):
                at = HC * (NF * t + j)
                g.s1[j, :, HC * t : HC * t + HC] = g.w1_v[:, at : at + HC].astype(BF)
        A1[p, pl.ds(pl.multiple_of(R * f, R), R), :] = g.s1[f]
        part = lambda j: A1.at[p, pl.ds(pl.multiple_of(R * j, R), R), :]
        w1_ring[0].before = scatter(lambda j: g.s1.at[j], part, A1.at[0, pl.ds(0, 3 * R), :])

    def tokens_start():
        loads[4].wait()
        st.tok = AllGather4(lambda j: TA.at[j])

    def cot_start():
        loads[6].wait()
        st.cot = AllGather4(lambda j: CA.at[j])

    def wo_start():
        o_ring.finish()
        st.wo = AllGather4(lambda j: WO.at[:, j])

    ends = []
    total_len = jnp.int32(0)
    for k in range(g.lengths.shape[1]):
        total_len = total_len + g.lengths[0, k]
        ends.append(total_len)

    def key_segments():
        keyrow = lax.broadcasted_iota(jnp.int32, (1, S_), 1)
        segrow = jnp.zeros((1, S_), jnp.int32)
        for end in ends:
            segrow += (keyrow >= end).astype(jnp.int32)
        return segrow

    def layout():
        row, _seg = column_segment(0, S_, ends)
        before = jnp.zeros((S_, 1), jnp.int32)
        for k, end in enumerate(ends):
            before += jnp.where(row >= end, g.lengths[0, k], 0)
        place = row - before
        img = GRID * GRID
        frame = jnp.zeros((S_, 1), jnp.int32)
        for t in range(1, FRAMES):
            frame += (place >= img * t).astype(jnp.int32)
        rest = place - img * frame
        grow = jnp.zeros((S_, 1), jnp.int32)
        for t in range(1, GRID):
            grow += (rest >= GRID * t).astype(jnp.int32)
        gcol = rest - GRID * grow
        lane = lax.broadcasted_iota(jnp.int32, (S_, 128), 1)
        hot = (lane == frame) | (lane == grow + FRAMES) | (lane == gcol + (FRAMES + GRID))
        g.OH[...] = jnp.where(hot, 1.0, 0.0).astype(BF)
        loads[7].wait()
        g.CS[...] = sum(dot(g.OH[...], g.trig_v[k]) for k in range(3))

    def visible():
        if s_ring.before:
            received(s_ring.before)
            s_ring.before = ()
        vis8 = jnp.concatenate([AS[p, j][4:6, :] for j in range(NF)], axis=0)
        above = lax.broadcasted_iota(jnp.int32, (128, 128), 0)
        tri = above <= lax.broadcasted_iota(jnp.int32, (128, 128), 1)
        within = dot(vis8.astype(BF), jnp.where(tri, 1.0, 0.0).astype(BF))
        base = jnp.zeros((1, 128), F32)
        pieces, vpieces = [], []
        for k in range(8):
            pieces.append(within[k : k + 1, :] + base)
            vpieces.append(vis8[k : k + 1, :])
            base = base + jnp.sum(vis8[k : k + 1, :], axis=1, keepdims=True)
        incl = jnp.concatenate(pieces, axis=1)
        visrow = jnp.concatenate(vpieces, axis=1)
        rank = jnp.where(visrow > 0.5, incl - 1.0, -1.0).astype(jnp.int32)
        sel = lax.broadcasted_iota(jnp.int32, (VP, S_), 0) == rank
        SM[...] = jnp.where(sel, 1.0, 0.0).astype(BF)

    def rounded(v):
        return v.astype(BF).astype(F32)

    def turn(v, by):
        by = by % 128
        return v if by == 0 else pltpu.roll(v, by, 1)

    def small_vectors():
        s_ring.finish()
        lane128 = lax.broadcasted_iota(jnp.int32, (n, 128), 1)
        rows0 = [AS[:, j, 0, :] for j in range(NF)]
        rows1 = [AS[:, j, 1, :] for j in range(NF)]
        rows2 = [AS[:, j, 2, :] for j in range(NF)]
        for k in range(6):
            src = rows0 if k < 4 else rows1
            piece = jnp.zeros((n, 128), F32)
            for j in range(NF):
                piece = jnp.where(lax.div(lane128, R) == j, turn(src[j], R * (j - k % 4)), piece)
            for q in range(n):
                VEC[k : k + 1, 128 * q : 128 * q + 128] = rounded(piece[q : q + 1, :])
        for q in range(n):
            VEC[6:7, 128 * q : 128 * q + 128] = rounded(AS[q, f][3:4, :])
        t0 = jnp.where(lane128 < 96, rows2[0], turn(rows2[1], 96))
        t1 = jnp.where(lane128 < 64, turn(rows2[1], -32), turn(rows2[2], 64))
        t2 = jnp.where(lane128 < 32, turn(rows2[2], -64), turn(rows2[3], 32))
        for q in range(n):
            for k, t in enumerate((t0, t1, t2)):
                BQ[0:1, 384 * q + 128 * k : 384 * q + 128 * k + 128] = rounded(t[q : q + 1, :])

    def first_norm():
        st.tok.finish()

        def block(b, _):
            xhat, _inv = norm_stats(TA[b].astype(F32))
            N1[b] = (xhat * vec(0) + vec(1)).astype(BF)
            return 0

        lax.fori_loop(0, NF, block, 0)

    def project_half(part):
        finish(*q_ring)

        def block(b, _):
            rows = pl.ds(pl.multiple_of(b * T, T), T)
            cs = g.CS[rows, :]
            for t, dst in enumerate((Q, K, W)):
                out = dot(N1[b], AQ[:, :, C * t : C * t + C].reshape(D, C))
                out = out + BQ[0:1, pl.ds(pl.multiple_of(D * t + C * f, 128), C)]
                if t == 2:
                    dst[rows, :] = out.astype(BF)
                    continue
                for hh in range(C // 128):
                    u = out[:, 128 * hh : 128 * hh + 128]
                    u = (u * cs[:, :128] + swap_halves(u) * cs[:, 128:]).astype(BF)
                    dst[rows, 128 * hh : 128 * hh + 128] = u * BF(0.125) if t == 0 else u
            return 0

        lax.fori_loop(NF // 2 * part, NF // 2 * (part + 1), block, 0)

    lane_c = lax.broadcasted_iota(jnp.int32, (1, C), 1)
    hmask = [jnp.where(lax.div(lane_c, HDIM) == hd, 1.0, 0.0) for hd in range(C // HDIM)]

    def softmax(s):
        e = jnp.exp(s - jnp.max(s, axis=-1, keepdims=True))
        return e * (1.0 / jnp.sum(e, axis=-1, keepdims=True))

    def context_attention():
        for src, dst in ((Q, QV), (K, KV), (W, WV)):
            dst[...] = dot(SM[...], src[...]).astype(BF)
        segrow = key_segments()
        seg8 = jnp.broadcast_to(segrow.astype(F32), (8, S_)).astype(BF)
        segv_row = dot(seg8, SM[...], NT)[0:1, :].astype(jnp.int32)
        segv_col = jnp.sum(SM[...].astype(F32) * segrow.astype(F32), axis=1, keepdims=True).astype(jnp.int32)
        same = segv_col == segv_row
        acc = jnp.zeros((VP, C), F32)
        for hd in range(C // HDIM):
            s = dot(QV[...] * hmask[hd].astype(BF), KV[...], NT)
            pr = softmax(jnp.where(same, s, FILL))
            PV[hd] = pr
            acc += dot(pr.astype(BF), WV[...]) * hmask[hd]
        OV[f] = acc.astype(BF)
        st.ov = AllGather4(lambda j: OV.at[j])

    def attend_target(b, pair):
        rows = slice(T * b, T * b + T)
        _, segq = column_segment(b * T, T, ends)
        same = segq == key_segments()
        for hd in (2 * pair, 2 * pair + 1):
            s = dot(Q[rows, :] * hmask[hd].astype(BF), K[...], NT)
            pr = softmax(jnp.where(same, s, FILL)).astype(BF)
            o = dot(pr, W[...])
            cols = slice(HDIM * hd, HDIM * hd + HDIM)
            OA[f, rows, cols] = o[:, cols].astype(BF)

    def oa_start(part):
        rows = pl.ds(S_ // 2 * part, S_ // 2)
        st.oa[part] = AllGather4(lambda j: OA.at[j, rows, :])

    def select_rows():
        for cols in blocks:
            XV[:, cols] = dot(SM[...], TA[:, :, cols].reshape(S_, 256)).astype(BF)
            N1V[:, cols] = dot(SM[...], N1[:, :, cols].reshape(S_, 256)).astype(BF)

    def select_cot():
        st.cot.finish()
        for cols in blocks:
            DY[:, cols] = dot(SM[...], CA[:, :, cols].reshape(S_, 256)).astype(BF)

    def out_project(parts, cols):
        heads = [WO[n // NF * j : n // NF * (j + 1), :, :, cols].reshape(C, -1) for j in range(NF)]
        return sum(dot(parts(j), heads[j]) for j in range(NF))

    def context_middle():
        st.wo.finish()
        st.ov.finish()
        for cols in blocks:
            X1V[:, cols] = XV[:, cols].astype(F32) + (out_project(lambda j: OV[j], cols) + VEC[4:5, cols])
        xhat, _inv = norm_stats(X1V[...])
        N2V[...] = (xhat * vec(2) + vec(3)).astype(BF)

    def normal_cdf(hid):
        return 0.5 * (1.0 + lax.erf(hid * (1.0 / math.sqrt(2.0))))

    def context_hidden():
        finish(*w1_ring)
        for cols in blocks:
            hid = dot(N2V[...], A1[:, :, cols].reshape(D, 256)) + VEC[6:7, cols]
            cdf = normal_cdf(hid)
            GV[:, cols] = (hid * cdf).astype(BF)
            GP[:, cols] = cdf + hid * (jnp.exp(-0.5 * hid * hid) * (1.0 / math.sqrt(2.0 * math.pi)))

    def outer(dst, lhs, rhs):
        for k, cols in enumerate(blocks):
            g.LT[cols, :] = lhs[:, cols].astype(F32).T.astype(BF)

        def one(k, _):
            rows = pl.ds(pl.multiple_of(512 * k, 512), 512)
            for c in range(dst.shape[2] // 256):
                cols = slice(256 * c, 256 * c + 256)
                part = dot(g.LT[rows, :], rhs[:, cols]).astype(dst.dtype)
                dst[pl.ds(4 * k, 4), :, cols] = part.reshape(4, 128, 256)
            return 0

        lax.fori_loop(0, n // 4, one, 0)

    def put_grad(k, vrow):
        for q in range(n):
            VG[q, k : k + 1, :] = vrow[:, 128 * q : 128 * q + 128]

    def fc2_grad():
        outer(G2, GV, DY)

    def hidden_grad():
        finish(*w2_ring)
        for k, cols in enumerate(blocks):
            dg = dot(DY[...], A2[...].reshape(HF, D)[256 * k : 256 * k + 256, :], NT)
            dh = (dg * GP[:, cols]).astype(BF)
            DH[:, cols] = dh
            dc1 = jnp.sum(dh.astype(F32), axis=0, keepdims=True)
            for q in range(2):
                for j in range(NF):
                    piece = dc1[:, 128 * q : 128 * q + 128]
                    VG[2 * k + q, 9 + j : 10 + j, :] = jnp.where(f == j, piece, jnp.zeros((1, 128), F32))

    def second_grad():
        for k, cols in enumerate(blocks):
            part = dot(DH[...], A1[2 * k : 2 * k + 2].reshape(256, HF), NT).astype(BF)
            PN[:, :, cols] = part.reshape(NF, V, 256)
        st.n2 = ReduceScatter4(PN, g.PNr1, g.PNxs, g.PNr2)

    def fc1_grad():
        outer(G1, N2V, DH)

    def context_partial():
        for cols in blocks:
            part = dot(GV[...], A2[:, :, cols].reshape(HF, 256)).astype(BF)
            PF[:, :, cols] = part.reshape(NF, V, 256)
        st.pf = ReduceScatter4(PF, g.PFr1, g.PFxs, g.PFr2)

    def second_norm_back():
        st.n2.finish()
        dyo = DY[mine, :].astype(F32)
        dv, dgain, dshift = norm_back(X1V[mine, :], vec(2), st.n2.total())
        dx1 = dyo + dv
        g.DX1[...] = dx1
        low = dx1.astype(BF)
        g.DP[f] = low
        st.dp = AllGather4(lambda j: g.DP.at[j])
        put_grad(2, dgain)
        put_grad(3, dshift)
        put_grad(4, jnp.sum(low.astype(F32), axis=0, keepdims=True))
        put_grad(5, jnp.sum(dyo, axis=0, keepdims=True))

    def transpose_attended():
        st.ov.finish()
        for j in range(NF):
            ot = OV[j].astype(F32).T.astype(BF)
            OT[n // NF * j : n // NF * (j + 1)] = ot.reshape(n // NF, NF, R, VP)

    def out_grad():
        st.dp.finish()
        go = dot(OT[:, f].reshape(n * R, VP), g.DP[...].reshape(VP, D))
        GO[...] = go.reshape(n, R, D)

    def attended_grad():
        st.dp.finish()
        st.wo.finish()
        wo_heads = WO[pl.ds(n // NF * f, n // NF)].reshape(C, D)
        DO[...] = dot(g.DP[...].reshape(VP, D), wo_heads, NT).astype(BF)

    def attention_back():
        dq = jnp.zeros((VP, C), F32)
        dk = jnp.zeros((VP, C), F32)
        dw = jnp.zeros((VP, C), F32)
        for hd in range(C // HDIM):
            pr = PV[hd]
            dp = dot(DO[...] * hmask[hd].astype(BF), WV[...], NT)
            ds = (pr * (dp - jnp.sum(pr * dp, axis=-1, keepdims=True))).astype(BF)
            dq += dot(ds, KV[...]) * hmask[hd]
            dk += dot(ds, QV[...], TN) * hmask[hd]
            dw += dot(pr.astype(BF), DO[...], TN) * hmask[hd]
        csv = sum(dot(dot(SM[...], g.OH[...]).astype(BF), g.trig_v[k]) for k in range(3))
        for t, (grad, scale) in enumerate(((dq, 0.125), (dk, 1.0))):
            for hh in range(C // 128):
                u = grad[:, 128 * hh : 128 * hh + 128]
                u = u * csv[:, :128] - swap_halves(u) * csv[:, 128:]
                DPRE[:, C * t + 128 * hh : C * t + 128 * hh + 128] = (u * scale).astype(BF)
        DPRE[:, 2 * C :] = dw.astype(BF)

    def qkv_grad():
        outer(GQ, N1V, DPRE)

    def qkv_bias_grad():
        BG[...] = jnp.zeros(BG.shape, F32)
        db = jnp.sum(DPRE[...].astype(F32), axis=0, keepdims=True)
        for t in range(3):
            BG[0:1, pl.ds(pl.multiple_of(D * t + C * f, 128), C)] = db[:, C * t : C * t + C]
        for q in range(n):
            for t in range(3):
                VG[q, 6 + t : 7 + t, :] = BG[0:1, 384 * q + 128 * t : 384 * q + 128 * t + 128]
            VG[q, 13:16, :] = jnp.zeros((3, 128), F32)

    def first_grad():
        for k, cols in enumerate(blocks):
            part = dot(DPRE[...], AQ[2 * k : 2 * k + 2].reshape(256, 3 * C), NT).astype(BF)
            PN[:, :, cols] = part.reshape(NF, V, 256)
        st.n1 = ReduceScatter4(PN, g.PMr1, g.PMxs, g.PMr2)

    def first_norm_back():
        st.n1.finish()
        dv, dgain, dshift = norm_back(XV[mine, :].astype(F32), vec(0), st.n1.total())
        g.DX[f] = (g.DX1[...] + dv).astype(BF)
        st.dx = AllGather4(lambda j: g.DX.at[j])
        put_grad(0, dgain)
        put_grad(1, dshift)

    def context_result():
        st.pf.finish()
        g.CO[f] = (X1V[mine, :] + (st.pf.total() + vec(5))).astype(BF)
        st.co = AllGather4(lambda j: g.CO.at[j])

    def home(src, dst):
        s = SM[:, pl.ds(pl.multiple_of(T * f, 128), T)]
        for cols in blocks:
            dst[:, cols] = dot(s, src[:, :, cols].reshape(VP, 256), TN).astype(BF)

    def home_context():
        st.co.finish()
        home(g.CO, g.ctx_o)

    def home_grad():
        st.dx.finish()
        home(g.DX, g.dx_o)

    def target_middle(b):
        st.wo.finish()
        st.oa[b // 2].finish()
        for cols in blocks:
            g.X1B[:, cols] = TA[b, :, cols].astype(F32) + (
                out_project(lambda j: OA[j, T * b : T * b + T, :], cols) + VEC[4:5, cols]
            )
        x1 = g.X1B[...]
        xh, _inv = norm_stats(x1)
        N2[b] = (xh * vec(2) + vec(3)).astype(BF)

        @pl.when(f == b)
        def _():
            g.X1H[...] = x1

    def target_hidden(b):
        finish(*w1_ring)
        for cols in blocks:
            hid = dot(N2[b], A1[:, :, cols].reshape(D, 256)) + VEC[6:7, cols]
            GT[b, :, cols] = (hid * normal_cdf(hid)).astype(BF)

    def target_out(b):
        finish(*w2_ring)
        for cols in blocks:
            PT[b, :, cols] = dot(GT[b], A2[:, :, cols].reshape(HF, 256)).astype(BF)
        if b == NF - 1:
            st.pt = ReduceScatter4(PT, g.PTr1, g.PTxs, g.PTr2)

    def target_result():
        st.pt.finish()
        g.tgt_o[...] = (g.X1H[...] + (st.pt.total() + vec(5))).astype(BF)

    def fc2_grad_done():
        finish(*g2_ring)
        for k, ring in enumerate(g2_ring):
            g.g2_o[hc * k : hc * k + hc, :] = ring.total()

    def fc1_grad_trade():
        finish(*g1_ring)
        for k, ring in enumerate(g1_ring):
            E1[2 * k : 2 * k + 2] = ring.total().astype(BF).reshape(2, R, HF)
        F1[f] = E1[f]
        st.e1 = scatter(lambda j: E1.at[j], lambda j: F1.at[j], F1.at[pl.ds(0, 3)])

    def fc1_grad_done():
        received(st.e1)

    def out_grad_done():
        go_ring.finish()
        g.go_o[...] = go_ring.total()

    def qkv_grad_trade():
        finish(*gq_ring)
        for k, ring in enumerate(gq_ring):
            EQ[2 * k : 2 * k + 2] = ring.total().astype(BF).reshape(2, R, 3 * C)
        FQ[f] = EQ[f]
        st.eq = scatter(lambda j: EQ.at[j], lambda j: FQ.at[j], FQ.at[pl.ds(0, 3)])

    def qkv_grad_done():
        received(st.eq)

    def small_grad_trade():
        gs_ring.finish()
        SG[f] = gs_ring.total()
        st.sg = scatter(lambda j: SG.at[f], lambda j: SG.at[j], SG.at[pl.ds(0, 3)])

    def small_grad_done():
        received(st.sg)
        g.sg_o[...] = SG[0] + SG[1] + SG[2] + SG[3]

    start()
    o_ring.step(0)
    w2_ring[0].step(0)
    small_start()
    layout()
    cast_fc1()
    w2_ring[1].step(0)
    tokens_start()
    o_ring.step(1)
    cot_start()
    q_ring[0].step(0)
    visible()
    s_ring.step(0)
    q_ring[1].step(0)
    w1_ring[0].step(0)
    o_ring.step(2)
    q_ring[0].step(1)
    s_ring.step(1)
    q_ring[1].step(1)
    w1_ring[1].step(0)
    o_ring.step(3)
    st.tok.forward()
    q_ring[0].step(2)
    s_ring.step(2)
    q_ring[1].step(2)
    w1_ring[0].step(1)
    wo_start()
    w1_ring[1].step(1)
    s_ring.step(3)
    q_ring[0].step(3)
    st.cot.forward()
    q_ring[1].step(3)
    select_cot()
    w2_ring[0].step(1)
    w1_ring[0].step(2)
    small_vectors()
    first_norm()
    select_rows()
    w1_ring[1].step(2)
    project_half(0)
    project_half(1)
    context_attention()
    w1_ring[0].step(3)
    st.wo.forward()
    attend_target(3, 0)
    w2_ring[1].step(1)
    attend_target(0, 0)
    w1_ring[1].step(3)
    attend_target(3, 1)
    w2_ring[0].step(2)
    st.ov.forward()
    attend_target(2, 0)
    attend_target(2, 1)
    oa_start(1)
    context_middle()
    w2_ring[1].step(2)
    context_hidden()
    fc2_grad()
    g2_ring[1].step(0)
    attend_target(1, 0)
    w2_ring[0].step(3)
    attend_target(1, 1)
    transpose_attended()
    w2_ring[1].step(3)
    g2_ring[0].step(0)
    attend_target(0, 1)
    oa_start(0)
    st.oa[1].forward()
    g2_ring[1].step(1)
    hidden_grad()
    fc1_grad()
    g1_ring[0].step(0)
    context_partial()
    g2_ring[0].step(1)
    second_grad()
    g1_ring[1].step(0)
    st.pf.forward()
    st.n2.forward()
    g1_ring[0].step(1)
    st.oa[0].forward()
    target_middle(0)
    g2_ring[0].step(2)
    target_hidden(0)
    context_result()
    target_out(0)
    g1_ring[1].step(1)
    target_middle(1)
    target_hidden(1)
    second_norm_back()
    g1_ring[0].step(2)
    target_middle(2)
    target_middle(3)
    st.co.forward()
    target_hidden(2)
    target_out(2)
    g2_ring[0].step(3)
    home_context()
    g1_ring[1].step(2)
    st.dp.forward()
    target_hidden(3)
    target_out(1)
    attended_grad()
    attention_back()
    g1_ring[0].step(3)
    first_grad()
    target_out(3)
    qkv_grad()
    gq_ring[1].step(0)
    st.n1.forward()
    gq_ring[0].step(0)
    qkv_bias_grad()
    out_grad()
    g1_ring[1].step(3)
    st.pt.forward()
    gq_ring[1].step(1)
    first_norm_back()
    gs_ring.step(0)
    gq_ring[0].step(1)
    fc1_grad_trade()
    go_ring.step(0)
    g2_ring[1].step(2)
    gq_ring[1].step(2)
    gs_ring.step(1)
    gq_ring[0].step(2)
    target_result()
    go_ring.step(1)
    gq_ring[1].step(3)
    gs_ring.step(2)
    st.dx.forward()
    gq_ring[0].step(3)
    home_grad()
    fc1_grad_done()
    go_ring.step(2)
    gs_ring.step(3)
    g2_ring[1].step(3)
    qkv_grad_trade()
    go_ring.step(3)
    small_grad_trade()
    fc2_grad_done()
    qkv_grad_done()
    small_grad_done()
    out_grad_done()


def run_layer(n, tokens, cot, lengths, mask, counts, vectors, wqkv, wo, w1, w2, V):
    T, D = tokens.shape
    NF = 4
    FF = w1.shape[1]
    R = wo.shape[0]
    RP = R * NF
    HC = w2.shape[0]
    HF = HC * n
    C = D // NF
    VP = V * NF
    S_ = T * NF
    h2 = n // 2
    B, F = BF, F32
    vm = pltpu.VMEM
    scratch = dict(
        wqkv_v=vm((R, 3 * D), F), w1_v=vm((R, FF), F), wo_v=vm((R, D), F), w2_v=vm((HC, D), F),
        small_v=vm((8, 128), F), trig_v=vm((3, 128, 256), B),
        sq=vm((NF, R, 3 * C), B), s1=vm((NF, R, HF), B),
        AS=vm((n, NF, 8, 128), F), AQ=vm((n, RP, 3 * C), B), WO=vm((n, NF, R, D), B),
        A1=vm((n, RP, HF), B), A2=vm((n, HC, D), B),
        TA=vm((NF, T, D), B), CA=vm((NF, T, D), B), N1=vm((NF, T, D), B),
        OH=vm((S_, 128), B), CS=vm((S_, 256), F), SM=vm((VP, S_), B),
        VEC=vm((8, D), F), BQ=vm((8, 3 * D), F), BG=vm((8, 3 * D), F),
        Q=vm((S_, C), B), K=vm((S_, C), B), W=vm((S_, C), B),
        QV=vm((VP, C), B), KV=vm((VP, C), B), WV=vm((VP, C), B),
        OV=vm((NF, VP, C), B), PV=vm((C // HDIM, VP, VP), F), OA=vm((NF, S_, C), B),
        XV=vm((VP, D), B), N1V=vm((VP, D), B), DY=vm((VP, D), B),
        X1V=vm((VP, D), F), N2V=vm((VP, D), B), GV=vm((VP, HF), B), GP=vm((VP, HF), F),
        G2=vm((n, HC, D), B), G1=vm((n, RP, HF), B), GQ=vm((n, RP, 3 * C), B), GO=vm((n, R, D), F),
        VG=vm((n, 16, 128), F),
        st2=vm((HC, D), B), rr2=vm((h2, HC, D), B), rl2=vm((h2, HC, D), B),
        st1=vm((RP, HF), B), rr1=vm((h2, RP, HF), B), rl1=vm((h2, RP, HF), B),
        stq=vm((RP, 3 * C), B), rrq=vm((h2, RP, 3 * C), B), rlq=vm((h2, RP, 3 * C), B),
        sto=vm((R, D), B), rro=vm((h2, R, D), B), rlo=vm((h2, R, D), B),
        sts=vm((16, 128), F), rrs=vm((h2, 16, 128), F), rls=vm((h2, 16, 128), F),
        DH=vm((VP, HF), B), PN=vm((NF, V, D), B), PF=vm((NF, V, D), B),
        PNr1=vm((2, V, D), B), PNxs=vm((V, D), B), PNr2=vm((V, D), B),
        PMr1=vm((2, V, D), B), PMxs=vm((V, D), B), PMr2=vm((V, D), B),
        PFr1=vm((2, V, D), B), PFxs=vm((V, D), B), PFr2=vm((V, D), B),
        DX1=vm((V, D), F), DP=vm((NF, V, D), B), OT=vm((n, NF, R, VP), B), DO=vm((VP, C), B),
        DPRE=vm((VP, 3 * C), B), CO=vm((NF, V, D), B), DX=vm((NF, V, D), B),
        X1H=vm((T, D), F), GT=vm((NF, T, HF), B),
        PTr1=vm((2, T, D), B), PTxs=vm((T, D), B), PTr2=vm((T, D), B),
        SG=vm((NF, 16, 128), F),
        E1=vm((NF, R, HF), B), EQ=vm((NF, R, 3 * C), B),
        send_sems=pltpu.SemaphoreType.DMA((16,)), recv_sems=pltpu.SemaphoreType.DMA((59,)),
        local_sems=pltpu.SemaphoreType.DMA((16,)), mask_v=vm((1, T), jnp.int32), LT=vm((D, VP), B),
    )
    arr = jax.ShapeDtypeStruct
    ins = dict(
        lengths=lengths, counts=counts, tok=tokens, cot=cot, mask=mask.reshape(1, T), wqkv=wqkv, wo=wo,
        w1=w1, w2=w2, trig=jnp.asarray(trig_table()),
    )
    for k, v in enumerate(vectors):
        ins["in%d" % k] = v.reshape(1, -1)
        scratch["v%d" % k] = vm((1, v.shape[0]), F)
    outs = dict(
        tgt_o=vm((T, D), B), ctx_o=vm((T, D), B), dx_o=vm((T, D), B), gq_o=vm((NF, R, 3 * C), B),
        go_o=vm((R, D), F), g1_o=vm((NF, R, HF), B), g2_o=vm((HC, D), F), sg_o=vm((16, 128), F),
    )
    names = [*ins, *outs, *scratch]
    any_spec = pl.BlockSpec(memory_space=pl.ANY)
    return pl.pallas_call(
        functools.partial(layer_kernel, (n, D, FF, T, V), names),
        out_shape=list(outs.values()),
        in_specs=[pl.BlockSpec(memory_space=pltpu.SMEM)] * 2 + [any_spec] * (len(ins) - 2),
        out_specs=[pl.BlockSpec(memory_space=pltpu.VMEM)] * 8,
        scratch_shapes=list(scratch.values()),
        compiler_params=pltpu.CompilerParams(
            collective_id=0, has_side_effects=True, vmem_limit_bytes=62000000
        ),
        name="layer",
    )(*ins.values())


def outputs_kernel(dims, count, *refs):
    n, R, C, HC = dims
    NF = 4
    f = lax.axis_index("fsdp")
    tgt, ctx, dx, gq, go, g1, g2, sg = refs[:8]
    tgt_o, ctx_o, dx_o, gq_o, go_o, g1_o, g2_o = refs[8:15]
    vec_o = refs[15:23]
    gq_w, g1_w, sem_out = refs[23:]
    stores = []

    def store(src, dst):
        c = pltpu.make_async_copy(src, dst, sem_out.at[len(stores)])
        c.start()
        stores.append(c)

    for src, dst in ((g2, g2_o), (tgt, tgt_o), (ctx, ctx_o), (dx, dx_o), (go, go_o)):
        store(src, dst)
    D = NF * C
    for j in range(NF):
        for t in range(3):
            gq_w[:, D * t + C * j : D * t + C * j + C] = gq[j, :, C * t : C * t + C].astype(F32)
    store(gq_w, gq_o)
    for j in range(NF):
        for t in range(n):
            at = HC * (NF * t + j)
            g1_w[:, at : at + HC] = g1[j, :, HC * t : HC * t + HC].astype(F32)
    store(g1_w, g1_o)
    small = sg
    for k in range(6):
        vec_o[k][...] = pltpu.roll(small[k : k + 1, :], lax.rem(128 - R * f, 128), 1)[:, :R]
    rows = jnp.concatenate([small[6 + t : 7 + t, :] for t in range(3)], axis=1)
    vec_o[6][...] = pltpu.roll(rows, lax.rem(384 - 3 * R * f, 384), 1)[:, : 3 * R]
    mine = jnp.zeros((1, 128), F32)
    for j in range(NF):
        mine = jnp.where(f == j, small[9 + j : 10 + j, :], mine)
    vec_o[7][...] = mine
    for c in stores:
        c.wait()


def write_outputs(n, parts, R, D, FF, HC):
    NF = 4
    C = D // NF
    tgt = parts[0]
    arr = jax.ShapeDtypeStruct
    any_spec = pl.BlockSpec(memory_space=pl.ANY)
    big = [
        arr(tgt.shape, BF), arr(tgt.shape, BF), arr(tgt.shape, BF),
        arr((R, 3 * D), F32), arr((R, D), F32), arr((R, FF), F32), arr((HC, D), F32),
    ]
    small = [arr((1, w), F32) for w in (R,) * 6 + (3 * R, 4 * R)]
    return pl.pallas_call(
        functools.partial(outputs_kernel, (n, R, C, HC), 8),
        out_shape=big + small,
        in_specs=[pl.BlockSpec(memory_space=pltpu.VMEM)] * 8,
        out_specs=[any_spec] * 7 + [pl.BlockSpec(memory_space=pltpu.VMEM)] * 8,
        scratch_shapes=[
            pltpu.VMEM((R, 3 * D), F32), pltpu.VMEM((R, FF), F32), pltpu.SemaphoreType.DMA((7,)),
        ],
        compiler_params=pltpu.CompilerParams(vmem_limit_bytes=1 << 22),
        name="outputs",
    )(*[pltpu.with_memory_space_constraint(v, pltpu.VMEM) for v in parts])


def on_device(
    tokens, lengths, visibility_mask, visible_counts, ln1_gain, ln1_bias, qkv_weight, qkv_bias,
    out_weight, out_bias, ln2_gain, ln2_bias, fc1_weight, fc1_bias, fc2_weight, fc2_bias, context_cot,
):
    n = lax.axis_size("dp")
    R, D = out_weight.shape
    vectors = (ln1_gain, ln1_bias, ln2_gain, ln2_bias, out_bias, fc2_bias, qkv_bias, fc1_bias)
    parts = run_layer(
        n, tokens, context_cot, lengths, visibility_mask, visible_counts, vectors,
        qkv_weight, out_weight, fc1_weight, fc2_weight, VIS_DEV,
    )
    tgt, ctx, dx, gq, go, g1, g2, *small = write_outputs(
        n, parts, R, D, fc1_weight.shape[1], fc2_weight.shape[0]
    )
    gg1, gb1, gg2, gb2, gbo, gc2, gbq, gc1 = [v.reshape(-1) for v in small]
    return (tgt, ctx, dx, gg1, gb1, gq, gbq, go, gbo, gg2, gb2, g1, gc1, g2, gc2)


def layer_norm(inputs, scale_vec, shift_vec):
    center = inputs - jnp.mean(inputs, axis=-1, keepdims=True)
    spread = jnp.mean(center * center, axis=-1, keepdims=True)
    return center * lax.rsqrt(spread + norm_eps) * scale_vec + shift_vec


def gelu_erf(values):
    return jax.nn.gelu(values, approximate=False)


def pack_layout(seq_lens, pack_len):
    seq_ends = jnp.cumsum(seq_lens)
    places = jnp.arange(pack_len, dtype=jnp.int32)
    passed = places[:, None] >= seq_ends[None, :]
    segment = jnp.sum(passed.astype(jnp.int32), axis=1)
    before = jnp.sum(jnp.where(passed, seq_lens[None, :], 0), axis=1)
    return (segment, places - before)


def rope_tables(places):
    frame_index = (places // (GRID * GRID)).astype(jnp.float32)
    grid_row = (places // GRID % GRID).astype(jnp.float32)
    grid_col = (places % GRID).astype(jnp.float32)
    pair_index = jnp.arange(HDIM // 2, dtype=jnp.int32)
    axis_pick = jnp.minimum(pair_index // 11, 2)
    pair_order = (pair_index - 11 * axis_pick).astype(jnp.float32)
    frequency = jnp.exp(pair_order * (-math.log(10000.0) / 11.0))
    angles = (
        frame_index[:, None] * (axis_pick == 0).astype(jnp.float32)[None, :]
        + grid_row[:, None] * (axis_pick == 1).astype(jnp.float32)[None, :]
        + grid_col[:, None] * (axis_pick == 2).astype(jnp.float32)[None, :]
    ) * frequency[None, :]
    return (jnp.cos(angles), jnp.sin(angles))


def rotate(heads, cosine_table, sine_table):
    half_size = heads.shape[-1] // 2
    first_half = heads[..., :half_size]
    second_half = heads[..., half_size:]
    cosine_cols = cosine_table[:, None, :]
    sine_cols = sine_table[:, None, :]
    return jnp.concatenate(
        [
            first_half * cosine_cols - second_half * sine_cols,
            second_half * cosine_cols + first_half * sine_cols,
        ],
        axis=-1,
    )


def rotate_back(grads, cosine_table, sine_table):
    half_size = grads.shape[-1] // 2
    first_half = grads[..., :half_size]
    second_half = grads[..., half_size:]
    cosine_cols = cosine_table[:, None, :]
    sine_cols = sine_table[:, None, :]
    return jnp.concatenate(
        [
            first_half * cosine_cols + second_half * sine_cols,
            second_half * cosine_cols - first_half * sine_cols,
        ],
        axis=-1,
    )


def project(token_rows, weights, cosine_table, sine_table):
    inputs = token_rows.astype(jnp.float32)
    row_count = inputs.shape[0]
    model_width = inputs.shape[1]
    normed = layer_norm(
        inputs, weights[0].astype(jnp.float32), weights[1].astype(jnp.float32)
    ).astype(jnp.bfloat16)
    joined = jnp.dot(normed, weights[2], preferred_element_type=jnp.float32) + weights[3].astype(
        jnp.float32
    )
    query_heads = rotate(
        joined[:, :model_width].reshape(row_count, HEADS, HDIM), cosine_table, sine_table
    ).astype(jnp.bfloat16)
    key_flat = (
        rotate(
            joined[:, model_width : 2 * model_width].reshape(row_count, HEADS, HDIM),
            cosine_table,
            sine_table,
        )
        .astype(jnp.bfloat16)
        .reshape(row_count, model_width)
    )
    value_flat = joined[:, 2 * model_width :].astype(jnp.bfloat16)
    return (inputs, normed, query_heads, key_flat, value_flat)


def attend(query_heads, key_flat, value_flat, seg_query, seg_key):
    key_heads = key_flat.reshape(key_flat.shape[0], HEADS, HDIM)
    value_heads = value_flat.reshape(value_flat.shape[0], HEADS, HDIM)
    scores = jnp.einsum(
        "qhd,khd->hqk", query_heads, key_heads, preferred_element_type=jnp.float32
    ) * HDIM ** (-0.5)
    allowed = seg_query[:, None] == seg_key[None, :]
    masked = jnp.where(allowed[None], scores, masked_fill)
    row_max = jnp.max(masked, axis=-1, keepdims=True)
    raised = jnp.exp(masked - row_max)
    totals = jnp.sum(raised, axis=-1, keepdims=True)
    attn_probs = (raised / totals).astype(jnp.bfloat16)
    attended = jnp.einsum(
        "hqk,khd->qhd", attn_probs, value_heads, preferred_element_type=jnp.float32
    )
    return (
        attended.reshape(query_heads.shape[0], -1).astype(jnp.bfloat16),
        row_max + jnp.log(totals),
    )


def attend_back(query_heads, key_flat, value_flat, seg_query, seg_key, log_total, grad_att):
    key_heads = key_flat.reshape(key_flat.shape[0], HEADS, HDIM)
    value_heads = value_flat.reshape(value_flat.shape[0], HEADS, HDIM)
    scale_factor = HDIM ** (-0.5)
    scores = (
        jnp.einsum("qhd,khd->hqk", query_heads, key_heads, preferred_element_type=jnp.float32)
        * scale_factor
    )
    allowed = seg_query[:, None] == seg_key[None, :]
    masked = jnp.where(allowed[None], scores, masked_fill)
    attn_probs = jnp.exp(masked - log_total)
    grad_heads = grad_att.reshape(grad_att.shape[0], HEADS, HDIM)
    grad_probs = jnp.einsum(
        "qhd,khd->hqk", grad_heads, value_heads, preferred_element_type=jnp.float32
    )
    row_delta = jnp.sum(attn_probs * grad_probs, axis=-1, keepdims=True)
    grad_scores = (attn_probs * (grad_probs - row_delta)).astype(jnp.bfloat16)
    grad_query = (
        jnp.einsum("hqk,khd->qhd", grad_scores, key_heads, preferred_element_type=jnp.float32)
        * scale_factor
    )
    grad_key = (
        jnp.einsum("hqk,qhd->khd", grad_scores, query_heads, preferred_element_type=jnp.float32)
        * scale_factor
    )
    grad_value = jnp.einsum(
        "hqk,qhd->khd",
        attn_probs.astype(jnp.bfloat16),
        grad_heads,
        preferred_element_type=jnp.float32,
    )
    return (
        grad_query,
        grad_key.reshape(key_flat.shape[0], -1),
        grad_value.reshape(value_flat.shape[0], -1),
    )


def finish(inputs, attended, weights):
    middle = inputs + (
        jnp.dot(attended, weights[4], preferred_element_type=jnp.float32)
        + weights[5].astype(jnp.float32)
    )
    second = layer_norm(
        middle, weights[6].astype(jnp.float32), weights[7].astype(jnp.float32)
    ).astype(jnp.bfloat16)
    hidden = jnp.dot(second, weights[8], preferred_element_type=jnp.float32) + weights[9].astype(
        jnp.float32
    )
    activated = gelu_erf(hidden).astype(jnp.bfloat16)
    result = middle + (
        jnp.dot(activated, weights[10], preferred_element_type=jnp.float32)
        + weights[11].astype(jnp.float32)
    )
    return (result, middle, second, hidden, activated)


def gathered_device(
    tokens,
    lengths,
    visibility_mask,
    visible_counts,
    ln1_gain,
    ln1_bias,
    qkv_weight,
    qkv_bias,
    out_weight,
    out_bias,
    ln2_gain,
    ln2_bias,
    fc1_weight,
    fc1_bias,
    fc2_weight,
    fc2_bias,
    context_cot,
):
    tok_rows = tokens.shape[0]
    model_width = tokens.shape[1]
    groups = lax.axis_size("fsdp")
    member = lax.axis_index("fsdp")
    pack_len = tok_rows * groups
    vis_rows = VIS_DEV
    vis_pack = vis_rows * groups
    zero_low = jnp.zeros((), jnp.bfloat16)
    shards = [
        weight.astype(jnp.bfloat16)
        for weight in (
            ln1_gain,
            ln1_bias,
            qkv_weight,
            qkv_bias,
            out_weight,
            out_bias,
            ln2_gain,
            ln2_bias,
            fc1_weight,
            fc1_bias,
            fc2_weight,
            fc2_bias,
        )
    ]
    weights = (
        lax.all_gather(shards[0], ("dp", "fsdp"), axis=0, tiled=True),
        lax.all_gather(shards[1], ("dp", "fsdp"), axis=0, tiled=True),
        lax.all_gather(shards[2], ("dp", "fsdp"), axis=0, tiled=True),
        lax.all_gather(shards[3], ("dp", "fsdp"), axis=0, tiled=True),
        lax.all_gather(shards[4], ("dp", "fsdp"), axis=0, tiled=True),
        lax.all_gather(shards[5], ("dp", "fsdp"), axis=0, tiled=True),
        lax.all_gather(shards[6], ("dp", "fsdp"), axis=0, tiled=True),
        lax.all_gather(shards[7], ("dp", "fsdp"), axis=0, tiled=True),
        lax.all_gather(shards[8], ("dp", "fsdp"), axis=0, tiled=True),
        lax.all_gather(shards[9], ("dp", "fsdp"), axis=0, tiled=True),
        lax.all_gather(shards[10], ("dp", "fsdp"), axis=0, tiled=True),
        lax.all_gather(shards[11], ("dp", "fsdp"), axis=0, tiled=True),
    )
    segment, places = pack_layout(lengths[0], pack_len)
    home_rows = member * tok_rows + jnp.arange(tok_rows, dtype=jnp.int32)
    seg_home = jnp.take(segment, home_rows)
    cos_home, sin_home = rope_tables(jnp.take(places, home_rows))
    inputs, normed, query_heads, key_flat, value_flat = project(tokens, weights, cos_home, sin_home)
    key_pack, value_pack = (
        lax.all_gather(key_flat, "fsdp", axis=0, tiled=True),
        lax.all_gather(value_flat, "fsdp", axis=0, tiled=True),
    )
    attended = attend(query_heads, key_pack, value_pack, seg_home, segment)[0]
    target_out = finish(inputs, attended, weights)[0].astype(jnp.bfloat16)
    running = jnp.cumsum(visibility_mask)
    visible_here = visibility_mask * (running <= visible_counts[0, 0]).astype(jnp.int32)
    visible_all = lax.all_gather(visible_here, "fsdp", axis=0, tiled=True)
    inclusive = jnp.cumsum(visible_all)
    rank_index = jnp.arange(vis_pack, dtype=jnp.int32)
    row_of = jnp.sum((inclusive[None, :] <= rank_index[:, None]).astype(jnp.int32), axis=1)
    owner_dev = row_of // tok_rows
    local_row = row_of % tok_rows
    mine_here = (owner_dev == member)[:, None]
    send_tokens = jnp.where(mine_here, jnp.take(tokens, local_row, axis=0), zero_low)
    send_cot = jnp.where(mine_here, jnp.take(context_cot, local_row, axis=0), zero_low)
    recv_tokens, recv_cot = (
        lax.all_to_all(send_tokens, "fsdp", split_axis=0, concat_axis=0, tiled=True),
        lax.all_to_all(send_cot, "fsdp", split_axis=0, concat_axis=0, tiled=True),
    )
    slot_index = jnp.arange(vis_rows, dtype=jnp.int32)
    my_ranks = member * vis_rows + slot_index
    my_owner = jnp.take(owner_dev, my_ranks)
    my_row = jnp.take(row_of, my_ranks)
    picked = my_owner * vis_rows + slot_index
    bal_tokens = jnp.take(recv_tokens, picked, axis=0)
    bal_cot = jnp.take(recv_cot, picked, axis=0)
    seg_bal = jnp.take(segment, my_row)
    seg_keys = jnp.take(segment, row_of)
    cos_bal, sin_bal = rope_tables(jnp.take(places, my_row))
    inputs_bal, normed_bal, query_bal, key_bal, value_bal = project(
        bal_tokens, weights, cos_bal, sin_bal
    )
    key_vis, value_vis = (
        lax.all_gather(key_bal, "fsdp", axis=0, tiled=True),
        lax.all_gather(value_bal, "fsdp", axis=0, tiled=True),
    )
    attended_bal, log_total = attend(query_bal, key_vis, value_vis, seg_bal, seg_keys)
    result_bal, middle_bal, second_bal, hidden_bal, activated_bal = finish(
        inputs_bal, attended_bal, weights
    )
    grad_result = bal_cot.astype(jnp.float32)
    result_low = grad_result.astype(jnp.bfloat16)
    grad_fc2 = jnp.einsum(
        "nf,nd->fd", activated_bal, result_low, preferred_element_type=jnp.float32
    )
    grad_bfc2 = jnp.sum(result_low.astype(jnp.float32), axis=0)
    grad_activated = jnp.einsum(
        "nd,fd->nf", result_low, weights[10], preferred_element_type=jnp.float32
    )
    gelu_pull = jax.vjp(gelu_erf, hidden_bal)[1]
    hidden_low = gelu_pull(grad_activated)[0].astype(jnp.bfloat16)
    grad_fc1 = jnp.einsum("nd,nf->df", second_bal, hidden_low, preferred_element_type=jnp.float32)
    grad_bfc1 = jnp.sum(hidden_low.astype(jnp.float32), axis=0)
    grad_second = jnp.einsum(
        "nf,df->nd", hidden_low, weights[8], preferred_element_type=jnp.float32
    )
    norm_two_pull = jax.vjp(
        layer_norm, middle_bal, weights[6].astype(jnp.float32), weights[7].astype(jnp.float32)
    )[1]
    grad_mid_norm, grad_gain_two, grad_shift_two = norm_two_pull(grad_second)
    grad_middle = grad_result + grad_mid_norm
    middle_low = grad_middle.astype(jnp.bfloat16)
    grad_wout = jnp.einsum(
        "nd,ne->de", attended_bal, middle_low, preferred_element_type=jnp.float32
    )
    grad_bout = jnp.sum(middle_low.astype(jnp.float32), axis=0)
    grad_att = jnp.einsum(
        "ne,de->nd", middle_low, weights[4], preferred_element_type=jnp.float32
    ).astype(jnp.bfloat16)
    grad_query, grad_key_all, grad_value_all = attend_back(
        query_bal, key_vis, value_vis, seg_bal, seg_keys, log_total, grad_att
    )
    grad_key_own, grad_value_own = (
        lax.psum_scatter(
            grad_key_all.astype(jnp.bfloat16), "fsdp", scatter_dimension=0, tiled=True
        ).astype(jnp.float32),
        lax.psum_scatter(
            grad_value_all.astype(jnp.bfloat16), "fsdp", scatter_dimension=0, tiled=True
        ).astype(jnp.float32),
    )
    grad_query_pre = rotate_back(grad_query, cos_bal, sin_bal).reshape(vis_rows, model_width)
    grad_key_pre = rotate_back(
        grad_key_own.reshape(vis_rows, HEADS, HDIM), cos_bal, sin_bal
    ).reshape(vis_rows, model_width)
    joined_low = jnp.concatenate([grad_query_pre, grad_key_pre, grad_value_own], axis=1).astype(
        jnp.bfloat16
    )
    grad_wqkv = jnp.einsum("nd,ne->de", normed_bal, joined_low, preferred_element_type=jnp.float32)
    grad_bqkv = jnp.sum(joined_low.astype(jnp.float32), axis=0)
    grad_normed = jnp.einsum(
        "ne,de->nd", joined_low, weights[2], preferred_element_type=jnp.float32
    )
    norm_one_pull = jax.vjp(
        layer_norm, inputs_bal, weights[0].astype(jnp.float32), weights[1].astype(jnp.float32)
    )[1]
    grad_in_norm, grad_gain_one, grad_shift_one = norm_one_pull(grad_normed)
    grad_inputs = grad_middle + grad_in_norm
    destinations = jnp.arange(groups, dtype=jnp.int32)
    route_mask = (my_owner[None, :] == destinations[:, None])[:, :, None]
    send_out = jnp.where(route_mask, result_bal.astype(jnp.bfloat16)[None], zero_low).reshape(
        vis_pack, model_width
    )
    send_grad = jnp.where(route_mask, grad_inputs.astype(jnp.bfloat16)[None], zero_low).reshape(
        vis_pack, model_width
    )
    back_out, back_grad = (
        lax.all_to_all(send_out, "fsdp", split_axis=0, concat_axis=0, tiled=True),
        lax.all_to_all(send_grad, "fsdp", split_axis=0, concat_axis=0, tiled=True),
    )
    rank_home = jnp.maximum(jnp.take(inclusive, home_rows) - 1, 0)
    is_visible = (visible_here > 0)[:, None]
    context_out = jnp.where(is_visible, jnp.take(back_out, rank_home, axis=0), zero_low)
    tokens_grad = jnp.where(is_visible, jnp.take(back_grad, rank_home, axis=0), zero_low)
    grad_list = [
        grad_gain_one,
        grad_shift_one,
        grad_wqkv,
        grad_bqkv,
        grad_wout,
        grad_bout,
        grad_gain_two,
        grad_shift_two,
        grad_fc1,
        grad_bfc1,
        grad_fc2,
        grad_bfc2,
    ]
    reduced = (
        lax.psum_scatter(grad_list[0], ("dp", "fsdp"), scatter_dimension=0, tiled=True),
        lax.psum_scatter(grad_list[1], ("dp", "fsdp"), scatter_dimension=0, tiled=True),
        lax.psum_scatter(grad_list[2], ("dp", "fsdp"), scatter_dimension=0, tiled=True),
        lax.psum_scatter(grad_list[3], ("dp", "fsdp"), scatter_dimension=0, tiled=True),
        lax.psum_scatter(grad_list[4], ("dp", "fsdp"), scatter_dimension=0, tiled=True),
        lax.psum_scatter(grad_list[5], ("dp", "fsdp"), scatter_dimension=0, tiled=True),
        lax.psum_scatter(grad_list[6], ("dp", "fsdp"), scatter_dimension=0, tiled=True),
        lax.psum_scatter(grad_list[7], ("dp", "fsdp"), scatter_dimension=0, tiled=True),
        lax.psum_scatter(grad_list[8], ("dp", "fsdp"), scatter_dimension=0, tiled=True),
        lax.psum_scatter(grad_list[9], ("dp", "fsdp"), scatter_dimension=0, tiled=True),
        lax.psum_scatter(grad_list[10], ("dp", "fsdp"), scatter_dimension=0, tiled=True),
        lax.psum_scatter(grad_list[11], ("dp", "fsdp"), scatter_dimension=0, tiled=True),
    )
    return (
        target_out,
        context_out,
        tokens_grad,
        reduced[0],
        reduced[1],
        reduced[2],
        reduced[3],
        reduced[4],
        reduced[5],
        reduced[6],
        reduced[7],
        reduced[8],
        reduced[9],
        reduced[10],
        reduced[11],
    )


def per_device(tokens, *rest):
    n, group = lax.axis_size("dp"), lax.axis_size("fsdp")
    out_rows = rest[7].shape[0]
    fits = group == 4 and n == 8 and out_rows * group == 128
    return (on_device if fits else gathered_device)(tokens, *rest)


def solution(mesh):
    both = ("dp", "fsdp")
    vec, mat = P(both), P(both, None)
    return jax.shard_map(
        per_device,
        mesh=mesh,
        in_specs=(
            mat, P("dp", None), vec, P("dp", "fsdp"), vec, vec, mat, vec, mat, vec, vec, vec,
            mat, vec, mat, vec, mat,
        ),
        out_specs=(mat, mat, mat, vec, vec, mat, vec, mat, vec, vec, vec, mat, vec, mat, vec),
        check_vma=False,
    )
```

```python
import functools
import math
import types

import jax
import jax.numpy as jnp
import numpy as np
from jax import lax
from jax.experimental import pallas as pl
from jax.experimental.pallas import tpu as pltpu
from jax.sharding import PartitionSpec as P

HEADS = 16
HDIM = 64
GRID = 14
VIS_DEV = 64
norm_eps = 1e-06
masked_fill = -1e30
FRAMES = 8
EPS = 1e-06
FILL = -1e30
BF = jnp.bfloat16
F32 = jnp.float32
MESH = pl.DeviceIdType.MESH
NT = (((1,), (1,)), ((), ()))
NN = (((1,), (0,)), ((), ()))
TN = (((0,), (0,)), ((), ()))


def dot(a, b, dims=NN):
    return lax.dot_general(a, b, dims, preferred_element_type=F32)


def trig_table():
    width = FRAMES + 2 * GRID
    lane = np.arange(2 * HDIM)
    pair = lane % (HDIM // 2)
    axis = np.minimum(pair // 11, 2)
    freq = np.exp(((pair - 11 * axis).astype(np.float32)) * np.float32(-math.log(10000.0) / 11.0))
    sign = np.where(lane % HDIM < HDIM // 2, -1.0, 1.0)
    table = np.zeros((128, 4 * HDIM), np.float32)
    row = np.arange(width)
    kind = np.where(row < FRAMES, 0, np.where(row < FRAMES + GRID, 1, 2))
    coord = np.where(kind == 0, row, np.where(kind == 1, row - FRAMES, row - FRAMES - GRID))
    angle = (coord[:, None].astype(np.float32) * freq[None, :].astype(np.float32)).astype(np.float64)
    here = kind[:, None] == axis[None, :]
    table[:width, : 2 * HDIM] = np.where(here, np.cos(angle), 0.0)
    table[:width, 2 * HDIM :] = np.where(here, np.sin(angle) * sign[None, :], 0.0)
    parts = []
    rest = table
    for _ in range(3):
        part = rest.astype(jnp.bfloat16)
        parts.append(part)
        rest = rest - part.astype(np.float32)
    return np.stack(parts)


def norm_stats(v):
    center = v - jnp.mean(v, axis=-1, keepdims=True)
    inv = lax.rsqrt(jnp.mean(center * center, axis=-1, keepdims=True) + EPS)
    return center * inv, inv


def norm_back(v, gain, grad):
    xhat, inv = norm_stats(v)
    gg = grad * gain
    dv = inv * (
        gg - jnp.mean(gg, axis=-1, keepdims=True) - xhat * jnp.mean(gg * xhat, axis=-1, keepdims=True)
    )
    return (
        dv,
        jnp.sum(grad * xhat, axis=0, keepdims=True),
        jnp.sum(grad, axis=0, keepdims=True),
    )


def swap_halves(u):
    lane = lax.broadcasted_iota(jnp.int32, u.shape, 1)
    return jnp.where(
        lax.rem(lane, HDIM) < HDIM // 2,
        pltpu.roll(u, u.shape[1] - HDIM // 2, 1),
        pltpu.roll(u, HDIM // 2, 1),
    )


def column_segment(start, rows, ends):
    row = start + lax.broadcasted_iota(jnp.int32, (rows, 1), 0)
    seg = jnp.zeros((rows, 1), jnp.int32)
    for end in ends:
        seg += (row >= end).astype(jnp.int32)
    return row, seg


ALIASES = dict(N2="N1", PT="N1", X1B="GP")


class Sems:
    def __init__(self, send, recv):
        self.send, self.recv = send, recv
        self.sends = self.recvs = self.clock = 0
        self.idle_sends, self.idle_recvs, self.waited = [], [], []

    def take_send(self):
        if self.idle_sends:
            return self.idle_sends.pop()
        self.sends += 1
        return self.send.at[self.sends - 1]

    def give_send(self, sem):
        self.idle_sends.append(sem)

    def take_recv(self):
        self.recvs += 1
        return self.recv.at[self.recvs - 1]

    def ring_sent(self):
        rs = self.idle_recvs.pop() if self.idle_recvs else self.take_recv()
        self.clock += 1
        return rs, self.clock

    def ring_landed(self, sem, sent):
        self.idle_recvs += [old for at, old in self.waited if at < sent]
        self.waited = [(at, old) for at, old in self.waited if at >= sent]
        self.waited.append((self.clock, sem))


def layer_kernel(dims, names, *refs):
    n, D, FF, T, V = dims
    NF = 4
    R = D // (n * NF)
    RP = R * NF
    HC = FF // (NF * n)
    HF = FF // NF
    C = D // NF
    VP = V * NF
    S_ = T * NF
    last = n // 2 - 1
    given = dict(zip(names, refs))
    g = types.SimpleNamespace(**given, **{a: given[b] for a, b in ALIASES.items()})
    sems = Sems(g.send_sems, g.recv_sems)
    lsem = g.local_sems

    p = lax.axis_index("dp")
    f = lax.axis_index("fsdp")
    f1 = f + 1 - 2 * lax.rem(f, 2)
    f2 = lax.rem(f + 2, NF)
    f3 = NF - 1 - f
    par = lax.rem(p, 2)
    half_p = lax.div(p, 2)
    pos = (1 - par) * half_p + par * (n - 1 - half_p)

    def idx(q):
        q = lax.rem(q + 2 * n, n)
        up = lax.div(q, n // 2)
        return (1 - up) * (2 * q) + up * (2 * (n - 1 - q) + 1)

    right, left = idx(pos + 1), idx(pos - 1)

    def launch(src, dst, ss, rs, to):
        c = pltpu.make_async_remote_copy(
            src_ref=src, dst_ref=dst, send_sem=ss, recv_sem=rs, device_id=to, device_id_type=MESH
        )
        c.start()
        return c

    def sent(copies):
        for c in copies:
            c.wait_send()
            sems.give_send(c.src_sem)

    def received(copies):
        for c in copies:
            c.wait_recv()
        sent(copies)

    def remote(src, dst, to):
        ss, rs = sems.take_send(), sems.take_recv()
        return launch(src, dst, ss, rs, to), ss, rs

    def arrival(dst, ss, rs, to):
        return pltpu.make_async_remote_copy(
            src_ref=dst, dst_ref=dst, send_sem=ss, recv_sem=rs, device_id=to, device_id_type=MESH
        )

    to1, to2, to3 = {"fsdp": f1}, {"fsdp": f2}, {"fsdp": f3}
    peers = ((f1, to1), (f2, to2), (f3, to3))

    barrier = pltpu.get_barrier_semaphore()
    for to in (to1, to2, to3, {"dp": right}, {"dp": left}):
        pl.semaphore_signal(barrier, inc=1, device_id=to, device_id_type=MESH)

    loads = {}
    for i, (src, dst) in enumerate(
        (
            (g.wqkv, g.wqkv_v),
            (g.w1, g.w1_v),
            (g.wo, g.wo_v),
            (g.mask, g.mask_v),
            (g.tok, g.TA.at[f]),
            (g.w2, g.w2_v),
            (g.cot, g.CA.at[f]),
            (g.trig, g.trig_v),
        )
    ):
        c = pltpu.make_async_copy(src, dst, lsem.at[i])
        c.start()
        loads[i] = c
    vectors = []
    for k in range(8):
        vectors.append(pltpu.make_async_copy(given["in%d" % k], given["v%d" % k], lsem.at[8 + k]))
        vectors[k].start()

    AS, AQ, WO, A1, A2 = g.AS, g.AQ, g.WO, g.A1, g.A2
    TA, CA = g.TA, g.CA

    loads[5].wait()
    A2[p] = g.w2_v[...].astype(BF)
    loads[0].wait()
    for j in range(NF):
        for t in range(3):
            g.sq[j, :, C * t : C * t + C] = g.wqkv_v[:, D * t + C * j : D * t + C * j + C].astype(BF)
    AQ[p, pl.ds(pl.multiple_of(R * f, R), R), :] = g.sq[f]
    loads[2].wait()
    WO[p, f] = g.wo_v[...].astype(BF)
    pl.semaphore_wait(barrier, 5)

    def scatter(src, dst, three):
        ss, rs = sems.take_send(), sems.take_recv()
        for fj, to in peers:
            launch(src(fj), dst(f), ss, rs, to)
        return (arrival(three, ss, rs, to1),)

    class AllGather4:
        def __init__(self, slot):
            self.slot = slot
            self.done = False
            c, ss, rs = remote(slot(f), slot(f), to2)
            d, sd, rd = remote(slot(f), slot(f), to1)
            self.across = arrival(slot(f2), ss, rs, to2)
            self.beside = arrival(slot(f1), sd, rd, to1)
            self.copies = [c, d]

        def forward(self):
            self.across.wait_recv()
            c, ss, rs = remote(self.slot(f2), self.slot(f2), to1)
            self.passed = arrival(self.slot(f3), ss, rs, to1)
            self.copies.append(c)

        def finish(self):
            if not self.done:
                self.done = True
                self.beside.wait_recv()
                self.passed.wait_recv()
                sent(self.copies)

    class ReduceScatter4:
        def __init__(self, part, r1, xs, r2):
            self.part, self.r1, self.xs, self.r2 = part, r1, xs, r2
            c, ss, rs = remote(part.at[f3], r1.at[1], to1)
            d, sd, rd = remote(part.at[f1], r1.at[0], to1)
            self.other = arrival(r1.at[1], ss, rs, to1)
            self.own = arrival(r1.at[0], sd, rd, to1)
            self.copies = [c, d]

        def forward(self):
            self.other.wait_recv()
            self.xs[...] = (self.part[f2].astype(F32) + self.r1[1].astype(F32)).astype(BF)
            c, ss, rs = remote(self.xs, self.r2, to2)
            self.across = arrival(self.r2, ss, rs, to2)
            self.copies.append(c)

        def finish(self):
            self.own.wait_recv()
            self.across.wait_recv()
            sent(self.copies)

        def total(self):
            return self.part[f].astype(F32) + self.r1[0].astype(F32) + self.r2[...].astype(F32)

    class RingGather:
        def __init__(self, view, pair, rows):
            self.view, self.pair, self.rows = view, pair, rows
            self.before, self.flight = (), None

        def landed(self):
            received(self.before)
            self.before = ()
            if self.flight is not None:
                received([self.flight])
                sems.ring_landed(self.flight.dst_sem, self.at)
                self.flight = None

        def step(self, r):
            self.landed()
            h = self.rows // 2
            spans = ((0, self.rows), (0, self.rows)) if r < last else ((0, h), (h, h))
            ss = sems.take_send()
            rs, self.at = sems.ring_sent()
            for way, (s, c) in zip((1, -1), spans):
                piece = self.view(idx(pos - way * r), s, c)
                launch(piece, piece, ss, rs, {"dp": right if way == 1 else left})
            both = self.pair if r < last else self.view(0, 0, self.rows)
            self.flight = arrival(both, ss, rs, {"dp": left})

        def finish(self):
            self.landed()

    def row_rings(ref):
        h = ref.shape[1] // 2

        def ring(offset):
            view = lambda slot, s, c: ref.at[slot, pl.ds(offset + s, c), :]
            return RingGather(view, ref.at[pl.ds(0, 2), pl.ds(offset, h), :], h)

        return [ring(0), ring(h)]

    q_ring, w1_ring, w2_ring = row_rings(AQ), row_rings(A1), row_rings(A2)
    o_ring = RingGather(lambda slot, s, c: WO.at[slot, f, pl.ds(s, c), :], WO.at[pl.ds(0, 2), f], R)
    s_ring = RingGather(lambda slot, s, c: AS.at[slot, pl.ds(s, c)], AS.at[pl.ds(0, 2)], NF)

    class RingReduce:
        def __init__(self, grads, start, rows, st, rr, rl, wire=BF):
            self.G, self.o, self.rows, self.st, self.rr, self.rl = grads, start, rows, st, rr, rl
            self.wire = wire
            self.flight = None

        def landed(self):
            if self.flight is not None:
                received([self.flight])
                sems.ring_landed(self.flight.dst_sem, self.at)
                self.flight = None

        def step(self, r):
            self.landed()
            o, rows = self.o, self.rows
            hh = rows // 2
            whole = pl.ds(o, rows)
            ss = sems.take_send()
            rs, self.at = sems.ring_sent()
            ways = ((1, self.rr, 0, {"dp": right}), (-1, self.rl, hh, {"dp": left}))
            if r == 0:
                far = idx(pos + n // 2)
                self.st[whole, :] = self.G[far, whole, :].astype(self.wire)
                for _, buf, s, to in ways:
                    half = pl.ds(o + s, hh)
                    launch(self.st.at[half, :], buf.at[0, half, :], ss, rs, to)
                self.flight = arrival(self.st.at[whole, :], ss, rs, {"dp": left})
                return
            for way, buf, s, to in ways:
                c = idx(pos + way * (n // 2 - r))
                if r == 1:
                    half, other = pl.ds(o + s, hh), pl.ds(o + hh - s, hh)
                    total = buf[0, half, :].astype(F32) + self.G[c, half, :].astype(F32)
                    buf[0, half, :] = total.astype(self.wire)
                    buf[0, other, :] = self.G[c, other, :].astype(self.wire)
                else:
                    total = buf[r - 1, whole, :].astype(F32) + self.G[c, whole, :].astype(F32)
                    buf[r - 1, whole, :] = total.astype(self.wire)
                launch(buf.at[r - 1, whole, :], buf.at[r, whole, :], ss, rs, to)
            self.flight = arrival(self.rr.at[pl.ds(0, 2), whole, :], ss, rs, {"dp": left})

        def finish(self):
            self.landed()

        def total(self):
            o, rows = self.o, self.rows
            return (
                self.G[p, pl.ds(o, rows), :].astype(F32)
                + self.rr[last, pl.ds(o, rows), :].astype(F32)
                + self.rl[last, pl.ds(o, rows), :].astype(F32)
            )

    st = types.SimpleNamespace(oa=[None, None])
    N1, N2, GT, PT = g.N1, g.N2, g.GT, g.PT
    VEC, BQ, BG, VG = g.VEC, g.BQ, g.BG, g.VG
    Q, K, W, QV, KV, WV = g.Q, g.K, g.W, g.QV, g.KV, g.WV
    SM, OV, PV, OA, OT = g.SM, g.OV, g.PV, g.OA, g.OT
    XV, N1V, DY, X1V, N2V = g.XV, g.N1V, g.DY, g.X1V, g.N2V
    GV, GP, DH, PN, PF = g.GV, g.GP, g.DH, g.PN, g.PF
    G2, G1, GQ, GO = g.G2, g.G1, g.GQ, g.GO
    DO, DPRE = g.DO, g.DPRE
    E1, F1, EQ, FQ, SG = g.E1, g.g1_o, g.EQ, g.gq_o, g.SG
    blocks = [slice(256 * k, 256 * k + 256) for k in range(D // 256)]
    mine = pl.ds(pl.multiple_of(V * f, V), V)
    hc, hr = HC // 2, RP // 2
    g2_ring = [
        RingReduce(G2, 0, hc, g.st2, g.rr2, g.rl2),
        RingReduce(G2, hc, hc, g.st2, g.rr2, g.rl2),
    ]
    g1_ring = [
        RingReduce(G1, 0, hr, g.st1, g.rr1, g.rl1),
        RingReduce(G1, hr, hr, g.st1, g.rr1, g.rl1),
    ]
    gq_ring = [
        RingReduce(GQ, 0, hr, g.stq, g.rrq, g.rlq),
        RingReduce(GQ, hr, hr, g.stq, g.rrq, g.rlq),
    ]
    go_ring = RingReduce(GO, 0, R, g.sto, g.rro, g.rlo)
    gs_ring = RingReduce(VG, 0, 16, g.sts, g.rrs, g.rls, F32)

    def finish(*rings):
        for r in rings:
            r.finish()

    def vec(k):
        return VEC[k : k + 1, :]

    def start():
        part = lambda j: AQ.at[p, pl.ds(pl.multiple_of(R * j, R), R), :]
        q_ring[0].before = scatter(lambda j: g.sq.at[j], part, AQ.at[0, pl.ds(0, 3 * R), :])

    def small_start():
        for c in vectors:
            c.wait()
        loads[3].wait()
        SV = g.small_v
        SV[...] = jnp.zeros(SV.shape, F32)
        for k in range(8):
            row, at = ((0, R * k), (1, R * (k - 4)), (2, 0), (3, 0))[0 if k < 4 else 1 if k < 6 else k - 4]
            value = given["v%d" % k][...]
            width = value.shape[1]
            wide = value if width == 128 else jnp.concatenate([value, jnp.zeros((1, 128 - width), F32)], axis=1)
            SV[row : row + 1, :] += wide if at == 0 else pltpu.roll(wide, at, 1)
        mask = g.mask_v[...].astype(F32)
        below = lax.broadcasted_iota(jnp.int32, (128, 128), 0) <= lax.broadcasted_iota(jnp.int32, (128, 128), 1)
        tri = jnp.where(below, 1.0, 0.0).astype(BF)
        count = g.counts[0, 0].astype(F32)
        before = jnp.zeros((1, 1), F32)
        for k in range(2):
            ones = mask[:, 128 * k : 128 * k + 128]
            running = dot(jnp.broadcast_to(ones, (8, 128)).astype(BF), tri)[0:1, :] + before
            SV[4 + k : 5 + k, :] = jnp.where(running <= count, ones, 0.0)
            before = before + jnp.sum(ones, axis=1, keepdims=True)
        AS[p, f] = SV[...]
        st.s = scatter(lambda j: AS.at[p, f], lambda j: AS.at[p, j], AS.at[0, pl.ds(0, 3)])
        s_ring.before = st.s

    def cast_fc1():
        loads[1].wait()
        for j in range(NF):
            for t in range(n):
                at = HC * (NF * t + j)
                g.s1[j, :, HC * t : HC * t + HC] = g.w1_v[:, at : at + HC].astype(BF)
        A1[p, pl.ds(pl.multiple_of(R * f, R), R), :] = g.s1[f]
        part = lambda j: A1.at[p, pl.ds(pl.multiple_of(R * j, R), R), :]
        w1_ring[0].before = scatter(lambda j: g.s1.at[j], part, A1.at[0, pl.ds(0, 3 * R), :])

    def tokens_start():
        loads[4].wait()
        st.tok = AllGather4(lambda j: TA.at[j])

    def cot_start():
        loads[6].wait()
        st.cot = AllGather4(lambda j: CA.at[j])

    def wo_start():
        o_ring.finish()
        st.wo = AllGather4(lambda j: WO.at[:, j])

    ends = []
    total_len = jnp.int32(0)
    for k in range(g.lengths.shape[1]):
        total_len = total_len + g.lengths[0, k]
        ends.append(total_len)

    def key_segments():
        keyrow = lax.broadcasted_iota(jnp.int32, (1, S_), 1)
        segrow = jnp.zeros((1, S_), jnp.int32)
        for end in ends:
            segrow += (keyrow >= end).astype(jnp.int32)
        return segrow

    def layout():
        row, _seg = column_segment(0, S_, ends)
        before = jnp.zeros((S_, 1), jnp.int32)
        for k, end in enumerate(ends):
            before += jnp.where(row >= end, g.lengths[0, k], 0)
        place = row - before
        img = GRID * GRID
        frame = jnp.zeros((S_, 1), jnp.int32)
        for t in range(1, FRAMES):
            frame += (place >= img * t).astype(jnp.int32)
        rest = place - img * frame
        grow = jnp.zeros((S_, 1), jnp.int32)
        for t in range(1, GRID):
            grow += (rest >= GRID * t).astype(jnp.int32)
        gcol = rest - GRID * grow
        lane = lax.broadcasted_iota(jnp.int32, (S_, 128), 1)
        hot = (lane == frame) | (lane == grow + FRAMES) | (lane == gcol + (FRAMES + GRID))
        g.OH[...] = jnp.where(hot, 1.0, 0.0).astype(BF)
        loads[7].wait()
        g.CS[...] = sum(dot(g.OH[...], g.trig_v[k]) for k in range(3))

    def visible():
        if s_ring.before:
            received(s_ring.before)
            s_ring.before = ()
        vis8 = jnp.concatenate([AS[p, j][4:6, :] for j in range(NF)], axis=0)
        above = lax.broadcasted_iota(jnp.int32, (128, 128), 0)
        tri = above <= lax.broadcasted_iota(jnp.int32, (128, 128), 1)
        within = dot(vis8.astype(BF), jnp.where(tri, 1.0, 0.0).astype(BF))
        base = jnp.zeros((1, 128), F32)
        pieces, vpieces = [], []
        for k in range(8):
            pieces.append(within[k : k + 1, :] + base)
            vpieces.append(vis8[k : k + 1, :])
            base = base + jnp.sum(vis8[k : k + 1, :], axis=1, keepdims=True)
        incl = jnp.concatenate(pieces, axis=1)
        visrow = jnp.concatenate(vpieces, axis=1)
        rank = jnp.where(visrow > 0.5, incl - 1.0, -1.0).astype(jnp.int32)
        sel = lax.broadcasted_iota(jnp.int32, (VP, S_), 0) == rank
        SM[...] = jnp.where(sel, 1.0, 0.0).astype(BF)

    def rounded(v):
        return v.astype(BF).astype(F32)

    def turn(v, by):
        by = by % 128
        return v if by == 0 else pltpu.roll(v, by, 1)

    def small_vectors():
        s_ring.finish()
        lane128 = lax.broadcasted_iota(jnp.int32, (n, 128), 1)
        rows0 = [AS[:, j, 0, :] for j in range(NF)]
        rows1 = [AS[:, j, 1, :] for j in range(NF)]
        rows2 = [AS[:, j, 2, :] for j in range(NF)]
        for k in range(6):
            src = rows0 if k < 4 else rows1
            piece = jnp.zeros((n, 128), F32)
            for j in range(NF):
                piece = jnp.where(lax.div(lane128, R) == j, turn(src[j], R * (j - k % 4)), piece)
            for q in range(n):
                VEC[k : k + 1, 128 * q : 128 * q + 128] = rounded(piece[q : q + 1, :])
        for q in range(n):
            VEC[6:7, 128 * q : 128 * q + 128] = rounded(AS[q, f][3:4, :])
        t0 = jnp.where(lane128 < 96, rows2[0], turn(rows2[1], 96))
        t1 = jnp.where(lane128 < 64, turn(rows2[1], -32), turn(rows2[2], 64))
        t2 = jnp.where(lane128 < 32, turn(rows2[2], -64), turn(rows2[3], 32))
        for q in range(n):
            for k, t in enumerate((t0, t1, t2)):
                BQ[0:1, 384 * q + 128 * k : 384 * q + 128 * k + 128] = rounded(t[q : q + 1, :])

    def first_norm():
        st.tok.finish()

        def block(b, _):
            xhat, _inv = norm_stats(TA[b].astype(F32))
            N1[b] = (xhat * vec(0) + vec(1)).astype(BF)
            return 0

        lax.fori_loop(0, NF, block, 0)

    def project_half(part):
        finish(*q_ring)

        def block(b, _):
            rows = pl.ds(pl.multiple_of(b * T, T), T)
            cs = g.CS[rows, :]
            for t, dst in enumerate((Q, K, W)):
                out = dot(N1[b], AQ[:, :, C * t : C * t + C].reshape(D, C))
                out = out + BQ[0:1, pl.ds(pl.multiple_of(D * t + C * f, 128), C)]
                if t == 2:
                    dst[rows, :] = out.astype(BF)
                    continue
                for hh in range(C // 128):
                    u = out[:, 128 * hh : 128 * hh + 128]
                    u = (u * cs[:, :128] + swap_halves(u) * cs[:, 128:]).astype(BF)
                    dst[rows, 128 * hh : 128 * hh + 128] = u * BF(0.125) if t == 0 else u
            return 0

        lax.fori_loop(NF // 2 * part, NF // 2 * (part + 1), block, 0)

    lane_c = lax.broadcasted_iota(jnp.int32, (1, C), 1)
    hmask = [jnp.where(lax.div(lane_c, HDIM) == hd, 1.0, 0.0) for hd in range(C // HDIM)]

    def softmax(s):
        e = jnp.exp(s - jnp.max(s, axis=-1, keepdims=True))
        return e * (1.0 / jnp.sum(e, axis=-1, keepdims=True))

    def context_attention():
        for src, dst in ((Q, QV), (K, KV), (W, WV)):
            dst[...] = dot(SM[...], src[...]).astype(BF)
        segrow = key_segments()
        seg8 = jnp.broadcast_to(segrow.astype(F32), (8, S_)).astype(BF)
        segv_row = dot(seg8, SM[...], NT)[0:1, :].astype(jnp.int32)
        segv_col = jnp.sum(SM[...].astype(F32) * segrow.astype(F32), axis=1, keepdims=True).astype(jnp.int32)
        same = segv_col == segv_row
        acc = jnp.zeros((VP, C), F32)
        for hd in range(C // HDIM):
            s = dot(QV[...] * hmask[hd].astype(BF), KV[...], NT)
            pr = softmax(jnp.where(same, s, FILL))
            PV[hd] = pr
            acc += dot(pr.astype(BF), WV[...]) * hmask[hd]
        OV[f] = acc.astype(BF)
        st.ov = AllGather4(lambda j: OV.at[j])

    def attend_target(b, pair):
        rows = slice(T * b, T * b + T)
        _, segq = column_segment(b * T, T, ends)
        same = segq == key_segments()
        for hd in (2 * pair, 2 * pair + 1):
            s = dot(Q[rows, :] * hmask[hd].astype(BF), K[...], NT)
            pr = softmax(jnp.where(same, s, FILL)).astype(BF)
            o = dot(pr, W[...])
            cols = slice(HDIM * hd, HDIM * hd + HDIM)
            OA[f, rows, cols] = o[:, cols].astype(BF)

    def oa_start(part):
        rows = pl.ds(S_ // 2 * part, S_ // 2)
        st.oa[part] = AllGather4(lambda j: OA.at[j, rows, :])

    def select_rows():
        for cols in blocks:
            XV[:, cols] = dot(SM[...], TA[:, :, cols].reshape(S_, 256)).astype(BF)
            N1V[:, cols] = dot(SM[...], N1[:, :, cols].reshape(S_, 256)).astype(BF)

    def select_cot():
        st.cot.finish()
        for cols in blocks:
            DY[:, cols] = dot(SM[...], CA[:, :, cols].reshape(S_, 256)).astype(BF)

    def out_project(parts, cols):
        heads = [WO[n // NF * j : n // NF * (j + 1), :, :, cols].reshape(C, -1) for j in range(NF)]
        return sum(dot(parts(j), heads[j]) for j in range(NF))

    def context_middle():
        st.wo.finish()
        st.ov.finish()
        for cols in blocks:
            X1V[:, cols] = XV[:, cols].astype(F32) + (out_project(lambda j: OV[j], cols) + VEC[4:5, cols])
        xhat, _inv = norm_stats(X1V[...])
        N2V[...] = (xhat * vec(2) + vec(3)).astype(BF)

    def normal_cdf(hid):
        return 0.5 * (1.0 + lax.erf(hid * (1.0 / math.sqrt(2.0))))

    def context_hidden():
        finish(*w1_ring)
        for cols in blocks:
            hid = dot(N2V[...], A1[:, :, cols].reshape(D, 256)) + VEC[6:7, cols]
            cdf = normal_cdf(hid)
            GV[:, cols] = (hid * cdf).astype(BF)
            GP[:, cols] = cdf + hid * (jnp.exp(-0.5 * hid * hid) * (1.0 / math.sqrt(2.0 * math.pi)))

    def outer(dst, lhs, rhs):
        for k, cols in enumerate(blocks):
            g.LT[cols, :] = lhs[:, cols].astype(F32).T.astype(BF)

        def one(k, _):
            rows = pl.ds(pl.multiple_of(256 * k, 256), 256)
            for c in range(dst.shape[2] // 256):
                cols = slice(256 * c, 256 * c + 256)
                part = dot(g.LT[rows, :], rhs[:, cols]).astype(dst.dtype)
                dst[pl.ds(2 * k, 2), :, cols] = part.reshape(2, 128, 256)
            return 0

        lax.fori_loop(0, n // 2, one, 0)

    def put_grad(k, vrow):
        for q in range(n):
            VG[q, k : k + 1, :] = vrow[:, 128 * q : 128 * q + 128]

    def fc2_grad():
        outer(G2, GV, DY)

    def hidden_grad():
        finish(*w2_ring)
        for k, cols in enumerate(blocks):
            dg = dot(DY[...], A2[...].reshape(HF, D)[256 * k : 256 * k + 256, :], NT)
            dh = (dg * GP[:, cols]).astype(BF)
            DH[:, cols] = dh
            dc1 = jnp.sum(dh.astype(F32), axis=0, keepdims=True)
            for q in range(2):
                for j in range(NF):
                    piece = dc1[:, 128 * q : 128 * q + 128]
                    VG[2 * k + q, 9 + j : 10 + j, :] = jnp.where(f == j, piece, jnp.zeros((1, 128), F32))

    def second_grad():
        for k, cols in enumerate(blocks):
            part = dot(DH[...], A1[2 * k : 2 * k + 2].reshape(256, HF), NT).astype(BF)
            PN[:, :, cols] = part.reshape(NF, V, 256)
        st.n2 = ReduceScatter4(PN, g.PNr1, g.PNxs, g.PNr2)

    def fc1_grad():
        outer(G1, N2V, DH)

    def context_partial():
        for cols in blocks:
            part = dot(GV[...], A2[:, :, cols].reshape(HF, 256)).astype(BF)
            PF[:, :, cols] = part.reshape(NF, V, 256)
        st.pf = ReduceScatter4(PF, g.PFr1, g.PFxs, g.PFr2)

    def second_norm_back():
        st.n2.finish()
        dyo = DY[mine, :].astype(F32)
        dv, dgain, dshift = norm_back(X1V[mine, :], vec(2), st.n2.total())
        dx1 = dyo + dv
        g.DX1[...] = dx1
        low = dx1.astype(BF)
        g.DP[f] = low
        st.dp = AllGather4(lambda j: g.DP.at[j])
        put_grad(2, dgain)
        put_grad(3, dshift)
        put_grad(4, jnp.sum(low.astype(F32), axis=0, keepdims=True))
        put_grad(5, jnp.sum(dyo, axis=0, keepdims=True))

    def transpose_attended():
        st.ov.finish()
        for j in range(NF):
            ot = OV[j].astype(F32).T.astype(BF)
            OT[n // NF * j : n // NF * (j + 1)] = ot.reshape(n // NF, NF, R, VP)

    def out_grad():
        st.dp.finish()
        go = dot(OT[:, f].reshape(n * R, VP), g.DP[...].reshape(VP, D))
        GO[...] = go.reshape(n, R, D)

    def attended_grad():
        st.dp.finish()
        st.wo.finish()
        wo_heads = WO[pl.ds(n // NF * f, n // NF)].reshape(C, D)
        DO[...] = dot(g.DP[...].reshape(VP, D), wo_heads, NT).astype(BF)

    def attention_back():
        dq = jnp.zeros((VP, C), F32)
        dk = jnp.zeros((VP, C), F32)
        dw = jnp.zeros((VP, C), F32)
        for hd in range(C // HDIM):
            pr = PV[hd]
            dp = dot(DO[...] * hmask[hd].astype(BF), WV[...], NT)
            ds = (pr * (dp - jnp.sum(pr * dp, axis=-1, keepdims=True))).astype(BF)
            dq += dot(ds, KV[...]) * hmask[hd]
            dk += dot(ds, QV[...], TN) * hmask[hd]
            dw += dot(pr.astype(BF), DO[...], TN) * hmask[hd]
        csv = sum(dot(dot(SM[...], g.OH[...]).astype(BF), g.trig_v[k]) for k in range(3))
        for t, (grad, scale) in enumerate(((dq, 0.125), (dk, 1.0))):
            for hh in range(C // 128):
                u = grad[:, 128 * hh : 128 * hh + 128]
                u = u * csv[:, :128] - swap_halves(u) * csv[:, 128:]
                DPRE[:, C * t + 128 * hh : C * t + 128 * hh + 128] = (u * scale).astype(BF)
        DPRE[:, 2 * C :] = dw.astype(BF)

    def qkv_grad():
        outer(GQ, N1V, DPRE)

    def qkv_bias_grad():
        BG[...] = jnp.zeros(BG.shape, F32)
        db = jnp.sum(DPRE[...].astype(F32), axis=0, keepdims=True)
        for t in range(3):
            BG[0:1, pl.ds(pl.multiple_of(D * t + C * f, 128), C)] = db[:, C * t : C * t + C]
        for q in range(n):
            for t in range(3):
                VG[q, 6 + t : 7 + t, :] = BG[0:1, 384 * q + 128 * t : 384 * q + 128 * t + 128]
            VG[q, 13:16, :] = jnp.zeros((3, 128), F32)

    def first_grad():
        for k, cols in enumerate(blocks):
            part = dot(DPRE[...], AQ[2 * k : 2 * k + 2].reshape(256, 3 * C), NT).astype(BF)
            PN[:, :, cols] = part.reshape(NF, V, 256)
        st.n1 = ReduceScatter4(PN, g.PMr1, g.PMxs, g.PMr2)

    def first_norm_back():
        st.n1.finish()
        dv, dgain, dshift = norm_back(XV[mine, :].astype(F32), vec(0), st.n1.total())
        g.DX[f] = (g.DX1[...] + dv).astype(BF)
        st.dx = AllGather4(lambda j: g.DX.at[j])
        put_grad(0, dgain)
        put_grad(1, dshift)

    def context_result():
        st.pf.finish()
        g.CO[f] = (X1V[mine, :] + (st.pf.total() + vec(5))).astype(BF)
        st.co = AllGather4(lambda j: g.CO.at[j])

    def home(src, dst):
        s = SM[:, pl.ds(pl.multiple_of(T * f, 128), T)]

        def one(k, _):
            cols = pl.ds(pl.multiple_of(256 * k, 256), 256)
            dst[:, cols] = dot(s, src[:, :, cols].reshape(VP, 256), TN).astype(BF)
            return 0

        lax.fori_loop(0, len(blocks), one, 0)

    def home_context():
        st.co.finish()
        home(g.CO, g.ctx_o)

    def home_grad():
        st.dx.finish()
        home(g.DX, g.dx_o)

    def target_middle(b):
        st.wo.finish()
        st.oa[b // 2].finish()
        for cols in blocks:
            g.X1B[:, cols] = TA[b, :, cols].astype(F32) + (
                out_project(lambda j: OA[j, T * b : T * b + T, :], cols) + VEC[4:5, cols]
            )
        x1 = g.X1B[...]
        xh, _inv = norm_stats(x1)
        N2[b] = (xh * vec(2) + vec(3)).astype(BF)

        @pl.when(f == b)
        def _():
            g.X1H[...] = x1

    def target_hidden(b):
        finish(*w1_ring)
        for cols in blocks:
            hid = dot(N2[b], A1[:, :, cols].reshape(D, 256)) + VEC[6:7, cols]
            GT[b, :, cols] = (hid * normal_cdf(hid)).astype(BF)

    def target_out(b):
        finish(*w2_ring)

        def one(k, _):
            cols = pl.ds(pl.multiple_of(256 * k, 256), 256)
            PT[b, :, cols] = dot(GT[b], A2[:, :, cols].reshape(HF, 256)).astype(BF)
            return 0

        lax.fori_loop(0, len(blocks), one, 0)
        if b == NF - 1:
            st.pt = ReduceScatter4(PT, g.PTr1, g.PTxs, g.PTr2)

    def target_result():
        st.pt.finish()
        g.tgt_o[...] = (g.X1H[...] + (st.pt.total() + vec(5))).astype(BF)

    def fc2_grad_done():
        finish(*g2_ring)
        for k, ring in enumerate(g2_ring):
            g.g2_o[hc * k : hc * k + hc, :] = ring.total()

    def fc1_grad_trade():
        finish(*g1_ring)
        for k, ring in enumerate(g1_ring):
            E1[2 * k : 2 * k + 2] = ring.total().astype(BF).reshape(2, R, HF)
        F1[f] = E1[f]
        st.e1 = scatter(lambda j: E1.at[j], lambda j: F1.at[j], F1.at[pl.ds(0, 3)])

    def fc1_grad_done():
        received(st.e1)

    def out_grad_done():
        go_ring.finish()
        g.go_o[...] = go_ring.total()

    def qkv_grad_trade():
        finish(*gq_ring)
        for k, ring in enumerate(gq_ring):
            EQ[2 * k : 2 * k + 2] = ring.total().astype(BF).reshape(2, R, 3 * C)
        FQ[f] = EQ[f]
        st.eq = scatter(lambda j: EQ.at[j], lambda j: FQ.at[j], FQ.at[pl.ds(0, 3)])

    def qkv_grad_done():
        received(st.eq)

    def small_grad_trade():
        gs_ring.finish()
        SG[f] = gs_ring.total()
        st.sg = scatter(lambda j: SG.at[f], lambda j: SG.at[j], SG.at[pl.ds(0, 3)])

    def small_grad_done():
        received(st.sg)
        g.sg_o[...] = SG[0] + SG[1] + SG[2] + SG[3]

    start()
    o_ring.step(0)
    w2_ring[0].step(0)
    small_start()
    layout()
    cast_fc1()
    w2_ring[1].step(0)
    tokens_start()
    o_ring.step(1)
    cot_start()
    q_ring[0].step(0)
    visible()
    s_ring.step(0)
    q_ring[1].step(0)
    w1_ring[0].step(0)
    o_ring.step(2)
    q_ring[0].step(1)
    s_ring.step(1)
    q_ring[1].step(1)
    w1_ring[1].step(0)
    o_ring.step(3)
    st.tok.forward()
    q_ring[0].step(2)
    s_ring.step(2)
    q_ring[1].step(2)
    w1_ring[0].step(1)
    wo_start()
    w1_ring[1].step(1)
    s_ring.step(3)
    q_ring[0].step(3)
    st.cot.forward()
    q_ring[1].step(3)
    select_cot()
    w2_ring[0].step(1)
    w1_ring[0].step(2)
    small_vectors()
    first_norm()
    select_rows()
    w1_ring[1].step(2)
    project_half(0)
    project_half(1)
    context_attention()
    w1_ring[0].step(3)
    st.wo.forward()
    attend_target(3, 0)
    w2_ring[1].step(1)
    attend_target(0, 0)
    w1_ring[1].step(3)
    attend_target(3, 1)
    w2_ring[0].step(2)
    st.ov.forward()
    attend_target(2, 0)
    attend_target(2, 1)
    oa_start(1)
    context_middle()
    w2_ring[1].step(2)
    context_hidden()
    fc2_grad()
    g2_ring[1].step(0)
    attend_target(1, 0)
    w2_ring[0].step(3)
    attend_target(1, 1)
    transpose_attended()
    w2_ring[1].step(3)
    g2_ring[0].step(0)
    attend_target(0, 1)
    oa_start(0)
    st.oa[1].forward()
    g2_ring[1].step(1)
    hidden_grad()
    fc1_grad()
    g1_ring[0].step(0)
    context_partial()
    g2_ring[0].step(1)
    second_grad()
    g1_ring[1].step(0)
    st.pf.forward()
    st.n2.forward()
    g1_ring[0].step(1)
    st.oa[0].forward()
    target_middle(0)
    g2_ring[0].step(2)
    target_hidden(0)
    context_result()
    target_out(0)
    g1_ring[1].step(1)
    target_middle(1)
    target_hidden(1)
    second_norm_back()
    g1_ring[0].step(2)
    target_middle(2)
    target_middle(3)
    st.co.forward()
    target_hidden(2)
    target_out(2)
    g2_ring[0].step(3)
    home_context()
    g1_ring[1].step(2)
    st.dp.forward()
    target_hidden(3)
    target_out(1)
    attended_grad()
    attention_back()
    g1_ring[0].step(3)
    first_grad()
    target_out(3)
    qkv_grad()
    gq_ring[1].step(0)
    st.n1.forward()
    gq_ring[0].step(0)
    qkv_bias_grad()
    out_grad()
    g1_ring[1].step(3)
    st.pt.forward()
    gq_ring[1].step(1)
    first_norm_back()
    gs_ring.step(0)
    gq_ring[0].step(1)
    fc1_grad_trade()
    go_ring.step(0)
    g2_ring[1].step(2)
    gq_ring[1].step(2)
    gs_ring.step(1)
    gq_ring[0].step(2)
    target_result()
    go_ring.step(1)
    gq_ring[1].step(3)
    gs_ring.step(2)
    st.dx.forward()
    gq_ring[0].step(3)
    home_grad()
    fc1_grad_done()
    go_ring.step(2)
    gs_ring.step(3)
    g2_ring[1].step(3)
    qkv_grad_trade()
    go_ring.step(3)
    small_grad_trade()
    fc2_grad_done()
    qkv_grad_done()
    small_grad_done()
    out_grad_done()


def run_layer(n, tokens, cot, lengths, mask, counts, vectors, wqkv, wo, w1, w2, V):
    T, D = tokens.shape
    NF = 4
    FF = w1.shape[1]
    R = wo.shape[0]
    RP = R * NF
    HC = w2.shape[0]
    HF = HC * n
    C = D // NF
    VP = V * NF
    S_ = T * NF
    h2 = n // 2
    B, F = BF, F32
    vm = pltpu.VMEM
    scratch = dict(
        wqkv_v=vm((R, 3 * D), F), w1_v=vm((R, FF), F), wo_v=vm((R, D), F), w2_v=vm((HC, D), F),
        small_v=vm((8, 128), F), trig_v=vm((3, 128, 256), B),
        sq=vm((NF, R, 3 * C), B), s1=vm((NF, R, HF), B),
        AS=vm((n, NF, 8, 128), F), AQ=vm((n, RP, 3 * C), B), WO=vm((n, NF, R, D), B),
        A1=vm((n, RP, HF), B), A2=vm((n, HC, D), B),
        TA=vm((NF, T, D), B), CA=vm((NF, T, D), B), N1=vm((NF, T, D), B),
        OH=vm((S_, 128), B), CS=vm((S_, 256), F), SM=vm((VP, S_), B),
        VEC=vm((8, D), F), BQ=vm((8, 3 * D), F), BG=vm((8, 3 * D), F),
        Q=vm((S_, C), B), K=vm((S_, C), B), W=vm((S_, C), B),
        QV=vm((VP, C), B), KV=vm((VP, C), B), WV=vm((VP, C), B),
        OV=vm((NF, VP, C), B), PV=vm((C // HDIM, VP, VP), F), OA=vm((NF, S_, C), B),
        XV=vm((VP, D), B), N1V=vm((VP, D), B), DY=vm((VP, D), B),
        X1V=vm((VP, D), F), N2V=vm((VP, D), B), GV=vm((VP, HF), B), GP=vm((VP, HF), F),
        G2=vm((n, HC, D), B), G1=vm((n, RP, HF), B), GQ=vm((n, RP, 3 * C), B), GO=vm((n, R, D), F),
        VG=vm((n, 16, 128), F),
        st2=vm((HC, D), B), rr2=vm((h2, HC, D), B), rl2=vm((h2, HC, D), B),
        st1=vm((RP, HF), B), rr1=vm((h2, RP, HF), B), rl1=vm((h2, RP, HF), B),
        stq=vm((RP, 3 * C), B), rrq=vm((h2, RP, 3 * C), B), rlq=vm((h2, RP, 3 * C), B),
        sto=vm((R, D), B), rro=vm((h2, R, D), B), rlo=vm((h2, R, D), B),
        sts=vm((16, 128), F), rrs=vm((h2, 16, 128), F), rls=vm((h2, 16, 128), F),
        DH=vm((VP, HF), B), PN=vm((NF, V, D), B), PF=vm((NF, V, D), B),
        PNr1=vm((2, V, D), B), PNxs=vm((V, D), B), PNr2=vm((V, D), B),
        PMr1=vm((2, V, D), B), PMxs=vm((V, D), B), PMr2=vm((V, D), B),
        PFr1=vm((2, V, D), B), PFxs=vm((V, D), B), PFr2=vm((V, D), B),
        DX1=vm((V, D), F), DP=vm((NF, V, D), B), OT=vm((n, NF, R, VP), B), DO=vm((VP, C), B),
        DPRE=vm((VP, 3 * C), B), CO=vm((NF, V, D), B), DX=vm((NF, V, D), B),
        X1H=vm((T, D), F), GT=vm((NF, T, HF), B),
        PTr1=vm((2, T, D), B), PTxs=vm((T, D), B), PTr2=vm((T, D), B),
        SG=vm((NF, 16, 128), F),
        E1=vm((NF, R, HF), B), EQ=vm((NF, R, 3 * C), B),
        send_sems=pltpu.SemaphoreType.DMA((16,)), recv_sems=pltpu.SemaphoreType.DMA((59,)),
        local_sems=pltpu.SemaphoreType.DMA((16,)), mask_v=vm((1, T), jnp.int32), LT=vm((D, VP), B),
    )
    arr = jax.ShapeDtypeStruct
    ins = dict(
        lengths=lengths, counts=counts, tok=tokens, cot=cot, mask=mask.reshape(1, T), wqkv=wqkv, wo=wo,
        w1=w1, w2=w2, trig=jnp.asarray(trig_table()),
    )
    for k, v in enumerate(vectors):
        ins["in%d" % k] = v.reshape(1, -1)
        scratch["v%d" % k] = vm((1, v.shape[0]), F)
    outs = dict(
        tgt_o=vm((T, D), B), ctx_o=vm((T, D), B), dx_o=vm((T, D), B), gq_o=vm((NF, R, 3 * C), B),
        go_o=vm((R, D), F), g1_o=vm((NF, R, HF), B), g2_o=vm((HC, D), F), sg_o=vm((16, 128), F),
    )
    names = [*ins, *outs, *scratch]
    any_spec = pl.BlockSpec(memory_space=pl.ANY)
    return pl.pallas_call(
        functools.partial(layer_kernel, (n, D, FF, T, V), names),
        out_shape=list(outs.values()),
        in_specs=[pl.BlockSpec(memory_space=pltpu.SMEM)] * 2 + [any_spec] * (len(ins) - 2),
        out_specs=[pl.BlockSpec(memory_space=pltpu.VMEM)] * 8,
        scratch_shapes=list(scratch.values()),
        compiler_params=pltpu.CompilerParams(
            collective_id=0, has_side_effects=True, vmem_limit_bytes=62000000
        ),
        name="layer",
    )(*ins.values())


def outputs_kernel(dims, count, *refs):
    n, R, C, HC = dims
    NF = 4
    f = lax.axis_index("fsdp")
    tgt, ctx, dx, gq, go, g1, g2, sg = refs[:8]
    tgt_o, ctx_o, dx_o, gq_o, go_o, g1_o, g2_o = refs[8:15]
    vec_o = refs[15:23]
    gq_w, g1_w, sem_out = refs[23:]
    stores = []

    def store(src, dst):
        c = pltpu.make_async_copy(src, dst, sem_out.at[len(stores)])
        c.start()
        stores.append(c)

    for src, dst in ((g2, g2_o), (tgt, tgt_o), (ctx, ctx_o), (dx, dx_o), (go, go_o)):
        store(src, dst)
    D = NF * C
    for j in range(NF):
        for t in range(3):
            gq_w[:, D * t + C * j : D * t + C * j + C] = gq[j, :, C * t : C * t + C].astype(F32)
    store(gq_w, gq_o)
    for j in range(NF):
        for t in range(n):
            at = HC * (NF * t + j)
            g1_w[:, at : at + HC] = g1[j, :, HC * t : HC * t + HC].astype(F32)
    store(g1_w, g1_o)
    small = sg
    for k in range(6):
        vec_o[k][...] = pltpu.roll(small[k : k + 1, :], lax.rem(128 - R * f, 128), 1)[:, :R]
    rows = jnp.concatenate([small[6 + t : 7 + t, :] for t in range(3)], axis=1)
    vec_o[6][...] = pltpu.roll(rows, lax.rem(384 - 3 * R * f, 384), 1)[:, : 3 * R]
    mine = jnp.zeros((1, 128), F32)
    for j in range(NF):
        mine = jnp.where(f == j, small[9 + j : 10 + j, :], mine)
    vec_o[7][...] = mine
    for c in stores:
        c.wait()


def write_outputs(n, parts, R, D, FF, HC):
    NF = 4
    C = D // NF
    tgt = parts[0]
    arr = jax.ShapeDtypeStruct
    any_spec = pl.BlockSpec(memory_space=pl.ANY)
    big = [
        arr(tgt.shape, BF), arr(tgt.shape, BF), arr(tgt.shape, BF),
        arr((R, 3 * D), F32), arr((R, D), F32), arr((R, FF), F32), arr((HC, D), F32),
    ]
    small = [arr((1, w), F32) for w in (R,) * 6 + (3 * R, 4 * R)]
    return pl.pallas_call(
        functools.partial(outputs_kernel, (n, R, C, HC), 8),
        out_shape=big + small,
        in_specs=[pl.BlockSpec(memory_space=pltpu.VMEM)] * 8,
        out_specs=[any_spec] * 7 + [pl.BlockSpec(memory_space=pltpu.VMEM)] * 8,
        scratch_shapes=[
            pltpu.VMEM((R, 3 * D), F32), pltpu.VMEM((R, FF), F32), pltpu.SemaphoreType.DMA((7,)),
        ],
        compiler_params=pltpu.CompilerParams(vmem_limit_bytes=1 << 22),
        name="outputs",
    )(*[pltpu.with_memory_space_constraint(v, pltpu.VMEM) for v in parts])


def on_device(
    tokens, lengths, visibility_mask, visible_counts, ln1_gain, ln1_bias, qkv_weight, qkv_bias,
    out_weight, out_bias, ln2_gain, ln2_bias, fc1_weight, fc1_bias, fc2_weight, fc2_bias, context_cot,
):
    n = lax.axis_size("dp")
    R, D = out_weight.shape
    vectors = (ln1_gain, ln1_bias, ln2_gain, ln2_bias, out_bias, fc2_bias, qkv_bias, fc1_bias)
    parts = run_layer(
        n, tokens, context_cot, lengths, visibility_mask, visible_counts, vectors,
        qkv_weight, out_weight, fc1_weight, fc2_weight, VIS_DEV,
    )
    tgt, ctx, dx, gq, go, g1, g2, *small = write_outputs(
        n, parts, R, D, fc1_weight.shape[1], fc2_weight.shape[0]
    )
    gg1, gb1, gg2, gb2, gbo, gc2, gbq, gc1 = [v.reshape(-1) for v in small]
    return (tgt, ctx, dx, gg1, gb1, gq, gbq, go, gbo, gg2, gb2, g1, gc1, g2, gc2)


def layer_norm(inputs, scale_vec, shift_vec):
    center = inputs - jnp.mean(inputs, axis=-1, keepdims=True)
    spread = jnp.mean(center * center, axis=-1, keepdims=True)
    return center * lax.rsqrt(spread + norm_eps) * scale_vec + shift_vec


def gelu_erf(values):
    return jax.nn.gelu(values, approximate=False)


def pack_layout(seq_lens, pack_len):
    seq_ends = jnp.cumsum(seq_lens)
    places = jnp.arange(pack_len, dtype=jnp.int32)
    passed = places[:, None] >= seq_ends[None, :]
    segment = jnp.sum(passed.astype(jnp.int32), axis=1)
    before = jnp.sum(jnp.where(passed, seq_lens[None, :], 0), axis=1)
    return (segment, places - before)


def rope_tables(places):
    frame_index = (places // (GRID * GRID)).astype(jnp.float32)
    grid_row = (places // GRID % GRID).astype(jnp.float32)
    grid_col = (places % GRID).astype(jnp.float32)
    pair_index = jnp.arange(HDIM // 2, dtype=jnp.int32)
    axis_pick = jnp.minimum(pair_index // 11, 2)
    pair_order = (pair_index - 11 * axis_pick).astype(jnp.float32)
    frequency = jnp.exp(pair_order * (-math.log(10000.0) / 11.0))
    angles = (
        frame_index[:, None] * (axis_pick == 0).astype(jnp.float32)[None, :]
        + grid_row[:, None] * (axis_pick == 1).astype(jnp.float32)[None, :]
        + grid_col[:, None] * (axis_pick == 2).astype(jnp.float32)[None, :]
    ) * frequency[None, :]
    return (jnp.cos(angles), jnp.sin(angles))


def rotate(heads, cosine_table, sine_table):
    half_size = heads.shape[-1] // 2
    first_half = heads[..., :half_size]
    second_half = heads[..., half_size:]
    cosine_cols = cosine_table[:, None, :]
    sine_cols = sine_table[:, None, :]
    return jnp.concatenate(
        [
            first_half * cosine_cols - second_half * sine_cols,
            second_half * cosine_cols + first_half * sine_cols,
        ],
        axis=-1,
    )


def rotate_back(grads, cosine_table, sine_table):
    half_size = grads.shape[-1] // 2
    first_half = grads[..., :half_size]
    second_half = grads[..., half_size:]
    cosine_cols = cosine_table[:, None, :]
    sine_cols = sine_table[:, None, :]
    return jnp.concatenate(
        [
            first_half * cosine_cols + second_half * sine_cols,
            second_half * cosine_cols - first_half * sine_cols,
        ],
        axis=-1,
    )


def project(token_rows, weights, cosine_table, sine_table):
    inputs = token_rows.astype(jnp.float32)
    row_count = inputs.shape[0]
    model_width = inputs.shape[1]
    normed = layer_norm(
        inputs, weights[0].astype(jnp.float32), weights[1].astype(jnp.float32)
    ).astype(jnp.bfloat16)
    joined = jnp.dot(normed, weights[2], preferred_element_type=jnp.float32) + weights[3].astype(
        jnp.float32
    )
    query_heads = rotate(
        joined[:, :model_width].reshape(row_count, HEADS, HDIM), cosine_table, sine_table
    ).astype(jnp.bfloat16)
    key_flat = (
        rotate(
            joined[:, model_width : 2 * model_width].reshape(row_count, HEADS, HDIM),
            cosine_table,
            sine_table,
        )
        .astype(jnp.bfloat16)
        .reshape(row_count, model_width)
    )
    value_flat = joined[:, 2 * model_width :].astype(jnp.bfloat16)
    return (inputs, normed, query_heads, key_flat, value_flat)


def attend(query_heads, key_flat, value_flat, seg_query, seg_key):
    key_heads = key_flat.reshape(key_flat.shape[0], HEADS, HDIM)
    value_heads = value_flat.reshape(value_flat.shape[0], HEADS, HDIM)
    scores = jnp.einsum(
        "qhd,khd->hqk", query_heads, key_heads, preferred_element_type=jnp.float32
    ) * HDIM ** (-0.5)
    allowed = seg_query[:, None] == seg_key[None, :]
    masked = jnp.where(allowed[None], scores, masked_fill)
    row_max = jnp.max(masked, axis=-1, keepdims=True)
    raised = jnp.exp(masked - row_max)
    totals = jnp.sum(raised, axis=-1, keepdims=True)
    attn_probs = (raised / totals).astype(jnp.bfloat16)
    attended = jnp.einsum(
        "hqk,khd->qhd", attn_probs, value_heads, preferred_element_type=jnp.float32
    )
    return (
        attended.reshape(query_heads.shape[0], -1).astype(jnp.bfloat16),
        row_max + jnp.log(totals),
    )


def attend_back(query_heads, key_flat, value_flat, seg_query, seg_key, log_total, grad_att):
    key_heads = key_flat.reshape(key_flat.shape[0], HEADS, HDIM)
    value_heads = value_flat.reshape(value_flat.shape[0], HEADS, HDIM)
    scale_factor = HDIM ** (-0.5)
    scores = (
        jnp.einsum("qhd,khd->hqk", query_heads, key_heads, preferred_element_type=jnp.float32)
        * scale_factor
    )
    allowed = seg_query[:, None] == seg_key[None, :]
    masked = jnp.where(allowed[None], scores, masked_fill)
    attn_probs = jnp.exp(masked - log_total)
    grad_heads = grad_att.reshape(grad_att.shape[0], HEADS, HDIM)
    grad_probs = jnp.einsum(
        "qhd,khd->hqk", grad_heads, value_heads, preferred_element_type=jnp.float32
    )
    row_delta = jnp.sum(attn_probs * grad_probs, axis=-1, keepdims=True)
    grad_scores = (attn_probs * (grad_probs - row_delta)).astype(jnp.bfloat16)
    grad_query = (
        jnp.einsum("hqk,khd->qhd", grad_scores, key_heads, preferred_element_type=jnp.float32)
        * scale_factor
    )
    grad_key = (
        jnp.einsum("hqk,qhd->khd", grad_scores, query_heads, preferred_element_type=jnp.float32)
        * scale_factor
    )
    grad_value = jnp.einsum(
        "hqk,qhd->khd",
        attn_probs.astype(jnp.bfloat16),
        grad_heads,
        preferred_element_type=jnp.float32,
    )
    return (
        grad_query,
        grad_key.reshape(key_flat.shape[0], -1),
        grad_value.reshape(value_flat.shape[0], -1),
    )


def finish(inputs, attended, weights):
    middle = inputs + (
        jnp.dot(attended, weights[4], preferred_element_type=jnp.float32)
        + weights[5].astype(jnp.float32)
    )
    second = layer_norm(
        middle, weights[6].astype(jnp.float32), weights[7].astype(jnp.float32)
    ).astype(jnp.bfloat16)
    hidden = jnp.dot(second, weights[8], preferred_element_type=jnp.float32) + weights[9].astype(
        jnp.float32
    )
    activated = gelu_erf(hidden).astype(jnp.bfloat16)
    result = middle + (
        jnp.dot(activated, weights[10], preferred_element_type=jnp.float32)
        + weights[11].astype(jnp.float32)
    )
    return (result, middle, second, hidden, activated)


def gathered_device(
    tokens,
    lengths,
    visibility_mask,
    visible_counts,
    ln1_gain,
    ln1_bias,
    qkv_weight,
    qkv_bias,
    out_weight,
    out_bias,
    ln2_gain,
    ln2_bias,
    fc1_weight,
    fc1_bias,
    fc2_weight,
    fc2_bias,
    context_cot,
):
    tok_rows = tokens.shape[0]
    model_width = tokens.shape[1]
    groups = lax.axis_size("fsdp")
    member = lax.axis_index("fsdp")
    pack_len = tok_rows * groups
    vis_rows = VIS_DEV
    vis_pack = vis_rows * groups
    zero_low = jnp.zeros((), jnp.bfloat16)
    shards = [
        weight.astype(jnp.bfloat16)
        for weight in (
            ln1_gain,
            ln1_bias,
            qkv_weight,
            qkv_bias,
            out_weight,
            out_bias,
            ln2_gain,
            ln2_bias,
            fc1_weight,
            fc1_bias,
            fc2_weight,
            fc2_bias,
        )
    ]
    weights = (
        lax.all_gather(shards[0], ("dp", "fsdp"), axis=0, tiled=True),
        lax.all_gather(shards[1], ("dp", "fsdp"), axis=0, tiled=True),
        lax.all_gather(shards[2], ("dp", "fsdp"), axis=0, tiled=True),
        lax.all_gather(shards[3], ("dp", "fsdp"), axis=0, tiled=True),
        lax.all_gather(shards[4], ("dp", "fsdp"), axis=0, tiled=True),
        lax.all_gather(shards[5], ("dp", "fsdp"), axis=0, tiled=True),
        lax.all_gather(shards[6], ("dp", "fsdp"), axis=0, tiled=True),
        lax.all_gather(shards[7], ("dp", "fsdp"), axis=0, tiled=True),
        lax.all_gather(shards[8], ("dp", "fsdp"), axis=0, tiled=True),
        lax.all_gather(shards[9], ("dp", "fsdp"), axis=0, tiled=True),
        lax.all_gather(shards[10], ("dp", "fsdp"), axis=0, tiled=True),
        lax.all_gather(shards[11], ("dp", "fsdp"), axis=0, tiled=True),
    )
    segment, places = pack_layout(lengths[0], pack_len)
    home_rows = member * tok_rows + jnp.arange(tok_rows, dtype=jnp.int32)
    seg_home = jnp.take(segment, home_rows)
    cos_home, sin_home = rope_tables(jnp.take(places, home_rows))
    inputs, normed, query_heads, key_flat, value_flat = project(tokens, weights, cos_home, sin_home)
    key_pack, value_pack = (
        lax.all_gather(key_flat, "fsdp", axis=0, tiled=True),
        lax.all_gather(value_flat, "fsdp", axis=0, tiled=True),
    )
    attended = attend(query_heads, key_pack, value_pack, seg_home, segment)[0]
    target_out = finish(inputs, attended, weights)[0].astype(jnp.bfloat16)
    running = jnp.cumsum(visibility_mask)
    visible_here = visibility_mask * (running <= visible_counts[0, 0]).astype(jnp.int32)
    visible_all = lax.all_gather(visible_here, "fsdp", axis=0, tiled=True)
    inclusive = jnp.cumsum(visible_all)
    rank_index = jnp.arange(vis_pack, dtype=jnp.int32)
    row_of = jnp.sum((inclusive[None, :] <= rank_index[:, None]).astype(jnp.int32), axis=1)
    owner_dev = row_of // tok_rows
    local_row = row_of % tok_rows
    mine_here = (owner_dev == member)[:, None]
    send_tokens = jnp.where(mine_here, jnp.take(tokens, local_row, axis=0), zero_low)
    send_cot = jnp.where(mine_here, jnp.take(context_cot, local_row, axis=0), zero_low)
    recv_tokens, recv_cot = (
        lax.all_to_all(send_tokens, "fsdp", split_axis=0, concat_axis=0, tiled=True),
        lax.all_to_all(send_cot, "fsdp", split_axis=0, concat_axis=0, tiled=True),
    )
    slot_index = jnp.arange(vis_rows, dtype=jnp.int32)
    my_ranks = member * vis_rows + slot_index
    my_owner = jnp.take(owner_dev, my_ranks)
    my_row = jnp.take(row_of, my_ranks)
    picked = my_owner * vis_rows + slot_index
    bal_tokens = jnp.take(recv_tokens, picked, axis=0)
    bal_cot = jnp.take(recv_cot, picked, axis=0)
    seg_bal = jnp.take(segment, my_row)
    seg_keys = jnp.take(segment, row_of)
    cos_bal, sin_bal = rope_tables(jnp.take(places, my_row))
    inputs_bal, normed_bal, query_bal, key_bal, value_bal = project(
        bal_tokens, weights, cos_bal, sin_bal
    )
    key_vis, value_vis = (
        lax.all_gather(key_bal, "fsdp", axis=0, tiled=True),
        lax.all_gather(value_bal, "fsdp", axis=0, tiled=True),
    )
    attended_bal, log_total = attend(query_bal, key_vis, value_vis, seg_bal, seg_keys)
    result_bal, middle_bal, second_bal, hidden_bal, activated_bal = finish(
        inputs_bal, attended_bal, weights
    )
    grad_result = bal_cot.astype(jnp.float32)
    result_low = grad_result.astype(jnp.bfloat16)
    grad_fc2 = jnp.einsum(
        "nf,nd->fd", activated_bal, result_low, preferred_element_type=jnp.float32
    )
    grad_bfc2 = jnp.sum(result_low.astype(jnp.float32), axis=0)
    grad_activated = jnp.einsum(
        "nd,fd->nf", result_low, weights[10], preferred_element_type=jnp.float32
    )
    gelu_pull = jax.vjp(gelu_erf, hidden_bal)[1]
    hidden_low = gelu_pull(grad_activated)[0].astype(jnp.bfloat16)
    grad_fc1 = jnp.einsum("nd,nf->df", second_bal, hidden_low, preferred_element_type=jnp.float32)
    grad_bfc1 = jnp.sum(hidden_low.astype(jnp.float32), axis=0)
    grad_second = jnp.einsum(
        "nf,df->nd", hidden_low, weights[8], preferred_element_type=jnp.float32
    )
    norm_two_pull = jax.vjp(
        layer_norm, middle_bal, weights[6].astype(jnp.float32), weights[7].astype(jnp.float32)
    )[1]
    grad_mid_norm, grad_gain_two, grad_shift_two = norm_two_pull(grad_second)
    grad_middle = grad_result + grad_mid_norm
    middle_low = grad_middle.astype(jnp.bfloat16)
    grad_wout = jnp.einsum(
        "nd,ne->de", attended_bal, middle_low, preferred_element_type=jnp.float32
    )
    grad_bout = jnp.sum(middle_low.astype(jnp.float32), axis=0)
    grad_att = jnp.einsum(
        "ne,de->nd", middle_low, weights[4], preferred_element_type=jnp.float32
    ).astype(jnp.bfloat16)
    grad_query, grad_key_all, grad_value_all = attend_back(
        query_bal, key_vis, value_vis, seg_bal, seg_keys, log_total, grad_att
    )
    grad_key_own, grad_value_own = (
        lax.psum_scatter(
            grad_key_all.astype(jnp.bfloat16), "fsdp", scatter_dimension=0, tiled=True
        ).astype(jnp.float32),
        lax.psum_scatter(
            grad_value_all.astype(jnp.bfloat16), "fsdp", scatter_dimension=0, tiled=True
        ).astype(jnp.float32),
    )
    grad_query_pre = rotate_back(grad_query, cos_bal, sin_bal).reshape(vis_rows, model_width)
    grad_key_pre = rotate_back(
        grad_key_own.reshape(vis_rows, HEADS, HDIM), cos_bal, sin_bal
    ).reshape(vis_rows, model_width)
    joined_low = jnp.concatenate([grad_query_pre, grad_key_pre, grad_value_own], axis=1).astype(
        jnp.bfloat16
    )
    grad_wqkv = jnp.einsum("nd,ne->de", normed_bal, joined_low, preferred_element_type=jnp.float32)
    grad_bqkv = jnp.sum(joined_low.astype(jnp.float32), axis=0)
    grad_normed = jnp.einsum(
        "ne,de->nd", joined_low, weights[2], preferred_element_type=jnp.float32
    )
    norm_one_pull = jax.vjp(
        layer_norm, inputs_bal, weights[0].astype(jnp.float32), weights[1].astype(jnp.float32)
    )[1]
    grad_in_norm, grad_gain_one, grad_shift_one = norm_one_pull(grad_normed)
    grad_inputs = grad_middle + grad_in_norm
    destinations = jnp.arange(groups, dtype=jnp.int32)
    route_mask = (my_owner[None, :] == destinations[:, None])[:, :, None]
    send_out = jnp.where(route_mask, result_bal.astype(jnp.bfloat16)[None], zero_low).reshape(
        vis_pack, model_width
    )
    send_grad = jnp.where(route_mask, grad_inputs.astype(jnp.bfloat16)[None], zero_low).reshape(
        vis_pack, model_width
    )
    back_out, back_grad = (
        lax.all_to_all(send_out, "fsdp", split_axis=0, concat_axis=0, tiled=True),
        lax.all_to_all(send_grad, "fsdp", split_axis=0, concat_axis=0, tiled=True),
    )
    rank_home = jnp.maximum(jnp.take(inclusive, home_rows) - 1, 0)
    is_visible = (visible_here > 0)[:, None]
    context_out = jnp.where(is_visible, jnp.take(back_out, rank_home, axis=0), zero_low)
    tokens_grad = jnp.where(is_visible, jnp.take(back_grad, rank_home, axis=0), zero_low)
    grad_list = [
        grad_gain_one,
        grad_shift_one,
        grad_wqkv,
        grad_bqkv,
        grad_wout,
        grad_bout,
        grad_gain_two,
        grad_shift_two,
        grad_fc1,
        grad_bfc1,
        grad_fc2,
        grad_bfc2,
    ]
    reduced = (
        lax.psum_scatter(grad_list[0], ("dp", "fsdp"), scatter_dimension=0, tiled=True),
        lax.psum_scatter(grad_list[1], ("dp", "fsdp"), scatter_dimension=0, tiled=True),
        lax.psum_scatter(grad_list[2], ("dp", "fsdp"), scatter_dimension=0, tiled=True),
        lax.psum_scatter(grad_list[3], ("dp", "fsdp"), scatter_dimension=0, tiled=True),
        lax.psum_scatter(grad_list[4], ("dp", "fsdp"), scatter_dimension=0, tiled=True),
        lax.psum_scatter(grad_list[5], ("dp", "fsdp"), scatter_dimension=0, tiled=True),
        lax.psum_scatter(grad_list[6], ("dp", "fsdp"), scatter_dimension=0, tiled=True),
        lax.psum_scatter(grad_list[7], ("dp", "fsdp"), scatter_dimension=0, tiled=True),
        lax.psum_scatter(grad_list[8], ("dp", "fsdp"), scatter_dimension=0, tiled=True),
        lax.psum_scatter(grad_list[9], ("dp", "fsdp"), scatter_dimension=0, tiled=True),
        lax.psum_scatter(grad_list[10], ("dp", "fsdp"), scatter_dimension=0, tiled=True),
        lax.psum_scatter(grad_list[11], ("dp", "fsdp"), scatter_dimension=0, tiled=True),
    )
    return (
        target_out,
        context_out,
        tokens_grad,
        reduced[0],
        reduced[1],
        reduced[2],
        reduced[3],
        reduced[4],
        reduced[5],
        reduced[6],
        reduced[7],
        reduced[8],
        reduced[9],
        reduced[10],
        reduced[11],
    )


def per_device(tokens, *rest):
    n, group = lax.axis_size("dp"), lax.axis_size("fsdp")
    out_rows = rest[7].shape[0]
    fits = group == 4 and n == 8 and out_rows * group == 128
    return (on_device if fits else gathered_device)(tokens, *rest)


def solution(mesh):
    both = ("dp", "fsdp")
    vec, mat = P(both), P(both, None)
    return jax.shard_map(
        per_device,
        mesh=mesh,
        in_specs=(
            mat, P("dp", None), vec, P("dp", "fsdp"), vec, vec, mat, vec, mat, vec, vec, vec,
            mat, vec, mat, vec, mat,
        ),
        out_specs=(mat, mat, mat, vec, vec, mat, vec, mat, vec, vec, vec, mat, vec, mat, vec),
        check_vma=False,
    )
```

```python
import functools
import math
import types

import jax
import jax.numpy as jnp
import numpy as np
from jax import lax
from jax.experimental import pallas as pl
from jax.experimental.pallas import tpu as pltpu
from jax.sharding import PartitionSpec as P

HEADS = 16
HDIM = 64
GRID = 14
VIS_DEV = 64
norm_eps = 1e-06
masked_fill = -1e30
FRAMES = 8
EPS = 1e-06
FILL = -1e30
BF = jnp.bfloat16
F32 = jnp.float32
MESH = pl.DeviceIdType.MESH
NT = (((1,), (1,)), ((), ()))
NN = (((1,), (0,)), ((), ()))
TN = (((0,), (0,)), ((), ()))


def dot(a, b, dims=NN):
    return lax.dot_general(a, b, dims, preferred_element_type=F32)


def trig_table():
    width = FRAMES + 2 * GRID
    lane = np.arange(2 * HDIM)
    pair = lane % (HDIM // 2)
    axis = np.minimum(pair // 11, 2)
    freq = np.exp(((pair - 11 * axis).astype(np.float32)) * np.float32(-math.log(10000.0) / 11.0))
    sign = np.where(lane % HDIM < HDIM // 2, -1.0, 1.0)
    table = np.zeros((128, 4 * HDIM), np.float32)
    row = np.arange(width)
    kind = np.where(row < FRAMES, 0, np.where(row < FRAMES + GRID, 1, 2))
    coord = np.where(kind == 0, row, np.where(kind == 1, row - FRAMES, row - FRAMES - GRID))
    angle = (coord[:, None].astype(np.float32) * freq[None, :].astype(np.float32)).astype(np.float64)
    here = kind[:, None] == axis[None, :]
    table[:width, : 2 * HDIM] = np.where(here, np.cos(angle), 0.0)
    table[:width, 2 * HDIM :] = np.where(here, np.sin(angle) * sign[None, :], 0.0)
    parts = []
    rest = table
    for _ in range(3):
        part = rest.astype(jnp.bfloat16)
        parts.append(part)
        rest = rest - part.astype(np.float32)
    return np.stack(parts)


def norm_stats(v):
    center = v - jnp.mean(v, axis=-1, keepdims=True)
    inv = lax.rsqrt(jnp.mean(center * center, axis=-1, keepdims=True) + EPS)
    return center * inv, inv


def norm_back(v, gain, grad):
    xhat, inv = norm_stats(v)
    gg = grad * gain
    dv = inv * (
        gg - jnp.mean(gg, axis=-1, keepdims=True) - xhat * jnp.mean(gg * xhat, axis=-1, keepdims=True)
    )
    return (
        dv,
        jnp.sum(grad * xhat, axis=0, keepdims=True),
        jnp.sum(grad, axis=0, keepdims=True),
    )


def swap_halves(u):
    lane = lax.broadcasted_iota(jnp.int32, u.shape, 1)
    return jnp.where(
        lax.rem(lane, HDIM) < HDIM // 2,
        pltpu.roll(u, u.shape[1] - HDIM // 2, 1),
        pltpu.roll(u, HDIM // 2, 1),
    )


def column_segment(start, rows, ends):
    row = start + lax.broadcasted_iota(jnp.int32, (rows, 1), 0)
    seg = jnp.zeros((rows, 1), jnp.int32)
    for end in ends:
        seg += (row >= end).astype(jnp.int32)
    return row, seg


ALIASES = dict(N2="N1", PT="N1", X1B="GP")


class Sems:
    def __init__(self, send, recv):
        self.send, self.recv = send, recv
        self.sends = self.recvs = self.clock = 0
        self.idle_sends, self.idle_recvs, self.waited = [], [], []

    def take_send(self):
        if self.idle_sends:
            return self.idle_sends.pop()
        self.sends += 1
        return self.send.at[self.sends - 1]

    def give_send(self, sem):
        self.idle_sends.append(sem)

    def take_recv(self):
        self.recvs += 1
        return self.recv.at[self.recvs - 1]

    def ring_sent(self):
        rs = self.idle_recvs.pop() if self.idle_recvs else self.take_recv()
        self.clock += 1
        return rs, self.clock

    def ring_landed(self, sem, sent):
        self.idle_recvs += [old for at, old in self.waited if at < sent]
        self.waited = [(at, old) for at, old in self.waited if at >= sent]
        self.waited.append((self.clock, sem))


def layer_kernel(dims, names, *refs):
    n, D, FF, T, V = dims
    NF = 4
    R = D // (n * NF)
    RP = R * NF
    HC = FF // (NF * n)
    HF = FF // NF
    C = D // NF
    VP = V * NF
    S_ = T * NF
    last = n // 2 - 1
    given = dict(zip(names, refs))
    g = types.SimpleNamespace(**given, **{a: given[b] for a, b in ALIASES.items()})
    sems = Sems(g.send_sems, g.recv_sems)
    lsem = g.local_sems

    p = lax.axis_index("dp")
    f = lax.axis_index("fsdp")
    f1 = f + 1 - 2 * lax.rem(f, 2)
    f2 = lax.rem(f + 2, NF)
    f3 = NF - 1 - f
    par = lax.rem(p, 2)
    half_p = lax.div(p, 2)
    pos = (1 - par) * half_p + par * (n - 1 - half_p)

    def idx(q):
        q = lax.rem(q + 2 * n, n)
        up = lax.div(q, n // 2)
        return (1 - up) * (2 * q) + up * (2 * (n - 1 - q) + 1)

    right, left = idx(pos + 1), idx(pos - 1)

    def launch(src, dst, ss, rs, to):
        c = pltpu.make_async_remote_copy(
            src_ref=src, dst_ref=dst, send_sem=ss, recv_sem=rs, device_id=to, device_id_type=MESH
        )
        c.start()
        return c

    def sent(copies):
        for c in copies:
            c.wait_send()
            sems.give_send(c.src_sem)

    def received(copies):
        for c in copies:
            c.wait_recv()
        sent(copies)

    def remote(src, dst, to):
        ss, rs = sems.take_send(), sems.take_recv()
        return launch(src, dst, ss, rs, to), ss, rs

    def arrival(dst, ss, rs, to):
        return pltpu.make_async_remote_copy(
            src_ref=dst, dst_ref=dst, send_sem=ss, recv_sem=rs, device_id=to, device_id_type=MESH
        )

    to1, to2, to3 = {"fsdp": f1}, {"fsdp": f2}, {"fsdp": f3}
    peers = ((f1, to1), (f2, to2), (f3, to3))

    barrier = pltpu.get_barrier_semaphore()
    for to in (to1, to2, to3, {"dp": right}, {"dp": left}):
        pl.semaphore_signal(barrier, inc=1, device_id=to, device_id_type=MESH)

    loads = {}
    for i, (src, dst) in enumerate(
        (
            (g.wqkv, g.wqkv_v),
            (g.w1, g.w1_v),
            (g.wo, g.wo_v),
            (g.mask, g.mask_v),
            (g.tok, g.TA.at[f]),
            (g.w2, g.w2_v),
            (g.cot, g.CA.at[f]),
            (g.trig, g.trig_v),
        )
    ):
        c = pltpu.make_async_copy(src, dst, lsem.at[i])
        c.start()
        loads[i] = c
    vectors = []
    for k in range(8):
        vectors.append(pltpu.make_async_copy(given["in%d" % k], given["v%d" % k], lsem.at[8 + k]))
        vectors[k].start()

    AS, AQ, WO, A1, A2 = g.AS, g.AQ, g.WO, g.A1, g.A2
    TA, CA = g.TA, g.CA

    loads[5].wait()
    A2[p] = g.w2_v[...].astype(BF)
    loads[0].wait()
    for j in range(NF):
        for t in range(3):
            g.sq[j, :, C * t : C * t + C] = g.wqkv_v[:, D * t + C * j : D * t + C * j + C].astype(BF)
    AQ[p, pl.ds(pl.multiple_of(R * f, R), R), :] = g.sq[f]
    loads[2].wait()
    WO[p, f] = g.wo_v[...].astype(BF)
    pl.semaphore_wait(barrier, 5)

    def scatter(src, dst, three):
        ss, rs = sems.take_send(), sems.take_recv()
        for fj, to in peers:
            launch(src(fj), dst(f), ss, rs, to)
        return (arrival(three, ss, rs, to1),)

    class AllGather4:
        def __init__(self, slot):
            self.slot = slot
            self.done = False
            c, ss, rs = remote(slot(f), slot(f), to2)
            d, sd, rd = remote(slot(f), slot(f), to1)
            self.across = arrival(slot(f2), ss, rs, to2)
            self.beside = arrival(slot(f1), sd, rd, to1)
            self.copies = [c, d]

        def forward(self):
            self.across.wait_recv()
            c, ss, rs = remote(self.slot(f2), self.slot(f2), to1)
            self.passed = arrival(self.slot(f3), ss, rs, to1)
            self.copies.append(c)

        def finish(self):
            if not self.done:
                self.done = True
                self.beside.wait_recv()
                self.passed.wait_recv()
                sent(self.copies)

    class ReduceScatter4:
        def __init__(self, part, r1, xs, r2):
            self.part, self.r1, self.xs, self.r2 = part, r1, xs, r2
            c, ss, rs = remote(part.at[f3], r1.at[1], to1)
            d, sd, rd = remote(part.at[f1], r1.at[0], to1)
            self.other = arrival(r1.at[1], ss, rs, to1)
            self.own = arrival(r1.at[0], sd, rd, to1)
            self.copies = [c, d]

        def forward(self):
            self.other.wait_recv()
            self.xs[...] = (self.part[f2].astype(F32) + self.r1[1].astype(F32)).astype(BF)
            c, ss, rs = remote(self.xs, self.r2, to2)
            self.across = arrival(self.r2, ss, rs, to2)
            self.copies.append(c)

        def finish(self):
            self.own.wait_recv()
            self.across.wait_recv()
            sent(self.copies)

        def total(self):
            return self.part[f].astype(F32) + self.r1[0].astype(F32) + self.r2[...].astype(F32)

    class RingGather:
        def __init__(self, view, pair, rows):
            self.view, self.pair, self.rows = view, pair, rows
            self.before, self.flight = (), None

        def landed(self):
            received(self.before)
            self.before = ()
            if self.flight is not None:
                received([self.flight])
                sems.ring_landed(self.flight.dst_sem, self.at)
                self.flight = None

        def step(self, r):
            self.landed()
            h = self.rows // 2
            spans = ((0, self.rows), (0, self.rows)) if r < last else ((0, h), (h, h))
            ss = sems.take_send()
            rs, self.at = sems.ring_sent()
            for way, (s, c) in zip((1, -1), spans):
                piece = self.view(idx(pos - way * r), s, c)
                launch(piece, piece, ss, rs, {"dp": right if way == 1 else left})
            both = self.pair if r < last else self.view(0, 0, self.rows)
            self.flight = arrival(both, ss, rs, {"dp": left})

        def finish(self):
            self.landed()

    def row_rings(ref):
        h = ref.shape[1] // 2

        def ring(offset):
            view = lambda slot, s, c: ref.at[slot, pl.ds(offset + s, c), :]
            return RingGather(view, ref.at[pl.ds(0, 2), pl.ds(offset, h), :], h)

        return [ring(0), ring(h)]

    q_ring, w1_ring, w2_ring = row_rings(AQ), row_rings(A1), row_rings(A2)
    o_ring = RingGather(lambda slot, s, c: WO.at[slot, f, pl.ds(s, c), :], WO.at[pl.ds(0, 2), f], R)
    s_ring = RingGather(lambda slot, s, c: AS.at[slot, pl.ds(s, c)], AS.at[pl.ds(0, 2)], NF)

    class RingReduce:
        def __init__(self, grads, start, rows, st, rr, rl, wire=BF):
            self.G, self.o, self.rows, self.st, self.rr, self.rl = grads, start, rows, st, rr, rl
            self.wire = wire
            self.flight = None

        def landed(self):
            if self.flight is not None:
                received([self.flight])
                sems.ring_landed(self.flight.dst_sem, self.at)
                self.flight = None

        def step(self, r):
            self.landed()
            o, rows = self.o, self.rows
            hh = rows // 2
            whole = pl.ds(o, rows)
            ss = sems.take_send()
            rs, self.at = sems.ring_sent()
            ways = ((1, self.rr, 0, {"dp": right}), (-1, self.rl, hh, {"dp": left}))
            if r == 0:
                far = idx(pos + n // 2)
                self.st[whole, :] = self.G[far, whole, :].astype(self.wire)
                for _, buf, s, to in ways:
                    half = pl.ds(o + s, hh)
                    launch(self.st.at[half, :], buf.at[0, half, :], ss, rs, to)
                self.flight = arrival(self.st.at[whole, :], ss, rs, {"dp": left})
                return
            for way, buf, s, to in ways:
                c = idx(pos + way * (n // 2 - r))
                if r == 1:
                    half, other = pl.ds(o + s, hh), pl.ds(o + hh - s, hh)
                    total = buf[0, half, :].astype(F32) + self.G[c, half, :].astype(F32)
                    buf[0, half, :] = total.astype(self.wire)
                    buf[0, other, :] = self.G[c, other, :].astype(self.wire)
                else:
                    total = buf[r - 1, whole, :].astype(F32) + self.G[c, whole, :].astype(F32)
                    buf[r - 1, whole, :] = total.astype(self.wire)
                launch(buf.at[r - 1, whole, :], buf.at[r, whole, :], ss, rs, to)
            self.flight = arrival(self.rr.at[pl.ds(0, 2), whole, :], ss, rs, {"dp": left})

        def finish(self):
            self.landed()

        def total(self):
            o, rows = self.o, self.rows
            return (
                self.G[p, pl.ds(o, rows), :].astype(F32)
                + self.rr[last, pl.ds(o, rows), :].astype(F32)
                + self.rl[last, pl.ds(o, rows), :].astype(F32)
            )

    st = types.SimpleNamespace(oa=[None, None])
    N1, N2, GT, PT = g.N1, g.N2, g.GT, g.PT
    VEC, BQ, BG, VG = g.VEC, g.BQ, g.BG, g.VG
    Q, K, W, QV, KV, WV = g.Q, g.K, g.W, g.QV, g.KV, g.WV
    SM, OV, PV, OA, OT = g.SM, g.OV, g.PV, g.OA, g.OT
    XV, N1V, DY, X1V, N2V = g.XV, g.N1V, g.DY, g.X1V, g.N2V
    GV, GP, DH, PN, PF = g.GV, g.GP, g.DH, g.PN, g.PF
    G2, G1, GQ, GO = g.G2, g.G1, g.GQ, g.GO
    DO, DPRE = g.DO, g.DPRE
    E1, F1, EQ, FQ, SG = g.E1, g.g1_o, g.EQ, g.gq_o, g.SG
    blocks = [slice(256 * k, 256 * k + 256) for k in range(D // 256)]
    mine = pl.ds(pl.multiple_of(V * f, V), V)
    hc, hr = HC // 2, RP // 2
    g2_ring = [
        RingReduce(G2, 0, hc, g.st2, g.rr2, g.rl2),
        RingReduce(G2, hc, hc, g.st2, g.rr2, g.rl2),
    ]
    g1_ring = [
        RingReduce(G1, 0, hr, g.st1, g.rr1, g.rl1),
        RingReduce(G1, hr, hr, g.st1, g.rr1, g.rl1),
    ]
    gq_ring = [
        RingReduce(GQ, 0, hr, g.stq, g.rrq, g.rlq),
        RingReduce(GQ, hr, hr, g.stq, g.rrq, g.rlq),
    ]
    go_ring = RingReduce(GO, 0, R, g.sto, g.rro, g.rlo)
    gs_ring = RingReduce(VG, 0, 16, g.sts, g.rrs, g.rls, F32)

    def finish(*rings):
        for r in rings:
            r.finish()

    def vec(k):
        return VEC[k : k + 1, :]

    def start():
        part = lambda j: AQ.at[p, pl.ds(pl.multiple_of(R * j, R), R), :]
        q_ring[0].before = scatter(lambda j: g.sq.at[j], part, AQ.at[0, pl.ds(0, 3 * R), :])

    def small_start():
        for c in vectors:
            c.wait()
        loads[3].wait()
        SV = g.small_v
        SV[...] = jnp.zeros(SV.shape, F32)
        for k in range(8):
            row, at = ((0, R * k), (1, R * (k - 4)), (2, 0), (3, 0))[0 if k < 4 else 1 if k < 6 else k - 4]
            value = given["v%d" % k][...]
            width = value.shape[1]
            wide = value if width == 128 else jnp.concatenate([value, jnp.zeros((1, 128 - width), F32)], axis=1)
            SV[row : row + 1, :] += wide if at == 0 else pltpu.roll(wide, at, 1)
        mask = g.mask_v[...].astype(F32)
        below = lax.broadcasted_iota(jnp.int32, (128, 128), 0) <= lax.broadcasted_iota(jnp.int32, (128, 128), 1)
        tri = jnp.where(below, 1.0, 0.0).astype(BF)
        count = g.counts[0, 0].astype(F32)
        before = jnp.zeros((1, 1), F32)
        for k in range(2):
            ones = mask[:, 128 * k : 128 * k + 128]
            running = dot(jnp.broadcast_to(ones, (8, 128)).astype(BF), tri)[0:1, :] + before
            SV[4 + k : 5 + k, :] = jnp.where(running <= count, ones, 0.0)
            before = before + jnp.sum(ones, axis=1, keepdims=True)
        AS[p, f] = SV[...]
        st.s = scatter(lambda j: AS.at[p, f], lambda j: AS.at[p, j], AS.at[0, pl.ds(0, 3)])
        s_ring.before = st.s

    def cast_fc1():
        loads[1].wait()
        for j in range(NF):
            for t in range(n):
                at = HC * (NF * t + j)
                g.s1[j, :, HC * t : HC * t + HC] = g.w1_v[:, at : at + HC].astype(BF)
        A1[p, pl.ds(pl.multiple_of(R * f, R), R), :] = g.s1[f]
        part = lambda j: A1.at[p, pl.ds(pl.multiple_of(R * j, R), R), :]
        w1_ring[0].before = scatter(lambda j: g.s1.at[j], part, A1.at[0, pl.ds(0, 3 * R), :])

    def tokens_start():
        loads[4].wait()
        st.tok = AllGather4(lambda j: TA.at[j])

    def cot_start():
        loads[6].wait()
        st.cot = AllGather4(lambda j: CA.at[j])

    def wo_start():
        o_ring.finish()
        st.wo = AllGather4(lambda j: WO.at[:, j])

    ends = []
    total_len = jnp.int32(0)
    for k in range(g.lengths.shape[1]):
        total_len = total_len + g.lengths[0, k]
        ends.append(total_len)

    def key_segments():
        keyrow = lax.broadcasted_iota(jnp.int32, (1, S_), 1)
        segrow = jnp.zeros((1, S_), jnp.int32)
        for end in ends:
            segrow += (keyrow >= end).astype(jnp.int32)
        return segrow

    def layout():
        row, _seg = column_segment(0, S_, ends)
        before = jnp.zeros((S_, 1), jnp.int32)
        for k, end in enumerate(ends):
            before += jnp.where(row >= end, g.lengths[0, k], 0)
        place = row - before
        img = GRID * GRID
        frame = jnp.zeros((S_, 1), jnp.int32)
        for t in range(1, FRAMES):
            frame += (place >= img * t).astype(jnp.int32)
        rest = place - img * frame
        grow = jnp.zeros((S_, 1), jnp.int32)
        for t in range(1, GRID):
            grow += (rest >= GRID * t).astype(jnp.int32)
        gcol = rest - GRID * grow
        lane = lax.broadcasted_iota(jnp.int32, (S_, 128), 1)
        hot = (lane == frame) | (lane == grow + FRAMES) | (lane == gcol + (FRAMES + GRID))
        g.OH[...] = jnp.where(hot, 1.0, 0.0).astype(BF)
        loads[7].wait()
        g.CS[...] = sum(dot(g.OH[...], g.trig_v[k]) for k in range(3))

    def visible():
        if s_ring.before:
            received(s_ring.before)
            s_ring.before = ()
        vis8 = jnp.concatenate([AS[p, j][4:6, :] for j in range(NF)], axis=0)
        above = lax.broadcasted_iota(jnp.int32, (128, 128), 0)
        tri = above <= lax.broadcasted_iota(jnp.int32, (128, 128), 1)
        within = dot(vis8.astype(BF), jnp.where(tri, 1.0, 0.0).astype(BF))
        base = jnp.zeros((1, 128), F32)
        pieces, vpieces = [], []
        for k in range(8):
            pieces.append(within[k : k + 1, :] + base)
            vpieces.append(vis8[k : k + 1, :])
            base = base + jnp.sum(vis8[k : k + 1, :], axis=1, keepdims=True)
        incl = jnp.concatenate(pieces, axis=1)
        visrow = jnp.concatenate(vpieces, axis=1)
        rank = jnp.where(visrow > 0.5, incl - 1.0, -1.0).astype(jnp.int32)
        sel = lax.broadcasted_iota(jnp.int32, (VP, S_), 0) == rank
        SM[...] = jnp.where(sel, 1.0, 0.0).astype(BF)

    def rounded(v):
        return v.astype(BF).astype(F32)

    def turn(v, by):
        by = by % 128
        return v if by == 0 else pltpu.roll(v, by, 1)

    def small_vectors():
        s_ring.finish()
        lane128 = lax.broadcasted_iota(jnp.int32, (n, 128), 1)
        rows0 = [AS[:, j, 0, :] for j in range(NF)]
        rows1 = [AS[:, j, 1, :] for j in range(NF)]
        rows2 = [AS[:, j, 2, :] for j in range(NF)]
        for k in range(6):
            src = rows0 if k < 4 else rows1
            piece = jnp.zeros((n, 128), F32)
            for j in range(NF):
                piece = jnp.where(lax.div(lane128, R) == j, turn(src[j], R * (j - k % 4)), piece)
            for q in range(n):
                VEC[k : k + 1, 128 * q : 128 * q + 128] = rounded(piece[q : q + 1, :])
        for q in range(n):
            VEC[6:7, 128 * q : 128 * q + 128] = rounded(AS[q, f][3:4, :])
        t0 = jnp.where(lane128 < 96, rows2[0], turn(rows2[1], 96))
        t1 = jnp.where(lane128 < 64, turn(rows2[1], -32), turn(rows2[2], 64))
        t2 = jnp.where(lane128 < 32, turn(rows2[2], -64), turn(rows2[3], 32))
        for q in range(n):
            for k, t in enumerate((t0, t1, t2)):
                BQ[0:1, 384 * q + 128 * k : 384 * q + 128 * k + 128] = rounded(t[q : q + 1, :])

    def first_norm():
        st.tok.finish()

        def block(b, _):
            xhat, _inv = norm_stats(TA[b].astype(F32))
            N1[b] = (xhat * vec(0) + vec(1)).astype(BF)
            return 0

        lax.fori_loop(0, NF, block, 0)

    def project_half(part):
        finish(*q_ring)

        def block(b, _):
            rows = pl.ds(pl.multiple_of(b * T, T), T)
            cs = g.CS[rows, :]
            for t, dst in enumerate((Q, K, W)):
                out = dot(N1[b], AQ[:, :, C * t : C * t + C].reshape(D, C))
                out = out + BQ[0:1, pl.ds(pl.multiple_of(D * t + C * f, 128), C)]
                if t == 2:
                    dst[rows, :] = out.astype(BF)
                    continue
                for hh in range(C // 128):
                    u = out[:, 128 * hh : 128 * hh + 128]
                    u = (u * cs[:, :128] + swap_halves(u) * cs[:, 128:]).astype(BF)
                    dst[rows, 128 * hh : 128 * hh + 128] = u * BF(0.125) if t == 0 else u
            return 0

        lax.fori_loop(NF // 2 * part, NF // 2 * (part + 1), block, 0)

    lane_c = lax.broadcasted_iota(jnp.int32, (1, C), 1)
    hmask = [jnp.where(lax.div(lane_c, HDIM) == hd, 1.0, 0.0) for hd in range(C // HDIM)]

    def softmax(s):
        e = jnp.exp(s - jnp.max(s, axis=-1, keepdims=True))
        return e * (1.0 / jnp.sum(e, axis=-1, keepdims=True))

    def context_attention():
        for src, dst in ((Q, QV), (K, KV), (W, WV)):
            dst[...] = dot(SM[...], src[...]).astype(BF)
        segrow = key_segments()
        seg8 = jnp.broadcast_to(segrow.astype(F32), (8, S_)).astype(BF)
        segv_row = dot(seg8, SM[...], NT)[0:1, :].astype(jnp.int32)
        segv_col = jnp.sum(SM[...].astype(F32) * segrow.astype(F32), axis=1, keepdims=True).astype(jnp.int32)
        same = segv_col == segv_row
        acc = jnp.zeros((VP, C), F32)
        for hd in range(C // HDIM):
            s = dot(QV[...] * hmask[hd].astype(BF), KV[...], NT)
            pr = softmax(jnp.where(same, s, FILL))
            PV[hd] = pr
            acc += dot(pr.astype(BF), WV[...]) * hmask[hd]
        OV[f] = acc.astype(BF)
        st.ov = AllGather4(lambda j: OV.at[j])

    def attend_target(b, pair):
        rows = slice(T * b, T * b + T)
        _, segq = column_segment(b * T, T, ends)
        same = segq == key_segments()
        for hd in (2 * pair, 2 * pair + 1):
            s = dot(Q[rows, :] * hmask[hd].astype(BF), K[...], NT)
            pr = softmax(jnp.where(same, s, FILL)).astype(BF)
            o = dot(pr, W[...])
            cols = slice(HDIM * hd, HDIM * hd + HDIM)
            OA[f, rows, cols] = o[:, cols].astype(BF)

    def oa_start(part):
        rows = pl.ds(S_ // 2 * part, S_ // 2)
        st.oa[part] = AllGather4(lambda j: OA.at[j, rows, :])

    def select_rows():
        for cols in blocks:
            XV[:, cols] = dot(SM[...], TA[:, :, cols].reshape(S_, 256)).astype(BF)
            N1V[:, cols] = dot(SM[...], N1[:, :, cols].reshape(S_, 256)).astype(BF)

    def select_cot():
        st.cot.finish()
        for cols in blocks:
            DY[:, cols] = dot(SM[...], CA[:, :, cols].reshape(S_, 256)).astype(BF)

    def out_project(parts, cols):
        heads = [WO[n // NF * j : n // NF * (j + 1), :, :, cols].reshape(C, -1) for j in range(NF)]
        return sum(dot(parts(j), heads[j]) for j in range(NF))

    def context_middle():
        st.wo.finish()
        st.ov.finish()
        for cols in blocks:
            X1V[:, cols] = XV[:, cols].astype(F32) + (out_project(lambda j: OV[j], cols) + VEC[4:5, cols])
        xhat, _inv = norm_stats(X1V[...])
        N2V[...] = (xhat * vec(2) + vec(3)).astype(BF)

    def normal_cdf(hid):
        return 0.5 * (1.0 + lax.erf(hid * (1.0 / math.sqrt(2.0))))

    def context_hidden():
        finish(*w1_ring)
        for cols in blocks:
            hid = dot(N2V[...], A1[:, :, cols].reshape(D, 256)) + VEC[6:7, cols]
            cdf = normal_cdf(hid)
            GV[:, cols] = (hid * cdf).astype(BF)
            GP[:, cols] = cdf + hid * (jnp.exp(-0.5 * hid * hid) * (1.0 / math.sqrt(2.0 * math.pi)))

    def outer(dst, lhs, rhs):
        for k, cols in enumerate(blocks):
            g.LT[cols, :] = lhs[:, cols].astype(F32).T.astype(BF)

        def one(k, _):
            rows = pl.ds(pl.multiple_of(512 * k, 512), 512)
            for c in range(dst.shape[2] // 256):
                cols = slice(256 * c, 256 * c + 256)
                part = dot(g.LT[rows, :], rhs[:, cols]).astype(dst.dtype)
                dst[pl.ds(4 * k, 4), :, cols] = part.reshape(4, 128, 256)
            return 0

        lax.fori_loop(0, n // 4, one, 0)

    def put_grad(k, vrow):
        for q in range(n):
            VG[q, k : k + 1, :] = vrow[:, 128 * q : 128 * q + 128]

    def fc2_grad():
        outer(G2, GV, DY)

    def hidden_grad():
        finish(*w2_ring)
        for k, cols in enumerate(blocks):
            dg = dot(DY[...], A2[...].reshape(HF, D)[256 * k : 256 * k + 256, :], NT)
            dh = (dg * GP[:, cols]).astype(BF)
            DH[:, cols] = dh
            dc1 = jnp.sum(dh.astype(F32), axis=0, keepdims=True)
            for q in range(2):
                for j in range(NF):
                    piece = dc1[:, 128 * q : 128 * q + 128]
                    VG[2 * k + q, 9 + j : 10 + j, :] = jnp.where(f == j, piece, jnp.zeros((1, 128), F32))

    def second_grad():
        for k, cols in enumerate(blocks):
            part = dot(DH[...], A1[2 * k : 2 * k + 2].reshape(256, HF), NT).astype(BF)
            PN[:, :, cols] = part.reshape(NF, V, 256)
        st.n2 = ReduceScatter4(PN, g.PNr1, g.PNxs, g.PNr2)

    def fc1_grad():
        outer(G1, N2V, DH)

    def context_partial():
        for cols in blocks:
            part = dot(GV[...], A2[:, :, cols].reshape(HF, 256)).astype(BF)
            PF[:, :, cols] = part.reshape(NF, V, 256)
        st.pf = ReduceScatter4(PF, g.PFr1, g.PFxs, g.PFr2)

    def second_norm_back():
        st.n2.finish()
        dyo = DY[mine, :].astype(F32)
        dv, dgain, dshift = norm_back(X1V[mine, :], vec(2), st.n2.total())
        dx1 = dyo + dv
        g.DX1[...] = dx1
        low = dx1.astype(BF)
        g.DP[f] = low
        st.dp = AllGather4(lambda j: g.DP.at[j])
        put_grad(2, dgain)
        put_grad(3, dshift)
        put_grad(4, jnp.sum(low.astype(F32), axis=0, keepdims=True))
        put_grad(5, jnp.sum(dyo, axis=0, keepdims=True))

    def transpose_attended():
        st.ov.finish()
        for j in range(NF):
            ot = OV[j].astype(F32).T.astype(BF)
            OT[n // NF * j : n // NF * (j + 1)] = ot.reshape(n // NF, NF, R, VP)

    def out_grad():
        st.dp.finish()
        go = dot(OT[:, f].reshape(n * R, VP), g.DP[...].reshape(VP, D))
        GO[...] = go.reshape(n, R, D)

    def attended_grad():
        st.dp.finish()
        st.wo.finish()
        wo_heads = WO[pl.ds(n // NF * f, n // NF)].reshape(C, D)
        DO[...] = dot(g.DP[...].reshape(VP, D), wo_heads, NT).astype(BF)

    def attention_back():
        dq = jnp.zeros((VP, C), F32)
        dk = jnp.zeros((VP, C), F32)
        dw = jnp.zeros((VP, C), F32)
        for hd in range(C // HDIM):
            pr = PV[hd]
            dp = dot(DO[...] * hmask[hd].astype(BF), WV[...], NT)
            ds = (pr * (dp - jnp.sum(pr * dp, axis=-1, keepdims=True))).astype(BF)
            dq += dot(ds, KV[...]) * hmask[hd]
            dk += dot(ds, QV[...], TN) * hmask[hd]
            dw += dot(pr.astype(BF), DO[...], TN) * hmask[hd]
        csv = sum(dot(dot(SM[...], g.OH[...]).astype(BF), g.trig_v[k]) for k in range(3))
        for t, (grad, scale) in enumerate(((dq, 0.125), (dk, 1.0))):
            for hh in range(C // 128):
                u = grad[:, 128 * hh : 128 * hh + 128]
                u = u * csv[:, :128] - swap_halves(u) * csv[:, 128:]
                DPRE[:, C * t + 128 * hh : C * t + 128 * hh + 128] = (u * scale).astype(BF)
        DPRE[:, 2 * C :] = dw.astype(BF)

    def qkv_grad():
        outer(GQ, N1V, DPRE)

    def qkv_bias_grad():
        BG[...] = jnp.zeros(BG.shape, F32)
        db = jnp.sum(DPRE[...].astype(F32), axis=0, keepdims=True)
        for t in range(3):
            BG[0:1, pl.ds(pl.multiple_of(D * t + C * f, 128), C)] = db[:, C * t : C * t + C]
        for q in range(n):
            for t in range(3):
                VG[q, 6 + t : 7 + t, :] = BG[0:1, 384 * q + 128 * t : 384 * q + 128 * t + 128]
            VG[q, 13:16, :] = jnp.zeros((3, 128), F32)

    def first_grad():
        for k, cols in enumerate(blocks):
            part = dot(DPRE[...], AQ[2 * k : 2 * k + 2].reshape(256, 3 * C), NT).astype(BF)
            PN[:, :, cols] = part.reshape(NF, V, 256)
        st.n1 = ReduceScatter4(PN, g.PMr1, g.PMxs, g.PMr2)

    def first_norm_back():
        st.n1.finish()
        dv, dgain, dshift = norm_back(XV[mine, :].astype(F32), vec(0), st.n1.total())
        g.DX[f] = (g.DX1[...] + dv).astype(BF)
        st.dx = AllGather4(lambda j: g.DX.at[j])
        put_grad(0, dgain)
        put_grad(1, dshift)

    def context_result():
        st.pf.finish()
        g.CO[f] = (X1V[mine, :] + (st.pf.total() + vec(5))).astype(BF)
        st.co = AllGather4(lambda j: g.CO.at[j])

    def home(src, dst):
        s = SM[:, pl.ds(pl.multiple_of(T * f, 128), T)]
        for cols in blocks:
            dst[:, cols] = dot(s, src[:, :, cols].reshape(VP, 256), TN).astype(BF)

    def home_context():
        st.co.finish()
        home(g.CO, g.ctx_o)

    def home_grad():
        st.dx.finish()
        home(g.DX, g.dx_o)

    def target_middle(b):
        st.wo.finish()
        st.oa[b // 2].finish()
        for cols in blocks:
            g.X1B[:, cols] = TA[b, :, cols].astype(F32) + (
                out_project(lambda j: OA[j, T * b : T * b + T, :], cols) + VEC[4:5, cols]
            )
        x1 = g.X1B[...]
        xh, _inv = norm_stats(x1)
        N2[b] = (xh * vec(2) + vec(3)).astype(BF)

        @pl.when(f == b)
        def _():
            g.X1H[...] = x1

    def target_hidden(b):
        finish(*w1_ring)
        for cols in blocks:
            hid = dot(N2[b], A1[:, :, cols].reshape(D, 256)) + VEC[6:7, cols]
            GT[b, :, cols] = (hid * normal_cdf(hid)).astype(BF)

    def target_out(b):
        finish(*w2_ring)

        def one(k, _):
            cols = pl.ds(pl.multiple_of(256 * k, 256), 256)
            PT[b, :, cols] = dot(GT[b], A2[:, :, cols].reshape(HF, 256)).astype(BF)
            return 0

        lax.fori_loop(0, len(blocks), one, 0)
        if b == NF - 1:
            st.pt = ReduceScatter4(PT, g.PTr1, g.PTxs, g.PTr2)

    def target_result():
        st.pt.finish()
        g.tgt_o[...] = (g.X1H[...] + (st.pt.total() + vec(5))).astype(BF)

    def fc2_grad_done():
        finish(*g2_ring)
        for k, ring in enumerate(g2_ring):
            g.g2_o[hc * k : hc * k + hc, :] = ring.total()

    def fc1_grad_trade():
        finish(*g1_ring)
        for k, ring in enumerate(g1_ring):
            E1[2 * k : 2 * k + 2] = ring.total().astype(BF).reshape(2, R, HF)
        F1[f] = E1[f]
        st.e1 = scatter(lambda j: E1.at[j], lambda j: F1.at[j], F1.at[pl.ds(0, 3)])

    def fc1_grad_done():
        received(st.e1)

    def out_grad_done():
        go_ring.finish()
        g.go_o[...] = go_ring.total()

    def qkv_grad_trade():
        finish(*gq_ring)
        for k, ring in enumerate(gq_ring):
            EQ[2 * k : 2 * k + 2] = ring.total().astype(BF).reshape(2, R, 3 * C)
        FQ[f] = EQ[f]
        st.eq = scatter(lambda j: EQ.at[j], lambda j: FQ.at[j], FQ.at[pl.ds(0, 3)])

    def qkv_grad_done():
        received(st.eq)

    def small_grad_trade():
        gs_ring.finish()
        SG[f] = gs_ring.total()
        st.sg = scatter(lambda j: SG.at[f], lambda j: SG.at[j], SG.at[pl.ds(0, 3)])

    def small_grad_done():
        received(st.sg)
        g.sg_o[...] = SG[0] + SG[1] + SG[2] + SG[3]

    start()
    o_ring.step(0)
    w2_ring[0].step(0)
    small_start()
    layout()
    cast_fc1()
    w2_ring[1].step(0)
    tokens_start()
    o_ring.step(1)
    cot_start()
    q_ring[0].step(0)
    visible()
    s_ring.step(0)
    q_ring[1].step(0)
    w1_ring[0].step(0)
    o_ring.step(2)
    q_ring[0].step(1)
    s_ring.step(1)
    q_ring[1].step(1)
    w1_ring[1].step(0)
    o_ring.step(3)
    st.tok.forward()
    q_ring[0].step(2)
    s_ring.step(2)
    q_ring[1].step(2)
    w1_ring[0].step(1)
    wo_start()
    w1_ring[1].step(1)
    s_ring.step(3)
    q_ring[0].step(3)
    st.cot.forward()
    q_ring[1].step(3)
    select_cot()
    w2_ring[0].step(1)
    w1_ring[0].step(2)
    small_vectors()
    first_norm()
    select_rows()
    w1_ring[1].step(2)
    project_half(0)
    project_half(1)
    context_attention()
    w1_ring[0].step(3)
    st.wo.forward()
    attend_target(3, 0)
    w2_ring[1].step(1)
    attend_target(0, 0)
    w1_ring[1].step(3)
    attend_target(3, 1)
    w2_ring[0].step(2)
    st.ov.forward()
    attend_target(2, 0)
    attend_target(2, 1)
    oa_start(1)
    context_middle()
    w2_ring[1].step(2)
    context_hidden()
    fc2_grad()
    g2_ring[1].step(0)
    attend_target(1, 0)
    w2_ring[0].step(3)
    attend_target(1, 1)
    transpose_attended()
    w2_ring[1].step(3)
    g2_ring[0].step(0)
    attend_target(0, 1)
    oa_start(0)
    st.oa[1].forward()
    g2_ring[1].step(1)
    hidden_grad()
    fc1_grad()
    g1_ring[0].step(0)
    context_partial()
    g2_ring[0].step(1)
    second_grad()
    g1_ring[1].step(0)
    st.pf.forward()
    st.n2.forward()
    g1_ring[0].step(1)
    st.oa[0].forward()
    target_middle(0)
    g2_ring[0].step(2)
    target_hidden(0)
    context_result()
    target_out(0)
    g1_ring[1].step(1)
    target_middle(1)
    target_hidden(1)
    second_norm_back()
    g1_ring[0].step(2)
    target_middle(2)
    target_middle(3)
    st.co.forward()
    target_hidden(2)
    target_out(2)
    g2_ring[0].step(3)
    home_context()
    g1_ring[1].step(2)
    st.dp.forward()
    target_hidden(3)
    target_out(1)
    attended_grad()
    attention_back()
    g1_ring[0].step(3)
    first_grad()
    target_out(3)
    qkv_grad()
    gq_ring[1].step(0)
    st.n1.forward()
    gq_ring[0].step(0)
    qkv_bias_grad()
    out_grad()
    g1_ring[1].step(3)
    st.pt.forward()
    gq_ring[1].step(1)
    first_norm_back()
    gs_ring.step(0)
    gq_ring[0].step(1)
    fc1_grad_trade()
    go_ring.step(0)
    g2_ring[1].step(2)
    gq_ring[1].step(2)
    gs_ring.step(1)
    gq_ring[0].step(2)
    target_result()
    go_ring.step(1)
    gq_ring[1].step(3)
    gs_ring.step(2)
    st.dx.forward()
    gq_ring[0].step(3)
    home_grad()
    fc1_grad_done()
    go_ring.step(2)
    gs_ring.step(3)
    g2_ring[1].step(3)
    qkv_grad_trade()
    go_ring.step(3)
    small_grad_trade()
    fc2_grad_done()
    qkv_grad_done()
    small_grad_done()
    out_grad_done()


def run_layer(n, tokens, cot, lengths, mask, counts, vectors, wqkv, wo, w1, w2, V):
    T, D = tokens.shape
    NF = 4
    FF = w1.shape[1]
    R = wo.shape[0]
    RP = R * NF
    HC = w2.shape[0]
    HF = HC * n
    C = D // NF
    VP = V * NF
    S_ = T * NF
    h2 = n // 2
    B, F = BF, F32
    vm = pltpu.VMEM
    scratch = dict(
        wqkv_v=vm((R, 3 * D), F), w1_v=vm((R, FF), F), wo_v=vm((R, D), F), w2_v=vm((HC, D), F),
        small_v=vm((8, 128), F), trig_v=vm((3, 128, 256), B),
        sq=vm((NF, R, 3 * C), B), s1=vm((NF, R, HF), B),
        AS=vm((n, NF, 8, 128), F), AQ=vm((n, RP, 3 * C), B), WO=vm((n, NF, R, D), B),
        A1=vm((n, RP, HF), B), A2=vm((n, HC, D), B),
        TA=vm((NF, T, D), B), CA=vm((NF, T, D), B), N1=vm((NF, T, D), B),
        OH=vm((S_, 128), B), CS=vm((S_, 256), F), SM=vm((VP, S_), B),
        VEC=vm((8, D), F), BQ=vm((8, 3 * D), F), BG=vm((8, 3 * D), F),
        Q=vm((S_, C), B), K=vm((S_, C), B), W=vm((S_, C), B),
        QV=vm((VP, C), B), KV=vm((VP, C), B), WV=vm((VP, C), B),
        OV=vm((NF, VP, C), B), PV=vm((C // HDIM, VP, VP), F), OA=vm((NF, S_, C), B),
        XV=vm((VP, D), B), N1V=vm((VP, D), B), DY=vm((VP, D), B),
        X1V=vm((VP, D), F), N2V=vm((VP, D), B), GV=vm((VP, HF), B), GP=vm((VP, HF), F),
        G2=vm((n, HC, D), B), G1=vm((n, RP, HF), B), GQ=vm((n, RP, 3 * C), B), GO=vm((n, R, D), F),
        VG=vm((n, 16, 128), F),
        st2=vm((HC, D), B), rr2=vm((h2, HC, D), B), rl2=vm((h2, HC, D), B),
        st1=vm((RP, HF), B), rr1=vm((h2, RP, HF), B), rl1=vm((h2, RP, HF), B),
        stq=vm((RP, 3 * C), B), rrq=vm((h2, RP, 3 * C), B), rlq=vm((h2, RP, 3 * C), B),
        sto=vm((R, D), B), rro=vm((h2, R, D), B), rlo=vm((h2, R, D), B),
        sts=vm((16, 128), F), rrs=vm((h2, 16, 128), F), rls=vm((h2, 16, 128), F),
        DH=vm((VP, HF), B), PN=vm((NF, V, D), B), PF=vm((NF, V, D), B),
        PNr1=vm((2, V, D), B), PNxs=vm((V, D), B), PNr2=vm((V, D), B),
        PMr1=vm((2, V, D), B), PMxs=vm((V, D), B), PMr2=vm((V, D), B),
        PFr1=vm((2, V, D), B), PFxs=vm((V, D), B), PFr2=vm((V, D), B),
        DX1=vm((V, D), F), DP=vm((NF, V, D), B), OT=vm((n, NF, R, VP), B), DO=vm((VP, C), B),
        DPRE=vm((VP, 3 * C), B), CO=vm((NF, V, D), B), DX=vm((NF, V, D), B),
        X1H=vm((T, D), F), GT=vm((NF, T, HF), B),
        PTr1=vm((2, T, D), B), PTxs=vm((T, D), B), PTr2=vm((T, D), B),
        SG=vm((NF, 16, 128), F),
        E1=vm((NF, R, HF), B), EQ=vm((NF, R, 3 * C), B),
        send_sems=pltpu.SemaphoreType.DMA((16,)), recv_sems=pltpu.SemaphoreType.DMA((59,)),
        local_sems=pltpu.SemaphoreType.DMA((16,)), mask_v=vm((1, T), jnp.int32), LT=vm((D, VP), B),
    )
    arr = jax.ShapeDtypeStruct
    ins = dict(
        lengths=lengths, counts=counts, tok=tokens, cot=cot, mask=mask.reshape(1, T), wqkv=wqkv, wo=wo,
        w1=w1, w2=w2, trig=jnp.asarray(trig_table()),
    )
    for k, v in enumerate(vectors):
        ins["in%d" % k] = v.reshape(1, -1)
        scratch["v%d" % k] = vm((1, v.shape[0]), F)
    outs = dict(
        tgt_o=vm((T, D), B), ctx_o=vm((T, D), B), dx_o=vm((T, D), B), gq_o=vm((NF, R, 3 * C), B),
        go_o=vm((R, D), F), g1_o=vm((NF, R, HF), B), g2_o=vm((HC, D), F), sg_o=vm((16, 128), F),
    )
    names = [*ins, *outs, *scratch]
    any_spec = pl.BlockSpec(memory_space=pl.ANY)
    return pl.pallas_call(
        functools.partial(layer_kernel, (n, D, FF, T, V), names),
        out_shape=list(outs.values()),
        in_specs=[pl.BlockSpec(memory_space=pltpu.SMEM)] * 2 + [any_spec] * (len(ins) - 2),
        out_specs=[pl.BlockSpec(memory_space=pltpu.VMEM)] * 8,
        scratch_shapes=list(scratch.values()),
        compiler_params=pltpu.CompilerParams(
            collective_id=0, has_side_effects=True, vmem_limit_bytes=62000000
        ),
        name="layer",
    )(*ins.values())


def outputs_kernel(dims, count, *refs):
    n, R, C, HC = dims
    NF = 4
    f = lax.axis_index("fsdp")
    tgt, ctx, dx, gq, go, g1, g2, sg = refs[:8]
    tgt_o, ctx_o, dx_o, gq_o, go_o, g1_o, g2_o = refs[8:15]
    vec_o = refs[15:23]
    gq_w, g1_w, sem_out = refs[23:]
    stores = []

    def store(src, dst):
        c = pltpu.make_async_copy(src, dst, sem_out.at[len(stores)])
        c.start()
        stores.append(c)

    for src, dst in ((g2, g2_o), (tgt, tgt_o), (ctx, ctx_o), (dx, dx_o), (go, go_o)):
        store(src, dst)
    D = NF * C
    for j in range(NF):
        for t in range(3):
            gq_w[:, D * t + C * j : D * t + C * j + C] = gq[j, :, C * t : C * t + C].astype(F32)
    store(gq_w, gq_o)
    for j in range(NF):
        for t in range(n):
            at = HC * (NF * t + j)
            g1_w[:, at : at + HC] = g1[j, :, HC * t : HC * t + HC].astype(F32)
    store(g1_w, g1_o)
    small = sg
    for k in range(6):
        vec_o[k][...] = pltpu.roll(small[k : k + 1, :], lax.rem(128 - R * f, 128), 1)[:, :R]
    rows = jnp.concatenate([small[6 + t : 7 + t, :] for t in range(3)], axis=1)
    vec_o[6][...] = pltpu.roll(rows, lax.rem(384 - 3 * R * f, 384), 1)[:, : 3 * R]
    mine = jnp.zeros((1, 128), F32)
    for j in range(NF):
        mine = jnp.where(f == j, small[9 + j : 10 + j, :], mine)
    vec_o[7][...] = mine
    for c in stores:
        c.wait()


def write_outputs(n, parts, R, D, FF, HC):
    NF = 4
    C = D // NF
    tgt = parts[0]
    arr = jax.ShapeDtypeStruct
    any_spec = pl.BlockSpec(memory_space=pl.ANY)
    big = [
        arr(tgt.shape, BF), arr(tgt.shape, BF), arr(tgt.shape, BF),
        arr((R, 3 * D), F32), arr((R, D), F32), arr((R, FF), F32), arr((HC, D), F32),
    ]
    small = [arr((1, w), F32) for w in (R,) * 6 + (3 * R, 4 * R)]
    return pl.pallas_call(
        functools.partial(outputs_kernel, (n, R, C, HC), 8),
        out_shape=big + small,
        in_specs=[pl.BlockSpec(memory_space=pltpu.VMEM)] * 8,
        out_specs=[any_spec] * 7 + [pl.BlockSpec(memory_space=pltpu.VMEM)] * 8,
        scratch_shapes=[
            pltpu.VMEM((R, 3 * D), F32), pltpu.VMEM((R, FF), F32), pltpu.SemaphoreType.DMA((7,)),
        ],
        compiler_params=pltpu.CompilerParams(vmem_limit_bytes=1 << 22),
        name="outputs",
    )(*[pltpu.with_memory_space_constraint(v, pltpu.VMEM) for v in parts])


def on_device(
    tokens, lengths, visibility_mask, visible_counts, ln1_gain, ln1_bias, qkv_weight, qkv_bias,
    out_weight, out_bias, ln2_gain, ln2_bias, fc1_weight, fc1_bias, fc2_weight, fc2_bias, context_cot,
):
    n = lax.axis_size("dp")
    R, D = out_weight.shape
    vectors = (ln1_gain, ln1_bias, ln2_gain, ln2_bias, out_bias, fc2_bias, qkv_bias, fc1_bias)
    parts = run_layer(
        n, tokens, context_cot, lengths, visibility_mask, visible_counts, vectors,
        qkv_weight, out_weight, fc1_weight, fc2_weight, VIS_DEV,
    )
    tgt, ctx, dx, gq, go, g1, g2, *small = write_outputs(
        n, parts, R, D, fc1_weight.shape[1], fc2_weight.shape[0]
    )
    gg1, gb1, gg2, gb2, gbo, gc2, gbq, gc1 = [v.reshape(-1) for v in small]
    return (tgt, ctx, dx, gg1, gb1, gq, gbq, go, gbo, gg2, gb2, g1, gc1, g2, gc2)


def layer_norm(inputs, scale_vec, shift_vec):
    center = inputs - jnp.mean(inputs, axis=-1, keepdims=True)
    spread = jnp.mean(center * center, axis=-1, keepdims=True)
    return center * lax.rsqrt(spread + norm_eps) * scale_vec + shift_vec


def gelu_erf(values):
    return jax.nn.gelu(values, approximate=False)


def pack_layout(seq_lens, pack_len):
    seq_ends = jnp.cumsum(seq_lens)
    places = jnp.arange(pack_len, dtype=jnp.int32)
    passed = places[:, None] >= seq_ends[None, :]
    segment = jnp.sum(passed.astype(jnp.int32), axis=1)
    before = jnp.sum(jnp.where(passed, seq_lens[None, :], 0), axis=1)
    return (segment, places - before)


def rope_tables(places):
    frame_index = (places // (GRID * GRID)).astype(jnp.float32)
    grid_row = (places // GRID % GRID).astype(jnp.float32)
    grid_col = (places % GRID).astype(jnp.float32)
    pair_index = jnp.arange(HDIM // 2, dtype=jnp.int32)
    axis_pick = jnp.minimum(pair_index // 11, 2)
    pair_order = (pair_index - 11 * axis_pick).astype(jnp.float32)
    frequency = jnp.exp(pair_order * (-math.log(10000.0) / 11.0))
    angles = (
        frame_index[:, None] * (axis_pick == 0).astype(jnp.float32)[None, :]
        + grid_row[:, None] * (axis_pick == 1).astype(jnp.float32)[None, :]
        + grid_col[:, None] * (axis_pick == 2).astype(jnp.float32)[None, :]
    ) * frequency[None, :]
    return (jnp.cos(angles), jnp.sin(angles))


def rotate(heads, cosine_table, sine_table):
    half_size = heads.shape[-1] // 2
    first_half = heads[..., :half_size]
    second_half = heads[..., half_size:]
    cosine_cols = cosine_table[:, None, :]
    sine_cols = sine_table[:, None, :]
    return jnp.concatenate(
        [
            first_half * cosine_cols - second_half * sine_cols,
            second_half * cosine_cols + first_half * sine_cols,
        ],
        axis=-1,
    )


def rotate_back(grads, cosine_table, sine_table):
    half_size = grads.shape[-1] // 2
    first_half = grads[..., :half_size]
    second_half = grads[..., half_size:]
    cosine_cols = cosine_table[:, None, :]
    sine_cols = sine_table[:, None, :]
    return jnp.concatenate(
        [
            first_half * cosine_cols + second_half * sine_cols,
            second_half * cosine_cols - first_half * sine_cols,
        ],
        axis=-1,
    )


def project(token_rows, weights, cosine_table, sine_table):
    inputs = token_rows.astype(jnp.float32)
    row_count = inputs.shape[0]
    model_width = inputs.shape[1]
    normed = layer_norm(
        inputs, weights[0].astype(jnp.float32), weights[1].astype(jnp.float32)
    ).astype(jnp.bfloat16)
    joined = jnp.dot(normed, weights[2], preferred_element_type=jnp.float32) + weights[3].astype(
        jnp.float32
    )
    query_heads = rotate(
        joined[:, :model_width].reshape(row_count, HEADS, HDIM), cosine_table, sine_table
    ).astype(jnp.bfloat16)
    key_flat = (
        rotate(
            joined[:, model_width : 2 * model_width].reshape(row_count, HEADS, HDIM),
            cosine_table,
            sine_table,
        )
        .astype(jnp.bfloat16)
        .reshape(row_count, model_width)
    )
    value_flat = joined[:, 2 * model_width :].astype(jnp.bfloat16)
    return (inputs, normed, query_heads, key_flat, value_flat)


def attend(query_heads, key_flat, value_flat, seg_query, seg_key):
    key_heads = key_flat.reshape(key_flat.shape[0], HEADS, HDIM)
    value_heads = value_flat.reshape(value_flat.shape[0], HEADS, HDIM)
    scores = jnp.einsum(
        "qhd,khd->hqk", query_heads, key_heads, preferred_element_type=jnp.float32
    ) * HDIM ** (-0.5)
    allowed = seg_query[:, None] == seg_key[None, :]
    masked = jnp.where(allowed[None], scores, masked_fill)
    row_max = jnp.max(masked, axis=-1, keepdims=True)
    raised = jnp.exp(masked - row_max)
    totals = jnp.sum(raised, axis=-1, keepdims=True)
    attn_probs = (raised / totals).astype(jnp.bfloat16)
    attended = jnp.einsum(
        "hqk,khd->qhd", attn_probs, value_heads, preferred_element_type=jnp.float32
    )
    return (
        attended.reshape(query_heads.shape[0], -1).astype(jnp.bfloat16),
        row_max + jnp.log(totals),
    )


def attend_back(query_heads, key_flat, value_flat, seg_query, seg_key, log_total, grad_att):
    key_heads = key_flat.reshape(key_flat.shape[0], HEADS, HDIM)
    value_heads = value_flat.reshape(value_flat.shape[0], HEADS, HDIM)
    scale_factor = HDIM ** (-0.5)
    scores = (
        jnp.einsum("qhd,khd->hqk", query_heads, key_heads, preferred_element_type=jnp.float32)
        * scale_factor
    )
    allowed = seg_query[:, None] == seg_key[None, :]
    masked = jnp.where(allowed[None], scores, masked_fill)
    attn_probs = jnp.exp(masked - log_total)
    grad_heads = grad_att.reshape(grad_att.shape[0], HEADS, HDIM)
    grad_probs = jnp.einsum(
        "qhd,khd->hqk", grad_heads, value_heads, preferred_element_type=jnp.float32
    )
    row_delta = jnp.sum(attn_probs * grad_probs, axis=-1, keepdims=True)
    grad_scores = (attn_probs * (grad_probs - row_delta)).astype(jnp.bfloat16)
    grad_query = (
        jnp.einsum("hqk,khd->qhd", grad_scores, key_heads, preferred_element_type=jnp.float32)
        * scale_factor
    )
    grad_key = (
        jnp.einsum("hqk,qhd->khd", grad_scores, query_heads, preferred_element_type=jnp.float32)
        * scale_factor
    )
    grad_value = jnp.einsum(
        "hqk,qhd->khd",
        attn_probs.astype(jnp.bfloat16),
        grad_heads,
        preferred_element_type=jnp.float32,
    )
    return (
        grad_query,
        grad_key.reshape(key_flat.shape[0], -1),
        grad_value.reshape(value_flat.shape[0], -1),
    )


def finish(inputs, attended, weights):
    middle = inputs + (
        jnp.dot(attended, weights[4], preferred_element_type=jnp.float32)
        + weights[5].astype(jnp.float32)
    )
    second = layer_norm(
        middle, weights[6].astype(jnp.float32), weights[7].astype(jnp.float32)
    ).astype(jnp.bfloat16)
    hidden = jnp.dot(second, weights[8], preferred_element_type=jnp.float32) + weights[9].astype(
        jnp.float32
    )
    activated = gelu_erf(hidden).astype(jnp.bfloat16)
    result = middle + (
        jnp.dot(activated, weights[10], preferred_element_type=jnp.float32)
        + weights[11].astype(jnp.float32)
    )
    return (result, middle, second, hidden, activated)


def gathered_device(
    tokens,
    lengths,
    visibility_mask,
    visible_counts,
    ln1_gain,
    ln1_bias,
    qkv_weight,
    qkv_bias,
    out_weight,
    out_bias,
    ln2_gain,
    ln2_bias,
    fc1_weight,
    fc1_bias,
    fc2_weight,
    fc2_bias,
    context_cot,
):
    tok_rows = tokens.shape[0]
    model_width = tokens.shape[1]
    groups = lax.axis_size("fsdp")
    member = lax.axis_index("fsdp")
    pack_len = tok_rows * groups
    vis_rows = VIS_DEV
    vis_pack = vis_rows * groups
    zero_low = jnp.zeros((), jnp.bfloat16)
    shards = [
        weight.astype(jnp.bfloat16)
        for weight in (
            ln1_gain,
            ln1_bias,
            qkv_weight,
            qkv_bias,
            out_weight,
            out_bias,
            ln2_gain,
            ln2_bias,
            fc1_weight,
            fc1_bias,
            fc2_weight,
            fc2_bias,
        )
    ]
    weights = (
        lax.all_gather(shards[0], ("dp", "fsdp"), axis=0, tiled=True),
        lax.all_gather(shards[1], ("dp", "fsdp"), axis=0, tiled=True),
        lax.all_gather(shards[2], ("dp", "fsdp"), axis=0, tiled=True),
        lax.all_gather(shards[3], ("dp", "fsdp"), axis=0, tiled=True),
        lax.all_gather(shards[4], ("dp", "fsdp"), axis=0, tiled=True),
        lax.all_gather(shards[5], ("dp", "fsdp"), axis=0, tiled=True),
        lax.all_gather(shards[6], ("dp", "fsdp"), axis=0, tiled=True),
        lax.all_gather(shards[7], ("dp", "fsdp"), axis=0, tiled=True),
        lax.all_gather(shards[8], ("dp", "fsdp"), axis=0, tiled=True),
        lax.all_gather(shards[9], ("dp", "fsdp"), axis=0, tiled=True),
        lax.all_gather(shards[10], ("dp", "fsdp"), axis=0, tiled=True),
        lax.all_gather(shards[11], ("dp", "fsdp"), axis=0, tiled=True),
    )
    segment, places = pack_layout(lengths[0], pack_len)
    home_rows = member * tok_rows + jnp.arange(tok_rows, dtype=jnp.int32)
    seg_home = jnp.take(segment, home_rows)
    cos_home, sin_home = rope_tables(jnp.take(places, home_rows))
    inputs, normed, query_heads, key_flat, value_flat = project(tokens, weights, cos_home, sin_home)
    key_pack, value_pack = (
        lax.all_gather(key_flat, "fsdp", axis=0, tiled=True),
        lax.all_gather(value_flat, "fsdp", axis=0, tiled=True),
    )
    attended = attend(query_heads, key_pack, value_pack, seg_home, segment)[0]
    target_out = finish(inputs, attended, weights)[0].astype(jnp.bfloat16)
    running = jnp.cumsum(visibility_mask)
    visible_here = visibility_mask * (running <= visible_counts[0, 0]).astype(jnp.int32)
    visible_all = lax.all_gather(visible_here, "fsdp", axis=0, tiled=True)
    inclusive = jnp.cumsum(visible_all)
    rank_index = jnp.arange(vis_pack, dtype=jnp.int32)
    row_of = jnp.sum((inclusive[None, :] <= rank_index[:, None]).astype(jnp.int32), axis=1)
    owner_dev = row_of // tok_rows
    local_row = row_of % tok_rows
    mine_here = (owner_dev == member)[:, None]
    send_tokens = jnp.where(mine_here, jnp.take(tokens, local_row, axis=0), zero_low)
    send_cot = jnp.where(mine_here, jnp.take(context_cot, local_row, axis=0), zero_low)
    recv_tokens, recv_cot = (
        lax.all_to_all(send_tokens, "fsdp", split_axis=0, concat_axis=0, tiled=True),
        lax.all_to_all(send_cot, "fsdp", split_axis=0, concat_axis=0, tiled=True),
    )
    slot_index = jnp.arange(vis_rows, dtype=jnp.int32)
    my_ranks = member * vis_rows + slot_index
    my_owner = jnp.take(owner_dev, my_ranks)
    my_row = jnp.take(row_of, my_ranks)
    picked = my_owner * vis_rows + slot_index
    bal_tokens = jnp.take(recv_tokens, picked, axis=0)
    bal_cot = jnp.take(recv_cot, picked, axis=0)
    seg_bal = jnp.take(segment, my_row)
    seg_keys = jnp.take(segment, row_of)
    cos_bal, sin_bal = rope_tables(jnp.take(places, my_row))
    inputs_bal, normed_bal, query_bal, key_bal, value_bal = project(
        bal_tokens, weights, cos_bal, sin_bal
    )
    key_vis, value_vis = (
        lax.all_gather(key_bal, "fsdp", axis=0, tiled=True),
        lax.all_gather(value_bal, "fsdp", axis=0, tiled=True),
    )
    attended_bal, log_total = attend(query_bal, key_vis, value_vis, seg_bal, seg_keys)
    result_bal, middle_bal, second_bal, hidden_bal, activated_bal = finish(
        inputs_bal, attended_bal, weights
    )
    grad_result = bal_cot.astype(jnp.float32)
    result_low = grad_result.astype(jnp.bfloat16)
    grad_fc2 = jnp.einsum(
        "nf,nd->fd", activated_bal, result_low, preferred_element_type=jnp.float32
    )
    grad_bfc2 = jnp.sum(result_low.astype(jnp.float32), axis=0)
    grad_activated = jnp.einsum(
        "nd,fd->nf", result_low, weights[10], preferred_element_type=jnp.float32
    )
    gelu_pull = jax.vjp(gelu_erf, hidden_bal)[1]
    hidden_low = gelu_pull(grad_activated)[0].astype(jnp.bfloat16)
    grad_fc1 = jnp.einsum("nd,nf->df", second_bal, hidden_low, preferred_element_type=jnp.float32)
    grad_bfc1 = jnp.sum(hidden_low.astype(jnp.float32), axis=0)
    grad_second = jnp.einsum(
        "nf,df->nd", hidden_low, weights[8], preferred_element_type=jnp.float32
    )
    norm_two_pull = jax.vjp(
        layer_norm, middle_bal, weights[6].astype(jnp.float32), weights[7].astype(jnp.float32)
    )[1]
    grad_mid_norm, grad_gain_two, grad_shift_two = norm_two_pull(grad_second)
    grad_middle = grad_result + grad_mid_norm
    middle_low = grad_middle.astype(jnp.bfloat16)
    grad_wout = jnp.einsum(
        "nd,ne->de", attended_bal, middle_low, preferred_element_type=jnp.float32
    )
    grad_bout = jnp.sum(middle_low.astype(jnp.float32), axis=0)
    grad_att = jnp.einsum(
        "ne,de->nd", middle_low, weights[4], preferred_element_type=jnp.float32
    ).astype(jnp.bfloat16)
    grad_query, grad_key_all, grad_value_all = attend_back(
        query_bal, key_vis, value_vis, seg_bal, seg_keys, log_total, grad_att
    )
    grad_key_own, grad_value_own = (
        lax.psum_scatter(
            grad_key_all.astype(jnp.bfloat16), "fsdp", scatter_dimension=0, tiled=True
        ).astype(jnp.float32),
        lax.psum_scatter(
            grad_value_all.astype(jnp.bfloat16), "fsdp", scatter_dimension=0, tiled=True
        ).astype(jnp.float32),
    )
    grad_query_pre = rotate_back(grad_query, cos_bal, sin_bal).reshape(vis_rows, model_width)
    grad_key_pre = rotate_back(
        grad_key_own.reshape(vis_rows, HEADS, HDIM), cos_bal, sin_bal
    ).reshape(vis_rows, model_width)
    joined_low = jnp.concatenate([grad_query_pre, grad_key_pre, grad_value_own], axis=1).astype(
        jnp.bfloat16
    )
    grad_wqkv = jnp.einsum("nd,ne->de", normed_bal, joined_low, preferred_element_type=jnp.float32)
    grad_bqkv = jnp.sum(joined_low.astype(jnp.float32), axis=0)
    grad_normed = jnp.einsum(
        "ne,de->nd", joined_low, weights[2], preferred_element_type=jnp.float32
    )
    norm_one_pull = jax.vjp(
        layer_norm, inputs_bal, weights[0].astype(jnp.float32), weights[1].astype(jnp.float32)
    )[1]
    grad_in_norm, grad_gain_one, grad_shift_one = norm_one_pull(grad_normed)
    grad_inputs = grad_middle + grad_in_norm
    destinations = jnp.arange(groups, dtype=jnp.int32)
    route_mask = (my_owner[None, :] == destinations[:, None])[:, :, None]
    send_out = jnp.where(route_mask, result_bal.astype(jnp.bfloat16)[None], zero_low).reshape(
        vis_pack, model_width
    )
    send_grad = jnp.where(route_mask, grad_inputs.astype(jnp.bfloat16)[None], zero_low).reshape(
        vis_pack, model_width
    )
    back_out, back_grad = (
        lax.all_to_all(send_out, "fsdp", split_axis=0, concat_axis=0, tiled=True),
        lax.all_to_all(send_grad, "fsdp", split_axis=0, concat_axis=0, tiled=True),
    )
    rank_home = jnp.maximum(jnp.take(inclusive, home_rows) - 1, 0)
    is_visible = (visible_here > 0)[:, None]
    context_out = jnp.where(is_visible, jnp.take(back_out, rank_home, axis=0), zero_low)
    tokens_grad = jnp.where(is_visible, jnp.take(back_grad, rank_home, axis=0), zero_low)
    grad_list = [
        grad_gain_one,
        grad_shift_one,
        grad_wqkv,
        grad_bqkv,
        grad_wout,
        grad_bout,
        grad_gain_two,
        grad_shift_two,
        grad_fc1,
        grad_bfc1,
        grad_fc2,
        grad_bfc2,
    ]
    reduced = (
        lax.psum_scatter(grad_list[0], ("dp", "fsdp"), scatter_dimension=0, tiled=True),
        lax.psum_scatter(grad_list[1], ("dp", "fsdp"), scatter_dimension=0, tiled=True),
        lax.psum_scatter(grad_list[2], ("dp", "fsdp"), scatter_dimension=0, tiled=True),
        lax.psum_scatter(grad_list[3], ("dp", "fsdp"), scatter_dimension=0, tiled=True),
        lax.psum_scatter(grad_list[4], ("dp", "fsdp"), scatter_dimension=0, tiled=True),
        lax.psum_scatter(grad_list[5], ("dp", "fsdp"), scatter_dimension=0, tiled=True),
        lax.psum_scatter(grad_list[6], ("dp", "fsdp"), scatter_dimension=0, tiled=True),
        lax.psum_scatter(grad_list[7], ("dp", "fsdp"), scatter_dimension=0, tiled=True),
        lax.psum_scatter(grad_list[8], ("dp", "fsdp"), scatter_dimension=0, tiled=True),
        lax.psum_scatter(grad_list[9], ("dp", "fsdp"), scatter_dimension=0, tiled=True),
        lax.psum_scatter(grad_list[10], ("dp", "fsdp"), scatter_dimension=0, tiled=True),
        lax.psum_scatter(grad_list[11], ("dp", "fsdp"), scatter_dimension=0, tiled=True),
    )
    return (
        target_out,
        context_out,
        tokens_grad,
        reduced[0],
        reduced[1],
        reduced[2],
        reduced[3],
        reduced[4],
        reduced[5],
        reduced[6],
        reduced[7],
        reduced[8],
        reduced[9],
        reduced[10],
        reduced[11],
    )


def per_device(tokens, *rest):
    n, group = lax.axis_size("dp"), lax.axis_size("fsdp")
    out_rows = rest[7].shape[0]
    fits = group == 4 and n == 8 and out_rows * group == 128
    return (on_device if fits else gathered_device)(tokens, *rest)


def solution(mesh):
    both = ("dp", "fsdp")
    vec, mat = P(both), P(both, None)
    return jax.shard_map(
        per_device,
        mesh=mesh,
        in_specs=(
            mat, P("dp", None), vec, P("dp", "fsdp"), vec, vec, mat, vec, mat, vec, vec, vec,
            mat, vec, mat, vec, mat,
        ),
        out_specs=(mat, mat, mat, vec, vec, mat, vec, mat, vec, vec, vec, mat, vec, mat, vec),
        check_vma=False,
    )
```
